32 devices in a mesh: fsdp: 16 (over z, y, core), seq: 2 (over x).
Axes of the slice: x: 2, y: 2, z: 4, core: 2. Of those that a mesh axis runs over, the one named last changes fastest.
Arguments:
- activations: bfloat16 [32, 736, 1152], P('fsdp', 'seq'), may hold values from -6 to 6
- group_image_count: int32 [16], P('fsdp'), may hold values from 1 to 2, as said below
- image_adapter_index: int32 [32], P('fsdp'), may hold values from 0 to 7
- lengths: int32 [32], P('fsdp'), may hold values from 644 to 736
- frozen: bfloat16 [2, 15269888], P(None, 'fsdp')
- attention_adapter_weights: bfloat16 [2, 8, 8, 16, 1152], replicated
- narrow_adapter_weights: bfloat16 [2, 2, 8, 16, 1152], replicated
- broad_adapter_weights: bfloat16 [2, 2, 8, 16, 4304], replicated
- cotangent: bfloat16 [32, 736, 1152], P('fsdp', 'seq'), may hold values from -6 to 6
Outputs:
- output: bfloat16 [32, 736, 1152], P('fsdp', 'seq')
- input_grad: float32 [32, 736, 1152], P('fsdp', 'seq')
- grad_attn: float32 [2, 8, 8, 16, 1152], replicated
- grad_narrow: float32 [2, 2, 8, 16, 1152], replicated
- grad_wide: float32 [2, 2, 8, 16, 4304], replicated
The draws below stay inside these ranges and needn't reach their ends.
Inputs may be any that keep to these rules, and one draw needn't show every extreme that they name: `group_image_count`: the images of a group fill its first slots. Some group holds 2 images and some other group holds one.
All inputs are finite; a program needn't handle non-finite values.
Results may differ from the reference program's by a relative error of at most 0.025.
Values may be sent and summed in bfloat16 or wider, within the bound.
A program may use at most 448 MiB of HBM per device.

```python
import math
import jax
import jax.numpy as jnp
from jax import lax

D = 1152
H = 16
HD = 72
FF = 4304
R = 16
E = 8
LEN = 736
SLOTS = 2
LAYERS = 2
GROUPS = 16
ROWS = 32
FLAT = 15269888


def draw_group_image_count(key, part):
    counts = jax.random.randint(jax.random.fold_in(key, 11), (GROUPS,), 1, SLOTS + 1)
    fullest = jax.random.randint(jax.random.fold_in(key, 12), (), 0, GROUPS)
    emptiest = (fullest + 1 + jax.random.randint(jax.random.fold_in(key, 13), (), 0, GROUPS - 1)) % GROUPS
    places = jnp.arange(GROUPS, dtype=jnp.int32)
    counts = jnp.where(places == fullest, SLOTS, counts)
    counts = jnp.where(places == emptiest, 1, counts)
    return counts.astype(jnp.int32)


def draw_frozen(key, part):
    random_part = jax.random.normal(jax.random.fold_in(key, 21), (LAYERS, FLAT), jnp.float32)
    position = jnp.arange(FLAT, dtype=jnp.int32)
    cut_qkv = 3 * D * D
    cut_out = cut_qkv + D * D
    cut_up = cut_out + D * FF
    cut_down = cut_up + FF * D
    column = position % (3 * D)
    scales = jnp.where(column < 2 * D, 1.5, 1.0) / math.sqrt(D)
    scales = jnp.where(position >= cut_qkv, 4.0 / math.sqrt(D), scales)
    scales = jnp.where(position >= cut_out, 1.0 / math.sqrt(D), scales)
    scales = jnp.where(position >= cut_up, 1.0 / math.sqrt(FF), scales)
    scales = jnp.where(position >= cut_down, 0.3, scales)
    gain_mask = (position >= cut_down) & (position < cut_down + D) | (position >= cut_down + 2 * D) & (position < cut_down + 3 * D)
    values = jnp.where(gain_mask[None, :], 1.0 + 0.1 * random_part, scales[None, :] * random_part)
    return values.astype(jnp.bfloat16)


def draw_attention_adapter_weights(key, part):
    random_part = jax.random.normal(jax.random.fold_in(key, 31), (LAYERS, 8, E, R, D), jnp.float32)
    role_index = jnp.arange(8, dtype=jnp.int32)
    scales = jnp.where(role_index < 4, 1.0 / math.sqrt(D), jnp.where(role_index == 7, 2.0, 0.5) / math.sqrt(R))
    return (random_part * scales[None, :, None, None, None]).astype(jnp.bfloat16)


def draw_narrow_adapter_weights(key, part):
    random_part = jax.random.normal(jax.random.fold_in(key, 41), (LAYERS, 2, E, R, D), jnp.float32)
    scales = jnp.array([1.0 / math.sqrt(D), 0.5 / math.sqrt(R)], jnp.float32)
    return (random_part * scales[None, :, None, None, None]).astype(jnp.bfloat16)


def draw_broad_adapter_weights(key, part):
    random_part = jax.random.normal(jax.random.fold_in(key, 51), (LAYERS, 2, E, R, FF), jnp.float32)
    scales = jnp.array([0.5 / math.sqrt(R), 1.0 / math.sqrt(FF)], jnp.float32)
    return (random_part * scales[None, :, None, None, None]).astype(jnp.bfloat16)


def plant(values, stream_key, smallest, largest):
    extent = values.shape
    place = [jax.random.randint(jax.random.fold_in(stream_key, axis), (), 0, extent[axis]) for axis in range(len(extent))]
    values = values.at[tuple(place)].set(smallest)
    longest = extent.index(max(extent))
    place[longest] = (place[longest] + 1) % extent[longest]
    return values.at[tuple(place)].set(largest)


def steps_of(rng, extent, pieces, low, top_value):
    level = 1.0
    for dim, parts in pieces:
        heights = jax.random.uniform(jax.random.fold_in(jax.random.fold_in(rng, 6), dim), (parts,), jnp.float32, low / len(pieces), top_value / len(pieces))
        level = level * jnp.repeat(jnp.exp(heights), extent[dim] // parts).reshape((-1,) + (1,) * (len(extent) - 1 - dim))
    return level


def bell_draw(key, dims, deviation, bound, cuts=(), held_as=jnp.bfloat16):
    entries = jax.random.normal(key, dims, jnp.float32) * deviation
    if len(cuts) > 0:
        entries = steps_of(key, dims, cuts, -0.22, 0.18) * entries
    return jnp.clip(entries, min=-bound, max=bound).astype(held_as)


def setup_inputs(seed: int = 0) -> dict:
    arg_keys = jax.random.split(jax.random.key(seed), 10)
    activations = bell_draw(arg_keys[0], (ROWS, LEN, D), 1.0, 6.0, ((0, 16), (1, 2)))
    group_image_count = draw_group_image_count(jax.random.fold_in(arg_keys[9], 71), 0)
    image_adapter_index = plant(jax.random.randint(arg_keys[2], (ROWS,), 0, E), jax.random.fold_in(arg_keys[2], 1), 0, E - 1).astype(jnp.int32)
    lengths = plant(jax.random.randint(arg_keys[3], (ROWS,), LEN - LEN // 8, LEN + 1), jax.random.fold_in(arg_keys[3], 1), LEN - LEN // 8, LEN).astype(jnp.int32)
    frozen = draw_frozen(jax.random.fold_in(arg_keys[9], 71), 0)
    attention_adapter_weights = draw_attention_adapter_weights(jax.random.fold_in(arg_keys[9], 71), 0)
    narrow_adapter_weights = draw_narrow_adapter_weights(jax.random.fold_in(arg_keys[9], 71), 0)
    broad_adapter_weights = draw_broad_adapter_weights(jax.random.fold_in(arg_keys[9], 71), 0)
    cotangent = bell_draw(arg_keys[8], (ROWS, LEN, D), 1.0, 6.0, ((0, 16), (1, 2)))
    return {"activations": activations, "group_image_count": group_image_count, "image_adapter_index": image_adapter_index, "lengths": lengths, "frozen": frozen, "attention_adapter_weights": attention_adapter_weights, "narrow_adapter_weights": narrow_adapter_weights, "broad_adapter_weights": broad_adapter_weights, "cotangent": cotangent}


epsilon = 1e-06
exact_product = lax.Precision.HIGHEST

@jax.custom_vjp
def low(v):
    return lax.optimization_barrier(v.astype(jnp.bfloat16)).astype(jnp.float32)

@jax.custom_vjp
def lowrank_backward(v):
    return v

def low_keep(v):
    return (low(v), None)

def low_pass(kept, grad):
    return (grad,)

def back_keep(v):
    return (v, None)

def back_low(kept, grad):
    return (low(grad),)
low.defvjp(low_keep, low_pass)
lowrank_backward.defvjp(back_keep, back_low)

def round_pair_values(tensor):
    return lowrank_backward(low(tensor))

def gelu_tanh(tensor):
    return 0.5 * tensor * (1.0 + jnp.tanh(0.7978845608028654 * (tensor + 0.044715 * tensor * tensor * tensor)))

def layer_norm(tensor, gain, offset):
    average = lax.optimization_barrier(jnp.mean(tensor, axis=-1, keepdims=True))
    centred = tensor - average
    variance = lax.optimization_barrier(jnp.mean(centred * centred, axis=-1, keepdims=True))
    return centred * lax.rsqrt(variance + epsilon) * gain + offset

def unpack(flat_weights):
    cut_qkv = D * 3 * D
    cut_out = cut_qkv + D * D
    cut_up = cut_out + D * FF
    cut_down = cut_up + FF * D
    w_qkv = flat_weights[:cut_qkv].reshape(D, 3 * D)
    output_weight = flat_weights[cut_qkv:cut_out].reshape(D, D)
    up_weight = flat_weights[cut_out:cut_up].reshape(D, FF)
    down_weight = flat_weights[cut_up:cut_down].reshape(FF, D)
    token_vectors = flat_weights[cut_down:cut_down + 8 * D].reshape(8, D)
    up_bias = flat_weights[cut_down + 8 * D:cut_down + 8 * D + FF]
    return (w_qkv, output_weight, up_weight, down_weight, token_vectors, up_bias)

def attend(inputs_slot):
    query, key_block, value_block, valid_keys = inputs_slot
    scores = lowrank_backward(jnp.einsum('qhd,khd->hqk', query, key_block, precision=exact_product) * (1.0 / math.sqrt(HD)))
    scores = jnp.where(valid_keys[None, None, :], scores, -1e+30)
    highest = lax.optimization_barrier(jnp.max(scores, axis=-1, keepdims=True))
    weights = jnp.exp(scores - highest)
    probable = weights / lax.optimization_barrier(jnp.sum(weights, axis=-1, keepdims=True))
    return jnp.einsum('hqk,khd->qhd', low(probable), value_block, precision=exact_product).reshape(LEN, D)

def group_forward(hidden, row_mask, valid_keys, select_adapter_rows, frozen_wide, attn_table, narrow_table, wide_table):
    for current_layer_index in range(LAYERS):
        w_qkv, output_weight, up_weight, down_weight, token_vectors, up_bias = unpack(frozen_wide[current_layer_index])
        select_attention_adapters = jnp.einsum('se,cerd->scrd', select_adapter_rows, attn_table[current_layer_index], precision=exact_product)
        select_narrow_adapters = jnp.einsum('se,cerd->scrd', select_adapter_rows, narrow_table[current_layer_index], precision=exact_product)
        select_broad_adapters = jnp.einsum('se,cerd->scrd', select_adapter_rows, wide_table[current_layer_index], precision=exact_product)
        normalized_input = low(layer_norm(hidden, token_vectors[0], token_vectors[1]))
        inner_query_key_value = round_pair_values(jnp.einsum('zqx,zohx->zqoh', normalized_input, select_attention_adapters[:, 0:3], precision=exact_product))
        lifted = jnp.einsum('slcr,scrd->slcd', inner_query_key_value, select_attention_adapters[:, 4:7], precision=exact_product).reshape(SLOTS, LEN, 3 * D)
        bias_qkv = jnp.concatenate([token_vectors[4], jnp.zeros((D,), jnp.float32), token_vectors[5]])
        qkv = round_pair_values(jnp.dot(normalized_input, w_qkv, precision=exact_product) + bias_qkv + lifted)
        heads = qkv.reshape(SLOTS, LEN, 3, H, HD)
        attention_output = round_pair_values(lax.map(jax.checkpoint(attend), (heads[:, :, 0], heads[:, :, 1], heads[:, :, 2], valid_keys)))
        inner_output = round_pair_values(jnp.einsum('mxb,mkb->mxk', attention_output, select_attention_adapters[:, 3], precision=exact_product))
        residual_branch = lowrank_backward(jnp.dot(attention_output, output_weight, precision=exact_product) + token_vectors[6] + jnp.einsum('cgy,cyz->cgz', inner_output, select_attention_adapters[:, 7], precision=exact_product))
        middle = hidden + residual_branch
        second_normalized_input = low(layer_norm(middle, token_vectors[2], token_vectors[3]))
        inner_upward = round_pair_values(jnp.einsum('mxb,mkb->mxk', second_normalized_input, select_narrow_adapters[:, 0], precision=exact_product))
        gate_pre = lowrank_backward(jnp.dot(second_normalized_input, up_weight, precision=exact_product) + up_bias + jnp.einsum('slr,srf->slf', inner_upward, select_broad_adapters[:, 0], precision=exact_product))
        gelu_applied = low(gelu_tanh(gate_pre))
        inner_downward = round_pair_values(jnp.einsum('slf,srf->slr', gelu_applied, select_broad_adapters[:, 1], precision=exact_product))
        second_residual_branch = lowrank_backward(jnp.dot(gelu_applied, down_weight, precision=exact_product) + token_vectors[7] + jnp.einsum('cgy,cyz->cgz', inner_downward, select_narrow_adapters[:, 1], precision=exact_product))
        hidden = middle + second_residual_branch
    return hidden * row_mask[..., None]

def reference(activations, group_image_count, image_adapter_index, lengths, frozen, attention_adapter_weights, narrow_adapter_weights, broad_adapter_weights, cotangent):
    positions = jnp.arange(LEN, dtype=jnp.int32)
    slot_place = jnp.arange(ROWS, dtype=jnp.int32) % SLOTS
    is_live = slot_place < jnp.repeat(group_image_count, SLOTS, total_repeat_length=ROWS)
    valid_keys = positions[None, :] < lengths[:, None]
    row_mask = (valid_keys & is_live[:, None]).astype(jnp.float32)
    select_adapter_rows = (image_adapter_index[:, None] == jnp.arange(E, dtype=jnp.int32)[None, :]).astype(jnp.float32)
    frozen_wide = frozen.astype(jnp.float32)

    def forward_layers(inputs, attn_table, narrow_table, wide_table):

        def group_step(unused, group):
            hidden, mask_rows, keys_valid, select_rows = group
            result = group_forward(hidden * mask_rows[..., None], mask_rows, keys_valid, select_rows, frozen_wide, attn_table, narrow_table, wide_table)
            return (unused, result)
        grouped = (inputs.reshape(GROUPS, SLOTS, LEN, D), row_mask.reshape(GROUPS, SLOTS, LEN), valid_keys.reshape(GROUPS, SLOTS, LEN), select_adapter_rows.reshape(GROUPS, SLOTS, E))
        unused, result = lax.scan(jax.checkpoint(group_step), jnp.zeros((), jnp.float32), grouped)
        return result.reshape(ROWS, LEN, D)
    output, vector_jacobian_product = jax.vjp(forward_layers, activations.astype(jnp.float32), attention_adapter_weights.astype(jnp.float32), narrow_adapter_weights.astype(jnp.float32), broad_adapter_weights.astype(jnp.float32))
    input_grad, grad_attn, grad_narrow, grad_wide = vector_jacobian_product(cotangent.astype(jnp.float32))
    return (output.astype(jnp.bfloat16), input_grad, grad_attn, grad_narrow, grad_wide)
```

```python
import functools
import math

import jax
import jax.numpy as jnp
from jax import lax
from jax.experimental import pallas as pl
from jax.experimental.pallas import tpu as pltpu
from jax.sharding import PartitionSpec as P

D = 1152
HD = 72
H = 16
FF = 4304
R = 16
LANES = 128
BF16 = jnp.bfloat16
F32 = jnp.float32
VMEM_LIMIT = 60 << 20
C2 = math.log2(math.e) / math.sqrt(HD)
SCALE = 1.0 / math.sqrt(HD)
NEG = -1e30
epsilon = 1e-06
CUT_OUT = 3 * D * D // LANES
CUT_UP = CUT_OUT + D * D // LANES
CUT_DOWN = CUT_UP + D * FF // LANES
CUT_VECTORS = CUT_DOWN + FF * D // LANES


def dot(a, b):
    return jnp.dot(a, b, preferred_element_type=F32)


def dot_t(a, b):
    return lax.dot_general(a, b, (((1,), (1,)), ((), ())), preferred_element_type=F32)


def dot_l(a, b):
    return lax.dot_general(a, b, (((0,), (0,)), ((), ())), preferred_element_type=F32)


def rows_aligned_kernel(panels, rows, in_ref, out_ref, wide):
    wide[...] = in_ref[...].astype(F32)
    for c in range(panels):
        out_ref[:, c * LANES : (c + 1) * LANES] = wide[pl.ds(c, rows, stride=panels), :].astype(BF16)


def rows_aligned(flat, start, count, panels, rows):
    step = rows * panels
    return pl.pallas_call(
        functools.partial(rows_aligned_kernel, panels, rows),
        grid=(pl.cdiv(count, rows),),
        in_specs=[
            pl.BlockSpec(
                (pl.Element(step), pl.Element(LANES)),
                lambda i: (pl.multiple_of(start + i * step, 16), 0),
            )
        ],
        out_specs=pl.BlockSpec((rows, panels * LANES), lambda i: (i, 0)),
        out_shape=jax.ShapeDtypeStruct((count, panels * LANES), BF16),
        scratch_shapes=[pltpu.VMEM((step, LANES), F32)],
        cost_estimate=pl.CostEstimate(
            flops=0, bytes_accessed=4 * count * panels * LANES, transcendentals=0
        ),
        compiler_params=pltpu.CompilerParams(vmem_limit_bytes=VMEM_LIMIT),
        name="weight_rows",
    )(flat)


PERIOD = 8
PERIOD_ROWS = PERIOD * FF // LANES


def rows_odd_kernel(rows, in_ref, out_ref, wide, turned):
    groups = rows // PERIOD
    panels = -(-FF // LANES)
    wide[...] = in_ref[...].astype(F32)
    lane = lax.broadcasted_iota(jnp.int32, (groups, LANES), 1)
    for j in range(PERIOD):
        first, shift = (FF * j) // LANES, (FF * j) % LANES
        held = wide[pl.ds(first, groups, stride=PERIOD_ROWS), :]
        for c in range(panels):
            after = min(first + c + 1, PERIOD_ROWS - 1)
            after = wide[pl.ds(after, groups, stride=PERIOD_ROWS), :]
            value = held
            if shift:
                value = jnp.where(
                    lane < LANES - shift,
                    pltpu.roll(held, LANES - shift, 1),
                    pltpu.roll(after, LANES - shift, 1),
                )
            held = after
            turned[pl.ds(c * rows + j, groups, stride=PERIOD), :] = value
    for c in range(panels):
        width = min(LANES, FF - c * LANES)
        out_ref[:, c * LANES : c * LANES + width] = turned[pl.ds(c * rows, rows), :][:, :width].astype(BF16)


def rows_odd(flat, start, count, rows):
    step = rows * FF // LANES
    return pl.pallas_call(
        functools.partial(rows_odd_kernel, rows),
        grid=(count // rows,),
        in_specs=[
            pl.BlockSpec(
                (pl.Element(step), pl.Element(LANES)),
                lambda i: (pl.multiple_of(start + i * step, 16), 0),
            )
        ],
        out_specs=pl.BlockSpec((rows, FF), lambda i: (i, 0)),
        out_shape=jax.ShapeDtypeStruct((count, FF), BF16),
        scratch_shapes=[
            pltpu.VMEM((step, LANES), F32),
            pltpu.VMEM((-(-FF // LANES) * rows, LANES), F32),
        ],
        cost_estimate=pl.CostEstimate(flops=0, bytes_accessed=4 * count * FF, transcendentals=0),
        compiler_params=pltpu.CompilerParams(vmem_limit_bytes=VMEM_LIMIT),
        name="weight_rows_odd",
    )(flat)


def unpack(flat):
    return (
        rows_aligned(flat, 0, D, 3 * D // LANES, 64),
        rows_aligned(flat, CUT_OUT, D, D // LANES, 192),
        rows_odd(flat, CUT_UP, D, 128),
        rows_aligned(flat, CUT_DOWN, FF, D // LANES, 288),
    )


def pad_lanes(x, extra=None):
    if extra is None:
        extra = jnp.zeros((x.shape[0], LANES - HD), x.dtype)
    return jnp.concatenate([x, extra], axis=1)


def first_lane(rows, value):
    lane = lax.broadcasted_iota(jnp.int32, (rows, LANES - HD), 1)
    return jnp.where(lane == 0, value, 0.0).astype(BF16)


def key_bias(rows, length):
    key = lax.broadcasted_iota(jnp.int32, (rows, LANES - HD), 0)
    return first_lane(rows, jnp.where(key < length, 0.0, NEG))


def attn_fwd_kernel(offset, len_ref, qkv_ref, kv_ref, o_ref, st_ref, q_s, k_s, v_s):
    if kv_ref is None:
        kv_ref = qkv_ref
    rows, keys = qkv_ref.shape[0], kv_ref.shape[0]
    one = first_lane(rows, F32(1.0))
    bias = key_bias(keys, len_ref[0])
    for h in range(H):
        q_s[h] = pad_lanes(qkv_ref[:, h * HD : (h + 1) * HD], one)
        k_s[h] = pad_lanes(kv_ref[:, offset + h * HD : offset + (h + 1) * HD], bias)
        v_s[h] = pad_lanes(kv_ref[:, offset + D + h * HD : offset + D + (h + 1) * HD])
    st_ref[...] = jnp.zeros_like(st_ref)
    lane = lax.broadcasted_iota(jnp.int32, (rows, LANES), 1)

    def body(h, carry):
        s = dot_t(q_s[h], k_s[h])
        m = jnp.max(s, axis=1, keepdims=True)
        p = jnp.exp2((s - m) * C2)
        total = jnp.sum(p, axis=1, keepdims=True)
        o = dot(p.astype(BF16), v_s[h])
        q_s[h] = (o * (1.0 / total)).astype(BF16)
        st_ref[...] = jnp.where(lane == h, m * C2 + jnp.log2(total), st_ref[...])
        return carry

    lax.fori_loop(0, H, body, 0)
    for h in range(H):
        o_ref[:, h * HD : (h + 1) * HD] = q_s[h][:, :HD]


def attn_fwd(length, qkv, kv=None):
    rows = qkv.shape[0]
    keys = rows if kv is None else kv.shape[0]
    vm = pl.BlockSpec(memory_space=pltpu.VMEM)
    if kv is None:
        kernel = lambda a, b, *rest: attn_fwd_kernel(D, a, b, None, *rest)
        operands = (length, qkv)
    else:
        kernel = functools.partial(attn_fwd_kernel, 0)
        operands = (length, qkv, kv)
    return pl.pallas_call(
        kernel,
        in_specs=[pl.BlockSpec(memory_space=pltpu.SMEM)] + [vm] * (len(operands) - 1),
        out_specs=[vm, vm],
        out_shape=[
            jax.ShapeDtypeStruct((rows, D), BF16),
            jax.ShapeDtypeStruct((rows, LANES), F32),
        ],
        scratch_shapes=[
            pltpu.VMEM((H, rows, LANES), BF16),
            pltpu.VMEM((H, keys, LANES), BF16),
            pltpu.VMEM((H, keys, LANES), BF16),
        ],
        cost_estimate=pl.CostEstimate(
            flops=H * rows * keys * 256 * 4, bytes_accessed=rows * D * 8, transcendentals=H * rows * keys
        ),
        compiler_params=pltpu.CompilerParams(vmem_limit_bytes=VMEM_LIMIT),
        name="attention_forward",
    )(*operands)


def attn_bwd_kernel(
    offset, len_ref, qkv_ref, kv_ref, do_ref, o_ref, st_ref, dq_ref, dkv_ref, q_s, k_s, v_s, do_s, st_t, dl_t
):
    if kv_ref is None:
        kv_ref, dkv_ref = qkv_ref, dq_ref
    rows, keys = qkv_ref.shape[0], kv_ref.shape[0]
    one = first_lane(rows, F32(1.0))
    bias = key_bias(keys, len_ref[0])
    lane = lax.broadcasted_iota(jnp.int32, (rows, LANES), 1)
    delta = jnp.zeros((rows, LANES), F32)
    for h in range(H):
        q_s[h] = pad_lanes(qkv_ref[:, h * HD : (h + 1) * HD], one)
        k_s[h] = pad_lanes(kv_ref[:, offset + h * HD : offset + (h + 1) * HD], bias)
        v_s[h] = pad_lanes(kv_ref[:, offset + D + h * HD : offset + D + (h + 1) * HD])
        do = do_ref[:, h * HD : (h + 1) * HD]
        do_s[h] = pad_lanes(do)
        o = o_ref[:, h * HD : (h + 1) * HD].astype(F32)
        d = jnp.sum(do.astype(F32) * o, axis=1, keepdims=True)
        delta = jnp.where(lane == h, d, delta)
    st_t[...] = st_ref[...].T
    dl_t[...] = delta.T

    def body(h, carry):
        q, k, do = q_s[h], k_s[h], do_s[h]
        p = jnp.exp2(dot_t(k, q) * C2 - st_t[pl.ds(h, 1), :])
        dv = dot(p.astype(BF16), do)
        dp = dot_t(v_s[h], do)
        ds = (p * (dp - dl_t[pl.ds(h, 1), :])).astype(BF16)
        dk = dot(ds, q)
        dq = dot(k.T, ds)
        v_s[h] = dv.astype(BF16)
        k_s[h] = (dk * SCALE).astype(BF16)
        q_s[h] = (dq * SCALE).astype(BF16).T
        return carry

    lax.fori_loop(0, H, body, 0)
    for h in range(H):
        dq_ref[:, h * HD : (h + 1) * HD] = q_s[h][:, :HD]
        dkv_ref[:, offset + h * HD : offset + (h + 1) * HD] = k_s[h][:, :HD]
        dkv_ref[:, offset + D + h * HD : offset + D + (h + 1) * HD] = v_s[h][:, :HD]


def attn_bwd(length, qkv, do, o, st, kv=None):
    rows = qkv.shape[0]
    keys = rows if kv is None else kv.shape[0]
    vm = pl.BlockSpec(memory_space=pltpu.VMEM)
    if kv is None:
        kernel = lambda a, b, c, d, e, f, *rest: attn_bwd_kernel(
            D, a, b, None, c, d, e, f, None, *rest
        )
        operands = (length, qkv, do, o, st)
        outs = [jax.ShapeDtypeStruct((rows, 3 * D), BF16)]
    else:
        kernel = functools.partial(attn_bwd_kernel, 0)
        operands = (length, qkv, kv, do, o, st)
        outs = [jax.ShapeDtypeStruct((rows, D), BF16), jax.ShapeDtypeStruct((keys, 2 * D), BF16)]
    return pl.pallas_call(
        kernel,
        in_specs=[pl.BlockSpec(memory_space=pltpu.SMEM)] + [vm] * (len(operands) - 1),
        out_specs=[vm] * len(outs),
        out_shape=outs,
        scratch_shapes=[
            pltpu.VMEM((H, rows, LANES), BF16),
            pltpu.VMEM((H, keys, LANES), BF16),
            pltpu.VMEM((H, keys, LANES), BF16),
            pltpu.VMEM((H, rows, LANES), BF16),
            pltpu.VMEM((LANES, rows), F32),
            pltpu.VMEM((LANES, rows), F32),
        ],
        cost_estimate=pl.CostEstimate(
            flops=H * rows * keys * 256 * 10, bytes_accessed=rows * D * 16, transcendentals=H * rows * keys
        ),
        compiler_params=pltpu.CompilerParams(vmem_limit_bytes=VMEM_LIMIT),
        name="attention_backward",
    )(*operands)


def gelu_tanh(tensor):
    return (
        0.5
        * tensor
        * (1.0 + jnp.tanh(0.7978845608028654 * (tensor + 0.044715 * tensor * tensor * tensor)))
    )


def layer_norm(tensor, gain, offset):
    average = jnp.mean(tensor, axis=-1, keepdims=True)
    centred = tensor - average
    variance = jnp.mean(centred * centred, axis=-1, keepdims=True)
    return centred * lax.rsqrt(variance + epsilon) * gain + offset


def local(
    activations,
    group_image_count,
    image_adapter_index,
    lengths,
    frozen,
    attention_adapter_weights,
    narrow_adapter_weights,
    broad_adapter_weights,
    cotangent,
):
    slots, local_len, _ = activations.shape
    seq_parts = lax.axis_size("seq")
    fsdp_parts = lax.axis_size("fsdp")
    device_count = seq_parts * fsdp_parts
    me = lax.axis_index("seq")
    seq_total = local_len * seq_parts
    layer_count = frozen.shape[0]
    adapters = attention_adapter_weights.shape[2]
    parts = seq_parts // slots
    slot = me // parts
    part = me % parts
    tokens = seq_total // parts
    groups = [[s * parts + p for p in range(parts)] for s in range(slots)]

    def to_image(v):
        if parts == 1 and slots == 2:
            mine = lax.dynamic_index_in_dim(v, slot, 0, keepdims=False)
            other = lax.dynamic_index_in_dim(v, 1 - slot, 0, keepdims=False)
            other = lax.ppermute(other, "seq", [(0, 1), (1, 0)])
            return jnp.where(
                slot == 0,
                jnp.concatenate([mine, other], 0),
                jnp.concatenate([other, mine], 0),
            )
        whole = lax.all_gather(v, "seq", axis=1, tiled=True)
        whole = lax.dynamic_index_in_dim(whole, slot, 0, keepdims=False)
        return lax.dynamic_slice_in_dim(whole, part * tokens, tokens, 0)

    def to_tokens(v):
        if parts == 1 and slots == 2:
            mine = lax.dynamic_slice_in_dim(v, slot * local_len, local_len, 0)
            other = lax.dynamic_slice_in_dim(v, (1 - slot) * local_len, local_len, 0)
            other = lax.ppermute(other, "seq", [(0, 1), (1, 0)])
            return jnp.where(slot == 0, jnp.stack([mine, other]), jnp.stack([other, mine]))
        whole = lax.all_gather(v, "seq", axis=0, tiled=True).reshape(slots, seq_total, -1)
        return lax.dynamic_slice_in_dim(whole, me * local_len, local_len, 1)

    length = lax.dynamic_slice_in_dim(lengths, slot, 1, 0)
    adapter = lax.dynamic_index_in_dim(image_adapter_index, slot, 0, keepdims=False)
    is_live = slot < group_image_count[0]
    positions = part * tokens + jnp.arange(tokens, dtype=jnp.int32)
    row_mask = ((positions < length[0]) & is_live).astype(F32)[:, None]
    adapter_of = lax.all_gather(adapter, ("fsdp", "seq"))
    choice = (
        jnp.arange(adapters, dtype=jnp.int32)[:, None] == adapter_of[None, :]
    ).astype(F32)

    def pick(table):
        return lax.dynamic_index_in_dim(table, adapter, 1, keepdims=False)

    hidden = to_image(activations).astype(F32) * row_mask
    stored = []
    weights = []
    for layer in range(layer_count):
        flat = lax.all_gather(frozen[layer].reshape(-1, LANES), "fsdp", axis=0, tiled=True)
        w_qkv, w_o, w_1, w_2 = unpack(flat)
        vectors = lax.slice_in_dim(flat, CUT_VECTORS, CUT_VECTORS + 106, axis=0).reshape(-1)
        vectors, b_1 = vectors[: 8 * D].reshape(8, D).astype(F32), vectors[8 * D : 8 * D + FF]
        b_1 = b_1.astype(F32)
        attn = pick(attention_adapter_weights[layer])
        narrow = pick(narrow_adapter_weights[layer])
        wide = pick(broad_adapter_weights[layer])
        weights.append((w_qkv, w_o, w_1, w_2, vectors, attn, narrow, wide))
        normed = layer_norm(hidden, vectors[0], vectors[1]).astype(BF16)
        inner_qkv = dot_t(normed, attn[0:3].reshape(3 * R, D)).astype(BF16)
        lifted = jnp.concatenate(
            [dot(inner_qkv[:, c * R : (c + 1) * R], attn[4 + c]) for c in range(3)], axis=1
        )
        bias_qkv = jnp.concatenate([vectors[4], jnp.zeros((D,), F32), vectors[5]])
        qkv = (dot(normed, w_qkv) + bias_qkv + lifted).astype(BF16)
        keys = None
        if parts > 1:
            keys = lax.all_gather(
                qkv[:, D:], "seq", axis=0, tiled=True, axis_index_groups=groups
            )
        attended, stats = attn_fwd(length, qkv, keys)
        inner_o = dot_t(attended, attn[3]).astype(BF16)
        middle = hidden + (dot(attended, w_o) + vectors[6] + dot(inner_o, attn[7]))
        normed_two = layer_norm(middle, vectors[2], vectors[3]).astype(BF16)
        inner_up = dot_t(normed_two, narrow[0]).astype(BF16)
        gate = dot(normed_two, w_1) + b_1 + dot(inner_up, wide[0])
        activated = gelu_tanh(gate).astype(BF16)
        inner_down = dot_t(activated, wide[1]).astype(BF16)
        stored.append(
            (
                hidden,
                normed,
                inner_qkv,
                qkv,
                keys,
                stats,
                attended,
                inner_o,
                middle,
                normed_two,
                inner_up,
                gate,
                activated,
                inner_down,
            )
        )
        hidden = middle + (dot(activated, w_2) + vectors[7] + dot(inner_down, narrow[1]))
    output = to_tokens((hidden * row_mask).astype(BF16))
    gradient = to_image(cotangent).astype(F32) * row_mask
    collected = [None] * layer_count
    for layer in reversed(range(layer_count)):
        (
            layer_input,
            normed,
            inner_qkv,
            qkv,
            keys,
            stats,
            attended,
            inner_o,
            middle,
            normed_two,
            inner_up,
            gate,
            activated,
            inner_down,
        ) = stored[layer]
        w_qkv, w_o, w_1, w_2, vectors, attn, narrow, wide = weights[layer]
        d_branch = gradient.astype(BF16)
        d_inner_down = dot_t(d_branch, narrow[1]).astype(BF16)
        up_second = dot_l(inner_down, d_branch)
        d_activated = dot_t(d_branch, w_2) + dot(d_inner_down, wide[1])
        down_second = dot_l(d_inner_down, activated)
        d_gate = jax.vjp(gelu_tanh, gate)[1](d_activated)[0].astype(BF16)
        d_inner_up = dot_t(d_gate, wide[0]).astype(BF16)
        up_first = dot_l(inner_up, d_gate)
        d_normed_two = dot_t(d_gate, w_1) + dot(d_inner_up, narrow[0])
        down_first = dot_l(d_inner_up, normed_two)
        norm_two = jax.vjp(lambda t: layer_norm(t, vectors[2], vectors[3]), middle)[1]
        d_middle = gradient + norm_two(d_normed_two)[0]
        d_out = d_middle.astype(BF16)
        d_inner_o = dot_t(d_out, attn[7]).astype(BF16)
        up_o = dot_l(inner_o, d_out)
        d_attended = (dot_t(d_out, w_o) + dot(d_inner_o, attn[3])).astype(BF16)
        down_o = dot_l(d_inner_o, attended)
        d_qkv = attn_bwd(length, qkv, d_attended, attended, stats, keys)
        if parts > 1:
            d_keys = lax.psum_scatter(
                d_qkv[1].astype(F32),
                "seq",
                scatter_dimension=0,
                tiled=True,
                axis_index_groups=groups,
            )
            d_qkv = jnp.concatenate([d_qkv[0], d_keys.astype(BF16)], axis=1)
        else:
            d_qkv = d_qkv[0]
        d_inner_qkv = jnp.concatenate(
            [dot_t(d_qkv[:, c * D : (c + 1) * D], attn[4 + c]) for c in range(3)], axis=1
        ).astype(BF16)
        up_qkv = jnp.stack(
            [
                dot_l(inner_qkv[:, c * R : (c + 1) * R], d_qkv[:, c * D : (c + 1) * D])
                for c in range(3)
            ]
        )
        d_normed = dot_t(d_qkv, w_qkv) + dot(d_inner_qkv, attn[0:3].reshape(3 * R, D))
        down_qkv = dot_l(d_inner_qkv, normed).reshape(3, R, D)
        norm_one = jax.vjp(lambda t: layer_norm(t, vectors[0], vectors[1]), layer_input)[1]
        gradient = d_middle + norm_one(d_normed)[0]
        rows_narrow = jnp.concatenate(
            [
                down_qkv.reshape(3 * R, D),
                down_o,
                up_qkv.reshape(3 * R, D),
                up_o,
                down_first,
                up_second,
            ]
        ).astype(BF16)
        rows_wide = jnp.concatenate([up_first, down_second]).astype(BF16)

        def total(rows):
            count, width = rows.shape
            share = -(-count // device_count)
            rows = jnp.pad(rows, ((0, share * device_count - count), (0, 0)))
            mine = lax.all_to_all(
                rows.reshape(device_count, share * width),
                ("fsdp", "seq"),
                split_axis=0,
                concat_axis=0,
                tiled=True,
            )
            mine = jnp.dot(choice, mine.astype(F32), precision=lax.Precision.HIGHEST)
            every = lax.all_gather(
                mine.astype(BF16).reshape(1, adapters, share, width), ("fsdp", "seq"), tiled=True
            )
            every = every.transpose(1, 0, 2, 3).reshape(adapters, device_count * share, width)
            every = every[:, :count].reshape(adapters, count // R, R, width)
            return every.transpose(1, 0, 2, 3).astype(F32)

        collected[layer] = (total(rows_narrow), total(rows_wide))
    grad_attn = jnp.stack([entry[0][0:8] for entry in collected], axis=0)
    grad_narrow = jnp.stack([entry[0][8:10] for entry in collected], axis=0)
    grad_wide = jnp.stack([entry[1] for entry in collected], axis=0)
    input_grad = to_tokens((gradient * row_mask).astype(BF16)).astype(F32)
    return (output, input_grad, grad_attn, grad_narrow, grad_wide)


def solution(mesh):
    in_specs = (
        P("fsdp", "seq", None),
        P("fsdp"),
        P("fsdp"),
        P("fsdp"),
        P(None, "fsdp"),
        P(),
        P(),
        P(),
        P("fsdp", "seq", None),
    )
    out_specs = (P("fsdp", "seq", None), P("fsdp", "seq", None), P(), P(), P())
    return jax.shard_map(local, mesh=mesh, in_specs=in_specs, out_specs=out_specs, check_vma=False)
```

```python
import functools
import math

import jax
import jax.numpy as jnp
from jax import lax
from jax.experimental import pallas as pl
from jax.experimental.pallas import tpu as pltpu
from jax.sharding import PartitionSpec as P

D = 1152
HD = 72
H = 16
FF = 4304
R = 16
LANES = 128
BF16 = jnp.bfloat16
F32 = jnp.float32
MESH = pl.DeviceIdType.MESH
VMEM_LIMIT = 60 << 20
C2 = math.log2(math.e) / math.sqrt(HD)
SCALE = 1.0 / math.sqrt(HD)
NEG = -1e30
epsilon = 1e-06
CUT_OUT = 3 * D * D // LANES
CUT_UP = CUT_OUT + D * D // LANES
CUT_DOWN = CUT_UP + D * FF // LANES
CUT_VECTORS = CUT_DOWN + FF * D // LANES


def dot(a, b):
    return jnp.dot(a, b, preferred_element_type=F32)


def dot_t(a, b):
    return lax.dot_general(a, b, (((1,), (1,)), ((), ())), preferred_element_type=F32)


def dot_l(a, b):
    return lax.dot_general(a, b, (((0,), (0,)), ((), ())), preferred_element_type=F32)


def rows_aligned_kernel(panels, rows, in_ref, out_ref, wide):
    wide[...] = in_ref[...].astype(F32)
    for c in range(panels):
        out_ref[:, c * LANES : (c + 1) * LANES] = wide[pl.ds(c, rows, stride=panels), :].astype(BF16)


def rows_aligned(flat, start, count, panels, rows):
    step = rows * panels
    return pl.pallas_call(
        functools.partial(rows_aligned_kernel, panels, rows),
        grid=(pl.cdiv(count, rows),),
        in_specs=[
            pl.BlockSpec(
                (pl.Element(step), pl.Element(LANES)),
                lambda i: (pl.multiple_of(start + i * step, 16), 0),
            )
        ],
        out_specs=pl.BlockSpec((rows, panels * LANES), lambda i: (i, 0)),
        out_shape=jax.ShapeDtypeStruct((count, panels * LANES), BF16),
        scratch_shapes=[pltpu.VMEM((step, LANES), F32)],
        cost_estimate=pl.CostEstimate(
            flops=0, bytes_accessed=4 * count * panels * LANES, transcendentals=0
        ),
        compiler_params=pltpu.CompilerParams(vmem_limit_bytes=VMEM_LIMIT),
        name="weight_rows",
    )(flat)


PERIOD = 8
PERIOD_ROWS = PERIOD * FF // LANES


def rows_odd_kernel(rows, in_ref, out_ref, wide, turned):
    groups = rows // PERIOD
    panels = -(-FF // LANES)
    wide[...] = in_ref[...].astype(F32)
    lane = lax.broadcasted_iota(jnp.int32, (groups, LANES), 1)
    for j in range(PERIOD):
        first, shift = (FF * j) // LANES, (FF * j) % LANES
        held = wide[pl.ds(first, groups, stride=PERIOD_ROWS), :]
        for c in range(panels):
            after = min(first + c + 1, PERIOD_ROWS - 1)
            after = wide[pl.ds(after, groups, stride=PERIOD_ROWS), :]
            value = held
            if shift:
                value = jnp.where(
                    lane < LANES - shift,
                    pltpu.roll(held, LANES - shift, 1),
                    pltpu.roll(after, LANES - shift, 1),
                )
            held = after
            turned[pl.ds(c * rows + j, groups, stride=PERIOD), :] = value
    for c in range(panels):
        width = min(LANES, FF - c * LANES)
        out_ref[:, c * LANES : c * LANES + width] = turned[pl.ds(c * rows, rows), :][:, :width].astype(BF16)


def rows_odd(flat, start, count, rows):
    step = rows * FF // LANES
    return pl.pallas_call(
        functools.partial(rows_odd_kernel, rows),
        grid=(count // rows,),
        in_specs=[
            pl.BlockSpec(
                (pl.Element(step), pl.Element(LANES)),
                lambda i: (pl.multiple_of(start + i * step, 16), 0),
            )
        ],
        out_specs=pl.BlockSpec((rows, FF), lambda i: (i, 0)),
        out_shape=jax.ShapeDtypeStruct((count, FF), BF16),
        scratch_shapes=[
            pltpu.VMEM((step, LANES), F32),
            pltpu.VMEM((-(-FF // LANES) * rows, LANES), F32),
        ],
        cost_estimate=pl.CostEstimate(flops=0, bytes_accessed=4 * count * FF, transcendentals=0),
        compiler_params=pltpu.CompilerParams(vmem_limit_bytes=VMEM_LIMIT),
        name="weight_rows_odd",
    )(flat)


def unpack(flat):
    return (
        rows_aligned(flat, 0, D, 3 * D // LANES, 64),
        rows_aligned(flat, CUT_OUT, D, D // LANES, 192),
        rows_odd(flat, CUT_UP, D, 128),
        rows_aligned(flat, CUT_DOWN, FF, D // LANES, 288),
    )


def pad_lanes(x, extra=None):
    if extra is None:
        extra = jnp.zeros((x.shape[0], LANES - HD), x.dtype)
    return jnp.concatenate([x, extra], axis=1)


def first_lane(rows, value):
    lane = lax.broadcasted_iota(jnp.int32, (rows, LANES - HD), 1)
    return jnp.where(lane == 0, value, 0.0).astype(BF16)


def key_bias(rows, length):
    key = lax.broadcasted_iota(jnp.int32, (rows, LANES - HD), 0)
    return first_lane(rows, jnp.where(key < length, 0.0, NEG))


def attn_fwd_kernel(offset, len_ref, qkv_ref, kv_ref, o_ref, st_ref, q_s, k_s, v_s):
    if kv_ref is None:
        kv_ref = qkv_ref
    rows, keys = qkv_ref.shape[0], kv_ref.shape[0]
    one = first_lane(rows, F32(1.0))
    bias = key_bias(keys, len_ref[0])
    for h in range(H):
        q_s[h] = pad_lanes(qkv_ref[:, h * HD : (h + 1) * HD], one)
        k_s[h] = pad_lanes(kv_ref[:, offset + h * HD : offset + (h + 1) * HD], bias)
        v_s[h] = pad_lanes(kv_ref[:, offset + D + h * HD : offset + D + (h + 1) * HD])
    st_ref[...] = jnp.zeros_like(st_ref)
    lane = lax.broadcasted_iota(jnp.int32, (rows, LANES), 1)

    def body(h, carry):
        s = dot_t(q_s[h], k_s[h])
        m = jnp.max(s, axis=1, keepdims=True)
        p = jnp.exp2((s - m) * C2)
        total = jnp.sum(p, axis=1, keepdims=True)
        o = dot(p.astype(BF16), v_s[h])
        q_s[h] = (o * (1.0 / total)).astype(BF16)
        st_ref[...] = jnp.where(lane == h, m * C2 + jnp.log2(total), st_ref[...])
        return carry

    lax.fori_loop(0, H, body, 0)
    for h in range(H):
        o_ref[:, h * HD : (h + 1) * HD] = q_s[h][:, :HD]


def attn_fwd(length, qkv, kv=None):
    rows = qkv.shape[0]
    keys = rows if kv is None else kv.shape[0]
    vm = pl.BlockSpec(memory_space=pltpu.VMEM)
    if kv is None:
        kernel = lambda a, b, *rest: attn_fwd_kernel(D, a, b, None, *rest)
        operands = (length, qkv)
    else:
        kernel = functools.partial(attn_fwd_kernel, 0)
        operands = (length, qkv, kv)
    return pl.pallas_call(
        kernel,
        in_specs=[pl.BlockSpec(memory_space=pltpu.SMEM)] + [vm] * (len(operands) - 1),
        out_specs=[vm, vm],
        out_shape=[
            jax.ShapeDtypeStruct((rows, D), BF16),
            jax.ShapeDtypeStruct((rows, LANES), F32),
        ],
        scratch_shapes=[
            pltpu.VMEM((H, rows, LANES), BF16),
            pltpu.VMEM((H, keys, LANES), BF16),
            pltpu.VMEM((H, keys, LANES), BF16),
        ],
        cost_estimate=pl.CostEstimate(
            flops=H * rows * keys * 256 * 4, bytes_accessed=rows * D * 8, transcendentals=H * rows * keys
        ),
        compiler_params=pltpu.CompilerParams(vmem_limit_bytes=VMEM_LIMIT),
        name="attention_forward",
    )(*operands)


def attn_bwd_kernel(
    offset, len_ref, qkv_ref, kv_ref, do_ref, o_ref, st_ref, dq_ref, dkv_ref, q_s, k_s, v_s, do_s, st_t, dl_t
):
    if kv_ref is None:
        kv_ref, dkv_ref = qkv_ref, dq_ref
    rows, keys = qkv_ref.shape[0], kv_ref.shape[0]
    one = first_lane(rows, F32(1.0))
    bias = key_bias(keys, len_ref[0])
    lane = lax.broadcasted_iota(jnp.int32, (rows, LANES), 1)
    delta = jnp.zeros((rows, LANES), F32)
    for h in range(H):
        q_s[h] = pad_lanes(qkv_ref[:, h * HD : (h + 1) * HD], one)
        k_s[h] = pad_lanes(kv_ref[:, offset + h * HD : offset + (h + 1) * HD], bias)
        v_s[h] = pad_lanes(kv_ref[:, offset + D + h * HD : offset + D + (h + 1) * HD])
        do = do_ref[:, h * HD : (h + 1) * HD]
        do_s[h] = pad_lanes(do)
        o = o_ref[:, h * HD : (h + 1) * HD].astype(F32)
        d = jnp.sum(do.astype(F32) * o, axis=1, keepdims=True)
        delta = jnp.where(lane == h, d, delta)
    st_t[...] = st_ref[...].T
    dl_t[...] = delta.T

    def body(h, carry):
        q, k, do = q_s[h], k_s[h], do_s[h]
        p = jnp.exp2(dot_t(k, q) * C2 - st_t[pl.ds(h, 1), :])
        dv = dot(p.astype(BF16), do)
        dp = dot_t(v_s[h], do)
        ds = (p * (dp - dl_t[pl.ds(h, 1), :])).astype(BF16)
        dk = dot(ds, q)
        dq = dot(k.T, ds)
        v_s[h] = dv.astype(BF16)
        k_s[h] = (dk * SCALE).astype(BF16)
        q_s[h] = (dq * SCALE).astype(BF16).T
        return carry

    lax.fori_loop(0, H, body, 0)
    for h in range(H):
        dq_ref[:, h * HD : (h + 1) * HD] = q_s[h][:, :HD]
        dkv_ref[:, offset + h * HD : offset + (h + 1) * HD] = k_s[h][:, :HD]
        dkv_ref[:, offset + D + h * HD : offset + D + (h + 1) * HD] = v_s[h][:, :HD]


def attn_bwd(length, qkv, do, o, st, kv=None):
    rows = qkv.shape[0]
    keys = rows if kv is None else kv.shape[0]
    vm = pl.BlockSpec(memory_space=pltpu.VMEM)
    if kv is None:
        kernel = lambda a, b, c, d, e, f, *rest: attn_bwd_kernel(
            D, a, b, None, c, d, e, f, None, *rest
        )
        operands = (length, qkv, do, o, st)
        outs = [jax.ShapeDtypeStruct((rows, 3 * D), BF16)]
    else:
        kernel = functools.partial(attn_bwd_kernel, 0)
        operands = (length, qkv, kv, do, o, st)
        outs = [jax.ShapeDtypeStruct((rows, D), BF16), jax.ShapeDtypeStruct((keys, 2 * D), BF16)]
    return pl.pallas_call(
        kernel,
        in_specs=[pl.BlockSpec(memory_space=pltpu.SMEM)] + [vm] * (len(operands) - 1),
        out_specs=[vm] * len(outs),
        out_shape=outs,
        scratch_shapes=[
            pltpu.VMEM((H, rows, LANES), BF16),
            pltpu.VMEM((H, keys, LANES), BF16),
            pltpu.VMEM((H, keys, LANES), BF16),
            pltpu.VMEM((H, rows, LANES), BF16),
            pltpu.VMEM((LANES, rows), F32),
            pltpu.VMEM((LANES, rows), F32),
        ],
        cost_estimate=pl.CostEstimate(
            flops=H * rows * keys * 256 * 10, bytes_accessed=rows * D * 16, transcendentals=H * rows * keys
        ),
        compiler_params=pltpu.CompilerParams(vmem_limit_bytes=VMEM_LIMIT),
        name="attention_backward",
    )(*operands)


def gather_kernel(
    src, out, stage, local_sem, z_recv, y_recv, b_recv, h_recv, c_recv_own, c_recv_z, c_recv_y, c_recv_b, c_recv_h,
    up_send, down_send, y_send, b_send, h_send, c_send_own, c_send_z, c_send_y, c_send_b, c_send_h,
):
    rows = src.shape[0]
    unit = rows // 6 // 16 * 16 + 16
    sizes = [unit, unit, rows // 2 - 2 * unit, rows // 2 - 2 * unit, unit]
    begins = [0, unit, 2 * unit, rows // 2, rows - 2 * unit]
    x = lax.axis_index("seq")
    f = lax.axis_index("fsdp")
    z, y, c = f // 4, (f // 2) % 2, f % 2

    def place(zb, yb, j, side, cb=None):
        owner = (zb * 2 + yb) * 2 + (c if cb is None else cb)
        begin = jnp.where(side == 0, begins[j], rows - begins[j] - sizes[j])
        return pl.multiple_of(owner * rows + begin, 16), sizes[j]

    def view(spot):
        return out.at[pl.ds(spot[0], spot[1]), :]

    def device(zb, yb, cb, xb):
        return ((zb * 2 + yb) * 2 + cb, xb)

    up, down = device(z + 1, y, c, x), device(z - 1, y, c, x)
    beside, across, mate = device(z, 1 - y, c, x), device(z, y, c, 1 - x), device(z, y, 1 - c, x)

    def copy(spot, send, recv, to, source=None):
        return pltpu.make_async_remote_copy(
            src_ref=view(spot) if source is None else source,
            dst_ref=view(spot),
            send_sem=send,
            recv_sem=recv,
            device_id=to,
            device_id_type=MESH,
        )

    def arrived(spot, recv):
        copy(spot, local_sem.at[1], recv, mate).wait_recv()

    barrier = pltpu.get_barrier_semaphore()
    for to in (beside, across, mate):
        pl.semaphore_signal(barrier, inc=1, device_id=to, device_id_type=MESH)

    @pl.when(z < 3)
    def _():
        pl.semaphore_signal(barrier, inc=1, device_id=up, device_id_type=MESH)

    @pl.when(z > 0)
    def _():
        pl.semaphore_signal(barrier, inc=1, device_id=down, device_id_type=MESH)

    pl.semaphore_wait(barrier, 3 + jnp.where(z < 3, 1, 0) + jnp.where(z > 0, 1, 0))

    def own(j):
        begin = jnp.where(x == 0, begins[j], rows - begins[j] - sizes[j])
        return src.at[pl.ds(pl.multiple_of(begin, 16), sizes[j]), :]

    whole = (pl.multiple_of(f * rows, 16), rows)
    for j in range(5):
        spot = place(z, y, j, x)

        @pl.when(z < 3)
        def _():
            copy(spot, up_send.at[z, j], z_recv.at[z, j], up, own(j)).start()

        @pl.when(z > 0)
        def _():
            copy(spot, down_send.at[z, j], z_recv.at[z, j], down, own(j)).start()

        if j < 3:
            copy(spot, y_send.at[z, j], y_recv.at[z, j], beside, own(j)).start()
    copy(whole, c_send_own.at[0], c_recv_own.at[0], mate, src).start()
    fetch = pltpu.make_async_copy(src, stage, local_sem.at[0])
    fetch.start()
    fetch.wait()
    keep = pltpu.make_async_copy(stage, view(whole), local_sem.at[0])
    keep.start()

    def z_event(d, j):
        def flow(zb, onward, to, sends):
            spot = place(zb, y, j, x)
            arrived(spot, z_recv.at[zb, j])

            @pl.when(onward)
            def _():
                copy(spot, sends.at[zb, j], z_recv.at[zb, j], to).start()

            if j == 0:
                copy(spot, b_send.at[zb], b_recv.at[zb], across).start()
            if j < 3:
                copy(spot, y_send.at[zb, j], y_recv.at[zb, j], beside).start()
            copy(spot, c_send_z.at[zb, j], c_recv_z.at[zb, j], mate).start()

        @pl.when(z - d >= 0)
        def _():
            flow(z - d, z < 3, up, up_send)

        @pl.when(z + d <= 3)
        def _():
            flow(z + d, z > 0, down, down_send)

    def each(d, act):
        if d == 0:
            act(z)
            return

        @pl.when(z - d >= 0)
        def _():
            act(z - d)

        @pl.when(z + d <= 3)
        def _():
            act(z + d)

    def y_event(d, j):
        def act(zb):
            spot = place(zb, 1 - y, j, x)
            arrived(spot, y_recv.at[zb, j])
            copy(spot, h_send.at[zb, j], h_recv.at[zb, j], across).start()
            copy(spot, c_send_y.at[zb, j], c_recv_y.at[zb, j], mate).start()

        each(d, act)

    def b_event(d):
        def act(zb):
            spot = place(zb, y, 0, 1 - x)
            arrived(spot, b_recv.at[zb])
            copy(spot, c_send_b.at[zb], c_recv_b.at[zb], mate).start()

        each(d, act)

    def h_event(d, j):
        def act(zb):
            spot = place(zb, 1 - y, j, 1 - x)
            arrived(spot, h_recv.at[zb, j])
            copy(spot, c_send_h.at[zb, j], c_recv_h.at[zb, j], mate).start()

        each(d, act)

    events = []
    for d in range(4):
        for j in range(5):
            at = (d - 1) * 5 + j + 1 if d else 0
            if d:
                events.append((at, functools.partial(z_event, d, j)))
                if j == 0:
                    events.append((at + 2, functools.partial(b_event, d)))
            if j < 3:
                ready = at + 1.5 if d else j + 1
                events.append((ready, functools.partial(y_event, d, j)))
                events.append((ready + 2, functools.partial(h_event, d, j)))
    for _, event in sorted(events, key=lambda e: e[0]):
        event()
    keep.wait()
    other = 1 - c

    def core_spot(zb, yb, j, side):
        return place(zb, yb, j, side, other)

    arrived((pl.multiple_of(((z * 2 + y) * 2 + other) * rows, 16), rows), c_recv_own.at[0])
    copy(whole, c_send_own.at[0], c_recv_own.at[0], mate).wait_send()
    for d in range(4):
        def drain(zb, d=d):
            for j in range(5):
                if d:
                    arrived(core_spot(zb, y, j, x), c_recv_z.at[zb, j])
                    copy(place(zb, y, j, x), c_send_z.at[zb, j], c_recv_z.at[zb, j], mate).wait_send()
                if j < 3:
                    arrived(core_spot(zb, 1 - y, j, x), c_recv_y.at[zb, j])
                    arrived(core_spot(zb, 1 - y, j, 1 - x), c_recv_h.at[zb, j])
                    spot = place(zb, 1 - y, j, x)
                    copy(spot, c_send_y.at[zb, j], c_recv_y.at[zb, j], mate).wait_send()
                    copy(spot, h_send.at[zb, j], h_recv.at[zb, j], across).wait_send()
                    spot = place(zb, 1 - y, j, 1 - x)
                    copy(spot, c_send_h.at[zb, j], c_recv_h.at[zb, j], mate).wait_send()
                    spot = place(zb, y, j, x)
                    copy(spot, y_send.at[zb, j], y_recv.at[zb, j], beside).wait_send()
            if d:
                arrived(core_spot(zb, y, 0, 1 - x), c_recv_b.at[zb])
                spot = place(zb, y, 0, 1 - x)
                copy(spot, c_send_b.at[zb], c_recv_b.at[zb], mate).wait_send()
                spot = place(zb, y, 0, x)
                copy(spot, b_send.at[zb], b_recv.at[zb], across).wait_send()

        each(d, drain)
        for j in range(5):
            @pl.when(jnp.logical_and(z - d >= 0, z < 3))
            def _():
                zb = z - d
                copy(place(zb, y, j, x), up_send.at[zb, j], z_recv.at[zb, j], up).wait_send()

            @pl.when(jnp.logical_and(z + d <= 3, z > 0))
            def _():
                zb = z + d
                copy(place(zb, y, j, x), down_send.at[zb, j], z_recv.at[zb, j], down).wait_send()


def gather_blocks(shard, collective_id):
    rows = shard.shape[0]
    dma = pltpu.SemaphoreType.DMA
    core = [dma((1,)), dma((4, 5)), dma((4, 3)), dma((4,)), dma((4, 3))]
    return pl.pallas_call(
        gather_kernel,
        in_specs=[pl.BlockSpec(memory_space=pl.ANY)],
        out_specs=pl.BlockSpec(memory_space=pl.ANY),
        out_shape=jax.ShapeDtypeStruct((16 * rows, LANES), BF16),
        scratch_shapes=[pltpu.VMEM((rows, LANES), BF16), dma((2,))]
        + [dma((4, 5)), dma((4, 3)), dma((4,)), dma((4, 3))] + core
        + [dma((4, 5)), dma((4, 5)), dma((4, 3)), dma((4,)), dma((4, 3))] + core,
        compiler_params=pltpu.CompilerParams(collective_id=collective_id, has_side_effects=True, vmem_limit_bytes=16 << 20),
        name="gather_blocks",
    )(shard)


def gelu_tanh(tensor):
    return (
        0.5
        * tensor
        * (1.0 + jnp.tanh(0.7978845608028654 * (tensor + 0.044715 * tensor * tensor * tensor)))
    )


def layer_norm(tensor, gain, offset):
    average = jnp.mean(tensor, axis=-1, keepdims=True)
    centred = tensor - average
    variance = jnp.mean(centred * centred, axis=-1, keepdims=True)
    return centred * lax.rsqrt(variance + epsilon) * gain + offset


def local(
    activations,
    group_image_count,
    image_adapter_index,
    lengths,
    frozen,
    attention_adapter_weights,
    narrow_adapter_weights,
    broad_adapter_weights,
    cotangent,
):
    slots, local_len, _ = activations.shape
    seq_parts = lax.axis_size("seq")
    fsdp_parts = lax.axis_size("fsdp")
    device_count = seq_parts * fsdp_parts
    me = lax.axis_index("seq")
    seq_total = local_len * seq_parts
    layer_count = frozen.shape[0]
    adapters = attention_adapter_weights.shape[2]
    parts = seq_parts // slots
    slot = me // parts
    part = me % parts
    tokens = seq_total // parts
    groups = [[s * parts + p for p in range(parts)] for s in range(slots)]

    def to_image(v):
        if parts == 1 and slots == 2:
            mine = lax.dynamic_index_in_dim(v, slot, 0, keepdims=False)
            other = lax.dynamic_index_in_dim(v, 1 - slot, 0, keepdims=False)
            other = lax.ppermute(other, "seq", [(0, 1), (1, 0)])
            return jnp.where(
                slot == 0,
                jnp.concatenate([mine, other], 0),
                jnp.concatenate([other, mine], 0),
            )
        whole = lax.all_gather(v, "seq", axis=1, tiled=True)
        whole = lax.dynamic_index_in_dim(whole, slot, 0, keepdims=False)
        return lax.dynamic_slice_in_dim(whole, part * tokens, tokens, 0)

    def to_tokens(v):
        if parts == 1 and slots == 2:
            mine = lax.dynamic_slice_in_dim(v, slot * local_len, local_len, 0)
            other = lax.dynamic_slice_in_dim(v, (1 - slot) * local_len, local_len, 0)
            other = lax.ppermute(other, "seq", [(0, 1), (1, 0)])
            return jnp.where(slot == 0, jnp.stack([mine, other]), jnp.stack([other, mine]))
        whole = lax.all_gather(v, "seq", axis=0, tiled=True).reshape(slots, seq_total, -1)
        return lax.dynamic_slice_in_dim(whole, me * local_len, local_len, 1)

    length = lax.dynamic_slice_in_dim(lengths, slot, 1, 0)
    adapter = lax.dynamic_index_in_dim(image_adapter_index, slot, 0, keepdims=False)
    is_live = slot < group_image_count[0]
    positions = part * tokens + jnp.arange(tokens, dtype=jnp.int32)
    row_mask = ((positions < length[0]) & is_live).astype(F32)[:, None]
    def pick(table):
        return lax.dynamic_index_in_dim(table, adapter, 1, keepdims=False)

    shards = lax.optimization_barrier(frozen.reshape(layer_count, -1, LANES))
    hidden = to_image(activations).astype(F32) * row_mask
    stored = []
    weights = []
    for layer in range(layer_count):
        if (fsdp_parts, seq_parts) == (16, 2):
            flat = gather_blocks(shards[layer], 0)
        else:
            flat = lax.all_gather(shards[layer], "fsdp", axis=0, tiled=True)
        w_qkv, w_o, w_1, w_2 = unpack(flat)
        vectors = lax.slice_in_dim(flat, CUT_VECTORS, CUT_VECTORS + 106, axis=0).reshape(-1)
        vectors, b_1 = vectors[: 8 * D].reshape(8, D).astype(F32), vectors[8 * D : 8 * D + FF]
        b_1 = b_1.astype(F32)
        attn = pick(attention_adapter_weights[layer])
        narrow = pick(narrow_adapter_weights[layer])
        wide = pick(broad_adapter_weights[layer])
        weights.append((w_qkv, w_o, w_1, w_2, vectors, attn, narrow, wide))
        normed = layer_norm(hidden, vectors[0], vectors[1]).astype(BF16)
        inner_qkv = dot_t(normed, attn[0:3].reshape(3 * R, D)).astype(BF16)
        lifted = jnp.concatenate(
            [dot(inner_qkv[:, c * R : (c + 1) * R], attn[4 + c]) for c in range(3)], axis=1
        )
        bias_qkv = jnp.concatenate([vectors[4], jnp.zeros((D,), F32), vectors[5]])
        qkv = (dot(normed, w_qkv) + bias_qkv + lifted).astype(BF16)
        keys = None
        if parts > 1:
            keys = lax.all_gather(
                qkv[:, D:], "seq", axis=0, tiled=True, axis_index_groups=groups
            )
        attended, stats = attn_fwd(length, qkv, keys)
        inner_o = dot_t(attended, attn[3]).astype(BF16)
        middle = hidden + (dot(attended, w_o) + vectors[6] + dot(inner_o, attn[7]))
        normed_two = layer_norm(middle, vectors[2], vectors[3]).astype(BF16)
        inner_up = dot_t(normed_two, narrow[0]).astype(BF16)
        gate = dot(normed_two, w_1) + b_1 + dot(inner_up, wide[0])
        activated = gelu_tanh(gate).astype(BF16)
        inner_down = dot_t(activated, wide[1]).astype(BF16)
        stored.append(
            (
                hidden,
                normed,
                inner_qkv,
                qkv,
                keys,
                stats,
                attended,
                inner_o,
                middle,
                normed_two,
                inner_up,
                gate,
                activated,
                inner_down,
            )
        )
        hidden = middle + (dot(activated, w_2) + vectors[7] + dot(inner_down, narrow[1]))
    output = to_tokens((hidden * row_mask).astype(BF16))
    gradient = to_image(cotangent).astype(F32) * row_mask
    collected = [None] * layer_count
    for layer in reversed(range(layer_count)):
        (
            layer_input,
            normed,
            inner_qkv,
            qkv,
            keys,
            stats,
            attended,
            inner_o,
            middle,
            normed_two,
            inner_up,
            gate,
            activated,
            inner_down,
        ) = stored[layer]
        w_qkv, w_o, w_1, w_2, vectors, attn, narrow, wide = weights[layer]
        d_branch = gradient.astype(BF16)
        d_inner_down = dot_t(d_branch, narrow[1]).astype(BF16)
        up_second = dot_l(inner_down, d_branch)
        d_activated = dot_t(d_branch, w_2) + dot(d_inner_down, wide[1])
        down_second = dot_l(d_inner_down, activated)
        d_gate = jax.vjp(gelu_tanh, gate)[1](d_activated)[0].astype(BF16)
        d_inner_up = dot_t(d_gate, wide[0]).astype(BF16)
        up_first = dot_l(inner_up, d_gate)
        d_normed_two = dot_t(d_gate, w_1) + dot(d_inner_up, narrow[0])
        down_first = dot_l(d_inner_up, normed_two)
        norm_two = jax.vjp(lambda t: layer_norm(t, vectors[2], vectors[3]), middle)[1]
        d_middle = gradient + norm_two(d_normed_two)[0]
        d_out = d_middle.astype(BF16)
        d_inner_o = dot_t(d_out, attn[7]).astype(BF16)
        up_o = dot_l(inner_o, d_out)
        d_attended = (dot_t(d_out, w_o) + dot(d_inner_o, attn[3])).astype(BF16)
        down_o = dot_l(d_inner_o, attended)
        d_qkv = attn_bwd(length, qkv, d_attended, attended, stats, keys)
        if parts > 1:
            d_keys = lax.psum_scatter(
                d_qkv[1].astype(F32),
                "seq",
                scatter_dimension=0,
                tiled=True,
                axis_index_groups=groups,
            )
            d_qkv = jnp.concatenate([d_qkv[0], d_keys.astype(BF16)], axis=1)
        else:
            d_qkv = d_qkv[0]
        d_inner_qkv = jnp.concatenate(
            [dot_t(d_qkv[:, c * D : (c + 1) * D], attn[4 + c]) for c in range(3)], axis=1
        ).astype(BF16)
        up_qkv = jnp.stack(
            [
                dot_l(inner_qkv[:, c * R : (c + 1) * R], d_qkv[:, c * D : (c + 1) * D])
                for c in range(3)
            ]
        )
        d_normed = dot_t(d_qkv, w_qkv) + dot(d_inner_qkv, attn[0:3].reshape(3 * R, D))
        down_qkv = dot_l(d_inner_qkv, normed).reshape(3, R, D)
        norm_one = jax.vjp(lambda t: layer_norm(t, vectors[0], vectors[1]), layer_input)[1]
        gradient = d_middle + norm_one(d_normed)[0]
        rows_narrow = jnp.concatenate(
            [
                down_qkv.reshape(3 * R, D),
                down_o,
                up_qkv.reshape(3 * R, D),
                up_o,
                down_first,
                up_second,
            ]
        ).astype(BF16)
        rows_wide = jnp.concatenate([up_first, down_second]).astype(BF16)

        def shares(rows):
            share = -(-rows.shape[0] // device_count)
            rows = jnp.pad(rows, ((0, share * device_count - rows.shape[0]), (0, 0)))
            return rows.reshape(device_count, share * rows.shape[1])

        terms = [shares(rows_narrow), shares(rows_wide)]
        used = terms[0].shape[1] + terms[1].shape[1]
        label = jnp.broadcast_to(adapter.astype(BF16), (device_count, -used % LANES + LANES))
        terms = lax.all_to_all(
            jnp.concatenate(terms + [label], axis=1),
            ("fsdp", "seq"),
            split_axis=0,
            concat_axis=0,
            tiled=True,
        )
        choice = jnp.arange(adapters, dtype=F32)[:, None] == terms[:, used].astype(F32)[None, :]
        sums = jnp.dot(choice.astype(F32), terms.astype(F32), precision=lax.Precision.HIGHEST)
        sums = lax.all_gather(sums.astype(BF16), ("fsdp", "seq")).transpose(1, 0, 2)
        split = -(-10 * R // device_count) * D

        def table(part, count, width):
            part = part.reshape(adapters, -1, width)[:, : count * R]
            return part.reshape(adapters, count, R, width).transpose(1, 0, 2, 3).astype(F32)

        collected[layer] = (table(sums[:, :, :split], 10, D), table(sums[:, :, split:used], 2, FF))
    grad_attn = jnp.stack([entry[0][0:8] for entry in collected], axis=0)
    grad_narrow = jnp.stack([entry[0][8:10] for entry in collected], axis=0)
    grad_wide = jnp.stack([entry[1] for entry in collected], axis=0)
    input_grad = to_tokens((gradient * row_mask).astype(BF16)).astype(F32)
    return (output, input_grad, grad_attn, grad_narrow, grad_wide)


def solution(mesh):
    in_specs = (
        P("fsdp", "seq", None),
        P("fsdp"),
        P("fsdp"),
        P("fsdp"),
        P(None, "fsdp"),
        P(),
        P(),
        P(),
        P("fsdp", "seq", None),
    )
    out_specs = (P("fsdp", "seq", None), P("fsdp", "seq", None), P(), P(), P())
    return jax.shard_map(local, mesh=mesh, in_specs=in_specs, out_specs=out_specs, check_vma=False)
```

```python
import functools
import math

import jax
import jax.numpy as jnp
from jax import lax
from jax.experimental import pallas as pl
from jax.experimental.pallas import tpu as pltpu
from jax.sharding import PartitionSpec as P

D = 1152
HD = 72
H = 16
FF = 4304
R = 16
LANES = 128
BF16 = jnp.bfloat16
F32 = jnp.float32
MESH = pl.DeviceIdType.MESH
VMEM_LIMIT = 60 << 20
C2 = math.log2(math.e) / math.sqrt(HD)
SCALE = 1.0 / math.sqrt(HD)
NEG = -1e30
epsilon = 1e-06
CUT_OUT = 3 * D * D // LANES
CUT_UP = CUT_OUT + D * D // LANES
CUT_DOWN = CUT_UP + D * FF // LANES
CUT_VECTORS = CUT_DOWN + FF * D // LANES


def dot(a, b):
    return jnp.dot(a, b, preferred_element_type=F32)


def dot_t(a, b):
    return lax.dot_general(a, b, (((1,), (1,)), ((), ())), preferred_element_type=F32)


def dot_l(a, b):
    return lax.dot_general(a, b, (((0,), (0,)), ((), ())), preferred_element_type=F32)


def rows_aligned_kernel(panels, rows, in_ref, out_ref, wide):
    wide[...] = in_ref[...].astype(F32)
    for c in range(panels):
        out_ref[:, c * LANES : (c + 1) * LANES] = wide[pl.ds(c, rows, stride=panels), :].astype(BF16)


def rows_aligned(flat, start, count, panels, rows):
    step = rows * panels
    return pl.pallas_call(
        functools.partial(rows_aligned_kernel, panels, rows),
        grid=(pl.cdiv(count, rows),),
        in_specs=[
            pl.BlockSpec(
                (pl.Element(step), pl.Element(LANES)),
                lambda i: (pl.multiple_of(start + i * step, 16), 0),
            )
        ],
        out_specs=pl.BlockSpec((rows, panels * LANES), lambda i: (i, 0)),
        out_shape=jax.ShapeDtypeStruct((count, panels * LANES), BF16),
        scratch_shapes=[pltpu.VMEM((step, LANES), F32)],
        cost_estimate=pl.CostEstimate(
            flops=0, bytes_accessed=4 * count * panels * LANES, transcendentals=0
        ),
        compiler_params=pltpu.CompilerParams(vmem_limit_bytes=VMEM_LIMIT),
        name="weight_rows",
    )(flat)


PERIOD = 8
PERIOD_ROWS = PERIOD * FF // LANES


def rows_odd_kernel(rows, in_ref, out_ref, wide, turned):
    groups = rows // PERIOD
    panels = -(-FF // LANES)
    wide[...] = in_ref[...].astype(F32)
    lane = lax.broadcasted_iota(jnp.int32, (groups, LANES), 1)
    for j in range(PERIOD):
        first, shift = (FF * j) // LANES, (FF * j) % LANES
        held = wide[pl.ds(first, groups, stride=PERIOD_ROWS), :]
        for c in range(panels):
            after = min(first + c + 1, PERIOD_ROWS - 1)
            after = wide[pl.ds(after, groups, stride=PERIOD_ROWS), :]
            value = held
            if shift:
                value = jnp.where(
                    lane < LANES - shift,
                    pltpu.roll(held, LANES - shift, 1),
                    pltpu.roll(after, LANES - shift, 1),
                )
            held = after
            turned[pl.ds(c * rows + j, groups, stride=PERIOD), :] = value
    for c in range(panels):
        width = min(LANES, FF - c * LANES)
        out_ref[:, c * LANES : c * LANES + width] = turned[pl.ds(c * rows, rows), :][:, :width].astype(BF16)


def rows_odd(flat, start, count, rows):
    step = rows * FF // LANES
    return pl.pallas_call(
        functools.partial(rows_odd_kernel, rows),
        grid=(count // rows,),
        in_specs=[
            pl.BlockSpec(
                (pl.Element(step), pl.Element(LANES)),
                lambda i: (pl.multiple_of(start + i * step, 16), 0),
            )
        ],
        out_specs=pl.BlockSpec((rows, FF), lambda i: (i, 0)),
        out_shape=jax.ShapeDtypeStruct((count, FF), BF16),
        scratch_shapes=[
            pltpu.VMEM((step, LANES), F32),
            pltpu.VMEM((-(-FF // LANES) * rows, LANES), F32),
        ],
        cost_estimate=pl.CostEstimate(flops=0, bytes_accessed=4 * count * FF, transcendentals=0),
        compiler_params=pltpu.CompilerParams(vmem_limit_bytes=VMEM_LIMIT),
        name="weight_rows_odd",
    )(flat)


def unpack(flat):
    return (
        rows_aligned(flat, 0, D, 3 * D // LANES, 64),
        rows_aligned(flat, CUT_OUT, D, D // LANES, 192),
        rows_odd(flat, CUT_UP, D, 128),
        rows_aligned(flat, CUT_DOWN, FF, D // LANES, 288),
    )


def pad_lanes(x, extra=None):
    if extra is None:
        extra = jnp.zeros((x.shape[0], LANES - HD), x.dtype)
    return jnp.concatenate([x, extra], axis=1)


def first_lane(rows, value):
    lane = lax.broadcasted_iota(jnp.int32, (rows, LANES - HD), 1)
    return jnp.where(lane == 0, value, 0.0).astype(BF16)


def key_bias(rows, length):
    key = lax.broadcasted_iota(jnp.int32, (rows, LANES - HD), 0)
    return first_lane(rows, jnp.where(key < length, 0.0, NEG))


def attn_fwd_kernel(offset, len_ref, qkv_ref, kv_ref, o_ref, st_ref, q_s, k_s, v_s):
    if kv_ref is None:
        kv_ref = qkv_ref
    rows, keys = qkv_ref.shape[0], kv_ref.shape[0]
    one = first_lane(rows, F32(1.0))
    bias = key_bias(keys, len_ref[0])
    for h in range(H):
        q_s[h] = pad_lanes(qkv_ref[:, h * HD : (h + 1) * HD], one)
        k_s[h] = pad_lanes(kv_ref[:, offset + h * HD : offset + (h + 1) * HD], bias)
        v_s[h] = pad_lanes(kv_ref[:, offset + D + h * HD : offset + D + (h + 1) * HD])
    st_ref[...] = jnp.zeros_like(st_ref)
    lane = lax.broadcasted_iota(jnp.int32, (rows, LANES), 1)

    def body(h, carry):
        s = dot_t(q_s[h], k_s[h])
        m = jnp.max(s, axis=1, keepdims=True)
        p = jnp.exp2((s - m) * C2)
        total = jnp.sum(p, axis=1, keepdims=True)
        o = dot(p.astype(BF16), v_s[h])
        q_s[h] = (o * (1.0 / total)).astype(BF16)
        st_ref[...] = jnp.where(lane == h, m * C2 + jnp.log2(total), st_ref[...])
        return carry

    lax.fori_loop(0, H, body, 0)
    for h in range(H):
        o_ref[:, h * HD : (h + 1) * HD] = q_s[h][:, :HD]


def attn_fwd(length, qkv, kv=None):
    rows = qkv.shape[0]
    keys = rows if kv is None else kv.shape[0]
    vm = pl.BlockSpec(memory_space=pltpu.VMEM)
    if kv is None:
        kernel = lambda a, b, *rest: attn_fwd_kernel(D, a, b, None, *rest)
        operands = (length, qkv)
    else:
        kernel = functools.partial(attn_fwd_kernel, 0)
        operands = (length, qkv, kv)
    return pl.pallas_call(
        kernel,
        in_specs=[pl.BlockSpec(memory_space=pltpu.SMEM)] + [vm] * (len(operands) - 1),
        out_specs=[vm, vm],
        out_shape=[
            jax.ShapeDtypeStruct((rows, D), BF16),
            jax.ShapeDtypeStruct((rows, LANES), F32),
        ],
        scratch_shapes=[
            pltpu.VMEM((H, rows, LANES), BF16),
            pltpu.VMEM((H, keys, LANES), BF16),
            pltpu.VMEM((H, keys, LANES), BF16),
        ],
        cost_estimate=pl.CostEstimate(
            flops=H * rows * keys * 256 * 4, bytes_accessed=rows * D * 8, transcendentals=H * rows * keys
        ),
        compiler_params=pltpu.CompilerParams(vmem_limit_bytes=VMEM_LIMIT),
        name="attention_forward",
    )(*operands)


def attn_bwd_kernel(
    offset, len_ref, qkv_ref, kv_ref, do_ref, o_ref, st_ref, dq_ref, dkv_ref, q_s, k_s, v_s, do_s, st_t, dl_t
):
    if kv_ref is None:
        kv_ref, dkv_ref = qkv_ref, dq_ref
    rows, keys = qkv_ref.shape[0], kv_ref.shape[0]
    one = first_lane(rows, F32(1.0))
    bias = key_bias(keys, len_ref[0])
    lane = lax.broadcasted_iota(jnp.int32, (rows, LANES), 1)
    delta = jnp.zeros((rows, LANES), F32)
    for h in range(H):
        q_s[h] = pad_lanes(qkv_ref[:, h * HD : (h + 1) * HD], one)
        k_s[h] = pad_lanes(kv_ref[:, offset + h * HD : offset + (h + 1) * HD], bias)
        v_s[h] = pad_lanes(kv_ref[:, offset + D + h * HD : offset + D + (h + 1) * HD])
        do = do_ref[:, h * HD : (h + 1) * HD]
        do_s[h] = pad_lanes(do)
        o = o_ref[:, h * HD : (h + 1) * HD].astype(F32)
        d = jnp.sum(do.astype(F32) * o, axis=1, keepdims=True)
        delta = jnp.where(lane == h, d, delta)
    st_t[...] = st_ref[...].T
    dl_t[...] = delta.T

    def body(h, carry):
        q, k, do = q_s[h], k_s[h], do_s[h]
        p = jnp.exp2(dot_t(k, q) * C2 - st_t[pl.ds(h, 1), :])
        dv = dot(p.astype(BF16), do)
        dp = dot_t(v_s[h], do)
        ds = (p * (dp - dl_t[pl.ds(h, 1), :])).astype(BF16)
        dk = dot(ds, q)
        dq = dot(k.T, ds)
        v_s[h] = dv.astype(BF16)
        k_s[h] = (dk * SCALE).astype(BF16)
        q_s[h] = (dq * SCALE).astype(BF16).T
        return carry

    lax.fori_loop(0, H, body, 0)
    for h in range(H):
        dq_ref[:, h * HD : (h + 1) * HD] = q_s[h][:, :HD]
        dkv_ref[:, offset + h * HD : offset + (h + 1) * HD] = k_s[h][:, :HD]
        dkv_ref[:, offset + D + h * HD : offset + D + (h + 1) * HD] = v_s[h][:, :HD]


def attn_bwd(length, qkv, do, o, st, kv=None):
    rows = qkv.shape[0]
    keys = rows if kv is None else kv.shape[0]
    vm = pl.BlockSpec(memory_space=pltpu.VMEM)
    if kv is None:
        kernel = lambda a, b, c, d, e, f, *rest: attn_bwd_kernel(
            D, a, b, None, c, d, e, f, None, *rest
        )
        operands = (length, qkv, do, o, st)
        outs = [jax.ShapeDtypeStruct((rows, 3 * D), BF16)]
    else:
        kernel = functools.partial(attn_bwd_kernel, 0)
        operands = (length, qkv, kv, do, o, st)
        outs = [jax.ShapeDtypeStruct((rows, D), BF16), jax.ShapeDtypeStruct((keys, 2 * D), BF16)]
    return pl.pallas_call(
        kernel,
        in_specs=[pl.BlockSpec(memory_space=pltpu.SMEM)] + [vm] * (len(operands) - 1),
        out_specs=[vm] * len(outs),
        out_shape=outs,
        scratch_shapes=[
            pltpu.VMEM((H, rows, LANES), BF16),
            pltpu.VMEM((H, keys, LANES), BF16),
            pltpu.VMEM((H, keys, LANES), BF16),
            pltpu.VMEM((H, rows, LANES), BF16),
            pltpu.VMEM((LANES, rows), F32),
            pltpu.VMEM((LANES, rows), F32),
        ],
        cost_estimate=pl.CostEstimate(
            flops=H * rows * keys * 256 * 10, bytes_accessed=rows * D * 16, transcendentals=H * rows * keys
        ),
        compiler_params=pltpu.CompilerParams(vmem_limit_bytes=VMEM_LIMIT),
        name="attention_backward",
    )(*operands)


def gather_kernel(
    src, out, stage, local_sem, z_recv, y_recv, b_recv, h_recv, c_recv_own, c_recv_z, c_recv_y, c_recv_b, c_recv_h,
    up_send, down_send, y_send, b_send, h_send, c_send_own, c_send_z, c_send_y, c_send_b, c_send_h,
):
    rows = src.shape[0]
    unit = rows // 6 // 16 * 16 + 16
    sizes = [unit, unit, rows // 2 - 2 * unit, rows // 2 - 2 * unit, unit]
    begins = [0, unit, 2 * unit, rows // 2, rows - 2 * unit]
    x = lax.axis_index("seq")
    f = lax.axis_index("fsdp")
    z, y, c = f // 4, (f // 2) % 2, f % 2

    def place(zb, yb, j, side, cb=None):
        owner = (zb * 2 + yb) * 2 + (c if cb is None else cb)
        begin = jnp.where(side == 0, begins[j], rows - begins[j] - sizes[j])
        return pl.multiple_of(owner * rows + begin, 16), sizes[j]

    def view(spot):
        return out.at[pl.ds(spot[0], spot[1]), :]

    def device(zb, yb, cb, xb):
        return ((zb * 2 + yb) * 2 + cb, xb)

    up, down = device(z + 1, y, c, x), device(z - 1, y, c, x)
    beside, across, mate = device(z, 1 - y, c, x), device(z, y, c, 1 - x), device(z, y, 1 - c, x)

    def copy(spot, send, recv, to, source=None):
        return pltpu.make_async_remote_copy(
            src_ref=view(spot) if source is None else source,
            dst_ref=view(spot),
            send_sem=send,
            recv_sem=recv,
            device_id=to,
            device_id_type=MESH,
        )

    def arrived(spot, recv):
        copy(spot, local_sem.at[1], recv, mate).wait_recv()

    barrier = pltpu.get_barrier_semaphore()
    for to in (beside, across, mate):
        pl.semaphore_signal(barrier, inc=1, device_id=to, device_id_type=MESH)

    @pl.when(z < 3)
    def _():
        pl.semaphore_signal(barrier, inc=1, device_id=up, device_id_type=MESH)

    @pl.when(z > 0)
    def _():
        pl.semaphore_signal(barrier, inc=1, device_id=down, device_id_type=MESH)

    pl.semaphore_wait(barrier, 3 + jnp.where(z < 3, 1, 0) + jnp.where(z > 0, 1, 0))

    def own(j):
        begin = jnp.where(x == 0, begins[j], rows - begins[j] - sizes[j])
        return src.at[pl.ds(pl.multiple_of(begin, 16), sizes[j]), :]

    whole = (pl.multiple_of(f * rows, 16), rows)
    for j in range(5):
        spot = place(z, y, j, x)

        @pl.when(z < 3)
        def _():
            copy(spot, up_send.at[z, j], z_recv.at[z, j], up, own(j)).start()

        @pl.when(z > 0)
        def _():
            copy(spot, down_send.at[z, j], z_recv.at[z, j], down, own(j)).start()

        if j < 3:
            copy(spot, y_send.at[z, j], y_recv.at[z, j], beside, own(j)).start()
    copy(whole, c_send_own.at[0], c_recv_own.at[0], mate, src).start()
    fetch = pltpu.make_async_copy(src, stage, local_sem.at[0])
    fetch.start()
    fetch.wait()
    keep = pltpu.make_async_copy(stage, view(whole), local_sem.at[0])
    keep.start()

    def z_event(d, j):
        def flow(zb, onward, to, sends):
            spot = place(zb, y, j, x)
            arrived(spot, z_recv.at[zb, j])

            @pl.when(onward)
            def _():
                copy(spot, sends.at[zb, j], z_recv.at[zb, j], to).start()

            if j == 0:
                copy(spot, b_send.at[zb], b_recv.at[zb], across).start()
            if j < 3:
                copy(spot, y_send.at[zb, j], y_recv.at[zb, j], beside).start()
            copy(spot, c_send_z.at[zb, j], c_recv_z.at[zb, j], mate).start()

        @pl.when(z - d >= 0)
        def _():
            flow(z - d, z < 3, up, up_send)

        @pl.when(z + d <= 3)
        def _():
            flow(z + d, z > 0, down, down_send)

    def each(d, act):
        if d == 0:
            act(z)
            return

        @pl.when(z - d >= 0)
        def _():
            act(z - d)

        @pl.when(z + d <= 3)
        def _():
            act(z + d)

    def y_event(d, j):
        def act(zb):
            spot = place(zb, 1 - y, j, x)
            arrived(spot, y_recv.at[zb, j])
            copy(spot, h_send.at[zb, j], h_recv.at[zb, j], across).start()
            copy(spot, c_send_y.at[zb, j], c_recv_y.at[zb, j], mate).start()

        each(d, act)

    def b_event(d):
        def act(zb):
            spot = place(zb, y, 0, 1 - x)
            arrived(spot, b_recv.at[zb])
            copy(spot, c_send_b.at[zb], c_recv_b.at[zb], mate).start()

        each(d, act)

    def h_event(d, j):
        def act(zb):
            spot = place(zb, 1 - y, j, 1 - x)
            arrived(spot, h_recv.at[zb, j])
            copy(spot, c_send_h.at[zb, j], c_recv_h.at[zb, j], mate).start()

        each(d, act)

    events = []
    for d in range(4):
        for j in range(5):
            at = (d - 1) * 5 + j + 1 if d else 0
            if d:
                events.append((at, functools.partial(z_event, d, j)))
                if j == 0:
                    events.append((at + 2, functools.partial(b_event, d)))
            if j < 3:
                ready = at + 1.5 if d else j + 1
                events.append((ready, functools.partial(y_event, d, j)))
                events.append((ready + 2, functools.partial(h_event, d, j)))
    for _, event in sorted(events, key=lambda e: e[0]):
        event()
    keep.wait()
    other = 1 - c

    def core_spot(zb, yb, j, side):
        return place(zb, yb, j, side, other)

    arrived((pl.multiple_of(((z * 2 + y) * 2 + other) * rows, 16), rows), c_recv_own.at[0])
    copy(whole, c_send_own.at[0], c_recv_own.at[0], mate).wait_send()
    for d in range(4):
        def drain(zb, d=d):
            for j in range(5):
                if d:
                    arrived(core_spot(zb, y, j, x), c_recv_z.at[zb, j])
                    copy(place(zb, y, j, x), c_send_z.at[zb, j], c_recv_z.at[zb, j], mate).wait_send()
                if j < 3:
                    arrived(core_spot(zb, 1 - y, j, x), c_recv_y.at[zb, j])
                    arrived(core_spot(zb, 1 - y, j, 1 - x), c_recv_h.at[zb, j])
                    spot = place(zb, 1 - y, j, x)
                    copy(spot, c_send_y.at[zb, j], c_recv_y.at[zb, j], mate).wait_send()
                    copy(spot, h_send.at[zb, j], h_recv.at[zb, j], across).wait_send()
                    spot = place(zb, 1 - y, j, 1 - x)
                    copy(spot, c_send_h.at[zb, j], c_recv_h.at[zb, j], mate).wait_send()
                    spot = place(zb, y, j, x)
                    copy(spot, y_send.at[zb, j], y_recv.at[zb, j], beside).wait_send()
            if d:
                arrived(core_spot(zb, y, 0, 1 - x), c_recv_b.at[zb])
                spot = place(zb, y, 0, 1 - x)
                copy(spot, c_send_b.at[zb], c_recv_b.at[zb], mate).wait_send()
                spot = place(zb, y, 0, x)
                copy(spot, b_send.at[zb], b_recv.at[zb], across).wait_send()

        each(d, drain)
        for j in range(5):
            @pl.when(jnp.logical_and(z - d >= 0, z < 3))
            def _():
                zb = z - d
                copy(place(zb, y, j, x), up_send.at[zb, j], z_recv.at[zb, j], up).wait_send()

            @pl.when(jnp.logical_and(z + d <= 3, z > 0))
            def _():
                zb = z + d
                copy(place(zb, y, j, x), down_send.at[zb, j], z_recv.at[zb, j], down).wait_send()


def gather_blocks(shard, collective_id):
    rows = shard.shape[0]
    dma = pltpu.SemaphoreType.DMA
    core = [dma((1,)), dma((4, 5)), dma((4, 3)), dma((4,)), dma((4, 3))]
    return pl.pallas_call(
        gather_kernel,
        in_specs=[pl.BlockSpec(memory_space=pl.ANY)],
        out_specs=pl.BlockSpec(memory_space=pl.ANY),
        out_shape=jax.ShapeDtypeStruct((16 * rows, LANES), BF16),
        scratch_shapes=[pltpu.VMEM((rows, LANES), BF16), dma((2,))]
        + [dma((4, 5)), dma((4, 3)), dma((4,)), dma((4, 3))] + core
        + [dma((4, 5)), dma((4, 5)), dma((4, 3)), dma((4,)), dma((4, 3))] + core,
        compiler_params=pltpu.CompilerParams(collective_id=collective_id, has_side_effects=True, vmem_limit_bytes=VMEM_LIMIT),
        name="gather_blocks",
    )(shard)


def gelu_parts(x):
    inner = 0.7978845608028654 * (x + 0.044715 * x * x * x)
    return jnp.tanh(inner)


def layer_norm(tensor, gain, offset):
    average = jnp.mean(tensor, axis=-1, keepdims=True)
    centred = tensor - average
    variance = jnp.mean(centred * centred, axis=-1, keepdims=True)
    return centred * lax.rsqrt(variance + epsilon) * gain + offset


def layer_norm_back(d_out, tensor, gain):
    average = jnp.mean(tensor, axis=-1, keepdims=True)
    centred = tensor - average
    variance = jnp.mean(centred * centred, axis=-1, keepdims=True)
    scale = lax.rsqrt(variance + epsilon)
    normal = centred * scale
    d_normal = d_out * gain
    mean_d = jnp.mean(d_normal, axis=-1, keepdims=True)
    mean_dn = jnp.mean(d_normal * normal, axis=-1, keepdims=True)
    return (d_normal - mean_d - normal * mean_dn) * scale


def dot_both(x, w, inner, up):
    cut = w.shape[0] // 256 * 256
    tail = dot(
        jnp.concatenate([x[:, cut:], inner], axis=1), jnp.concatenate([w[cut:], up], axis=0)
    )
    return dot(x[:, :cut], w[:cut]) + tail


def dot_both_t(x, w, inner, up_t):
    cut = w.shape[1] // 256 * 256
    tail = dot_t(
        jnp.concatenate([x[:, cut:], inner], axis=1), jnp.concatenate([w[:, cut:], up_t], axis=1)
    )
    return dot_t(x[:, :cut], w[:, :cut]) + tail


def whole(shape):
    return pl.BlockSpec(shape, lambda i: (0,) * len(shape), pipeline_mode=pl.Buffered(1))


def columns(rows, width):
    return pl.BlockSpec((rows, width), lambda i: (0, i))


def struct(shape, dtype):
    return jax.ShapeDtypeStruct(shape, dtype)


def dense_params(flops, bytes_accessed):
    return dict(
        cost_estimate=pl.CostEstimate(
            flops=flops, bytes_accessed=bytes_accessed, transcendentals=0
        ),
        compiler_params=pltpu.CompilerParams(vmem_limit_bytes=VMEM_LIMIT),
    )


def qkv_kernel(hidden, w, vec, down, up, normed, inner, qkv, parts):
    c = pl.program_id(0)

    @pl.when(c == 0)
    def _():
        value = layer_norm(hidden[...], vec[0:1], vec[1:2]).astype(BF16)
        normed[...] = value
        narrow = dot_t(value, down[...]).astype(BF16)
        inner[...] = narrow
        for part in range(3):
            parts[part] = narrow[:, part * R : (part + 1) * R]

    bias = vec[pl.ds(jnp.where(c == 2, 5, 4), 1), :] * jnp.where(c == 1, 0.0, 1.0)
    qkv[...] = (dot_both(normed[...], w[...], parts[c], up[0]) + bias).astype(BF16)


def qkv_forward(hidden, w_qkv, vectors, attn):
    rows = hidden.shape[0]
    return pl.pallas_call(
        qkv_kernel,
        grid=(3,),
        in_specs=[
            whole((rows, D)),
            columns(D, D),
            whole((8, D)),
            whole((3 * R, D)),
            pl.BlockSpec((1, R, D), lambda i: (i, 0, 0)),
        ],
        out_specs=[whole((rows, D)), whole((rows, 3 * R)), columns(rows, D)],
        out_shape=[
            struct((rows, D), BF16),
            struct((rows, 3 * R), BF16),
            struct((rows, 3 * D), BF16),
        ],
        scratch_shapes=[pltpu.VMEM((3, rows, R), BF16)],
        name="qkv_forward",
        **dense_params(6 * rows * D * D, 14 * rows * D + 6 * D * D),
    )(hidden, w_qkv, vectors, attn[0:3].reshape(3 * R, D), attn[4:7])


TILE = 512


def up_kernel(
    attended, hidden, w_o, vec, down_o, up_o, down_1, w_1, b_1, up_1,
    inner_o, middle, normed, inner_up, gate, activated,
):
    @pl.when(pl.program_id(0) == 0)
    def _():
        narrow = dot_t(attended[...], down_o[...]).astype(BF16)
        inner_o[...] = narrow
        middle[...] = hidden[...] + (dot_both(attended[...], w_o[...], narrow, up_o[...]) + vec[6:7])
        value = layer_norm(middle[...], vec[2:3], vec[3:4]).astype(BF16)
        normed[...] = value
        inner_up[...] = dot_t(value, down_1[...]).astype(BF16)

    x = dot_both(normed[...], w_1[...], inner_up[...], up_1[...]) + b_1[...]
    gate[...] = x.astype(BF16)
    activated[...] = (0.5 * x * (1.0 + gelu_parts(x))).astype(BF16)


def up_forward(attended, hidden, w_o, vectors, attn, narrow, w_1, b_1, wide):
    rows = hidden.shape[0]
    return pl.pallas_call(
        up_kernel,
        grid=(pl.cdiv(FF, TILE),),
        in_specs=[
            whole((rows, D)),
            whole((rows, D)),
            whole((D, D)),
            whole((8, D)),
            whole((R, D)),
            whole((R, D)),
            whole((R, D)),
            columns(D, TILE),
            columns(1, TILE),
            columns(R, TILE),
        ],
        out_specs=[
            whole((rows, R)),
            whole((rows, D)),
            whole((rows, D)),
            whole((rows, R)),
            columns(rows, TILE),
            columns(rows, TILE),
        ],
        out_shape=[
            struct((rows, R), BF16),
            struct((rows, D), F32),
            struct((rows, D), BF16),
            struct((rows, R), BF16),
            struct((rows, FF), BF16),
            struct((rows, FF), BF16),
        ],
        name="up_forward",
        **dense_params(2 * rows * D * (D + FF), 12 * rows * D + 4 * rows * FF + 2 * D * (D + FF)),
    )(attended, hidden, w_o, vectors, attn[3], attn[7], narrow[0], w_1, b_1, wide[0])


THIRD = D // 3


def down_kernel(activated, middle, w_2, b_2, down_2, up_2, inner, hidden):
    @pl.when(pl.program_id(0) == 0)
    def _():
        inner[...] = dot_t(activated[...], down_2[...]).astype(BF16)

    hidden[...] = middle[...] + (
        dot(activated[...], w_2[...]) + b_2[...] + dot(inner[...], up_2[...])
    )


def down_forward(activated, middle, w_2, b_2, narrow, wide):
    rows = middle.shape[0]
    return pl.pallas_call(
        down_kernel,
        grid=(3,),
        in_specs=[
            whole((rows, FF)),
            columns(rows, THIRD),
            columns(FF, THIRD),
            columns(1, THIRD),
            whole((R, FF)),
            columns(R, THIRD),
        ],
        out_specs=[whole((rows, R)), columns(rows, THIRD)],
        out_shape=[struct((rows, R), BF16), struct((rows, D), F32)],
        name="down_forward",
        **dense_params(2 * rows * D * FF, 8 * rows * D + 2 * rows * FF + 2 * D * FF),
    )(activated, middle, w_2, b_2, wide[1], narrow[1])


def gate_kernel(
    gradient, w_2, gate, down_2, up_1, up_2, inner_down, inner_up, d_gate, g_wide, d_inner_up, g_up_2,
    d_branch, d_inner_down, total,
):
    i = pl.program_id(0)

    @pl.when(i == 0)
    def _():
        value = gradient[...].astype(BF16)
        d_branch[...] = value
        d_inner_down[...] = dot_t(value, up_2[...]).astype(BF16)
        g_up_2[...] = dot_l(inner_down[...], value)
        total[...] = jnp.zeros_like(total)

    left = FF - i * TILE
    down = down_2[...]
    d_act = dot_t(d_branch[...], w_2[...]) + dot(d_inner_down[...], down)
    x = gate[...].astype(F32)
    t = gelu_parts(x)
    half = 0.5 * (1.0 + t)
    slope = half + 0.5 * x * (1.0 - t * t) * (
        0.7978845608028654 * (1.0 + 3 * 0.044715 * x * x)
    )
    keep = lax.broadcasted_iota(jnp.int32, (1, TILE), 1) < left
    value = jnp.where(keep, slope * d_act, 0.0).astype(BF16)
    d_gate[...] = value
    up = jnp.where(keep, up_1[...], jnp.zeros_like(up_1[...]))
    total[...] += dot_t(value, up)
    g_wide[0:R] = dot_l(inner_up[...], value)
    g_wide[R : 2 * R] = dot_l(d_inner_down[...], (x * half).astype(BF16))

    @pl.when(i == pl.num_programs(0) - 1)
    def _():
        d_inner_up[...] = total[...].astype(BF16)


def gate_backward(gradient, w_2, gate, narrow, wide, inner_down, inner_up):
    rows = gradient.shape[0]
    return pl.pallas_call(
        gate_kernel,
        grid=(pl.cdiv(FF, TILE),),
        in_specs=[
            whole((rows, D)),
            pl.BlockSpec((TILE, D), lambda i: (i, 0)),
            columns(rows, TILE),
            columns(R, TILE),
            columns(R, TILE),
            whole((R, D)),
            whole((rows, R)),
            whole((rows, R)),
        ],
        out_specs=[columns(rows, TILE), columns(2 * R, TILE), whole((rows, R)), whole((R, D))],
        out_shape=[
            struct((rows, FF), BF16),
            struct((2 * R, FF), F32),
            struct((rows, R), BF16),
            struct((R, D), F32),
        ],
        scratch_shapes=[
            pltpu.VMEM((rows, D), BF16),
            pltpu.VMEM((rows, R), BF16),
            pltpu.VMEM((rows, R), F32),
        ],
        name="gate_backward",
        **dense_params(2 * rows * D * FF, 4 * rows * D + 4 * rows * FF + 2 * D * FF),
    )(gradient, w_2, gate, wide[1], wide[0], narrow[1], inner_down, inner_up)


def middle_kernel(
    d_gate, w_1, d_inner_up, down_1, normed, middle, gradient, vec, w_o, down_o, up_o, inner_o, attended,
    d_middle, d_attended, g_rows, d_normed,
):
    i = pl.program_id(0)
    at = pl.ds(pl.multiple_of(i * THIRD, LANES), THIRD)
    d_normed[:, at] = dot_t(d_gate[...], w_1[...]) + dot(d_inner_up[...], down_1[:, at])

    @pl.when(i == pl.num_programs(0) - 1)
    def _():
        value = gradient[...] + layer_norm_back(d_normed[...], middle[...], vec[2:3])
        d_middle[...] = value
        d_out = value.astype(BF16)
        d_inner_o = dot_t(d_out, up_o[...]).astype(BF16)
        d_attended[...] = (dot_t(d_out, w_o[...]) + dot(d_inner_o, down_o[...])).astype(BF16)
        g_rows[0:R] = dot_l(d_inner_o, attended[...])
        g_rows[R : 2 * R] = dot_l(inner_o[...], d_out)
        g_rows[2 * R : 3 * R] = dot_l(d_inner_up[...], normed[...])


def middle_backward(
    d_gate, w_1, d_inner_up, narrow, normed, middle, gradient, vectors, w_o, attn, inner_o, attended
):
    rows = gradient.shape[0]
    return pl.pallas_call(
        middle_kernel,
        grid=(3,),
        in_specs=[
            whole((rows, FF)),
            pl.BlockSpec((THIRD, FF), lambda i: (i, 0)),
            whole((rows, R)),
            whole((R, D)),
            whole((rows, D)),
            whole((rows, D)),
            whole((rows, D)),
            whole((8, D)),
            whole((D, D)),
            whole((R, D)),
            whole((R, D)),
            whole((rows, R)),
            whole((rows, D)),
        ],
        out_specs=[whole((rows, D)), whole((rows, D)), whole((3 * R, D))],
        out_shape=[
            struct((rows, D), F32),
            struct((rows, D), BF16),
            struct((3 * R, D), F32),
        ],
        scratch_shapes=[pltpu.VMEM((rows, D), F32)],
        name="middle_backward",
        **dense_params(2 * rows * D * (D + FF), 18 * rows * D + 2 * rows * FF + 2 * D * (D + FF)),
    )(
        d_gate, w_1, d_inner_up, narrow[0], normed, middle, gradient, vectors, w_o, attn[3], attn[7],
        inner_o, attended,
    )


def input_kernel(
    d_qkv, w_qkv, down, up, normed, inner, hidden, d_middle, vec, gradient, g_rows, d_normed, d_inner
):
    i = pl.program_id(0)

    @pl.when(i == 0)
    def _():
        for c in range(3):
            part = d_qkv[:, c * D : (c + 1) * D]
            d_inner[:, c * R : (c + 1) * R] = dot_t(part, up[c]).astype(BF16)
            g_rows[(3 + c) * R : (4 + c) * R] = dot_l(inner[:, c * R : (c + 1) * R], part)
        g_rows[0 : 3 * R] = dot_l(d_inner[...], normed[...])

    at = pl.ds(pl.multiple_of(i * THIRD, LANES), THIRD)
    d_normed[:, at] = dot_t(d_qkv[...], w_qkv[...]) + dot(d_inner[...], down[:, at])

    @pl.when(i == pl.num_programs(0) - 1)
    def _():
        gradient[...] = d_middle[...] + layer_norm_back(d_normed[...], hidden[...], vec[0:1])


def input_backward(d_qkv, w_qkv, attn, normed, inner, hidden, d_middle, vectors):
    rows = hidden.shape[0]
    return pl.pallas_call(
        input_kernel,
        grid=(3,),
        in_specs=[
            whole((rows, 3 * D)),
            pl.BlockSpec((THIRD, 3 * D), lambda i: (i, 0)),
            whole((3 * R, D)),
            whole((3, R, D)),
            whole((rows, D)),
            whole((rows, 3 * R)),
            whole((rows, D)),
            whole((rows, D)),
            whole((8, D)),
        ],
        out_specs=[whole((rows, D)), whole((6 * R, D))],
        out_shape=[struct((rows, D), F32), struct((6 * R, D), F32)],
        scratch_shapes=[pltpu.VMEM((rows, D), F32), pltpu.VMEM((rows, 3 * R), BF16)],
        name="input_backward",
        **dense_params(6 * rows * D * D, 20 * rows * D + 6 * D * D),
    )(d_qkv, w_qkv, attn[0:3].reshape(3 * R, D), attn[4:7], normed, inner, hidden, d_middle, vectors)


def local(
    activations,
    group_image_count,
    image_adapter_index,
    lengths,
    frozen,
    attention_adapter_weights,
    narrow_adapter_weights,
    broad_adapter_weights,
    cotangent,
):
    slots, local_len, _ = activations.shape
    seq_parts = lax.axis_size("seq")
    fsdp_parts = lax.axis_size("fsdp")
    device_count = seq_parts * fsdp_parts
    me = lax.axis_index("seq")
    seq_total = local_len * seq_parts
    layer_count = frozen.shape[0]
    adapters = attention_adapter_weights.shape[2]
    parts = seq_parts // slots
    slot = me // parts
    part = me % parts
    tokens = seq_total // parts
    groups = [[s * parts + p for p in range(parts)] for s in range(slots)]

    def to_image(v):
        if parts == 1 and slots == 2:
            mine = lax.dynamic_index_in_dim(v, slot, 0, keepdims=False)
            other = lax.dynamic_index_in_dim(v, 1 - slot, 0, keepdims=False)
            other = lax.ppermute(other, "seq", [(0, 1), (1, 0)])
            return jnp.where(
                slot == 0,
                jnp.concatenate([mine, other], 0),
                jnp.concatenate([other, mine], 0),
            )
        whole = lax.all_gather(v, "seq", axis=1, tiled=True)
        whole = lax.dynamic_index_in_dim(whole, slot, 0, keepdims=False)
        return lax.dynamic_slice_in_dim(whole, part * tokens, tokens, 0)

    def to_tokens(v):
        if parts == 1 and slots == 2:
            mine = lax.dynamic_slice_in_dim(v, slot * local_len, local_len, 0)
            other = lax.dynamic_slice_in_dim(v, (1 - slot) * local_len, local_len, 0)
            other = lax.ppermute(other, "seq", [(0, 1), (1, 0)])
            return jnp.where(slot == 0, jnp.stack([mine, other]), jnp.stack([other, mine]))
        whole = lax.all_gather(v, "seq", axis=0, tiled=True).reshape(slots, seq_total, -1)
        return lax.dynamic_slice_in_dim(whole, me * local_len, local_len, 1)

    length = lax.dynamic_slice_in_dim(lengths, slot, 1, 0)
    adapter = lax.dynamic_index_in_dim(image_adapter_index, slot, 0, keepdims=False)
    is_live = slot < group_image_count[0]
    positions = part * tokens + jnp.arange(tokens, dtype=jnp.int32)
    row_mask = ((positions < length[0]) & is_live).astype(F32)[:, None]
    def pick(table):
        return lax.dynamic_index_in_dim(table, adapter, 1, keepdims=False)

    shards = lax.optimization_barrier(frozen.reshape(layer_count, -1, LANES))
    hidden = to_image(activations).astype(F32) * row_mask
    stored = []
    weights = []
    for layer in range(layer_count):
        if (fsdp_parts, seq_parts) == (16, 2):
            flat = gather_blocks(shards[layer], 0)
        else:
            flat = lax.all_gather(shards[layer], "fsdp", axis=0, tiled=True)
        w_qkv, w_o, w_1, w_2 = unpack(flat)
        vectors = lax.slice_in_dim(flat, CUT_VECTORS, CUT_VECTORS + 106, axis=0).reshape(-1)
        vectors, b_1 = vectors[: 8 * D].reshape(8, D).astype(F32), vectors[8 * D : 8 * D + FF]
        b_1 = b_1.astype(F32)[None, :]
        attn = pick(attention_adapter_weights[layer])
        narrow = pick(narrow_adapter_weights[layer])
        wide = pick(broad_adapter_weights[layer])
        weights.append((w_qkv, w_o, w_1, w_2, vectors, attn, narrow, wide))
        normed, inner_qkv, qkv = qkv_forward(hidden, w_qkv, vectors, attn)
        keys = None
        if parts > 1:
            keys = lax.all_gather(
                qkv[:, D:], "seq", axis=0, tiled=True, axis_index_groups=groups
            )
        attended, stats = attn_fwd(length, qkv, keys)
        inner_o, middle, normed_two, inner_up, gate, activated = up_forward(
            attended, hidden, w_o, vectors, attn, narrow, w_1, b_1, wide
        )
        inner_down, next_hidden = down_forward(
            activated, middle, w_2, vectors[7:8], narrow, wide
        )
        stored.append(
            (
                hidden,
                normed,
                inner_qkv,
                qkv,
                keys,
                stats,
                attended,
                inner_o,
                middle,
                normed_two,
                inner_up,
                gate,
                inner_down,
            )
        )
        hidden = next_hidden
    output = to_tokens((hidden * row_mask).astype(BF16))
    gradient = to_image(cotangent).astype(F32) * row_mask
    collected = [None] * layer_count
    for layer in reversed(range(layer_count)):
        (
            layer_input,
            normed,
            inner_qkv,
            qkv,
            keys,
            stats,
            attended,
            inner_o,
            middle,
            normed_two,
            inner_up,
            gate,
            inner_down,
        ) = stored[layer]
        w_qkv, w_o, w_1, w_2, vectors, attn, narrow, wide = weights[layer]
        d_gate, g_wide, d_inner_up, g_up_2 = gate_backward(
            gradient, w_2, gate, narrow, wide, inner_down, inner_up
        )
        d_middle, d_attended, g_middle = middle_backward(
            d_gate, w_1, d_inner_up, narrow, normed_two, middle, gradient, vectors, w_o, attn,
            inner_o, attended,
        )
        d_qkv = attn_bwd(length, qkv, d_attended, attended, stats, keys)
        if parts > 1:
            d_keys = lax.psum_scatter(
                d_qkv[1].astype(F32),
                "seq",
                scatter_dimension=0,
                tiled=True,
                axis_index_groups=groups,
            )
            d_qkv = jnp.concatenate([d_qkv[0], d_keys.astype(BF16)], axis=1)
        else:
            d_qkv = d_qkv[0]
        gradient, g_input = input_backward(
            d_qkv, w_qkv, attn, normed, inner_qkv, layer_input, d_middle, vectors
        )
        rows_narrow = jnp.concatenate(
            [
                g_input[: 3 * R],
                g_middle[:R],
                g_input[3 * R :],
                g_middle[R:],
                g_up_2,
            ]
        ).astype(BF16)
        rows_wide = g_wide.astype(BF16)

        def shares(rows):
            share = -(-rows.shape[0] // device_count)
            rows = jnp.pad(rows, ((0, share * device_count - rows.shape[0]), (0, 0)))
            return rows.reshape(device_count, share * rows.shape[1])

        terms = [shares(rows_narrow), shares(rows_wide)]
        used = terms[0].shape[1] + terms[1].shape[1]
        label = jnp.broadcast_to(adapter.astype(BF16), (device_count, -used % LANES + LANES))
        terms = lax.all_to_all(
            jnp.concatenate(terms + [label], axis=1),
            ("fsdp", "seq"),
            split_axis=0,
            concat_axis=0,
            tiled=True,
        )
        choice = jnp.arange(adapters, dtype=F32)[:, None] == terms[:, used].astype(F32)[None, :]
        sums = jnp.dot(choice.astype(F32), terms.astype(F32), precision=lax.Precision.HIGHEST)
        sums = lax.all_gather(sums.astype(BF16), ("fsdp", "seq")).transpose(1, 0, 2)
        split = -(-10 * R // device_count) * D

        def table(part, count, width):
            part = part.reshape(adapters, -1, width)[:, : count * R]
            return part.reshape(adapters, count, R, width).transpose(1, 0, 2, 3).astype(F32)

        collected[layer] = (table(sums[:, :, :split], 10, D), table(sums[:, :, split:used], 2, FF))
    grad_attn = jnp.stack([entry[0][0:8] for entry in collected], axis=0)
    grad_narrow = jnp.stack([entry[0][8:10] for entry in collected], axis=0)
    grad_wide = jnp.stack([entry[1] for entry in collected], axis=0)
    input_grad = to_tokens((gradient * row_mask).astype(BF16)).astype(F32)
    return (output, input_grad, grad_attn, grad_narrow, grad_wide)


def solution(mesh):
    in_specs = (
        P("fsdp", "seq", None),
        P("fsdp"),
        P("fsdp"),
        P("fsdp"),
        P(None, "fsdp"),
        P(),
        P(),
        P(),
        P("fsdp", "seq", None),
    )
    out_specs = (P("fsdp", "seq", None), P("fsdp", "seq", None), P(), P(), P())
    return jax.shard_map(local, mesh=mesh, in_specs=in_specs, out_specs=out_specs, check_vma=False)
```

```python
import functools
import math

import jax
import jax.numpy as jnp
from jax import lax
from jax.experimental import pallas as pl
from jax.experimental.pallas import tpu as pltpu
from jax.sharding import PartitionSpec as P

D = 1152
HD = 72
H = 16
FF = 4304
R = 16
LANES = 128
BF16 = jnp.bfloat16
F32 = jnp.float32
MESH = pl.DeviceIdType.MESH
VMEM_LIMIT = 60 << 20
C2 = math.log2(math.e) / math.sqrt(HD)
SCALE = 1.0 / math.sqrt(HD)
NEG = -1e30
epsilon = 1e-06
CUT_OUT = 3 * D * D // LANES
CUT_UP = CUT_OUT + D * D // LANES
CUT_DOWN = CUT_UP + D * FF // LANES
CUT_VECTORS = CUT_DOWN + FF * D // LANES


def dot(a, b):
    return jnp.dot(a, b, preferred_element_type=F32)


def dot_t(a, b):
    return lax.dot_general(a, b, (((1,), (1,)), ((), ())), preferred_element_type=F32)


def dot_l(a, b):
    return lax.dot_general(a, b, (((0,), (0,)), ((), ())), preferred_element_type=F32)


PANELS = (3 * D // LANES, D // LANES, 36, D // LANES)
UNITS = (D // 16, D // 16, D // 16, FF // 16)
TILES_AT = (0, 1944, 2592, 5184)
TILES_END = 7605
TILES_VECTORS = 22
TILES_HELD = 7776
FLAT_AT = (0, CUT_OUT, CUT_UP, CUT_DOWN)
WIDE = PANELS[2] * LANES
UP_ROWS = 16 * FF // LANES
HALO = 1600


def lay_kernel(own_rows, tiles, index_ref, before, own, after, out, flat, held, turned):
    d = index_ref[0]
    margin = 16 * PANELS[2]
    flat[0:HALO] = before[...].astype(F32)
    flat[HALO : HALO + own_rows] = own[...].astype(F32)
    flat[HALO + own_rows : 2 * HALO + own_rows] = after[...].astype(F32)
    flat_base = d * own_rows - HALO
    tile_base = d * tiles

    def span(at, units, panels):
        low = jnp.maximum(tile_base - at, 0) // panels
        high = jnp.clip((tile_base + tiles - at + panels - 1) // panels, 0, units)
        return low, jnp.maximum(high, low)

    for at, start, units, panels in zip(
        TILES_AT + (TILES_END,),
        FLAT_AT + (CUT_VECTORS,),
        UNITS + (TILES_VECTORS,),
        PANELS + (1,),
    ):
        low, high = span(at, units, panels)
        if start == CUT_UP:
            lane = lax.broadcasted_iota(jnp.int32, (8, LANES), 1)

            def up_units(b, carry):
                u = low + 8 * b
                source = pl.multiple_of(start + UP_ROWS * u - flat_base, 2)
                for j in range(16):
                    first, shift = (FF * j) // LANES, (FF * j) % LANES
                    turn = LANES - shift
                    now = flat[pl.ds(source + first, 8, stride=UP_ROWS), :]
                    now = pltpu.roll(now, turn, 1) if shift else now
                    for c in range(34):
                        value = now
                        if c < 33 or shift > LANES - FF % LANES:
                            now = flat[pl.ds(source + first + c + 1, 8, stride=UP_ROWS), :]
                            now = pltpu.roll(now, turn, 1) if shift else now
                            if shift:
                                value = jnp.where(lane < turn, value, now)
                        if c == 33:
                            value = jnp.where(lane < FF - 33 * LANES, value, 0.0)
                        turned[pl.ds(16 * c + j, 8, stride=16 * PANELS[2]), :] = value
                target = pl.multiple_of(16 * (at + PANELS[2] * u - tile_base) + margin, 16)
                held[pl.ds(target, 8 * 16 * PANELS[2]), :] = turned[...].astype(BF16)
                return carry

            turned[...] = jnp.zeros_like(turned)
            lax.fori_loop(0, (high - low + 7) // 8, up_units, 0)
        else:

            def unit(u, carry):
                source = pl.multiple_of(start + 16 * panels * u - flat_base, 16)
                target = pl.multiple_of(16 * (at + panels * u - tile_base) + margin, 16)
                for c in range(panels):
                    value = flat[pl.ds(source + c, 16, stride=panels), :]
                    held[pl.ds(target + 16 * c, 16), :] = value.astype(BF16)
                return carry

            lax.fori_loop(low, high, unit, 0)
    out[...] = held[margin : margin + 16 * tiles]


def lay_shard(index, shard, tiles, perms):
    own_rows = shard.shape[0]
    before = lax.ppermute(shard[own_rows - HALO :], "fsdp", perms[0])
    after = lax.ppermute(shard[:HALO], "fsdp", perms[1])
    vm = pl.BlockSpec(memory_space=pltpu.VMEM)
    margin = 16 * PANELS[2]
    return pl.pallas_call(
        functools.partial(lay_kernel, own_rows, tiles),
        in_specs=[pl.BlockSpec(memory_space=pltpu.SMEM), vm, vm, vm],
        out_specs=vm,
        out_shape=jax.ShapeDtypeStruct((16 * tiles, LANES), BF16),
        scratch_shapes=[
            pltpu.VMEM((own_rows + 2 * HALO + 8 * UP_ROWS, LANES), F32),
            pltpu.VMEM((16 * tiles + 10 * margin, LANES), BF16),
            pltpu.VMEM((8 * margin, LANES), F32),
        ],
        compiler_params=pltpu.CompilerParams(vmem_limit_bytes=VMEM_LIMIT),
        name="lay_shard",
    )(index, before, shard, after)


def pad_lanes(x, extra=None):
    if extra is None:
        extra = jnp.zeros((x.shape[0], LANES - HD), x.dtype)
    return jnp.concatenate([x, extra], axis=1)


def first_lane(rows, value):
    lane = lax.broadcasted_iota(jnp.int32, (rows, LANES - HD), 1)
    return jnp.where(lane == 0, value, 0.0).astype(BF16)


def key_bias(rows, length):
    key = lax.broadcasted_iota(jnp.int32, (rows, LANES - HD), 0)
    return first_lane(rows, jnp.where(key < length, 0.0, NEG))


def attn_fwd_kernel(offset, len_ref, qkv_ref, kv_ref, o_ref, st_ref, q_s, k_s, v_s):
    if kv_ref is None:
        kv_ref = qkv_ref
    rows, keys = qkv_ref.shape[0], kv_ref.shape[0]
    one = first_lane(rows, F32(1.0))
    bias = key_bias(keys, len_ref[0])
    for h in range(H):
        q_s[h] = pad_lanes(qkv_ref[:, h * HD : (h + 1) * HD], one)
        k_s[h] = pad_lanes(kv_ref[:, offset + h * HD : offset + (h + 1) * HD], bias)
        v_s[h] = pad_lanes(kv_ref[:, offset + D + h * HD : offset + D + (h + 1) * HD])
    st_ref[...] = jnp.zeros_like(st_ref)
    lane = lax.broadcasted_iota(jnp.int32, (rows, LANES), 1)

    def body(h, carry):
        s = dot_t(q_s[h], k_s[h])
        m = jnp.max(s, axis=1, keepdims=True)
        p = jnp.exp2((s - m) * C2)
        total = jnp.sum(p, axis=1, keepdims=True)
        o = dot(p.astype(BF16), v_s[h])
        q_s[h] = (o * (1.0 / total)).astype(BF16)
        st_ref[...] = jnp.where(lane == h, m * C2 + jnp.log2(total), st_ref[...])
        return carry

    lax.fori_loop(0, H, body, 0)
    for h in range(H):
        o_ref[:, h * HD : (h + 1) * HD] = q_s[h][:, :HD]


def attn_fwd(length, qkv, kv=None):
    rows = qkv.shape[0]
    keys = rows if kv is None else kv.shape[0]
    vm = pl.BlockSpec(memory_space=pltpu.VMEM)
    if kv is None:
        kernel = lambda a, b, *rest: attn_fwd_kernel(D, a, b, None, *rest)
        operands = (length, qkv)
    else:
        kernel = functools.partial(attn_fwd_kernel, 0)
        operands = (length, qkv, kv)
    return pl.pallas_call(
        kernel,
        in_specs=[pl.BlockSpec(memory_space=pltpu.SMEM)] + [vm] * (len(operands) - 1),
        out_specs=[vm, vm],
        out_shape=[
            jax.ShapeDtypeStruct((rows, D), BF16),
            jax.ShapeDtypeStruct((rows, LANES), F32),
        ],
        scratch_shapes=[
            pltpu.VMEM((H, rows, LANES), BF16),
            pltpu.VMEM((H, keys, LANES), BF16),
            pltpu.VMEM((H, keys, LANES), BF16),
        ],
        cost_estimate=pl.CostEstimate(
            flops=H * rows * keys * 256 * 4, bytes_accessed=rows * D * 8, transcendentals=H * rows * keys
        ),
        compiler_params=pltpu.CompilerParams(vmem_limit_bytes=VMEM_LIMIT),
        name="attention_forward",
    )(*operands)


def attn_bwd_kernel(
    offset, len_ref, qkv_ref, kv_ref, do_ref, o_ref, st_ref, dq_ref, dkv_ref, q_s, k_s, v_s, do_s, st_t, dl_t
):
    if kv_ref is None:
        kv_ref, dkv_ref = qkv_ref, dq_ref
    rows, keys = qkv_ref.shape[0], kv_ref.shape[0]
    one = first_lane(rows, F32(1.0))
    bias = key_bias(keys, len_ref[0])
    lane = lax.broadcasted_iota(jnp.int32, (rows, LANES), 1)
    delta = jnp.zeros((rows, LANES), F32)
    for h in range(H):
        q_s[h] = pad_lanes(qkv_ref[:, h * HD : (h + 1) * HD], one)
        k_s[h] = pad_lanes(kv_ref[:, offset + h * HD : offset + (h + 1) * HD], bias)
        v_s[h] = pad_lanes(kv_ref[:, offset + D + h * HD : offset + D + (h + 1) * HD])
        do = do_ref[:, h * HD : (h + 1) * HD]
        do_s[h] = pad_lanes(do)
        o = o_ref[:, h * HD : (h + 1) * HD].astype(F32)
        d = jnp.sum(do.astype(F32) * o, axis=1, keepdims=True)
        delta = jnp.where(lane == h, d, delta)
    st_t[...] = st_ref[...].T
    dl_t[...] = delta.T

    def body(h, carry):
        q, k, do = q_s[h], k_s[h], do_s[h]
        p = jnp.exp2(dot_t(k, q) * C2 - st_t[pl.ds(h, 1), :])
        dv = dot(p.astype(BF16), do)
        dp = dot_t(v_s[h], do)
        ds = (p * (dp - dl_t[pl.ds(h, 1), :])).astype(BF16)
        dk = dot(ds, q)
        dq = dot(k.T, ds)
        v_s[h] = dv.astype(BF16)
        k_s[h] = (dk * SCALE).astype(BF16)
        q_s[h] = (dq * SCALE).astype(BF16).T
        return carry

    lax.fori_loop(0, H, body, 0)
    for h in range(H):
        dq_ref[:, h * HD : (h + 1) * HD] = q_s[h][:, :HD]
        dkv_ref[:, offset + h * HD : offset + (h + 1) * HD] = k_s[h][:, :HD]
        dkv_ref[:, offset + D + h * HD : offset + D + (h + 1) * HD] = v_s[h][:, :HD]


def attn_bwd(length, qkv, do, o, st, kv=None):
    rows = qkv.shape[0]
    keys = rows if kv is None else kv.shape[0]
    vm = pl.BlockSpec(memory_space=pltpu.VMEM)
    if kv is None:
        kernel = lambda a, b, c, d, e, f, *rest: attn_bwd_kernel(
            D, a, b, None, c, d, e, f, None, *rest
        )
        operands = (length, qkv, do, o, st)
        outs = [jax.ShapeDtypeStruct((rows, 3 * D), BF16)]
    else:
        kernel = functools.partial(attn_bwd_kernel, 0)
        operands = (length, qkv, kv, do, o, st)
        outs = [jax.ShapeDtypeStruct((rows, D), BF16), jax.ShapeDtypeStruct((keys, 2 * D), BF16)]
    return pl.pallas_call(
        kernel,
        in_specs=[pl.BlockSpec(memory_space=pltpu.SMEM)] + [vm] * (len(operands) - 1),
        out_specs=[vm] * len(outs),
        out_shape=outs,
        scratch_shapes=[
            pltpu.VMEM((H, rows, LANES), BF16),
            pltpu.VMEM((H, keys, LANES), BF16),
            pltpu.VMEM((H, keys, LANES), BF16),
            pltpu.VMEM((H, rows, LANES), BF16),
            pltpu.VMEM((LANES, rows), F32),
            pltpu.VMEM((LANES, rows), F32),
        ],
        cost_estimate=pl.CostEstimate(
            flops=H * rows * keys * 256 * 10, bytes_accessed=rows * D * 16, transcendentals=H * rows * keys
        ),
        compiler_params=pltpu.CompilerParams(vmem_limit_bytes=VMEM_LIMIT),
        name="attention_backward",
    )(*operands)


def gather_kernel(
    src, out, stage, local_sem, z_recv, y_recv, b_recv, h_recv, c_recv_own, c_recv_z, c_recv_y, c_recv_b, c_recv_h,
    up_send, down_send, y_send, b_send, h_send, c_send_own, c_send_z, c_send_y, c_send_b, c_send_h,
):
    rows = src.shape[0]
    unit = rows // 6 // 16 * 16 + 16
    sizes = [unit, unit, rows // 2 - 2 * unit, rows // 2 - 2 * unit, unit]
    begins = [0, unit, 2 * unit, rows // 2, rows - 2 * unit]
    x = lax.axis_index("seq")
    f = lax.axis_index("fsdp")
    z, y, c = f // 4, (f // 2) % 2, f % 2

    def place(zb, yb, j, side, cb=None):
        owner = (zb * 2 + yb) * 2 + (c if cb is None else cb)
        begin = jnp.where(side == 0, begins[j], rows - begins[j] - sizes[j])
        return pl.multiple_of(owner * rows + begin, 16), sizes[j]

    def view(spot):
        return out.at[pl.ds(spot[0], spot[1]), :]

    def device(zb, yb, cb, xb):
        return ((zb * 2 + yb) * 2 + cb, xb)

    up, down = device(z + 1, y, c, x), device(z - 1, y, c, x)
    beside, across, mate = device(z, 1 - y, c, x), device(z, y, c, 1 - x), device(z, y, 1 - c, x)

    def copy(spot, send, recv, to, source=None):
        return pltpu.make_async_remote_copy(
            src_ref=view(spot) if source is None else source,
            dst_ref=view(spot),
            send_sem=send,
            recv_sem=recv,
            device_id=to,
            device_id_type=MESH,
        )

    def arrived(spot, recv):
        copy(spot, local_sem.at[1], recv, mate).wait_recv()

    barrier = pltpu.get_barrier_semaphore()
    for to in (beside, across, mate):
        pl.semaphore_signal(barrier, inc=1, device_id=to, device_id_type=MESH)

    @pl.when(z < 3)
    def _():
        pl.semaphore_signal(barrier, inc=1, device_id=up, device_id_type=MESH)

    @pl.when(z > 0)
    def _():
        pl.semaphore_signal(barrier, inc=1, device_id=down, device_id_type=MESH)

    pl.semaphore_wait(barrier, 3 + jnp.where(z < 3, 1, 0) + jnp.where(z > 0, 1, 0))

    def own(j):
        begin = jnp.where(x == 0, begins[j], rows - begins[j] - sizes[j])
        return src.at[pl.ds(pl.multiple_of(begin, 16), sizes[j]), :]

    whole = (pl.multiple_of(f * rows, 16), rows)
    for j in range(5):
        spot = place(z, y, j, x)

        @pl.when(z < 3)
        def _():
            copy(spot, up_send.at[z, j], z_recv.at[z, j], up, own(j)).start()

        @pl.when(z > 0)
        def _():
            copy(spot, down_send.at[z, j], z_recv.at[z, j], down, own(j)).start()

        if j < 3:
            copy(spot, y_send.at[z, j], y_recv.at[z, j], beside, own(j)).start()
    copy(whole, c_send_own.at[0], c_recv_own.at[0], mate, src).start()
    fetch = pltpu.make_async_copy(src, stage, local_sem.at[0])
    fetch.start()
    fetch.wait()
    keep = pltpu.make_async_copy(stage, view(whole), local_sem.at[0])
    keep.start()

    def z_event(d, j):
        def flow(zb, onward, to, sends):
            spot = place(zb, y, j, x)
            arrived(spot, z_recv.at[zb, j])

            @pl.when(onward)
            def _():
                copy(spot, sends.at[zb, j], z_recv.at[zb, j], to).start()

            if j == 0:
                copy(spot, b_send.at[zb], b_recv.at[zb], across).start()
            if j < 3:
                copy(spot, y_send.at[zb, j], y_recv.at[zb, j], beside).start()
            copy(spot, c_send_z.at[zb, j], c_recv_z.at[zb, j], mate).start()

        @pl.when(z - d >= 0)
        def _():
            flow(z - d, z < 3, up, up_send)

        @pl.when(z + d <= 3)
        def _():
            flow(z + d, z > 0, down, down_send)

    def each(d, act):
        if d == 0:
            act(z)
            return

        @pl.when(z - d >= 0)
        def _():
            act(z - d)

        @pl.when(z + d <= 3)
        def _():
            act(z + d)

    def y_event(d, j):
        def act(zb):
            spot = place(zb, 1 - y, j, x)
            arrived(spot, y_recv.at[zb, j])
            copy(spot, h_send.at[zb, j], h_recv.at[zb, j], across).start()
            copy(spot, c_send_y.at[zb, j], c_recv_y.at[zb, j], mate).start()

        each(d, act)

    def b_event(d):
        def act(zb):
            spot = place(zb, y, 0, 1 - x)
            arrived(spot, b_recv.at[zb])
            copy(spot, c_send_b.at[zb], c_recv_b.at[zb], mate).start()

        each(d, act)

    def h_event(d, j):
        def act(zb):
            spot = place(zb, 1 - y, j, 1 - x)
            arrived(spot, h_recv.at[zb, j])
            copy(spot, c_send_h.at[zb, j], c_recv_h.at[zb, j], mate).start()

        each(d, act)

    events = []
    for d in range(4):
        for j in range(5):
            at = (d - 1) * 5 + j + 1 if d else 0
            if d:
                events.append((at, functools.partial(z_event, d, j)))
                if j == 0:
                    events.append((at + 2, functools.partial(b_event, d)))
            if j < 3:
                ready = at + 1.5 if d else j + 1
                events.append((ready, functools.partial(y_event, d, j)))
                events.append((ready + 2, functools.partial(h_event, d, j)))
    for _, event in sorted(events, key=lambda e: e[0]):
        event()
    keep.wait()
    other = 1 - c

    def core_spot(zb, yb, j, side):
        return place(zb, yb, j, side, other)

    arrived((pl.multiple_of(((z * 2 + y) * 2 + other) * rows, 16), rows), c_recv_own.at[0])
    copy(whole, c_send_own.at[0], c_recv_own.at[0], mate).wait_send()
    for d in range(4):
        def drain(zb, d=d):
            for j in range(5):
                if d:
                    arrived(core_spot(zb, y, j, x), c_recv_z.at[zb, j])
                    copy(place(zb, y, j, x), c_send_z.at[zb, j], c_recv_z.at[zb, j], mate).wait_send()
                if j < 3:
                    arrived(core_spot(zb, 1 - y, j, x), c_recv_y.at[zb, j])
                    arrived(core_spot(zb, 1 - y, j, 1 - x), c_recv_h.at[zb, j])
                    spot = place(zb, 1 - y, j, x)
                    copy(spot, c_send_y.at[zb, j], c_recv_y.at[zb, j], mate).wait_send()
                    copy(spot, h_send.at[zb, j], h_recv.at[zb, j], across).wait_send()
                    spot = place(zb, 1 - y, j, 1 - x)
                    copy(spot, c_send_h.at[zb, j], c_recv_h.at[zb, j], mate).wait_send()
                    spot = place(zb, y, j, x)
                    copy(spot, y_send.at[zb, j], y_recv.at[zb, j], beside).wait_send()
            if d:
                arrived(core_spot(zb, y, 0, 1 - x), c_recv_b.at[zb])
                spot = place(zb, y, 0, 1 - x)
                copy(spot, c_send_b.at[zb], c_recv_b.at[zb], mate).wait_send()
                spot = place(zb, y, 0, x)
                copy(spot, b_send.at[zb], b_recv.at[zb], across).wait_send()

        each(d, drain)
        for j in range(5):
            @pl.when(jnp.logical_and(z - d >= 0, z < 3))
            def _():
                zb = z - d
                copy(place(zb, y, j, x), up_send.at[zb, j], z_recv.at[zb, j], up).wait_send()

            @pl.when(jnp.logical_and(z + d <= 3, z > 0))
            def _():
                zb = z + d
                copy(place(zb, y, j, x), down_send.at[zb, j], z_recv.at[zb, j], down).wait_send()


def gather_blocks(shard, collective_id, held_rows):
    rows = shard.shape[0]
    dma = pltpu.SemaphoreType.DMA
    core = [dma((1,)), dma((4, 5)), dma((4, 3)), dma((4,)), dma((4, 3))]
    return pl.pallas_call(
        gather_kernel,
        in_specs=[pl.BlockSpec(memory_space=pl.ANY)],
        out_specs=pl.BlockSpec(memory_space=pl.ANY),
        out_shape=jax.ShapeDtypeStruct((held_rows, LANES), BF16),
        scratch_shapes=[pltpu.VMEM((rows, LANES), BF16), dma((2,))]
        + [dma((4, 5)), dma((4, 3)), dma((4,)), dma((4, 3))] + core
        + [dma((4, 5)), dma((4, 5)), dma((4, 3)), dma((4,)), dma((4, 3))] + core,
        compiler_params=pltpu.CompilerParams(collective_id=collective_id, has_side_effects=True, vmem_limit_bytes=VMEM_LIMIT),
        name="gather_blocks",
    )(shard)


def gelu_parts(x):
    inner = 0.7978845608028654 * (x + 0.044715 * x * x * x)
    return jnp.tanh(inner)


def layer_norm(tensor, gain, offset):
    average = jnp.mean(tensor, axis=-1, keepdims=True)
    centred = tensor - average
    variance = jnp.mean(centred * centred, axis=-1, keepdims=True)
    return centred * lax.rsqrt(variance + epsilon) * gain + offset


def layer_norm_back(d_out, tensor, gain):
    average = jnp.mean(tensor, axis=-1, keepdims=True)
    centred = tensor - average
    variance = jnp.mean(centred * centred, axis=-1, keepdims=True)
    scale = lax.rsqrt(variance + epsilon)
    normal = centred * scale
    d_normal = d_out * gain
    mean_d = jnp.mean(d_normal, axis=-1, keepdims=True)
    mean_dn = jnp.mean(d_normal * normal, axis=-1, keepdims=True)
    return (d_normal - mean_d - normal * mean_dn) * scale


def dot_both(x, w, inner, up):
    cut = w.shape[0] // 256 * 256
    tail = dot(
        jnp.concatenate([x[:, cut:], inner], axis=1), jnp.concatenate([w[cut:], up], axis=0)
    )
    return dot(x[:, :cut], w[:cut]) + tail


def dot_both_t(x, w, inner, up_t):
    cut = w.shape[1] // 256 * 256
    tail = dot_t(
        jnp.concatenate([x[:, cut:], inner], axis=1), jnp.concatenate([w[:, cut:], up_t], axis=1)
    )
    return dot_t(x[:, :cut], w[:, :cut]) + tail


def matrix(ref, count=None):
    units, panels = ref.shape[:2]
    return jnp.concatenate(
        [ref[:, p].reshape(units * 16, LANES) for p in range(count or panels)], axis=1
    )


def unit_block(units, panels, place):
    return pl.BlockSpec((units, panels, 16, LANES), place)


def whole(shape):
    return pl.BlockSpec(shape, lambda i: (0,) * len(shape), pipeline_mode=pl.Buffered(1))


def columns(rows, width):
    return pl.BlockSpec((rows, width), lambda i: (0, i))


def struct(shape, dtype):
    return jax.ShapeDtypeStruct(shape, dtype)


def dense_params(flops, bytes_accessed):
    return dict(
        cost_estimate=pl.CostEstimate(
            flops=flops, bytes_accessed=bytes_accessed, transcendentals=0
        ),
        compiler_params=pltpu.CompilerParams(vmem_limit_bytes=VMEM_LIMIT),
    )


def qkv_kernel(hidden, w, vec, down, up, normed, inner, qkv, parts):
    c = pl.program_id(0)

    @pl.when(c == 0)
    def _():
        value = layer_norm(hidden[...], vec[0:1], vec[1:2]).astype(BF16)
        normed[...] = value
        narrow = dot_t(value, down[...]).astype(BF16)
        inner[...] = narrow
        for part in range(3):
            parts[part] = narrow[:, part * R : (part + 1) * R]

    bias = vec[pl.ds(jnp.where(c == 2, 5, 4), 1), :] * jnp.where(c == 1, 0.0, 1.0)
    qkv[...] = (dot_both(normed[...], matrix(w), parts[c], up[0]) + bias).astype(BF16)


def qkv_forward(hidden, w_qkv, vectors, attn):
    rows = hidden.shape[0]
    return pl.pallas_call(
        qkv_kernel,
        grid=(3,),
        in_specs=[
            whole((rows, D)),
            unit_block(72, 9, lambda i: (0, i, 0, 0)),
            whole((8, D)),
            whole((3 * R, D)),
            pl.BlockSpec((1, R, D), lambda i: (i, 0, 0)),
        ],
        out_specs=[whole((rows, D)), whole((rows, 3 * R)), columns(rows, D)],
        out_shape=[
            struct((rows, D), BF16),
            struct((rows, 3 * R), BF16),
            struct((rows, 3 * D), BF16),
        ],
        scratch_shapes=[pltpu.VMEM((3, rows, R), BF16)],
        name="qkv_forward",
        **dense_params(6 * rows * D * D, 14 * rows * D + 6 * D * D),
    )(hidden, w_qkv, vectors, attn[0:3].reshape(3 * R, D), attn[4:7])


TILE = 512
OUT_BLOCK = pl.BlockSpec(
    (72, 9, 16, LANES), lambda i: (3, 0, 0, 0), pipeline_mode=pl.Buffered(1)
)


def up_kernel(
    attended, hidden, w_o, vec, down_o, up_o, down_1, w_1, b_1, up_1,
    inner_o, middle, normed, inner_up, gate, activated,
):
    @pl.when(pl.program_id(0) == 0)
    def _():
        narrow = dot_t(attended[...], down_o[...]).astype(BF16)
        inner_o[...] = narrow
        middle[...] = hidden[...] + (dot_both(attended[...], matrix(w_o), narrow, up_o[...]) + vec[6:7])
        value = layer_norm(middle[...], vec[2:3], vec[3:4]).astype(BF16)
        normed[...] = value
        inner_up[...] = dot_t(value, down_1[...]).astype(BF16)

    x = dot_both(normed[...], matrix(w_1), inner_up[...], up_1[...]) + b_1[...]
    gate[...] = x.astype(BF16)
    activated[...] = (0.5 * x * (1.0 + gelu_parts(x))).astype(BF16)


def up_forward(attended, hidden, w_o, vectors, attn, narrow, w_1, b_1, wide):
    rows = hidden.shape[0]
    return pl.pallas_call(
        up_kernel,
        grid=(WIDE // TILE,),
        in_specs=[
            whole((rows, D)),
            whole((rows, D)),
            OUT_BLOCK,
            whole((8, D)),
            whole((R, D)),
            whole((R, D)),
            whole((R, D)),
            unit_block(72, 4, lambda i: (1, i, 0, 0)),
            columns(1, TILE),
            columns(R, TILE),
        ],
        out_specs=[
            whole((rows, R)),
            whole((rows, D)),
            whole((rows, D)),
            whole((rows, R)),
            columns(rows, TILE),
            columns(rows, TILE),
        ],
        out_shape=[
            struct((rows, R), BF16),
            struct((rows, D), F32),
            struct((rows, D), BF16),
            struct((rows, R), BF16),
            struct((rows, WIDE), BF16),
            struct((rows, WIDE), BF16),
        ],
        name="up_forward",
        **dense_params(2 * rows * D * (D + FF), 12 * rows * D + 4 * rows * FF + 2 * D * (D + FF)),
    )(attended, hidden, w_o, vectors, attn[3], attn[7], narrow[0], w_1, b_1, wide[0])


THIRD = D // 3


def down_kernel(activated, middle, w_2, b_2, down_2, up_2, inner, hidden):
    @pl.when(pl.program_id(0) == 0)
    def _():
        inner[...] = dot_t(activated[...], down_2[...]).astype(BF16)

    value = activated[:, :FF]

    hidden[...] = middle[...] + (
        dot(value, matrix(w_2)) + b_2[...] + dot(inner[...], up_2[...])
    )


def down_forward(activated, middle, w_2, b_2, narrow, wide):
    rows = middle.shape[0]
    return pl.pallas_call(
        down_kernel,
        grid=(3,),
        in_specs=[
            whole((rows, WIDE)),
            columns(rows, THIRD),
            pl.BlockSpec(
                (pl.Element(UNITS[3]), pl.Element(3), pl.Element(16), pl.Element(LANES)),
                lambda i: (TILES_AT[3] // 9, 3 * i, 0, 0),
            ),
            columns(1, THIRD),
            whole((R, WIDE)),
            columns(R, THIRD),
        ],
        out_specs=[whole((rows, R)), columns(rows, THIRD)],
        out_shape=[struct((rows, R), BF16), struct((rows, D), F32)],
        name="down_forward",
        **dense_params(2 * rows * D * FF, 8 * rows * D + 2 * rows * FF + 2 * D * FF),
    )(activated, middle, w_2, b_2, wide[1], narrow[1])


def gate_kernel(
    gradient, w_2, gate, down_2, up_1, up_2, inner_down, inner_up, d_gate, g_wide, d_inner_up, g_up_2,
    d_branch, d_inner_down, total,
):
    i = pl.program_id(0)

    @pl.when(i == 0)
    def _():
        value = gradient[...].astype(BF16)
        d_branch[...] = value
        d_inner_down[...] = dot_t(value, up_2[...]).astype(BF16)
        g_up_2[...] = dot_l(inner_down[...], value)
        total[...] = jnp.zeros_like(total)

    left = FF - i * TILE
    down = down_2[...]
    d_act = dot_t(d_branch[...], matrix(w_2)) + dot(d_inner_down[...], down)
    x = gate[...].astype(F32)
    t = gelu_parts(x)
    half = 0.5 * (1.0 + t)
    slope = half + 0.5 * x * (1.0 - t * t) * (
        0.7978845608028654 * (1.0 + 3 * 0.044715 * x * x)
    )
    keep = lax.broadcasted_iota(jnp.int32, (1, TILE), 1) < left
    value = jnp.where(keep, slope * d_act, 0.0).astype(BF16)
    d_gate[...] = value
    total[...] += dot_t(value, up_1[...])
    g_wide[0:R] = dot_l(inner_up[...], value)
    g_wide[R : 2 * R] = dot_l(d_inner_down[...], (x * half).astype(BF16))

    @pl.when(i == pl.num_programs(0) - 1)
    def _():
        d_inner_up[...] = total[...].astype(BF16)


def gate_backward(gradient, w_2, gate, narrow, wide, inner_down, inner_up):
    rows = gradient.shape[0]
    return pl.pallas_call(
        gate_kernel,
        grid=(WIDE // TILE,),
        in_specs=[
            whole((rows, D)),
            unit_block(TILE // 16, 9, lambda i: (TILES_AT[3] // 9 * 16 // TILE + i, 0, 0, 0)),
            columns(rows, TILE),
            columns(R, TILE),
            columns(R, TILE),
            whole((R, D)),
            whole((rows, R)),
            whole((rows, R)),
        ],
        out_specs=[columns(rows, TILE), columns(2 * R, TILE), whole((rows, R)), whole((R, D))],
        out_shape=[
            struct((rows, WIDE), BF16),
            struct((2 * R, WIDE), F32),
            struct((rows, R), BF16),
            struct((R, D), F32),
        ],
        scratch_shapes=[
            pltpu.VMEM((rows, D), BF16),
            pltpu.VMEM((rows, R), BF16),
            pltpu.VMEM((rows, R), F32),
        ],
        name="gate_backward",
        **dense_params(2 * rows * D * FF, 4 * rows * D + 4 * rows * FF + 2 * D * FF),
    )(gradient, w_2, gate, wide[1], wide[0], narrow[1], inner_down, inner_up)


def middle_kernel(
    d_gate, w_1, d_inner_up, down_1, normed, middle, gradient, vec, w_o, down_o, up_o, inner_o, attended,
    d_middle, d_attended, g_rows, d_normed,
):
    i = pl.program_id(0)
    at = pl.ds(pl.multiple_of(i * THIRD, LANES), THIRD)
    d_normed[:, at] = dot_t(d_gate[:, : 34 * LANES], matrix(w_1, 34)) + dot(
        d_inner_up[...], down_1[:, at]
    )

    @pl.when(i == pl.num_programs(0) - 1)
    def _():
        value = gradient[...] + layer_norm_back(d_normed[...], middle[...], vec[2:3])
        d_middle[...] = value
        d_out = value.astype(BF16)
        d_inner_o = dot_t(d_out, up_o[...]).astype(BF16)
        d_attended[...] = (dot_t(d_out, matrix(w_o)) + dot(d_inner_o, down_o[...])).astype(BF16)
        g_rows[0:R] = dot_l(d_inner_o, attended[...])
        g_rows[R : 2 * R] = dot_l(inner_o[...], d_out)
        g_rows[2 * R : 3 * R] = dot_l(d_inner_up[...], normed[...])


def middle_backward(
    d_gate, w_1, d_inner_up, narrow, normed, middle, gradient, vectors, w_o, attn, inner_o, attended
):
    rows = gradient.shape[0]
    return pl.pallas_call(
        middle_kernel,
        grid=(3,),
        in_specs=[
            whole((rows, WIDE)),
            unit_block(THIRD // 16, PANELS[2], lambda i: (3 + i, 0, 0, 0)),
            whole((rows, R)),
            whole((R, D)),
            whole((rows, D)),
            whole((rows, D)),
            whole((rows, D)),
            whole((8, D)),
            OUT_BLOCK,
            whole((R, D)),
            whole((R, D)),
            whole((rows, R)),
            whole((rows, D)),
        ],
        out_specs=[whole((rows, D)), whole((rows, D)), whole((3 * R, D))],
        out_shape=[
            struct((rows, D), F32),
            struct((rows, D), BF16),
            struct((3 * R, D), F32),
        ],
        scratch_shapes=[pltpu.VMEM((rows, D), F32)],
        name="middle_backward",
        **dense_params(2 * rows * D * (D + FF), 18 * rows * D + 2 * rows * FF + 2 * D * (D + FF)),
    )(
        d_gate, w_1, d_inner_up, narrow[0], normed, middle, gradient, vectors, w_o, attn[3], attn[7],
        inner_o, attended,
    )


def input_kernel(
    d_qkv, w_qkv, down, up, normed, inner, hidden, d_middle, vec, gradient, g_rows, d_normed, d_inner
):
    i = pl.program_id(0)

    @pl.when(i == 0)
    def _():
        for c in range(3):
            part = d_qkv[:, c * D : (c + 1) * D]
            d_inner[:, c * R : (c + 1) * R] = dot_t(part, up[c]).astype(BF16)
            g_rows[(3 + c) * R : (4 + c) * R] = dot_l(inner[:, c * R : (c + 1) * R], part)
        g_rows[0 : 3 * R] = dot_l(d_inner[...], normed[...])

    at = pl.ds(pl.multiple_of(i * THIRD, LANES), THIRD)
    d_normed[:, at] = dot_t(d_qkv[...], matrix(w_qkv)) + dot(d_inner[...], down[:, at])

    @pl.when(i == pl.num_programs(0) - 1)
    def _():
        gradient[...] = d_middle[...] + layer_norm_back(d_normed[...], hidden[...], vec[0:1])


def input_backward(d_qkv, w_qkv, attn, normed, inner, hidden, d_middle, vectors):
    rows = hidden.shape[0]
    return pl.pallas_call(
        input_kernel,
        grid=(3,),
        in_specs=[
            whole((rows, 3 * D)),
            unit_block(THIRD // 16, 27, lambda i: (i, 0, 0, 0)),
            whole((3 * R, D)),
            whole((3, R, D)),
            whole((rows, D)),
            whole((rows, 3 * R)),
            whole((rows, D)),
            whole((rows, D)),
            whole((8, D)),
        ],
        out_specs=[whole((rows, D)), whole((6 * R, D))],
        out_shape=[struct((rows, D), F32), struct((6 * R, D), F32)],
        scratch_shapes=[pltpu.VMEM((rows, D), F32), pltpu.VMEM((rows, 3 * R), BF16)],
        name="input_backward",
        **dense_params(6 * rows * D * D, 20 * rows * D + 6 * D * D),
    )(d_qkv, w_qkv, attn[0:3].reshape(3 * R, D), attn[4:7], normed, inner, hidden, d_middle, vectors)


SHARE = 5
SHARE_ROWS = SHARE * 16


def share_kernel(
    adapters, terms, label, out, held, labels, totals, sums, local_sem, send, recv, label_send, label_recv, pair_sem
):
    x = lax.axis_index("seq")
    f = lax.axis_index("fsdp")
    count = terms.shape[0]
    me = f * 2 + x
    barrier = pltpu.get_barrier_semaphore()

    def device(k):
        return (k // 2, k % 2)

    def greet(k, carry):
        to = (me + k) % count
        pl.semaphore_signal(barrier, inc=1, device_id=device(to), device_id_type=MESH)
        return carry

    lax.fori_loop(1, count, greet, 0)
    pl.semaphore_wait(barrier, count - 1)

    def share_to(to, slot):
        return pltpu.make_async_remote_copy(
            src_ref=terms.at[to],
            dst_ref=held.at[slot],
            send_sem=send.at[to],
            recv_sem=recv.at[slot],
            device_id=device(to),
            device_id_type=MESH,
        )

    def label_to(to, slot):
        return pltpu.make_async_remote_copy(
            src_ref=label,
            dst_ref=labels.at[slot],
            send_sem=label_send.at[to],
            recv_sem=label_recv.at[slot],
            device_id=device(to),
            device_id_type=MESH,
        )

    def post(k, carry):
        to = (me + k) % count
        label_to(to, me).start()
        share_to(to, me).start()
        return carry

    lax.fori_loop(1, count, post, 0)
    mine = pltpu.make_async_copy(terms.at[me], held.at[me], local_sem.at[0])
    named = pltpu.make_async_copy(label, labels.at[me], local_sem.at[1])
    mine.start()
    named.start()
    totals[...] = jnp.zeros_like(totals)

    def add(slot):
        value = held[slot].reshape(SHARE_ROWS, LANES).astype(F32)
        name = labels[slot][0:1]
        for e in range(adapters):
            totals[e] += jnp.where(name == float(e), value, 0.0)

    mine.wait()
    named.wait()
    add(me)

    def take(k, carry):
        slot = (me + count - k) % count
        label_to(slot, slot).wait_recv()
        share_to(slot, slot).wait_recv()
        add(slot)
        return carry

    lax.fori_loop(1, count, take, 0)
    sums[...] = totals[...].reshape(adapters * SHARE_ROWS, LANES).astype(BF16)
    rows = adapters * SHARE_ROWS
    part = out.at[pl.ds(pl.multiple_of(x * rows, 16), rows), :]
    keep = pltpu.make_async_copy(sums, part, local_sem.at[0])
    keep.start()
    keep.wait()
    across = pltpu.make_async_remote_copy(
        src_ref=part,
        dst_ref=part,
        send_sem=pair_sem.at[0],
        recv_sem=pair_sem.at[1],
        device_id=(f, 1 - x),
        device_id_type=MESH,
    )
    across.start()

    def sent(k, carry):
        to = (me + k) % count
        label_to(to, me).wait_send()
        share_to(to, me).wait_send()
        return carry

    lax.fori_loop(1, count, sent, 0)
    across.wait_send()
    other = out.at[pl.ds(pl.multiple_of((1 - x) * rows, 16), rows), :]
    pltpu.make_async_remote_copy(
        src_ref=other,
        dst_ref=other,
        send_sem=pair_sem.at[0],
        recv_sem=pair_sem.at[1],
        device_id=(f, 1 - x),
        device_id_type=MESH,
    ).wait_recv()


def share_terms(terms, label, adapters):
    count = terms.shape[0]
    dma = pltpu.SemaphoreType.DMA
    rows = adapters * SHARE_ROWS
    return pl.pallas_call(
        functools.partial(share_kernel, adapters),
        in_specs=[pl.BlockSpec(memory_space=pl.ANY)] * 2,
        out_specs=pl.BlockSpec(memory_space=pl.ANY),
        out_shape=jax.ShapeDtypeStruct((2 * rows, LANES), BF16),
        scratch_shapes=[
            pltpu.VMEM((count, SHARE, 16, LANES), BF16),
            pltpu.VMEM((count, 8, LANES), F32),
            pltpu.VMEM((adapters, SHARE_ROWS, LANES), F32),
            pltpu.VMEM((rows, LANES), BF16),
            dma((2,)),
            dma((count,)),
            dma((count,)),
            dma((count,)),
            dma((count,)),
            dma((2,)),
        ],
        compiler_params=pltpu.CompilerParams(
            collective_id=1, has_side_effects=True, vmem_limit_bytes=VMEM_LIMIT
        ),
        name="share_terms",
    )(terms, label)


def table_kernel(layers, *refs):
    attn, narrow, wide = refs[layers:]
    for layer in range(layers):
        source = refs[layer]
        for t in range(10 * 9 + 2 * 34):
            tile = source[t // SHARE, 0, t % SHARE].astype(F32)
            if t < 90:
                at = slice(t % 9 * LANES, (t % 9 + 1) * LANES)
                if t < 72:
                    attn[layer, t // 9, 0, :, at] = tile
                else:
                    narrow[layer, t // 9 - 8, 0, :, at] = tile
            else:
                c, p = (t - 90) // 34, (t - 90) % 34
                width = min(LANES, FF - p * LANES)
                wide[layer, c, 0, :, p * LANES : p * LANES + width] = tile[:, :width]


def gradient_tables(gathered, adapters):
    layers = len(gathered)
    count = gathered[0].shape[0] // (adapters * SHARE_ROWS)
    gathered = [g.reshape(count, adapters, SHARE, 16, LANES) for g in gathered]

    def out_block(kinds, width):
        return pl.BlockSpec((layers, kinds, 1, R, width), lambda e: (0, 0, e, 0, 0))

    return pl.pallas_call(
        functools.partial(table_kernel, layers),
        grid=(adapters,),
        in_specs=[pl.BlockSpec((count, 1, SHARE, 16, LANES), lambda e: (0, e, 0, 0, 0))] * layers,
        out_specs=[out_block(8, D), out_block(2, D), out_block(2, FF)],
        out_shape=[
            struct((layers, 8, adapters, R, D), F32),
            struct((layers, 2, adapters, R, D), F32),
            struct((layers, 2, adapters, R, FF), F32),
        ],
        compiler_params=pltpu.CompilerParams(vmem_limit_bytes=VMEM_LIMIT),
        name="gradient_tables",
    )(*gathered)


def local(
    activations,
    group_image_count,
    image_adapter_index,
    lengths,
    frozen,
    attention_adapter_weights,
    narrow_adapter_weights,
    broad_adapter_weights,
    cotangent,
):
    slots, local_len, _ = activations.shape
    seq_parts = lax.axis_size("seq")
    fsdp_parts = lax.axis_size("fsdp")
    device_count = seq_parts * fsdp_parts
    me = lax.axis_index("seq")
    seq_total = local_len * seq_parts
    layer_count = frozen.shape[0]
    adapters = attention_adapter_weights.shape[2]
    parts = seq_parts // slots
    on_block = (fsdp_parts, seq_parts, slots) == (16, 2, 2)
    slot = me // parts
    part = me % parts
    tokens = seq_total // parts
    groups = [[s * parts + p for p in range(parts)] for s in range(slots)]

    def to_image(v):
        if parts == 1 and slots == 2:
            mine = lax.dynamic_index_in_dim(v, slot, 0, keepdims=False)
            other = lax.dynamic_index_in_dim(v, 1 - slot, 0, keepdims=False)
            other = lax.ppermute(other, "seq", [(0, 1), (1, 0)])
            return jnp.where(
                slot == 0,
                jnp.concatenate([mine, other], 0),
                jnp.concatenate([other, mine], 0),
            )
        whole = lax.all_gather(v, "seq", axis=1, tiled=True)
        whole = lax.dynamic_index_in_dim(whole, slot, 0, keepdims=False)
        return lax.dynamic_slice_in_dim(whole, part * tokens, tokens, 0)

    def to_tokens(v):
        if parts == 1 and slots == 2:
            mine = lax.dynamic_slice_in_dim(v, slot * local_len, local_len, 0)
            other = lax.dynamic_slice_in_dim(v, (1 - slot) * local_len, local_len, 0)
            other = lax.ppermute(other, "seq", [(0, 1), (1, 0)])
            return jnp.where(slot == 0, jnp.stack([mine, other]), jnp.stack([other, mine]))
        whole = lax.all_gather(v, "seq", axis=0, tiled=True).reshape(slots, seq_total, -1)
        return lax.dynamic_slice_in_dim(whole, me * local_len, local_len, 1)

    length = lax.dynamic_slice_in_dim(lengths, slot, 1, 0)
    adapter = lax.dynamic_index_in_dim(image_adapter_index, slot, 0, keepdims=False)
    is_live = slot < group_image_count[0]
    positions = part * tokens + jnp.arange(tokens, dtype=jnp.int32)
    row_mask = ((positions < length[0]) & is_live).astype(F32)[:, None]
    def pick(table):
        return lax.dynamic_index_in_dim(table, adapter, 1, keepdims=False)

    shards = lax.optimization_barrier(frozen.reshape(layer_count, -1, LANES))
    steps = [(d, d + 1) for d in range(fsdp_parts - 1)]
    steps = (steps, [(b, a) for a, b in steps])
    tiles = -(-(TILES_END + TILES_VECTORS) // (2 * fsdp_parts)) * 2
    index = lax.axis_index("fsdp").astype(jnp.int32).reshape(1)
    shards = [lay_shard(index, shards[layer], tiles, steps) for layer in range(layer_count)]
    hidden = to_image(activations).astype(F32) * row_mask
    shards[0], hidden = lax.optimization_barrier((shards[0], hidden))
    stored = []
    weights = []
    for layer in range(layer_count):
        if on_block:
            flat = gather_blocks(shards[layer], 0, 16 * TILES_HELD)
        else:
            flat = lax.all_gather(shards[layer], "fsdp", axis=0, tiled=True)
            flat = jnp.pad(flat, ((0, 16 * TILES_HELD - flat.shape[0]), (0, 0)))
        if layer == layer_count - 1:
            cotangent, flat = lax.optimization_barrier((cotangent, flat))
            d_output = to_image(cotangent)
        w_qkv, w_o, w_1, w_2 = (flat.reshape(-1, panels, 16, LANES) for panels in PANELS)
        vectors = lax.slice_in_dim(flat, 16 * TILES_END, 16 * TILES_END + 106, axis=0).reshape(-1)
        vectors, b_1 = vectors[: 8 * D].reshape(8, D).astype(F32), vectors[8 * D : 8 * D + FF]
        b_1 = jnp.pad(b_1.astype(F32), (0, WIDE - FF))[None, :]
        attn = pick(attention_adapter_weights[layer])
        narrow = pick(narrow_adapter_weights[layer])
        wide = jnp.pad(pick(broad_adapter_weights[layer]), ((0, 0), (0, 0), (0, WIDE - FF)))
        weights.append((w_qkv, w_o, w_1, w_2, vectors, attn, narrow, wide))
        normed, inner_qkv, qkv = qkv_forward(hidden, w_qkv, vectors, attn)
        keys = None
        if parts > 1:
            keys = lax.all_gather(
                qkv[:, D:], "seq", axis=0, tiled=True, axis_index_groups=groups
            )
        attended, stats = attn_fwd(length, qkv, keys)
        inner_o, middle, normed_two, inner_up, gate, activated = up_forward(
            attended, hidden, w_o, vectors, attn, narrow, w_1, b_1, wide
        )
        inner_down, next_hidden = down_forward(
            activated, middle, w_2, vectors[7:8], narrow, wide
        )
        stored.append(
            (
                hidden,
                normed,
                inner_qkv,
                qkv,
                keys,
                stats,
                attended,
                inner_o,
                middle,
                normed_two,
                inner_up,
                gate,
                inner_down,
            )
        )
        hidden = next_hidden
    output = to_tokens((hidden * row_mask).astype(BF16))
    gradient = d_output.astype(F32) * row_mask
    collected = [None] * layer_count
    for layer in reversed(range(layer_count)):
        if layer == 0:
            output, gradient = lax.optimization_barrier((output, gradient))
        (
            layer_input,
            normed,
            inner_qkv,
            qkv,
            keys,
            stats,
            attended,
            inner_o,
            middle,
            normed_two,
            inner_up,
            gate,
            inner_down,
        ) = stored[layer]
        w_qkv, w_o, w_1, w_2, vectors, attn, narrow, wide = weights[layer]
        d_gate, g_wide, d_inner_up, g_up_2 = gate_backward(
            gradient, w_2, gate, narrow, wide, inner_down, inner_up
        )
        d_middle, d_attended, g_middle = middle_backward(
            d_gate, w_1, d_inner_up, narrow, normed_two, middle, gradient, vectors, w_o, attn,
            inner_o, attended,
        )
        d_qkv = attn_bwd(length, qkv, d_attended, attended, stats, keys)
        if parts > 1:
            d_keys = lax.psum_scatter(
                d_qkv[1].astype(F32),
                "seq",
                scatter_dimension=0,
                tiled=True,
                axis_index_groups=groups,
            )
            d_qkv = jnp.concatenate([d_qkv[0], d_keys.astype(BF16)], axis=1)
        else:
            d_qkv = d_qkv[0]
        gradient, g_input = input_backward(
            d_qkv, w_qkv, attn, normed, inner_qkv, layer_input, d_middle, vectors
        )
        rows_narrow = jnp.concatenate(
            [
                g_input[: 3 * R],
                g_middle[:R],
                g_input[3 * R :],
                g_middle[R:],
                g_up_2,
            ]
        )
        if on_block:
            terms = jnp.concatenate(
                [
                    rows_narrow.reshape(10, R, 9, LANES).transpose(0, 2, 1, 3).reshape(90, R, LANES),
                    g_wide.reshape(2, R, 36, LANES)
                    .transpose(0, 2, 1, 3)[:, :34]
                    .reshape(68, R, LANES),
                    jnp.zeros((2, R, LANES), F32),
                ]
            )
            terms = terms.astype(BF16).reshape(device_count, SHARE, R, LANES)
            label = jnp.broadcast_to(adapter.astype(F32), (8, LANES))
            sums = share_terms(terms, label, adapters)
            collected[layer] = gather_blocks(sums, 2, 16 * sums.shape[0])
            continue
        rows_narrow = rows_narrow.astype(BF16)
        rows_wide = g_wide[:, :FF].astype(BF16)

        def shares(rows):
            share = -(-rows.shape[0] // device_count)
            rows = jnp.pad(rows, ((0, share * device_count - rows.shape[0]), (0, 0)))
            return rows.reshape(device_count, share * rows.shape[1])

        terms = [shares(rows_narrow), shares(rows_wide)]
        used = terms[0].shape[1] + terms[1].shape[1]
        label = jnp.broadcast_to(adapter.astype(BF16), (device_count, -used % LANES + LANES))
        terms = lax.all_to_all(
            jnp.concatenate(terms + [label], axis=1),
            ("fsdp", "seq"),
            split_axis=0,
            concat_axis=0,
            tiled=True,
        )
        choice = jnp.arange(adapters, dtype=F32)[:, None] == terms[:, used].astype(F32)[None, :]
        sums = jnp.dot(choice.astype(F32), terms.astype(F32), precision=lax.Precision.HIGHEST)
        sums = lax.all_gather(sums.astype(BF16), ("fsdp", "seq")).transpose(1, 0, 2)
        split = -(-10 * R // device_count) * D

        def table(part, count, width):
            part = part.reshape(adapters, -1, width)[:, : count * R]
            return part.reshape(adapters, count, R, width).transpose(1, 0, 2, 3).astype(F32)

        collected[layer] = (table(sums[:, :, :split], 10, D), table(sums[:, :, split:used], 2, FF))
    if on_block:
        grad_attn, grad_narrow, grad_wide = gradient_tables(collected, adapters)
    else:
        grad_attn = jnp.stack([entry[0][0:8] for entry in collected], axis=0)
        grad_narrow = jnp.stack([entry[0][8:10] for entry in collected], axis=0)
        grad_wide = jnp.stack([entry[1] for entry in collected], axis=0)
    input_grad = to_tokens((gradient * row_mask).astype(BF16)).astype(F32)
    return (output, input_grad, grad_attn, grad_narrow, grad_wide)


def solution(mesh):
    in_specs = (
        P("fsdp", "seq", None),
        P("fsdp"),
        P("fsdp"),
        P("fsdp"),
        P(None, "fsdp"),
        P(),
        P(),
        P(),
        P("fsdp", "seq", None),
    )
    out_specs = (P("fsdp", "seq", None), P("fsdp", "seq", None), P(), P(), P())
    return jax.shard_map(local, mesh=mesh, in_specs=in_specs, out_specs=out_specs, check_vma=False)
```

```python
import functools
import math

import jax
import jax.numpy as jnp
from jax import lax
from jax.experimental import pallas as pl
from jax.experimental.pallas import tpu as pltpu
from jax.sharding import PartitionSpec as P

D = 1152
HD = 72
H = 16
FF = 4304
R = 16
LANES = 128
BF16 = jnp.bfloat16
F32 = jnp.float32
MESH = pl.DeviceIdType.MESH
VMEM_LIMIT = 60 << 20
VMEM_MOST = 67043328
C2 = math.log2(math.e) / math.sqrt(HD)
SCALE = 1.0 / math.sqrt(HD)
NEG = -1e30
epsilon = 1e-06
CUT_OUT = 3 * D * D // LANES
CUT_UP = CUT_OUT + D * D // LANES
CUT_DOWN = CUT_UP + D * FF // LANES
CUT_VECTORS = CUT_DOWN + FF * D // LANES


def dot(a, b):
    return jnp.dot(a, b, preferred_element_type=F32)


def dot_t(a, b):
    return lax.dot_general(a, b, (((1,), (1,)), ((), ())), preferred_element_type=F32)


def dot_l(a, b):
    return lax.dot_general(a, b, (((0,), (0,)), ((), ())), preferred_element_type=F32)


PANELS = (3 * D // LANES, D // LANES, 36, D // LANES)
UNITS = (D // 16, D // 16, D // 16, FF // 16)
TILES_AT = (0, 1944, 2592, 5184)
TILES_END = 7605
TILES_VECTORS = 22
TILES_HELD = 7776
FLAT_AT = (0, CUT_OUT, CUT_UP, CUT_DOWN)
WIDE = PANELS[2] * LANES
UP_ROWS = 16 * FF // LANES
HALO = 1600


def lay_kernel(own_rows, tiles, index_ref, before, own, after, out, flat, held, turned):
    d = index_ref[0]
    margin = 16 * PANELS[2]
    flat[0:HALO] = before[...].astype(F32)
    flat[HALO : HALO + own_rows] = own[...].astype(F32)
    flat[HALO + own_rows : 2 * HALO + own_rows] = after[...].astype(F32)
    flat_base = d * own_rows - HALO
    tile_base = d * tiles

    def span(at, units, panels):
        low = jnp.maximum(tile_base - at, 0) // panels
        high = jnp.clip((tile_base + tiles - at + panels - 1) // panels, 0, units)
        return low, jnp.maximum(high, low)

    for at, start, units, panels in zip(
        TILES_AT + (TILES_END,),
        FLAT_AT + (CUT_VECTORS,),
        UNITS + (TILES_VECTORS,),
        PANELS + (1,),
    ):
        low, high = span(at, units, panels)
        if start == CUT_UP:
            lane = lax.broadcasted_iota(jnp.int32, (8, LANES), 1)

            def up_units(b, carry):
                u = low + 8 * b
                source = pl.multiple_of(start + UP_ROWS * u - flat_base, 2)
                for j in range(16):
                    first, shift = (FF * j) // LANES, (FF * j) % LANES
                    turn = LANES - shift
                    now = flat[pl.ds(source + first, 8, stride=UP_ROWS), :]
                    now = pltpu.roll(now, turn, 1) if shift else now
                    for c in range(34):
                        value = now
                        if c < 33 or shift > LANES - FF % LANES:
                            now = flat[pl.ds(source + first + c + 1, 8, stride=UP_ROWS), :]
                            now = pltpu.roll(now, turn, 1) if shift else now
                            if shift:
                                value = jnp.where(lane < turn, value, now)
                        if c == 33:
                            value = jnp.where(lane < FF - 33 * LANES, value, 0.0)
                        turned[pl.ds(16 * c + j, 8, stride=16 * PANELS[2]), :] = value
                target = pl.multiple_of(16 * (at + PANELS[2] * u - tile_base) + margin, 16)
                held[pl.ds(target, 8 * 16 * PANELS[2]), :] = turned[...].astype(BF16)
                return carry

            turned[...] = jnp.zeros_like(turned)
            lax.fori_loop(0, (high - low + 7) // 8, up_units, 0)
        else:

            def unit(u, carry):
                source = pl.multiple_of(start + 16 * panels * u - flat_base, 16)
                target = pl.multiple_of(16 * (at + panels * u - tile_base) + margin, 16)
                for c in range(panels):
                    value = flat[pl.ds(source + c, 16, stride=panels), :]
                    held[pl.ds(target + 16 * c, 16), :] = value.astype(BF16)
                return carry

            lax.fori_loop(low, high, unit, 0)
    out[...] = held[margin : margin + 16 * tiles]


def lay_shard(index, shard, tiles, perms):
    own_rows = shard.shape[0]
    before = lax.ppermute(shard[own_rows - HALO :], "fsdp", perms[0])
    after = lax.ppermute(shard[:HALO], "fsdp", perms[1])
    vm = pl.BlockSpec(memory_space=pltpu.VMEM)
    margin = 16 * PANELS[2]
    return pl.pallas_call(
        functools.partial(lay_kernel, own_rows, tiles),
        in_specs=[pl.BlockSpec(memory_space=pltpu.SMEM), vm, vm, vm],
        out_specs=vm,
        out_shape=jax.ShapeDtypeStruct((16 * tiles, LANES), BF16),
        scratch_shapes=[
            pltpu.VMEM((own_rows + 2 * HALO + 8 * UP_ROWS, LANES), F32),
            pltpu.VMEM((16 * tiles + 10 * margin, LANES), BF16),
            pltpu.VMEM((8 * margin, LANES), F32),
        ],
        compiler_params=pltpu.CompilerParams(vmem_limit_bytes=VMEM_LIMIT),
        name="lay_shard",
    )(index, before, shard, after)


def pad_lanes(x, extra=None):
    if extra is None:
        extra = jnp.zeros((x.shape[0], LANES - HD), x.dtype)
    return jnp.concatenate([x, extra], axis=1)


def first_lane(rows, value):
    lane = lax.broadcasted_iota(jnp.int32, (rows, LANES - HD), 1)
    return jnp.where(lane == 0, value, 0.0).astype(BF16)


def key_bias(rows, length):
    key = lax.broadcasted_iota(jnp.int32, (rows, LANES - HD), 0)
    return first_lane(rows, jnp.where(key < length, 0.0, NEG))


def attn_fwd_kernel(offset, len_ref, qkv_ref, kv_ref, o_ref, st_ref, q_s, k_s, v_s):
    if kv_ref is None:
        kv_ref = qkv_ref
    rows, keys = qkv_ref.shape[0], kv_ref.shape[0]
    one = first_lane(rows, F32(1.0))
    bias = key_bias(keys, len_ref[0])
    for h in range(H):
        q_s[h] = pad_lanes(qkv_ref[:, h * HD : (h + 1) * HD], one)
        k_s[h] = pad_lanes(kv_ref[:, offset + h * HD : offset + (h + 1) * HD], bias)
        v_s[h] = pad_lanes(kv_ref[:, offset + D + h * HD : offset + D + (h + 1) * HD])
    st_ref[...] = jnp.zeros_like(st_ref)
    lane = lax.broadcasted_iota(jnp.int32, (rows, LANES), 1)

    def body(h, carry):
        s = dot_t(q_s[h], k_s[h])
        m = jnp.max(s, axis=1, keepdims=True)
        p = jnp.exp2((s - m) * C2)
        total = jnp.sum(p, axis=1, keepdims=True)
        o = dot(p.astype(BF16), v_s[h])
        q_s[h] = (o * (1.0 / total)).astype(BF16)
        st_ref[...] = jnp.where(lane == h, m * C2 + jnp.log2(total), st_ref[...])
        return carry

    lax.fori_loop(0, H, body, 0)
    for h in range(H):
        o_ref[:, h * HD : (h + 1) * HD] = q_s[h][:, :HD]


def attn_fwd(length, qkv, kv=None):
    rows = qkv.shape[0]
    keys = rows if kv is None else kv.shape[0]
    vm = pl.BlockSpec(memory_space=pltpu.VMEM)
    if kv is None:
        kernel = lambda a, b, *rest: attn_fwd_kernel(D, a, b, None, *rest)
        operands = (length, qkv)
    else:
        kernel = functools.partial(attn_fwd_kernel, 0)
        operands = (length, qkv, kv)
    return pl.pallas_call(
        kernel,
        in_specs=[pl.BlockSpec(memory_space=pltpu.SMEM)] + [vm] * (len(operands) - 1),
        out_specs=[vm, vm],
        out_shape=[
            jax.ShapeDtypeStruct((rows, D), BF16),
            jax.ShapeDtypeStruct((rows, LANES), F32),
        ],
        scratch_shapes=[
            pltpu.VMEM((H, rows, LANES), BF16),
            pltpu.VMEM((H, keys, LANES), BF16),
            pltpu.VMEM((H, keys, LANES), BF16),
        ],
        cost_estimate=pl.CostEstimate(
            flops=H * rows * keys * 256 * 4, bytes_accessed=rows * D * 8, transcendentals=H * rows * keys
        ),
        compiler_params=pltpu.CompilerParams(vmem_limit_bytes=VMEM_LIMIT),
        name="attention_forward",
    )(*operands)


def attn_bwd_kernel(
    offset, len_ref, qkv_ref, kv_ref, do_ref, o_ref, st_ref, dq_ref, dkv_ref, q_s, k_s, v_s, do_s, st_t, dl_t
):
    if kv_ref is None:
        kv_ref, dkv_ref = qkv_ref, dq_ref
    rows, keys = qkv_ref.shape[0], kv_ref.shape[0]
    one = first_lane(rows, F32(1.0))
    bias = key_bias(keys, len_ref[0])
    lane = lax.broadcasted_iota(jnp.int32, (rows, LANES), 1)
    delta = jnp.zeros((rows, LANES), F32)
    for h in range(H):
        q_s[h] = pad_lanes(qkv_ref[:, h * HD : (h + 1) * HD], one)
        k_s[h] = pad_lanes(kv_ref[:, offset + h * HD : offset + (h + 1) * HD], bias)
        v_s[h] = pad_lanes(kv_ref[:, offset + D + h * HD : offset + D + (h + 1) * HD])
        do = do_ref[:, h * HD : (h + 1) * HD]
        do_s[h] = pad_lanes(do)
        o = o_ref[:, h * HD : (h + 1) * HD].astype(F32)
        d = jnp.sum(do.astype(F32) * o, axis=1, keepdims=True)
        delta = jnp.where(lane == h, d, delta)
    st_t[...] = st_ref[...].T
    dl_t[...] = delta.T

    def body(h, carry):
        q, k, do = q_s[h], k_s[h], do_s[h]
        p = jnp.exp2(dot_t(k, q) * C2 - st_t[pl.ds(h, 1), :])
        dv = dot(p.astype(BF16), do)
        dp = dot_t(v_s[h], do)
        ds = (p * (dp - dl_t[pl.ds(h, 1), :])).astype(BF16)
        dk = dot(ds, q)
        dq = dot(k.T, ds)
        v_s[h] = dv.astype(BF16)
        k_s[h] = (dk * SCALE).astype(BF16)
        q_s[h] = (dq * SCALE).astype(BF16).T
        return carry

    lax.fori_loop(0, H, body, 0)
    for h in range(H):
        dq_ref[:, h * HD : (h + 1) * HD] = q_s[h][:, :HD]
        dkv_ref[:, offset + h * HD : offset + (h + 1) * HD] = k_s[h][:, :HD]
        dkv_ref[:, offset + D + h * HD : offset + D + (h + 1) * HD] = v_s[h][:, :HD]


def attn_bwd(length, qkv, do, o, st, kv=None):
    rows = qkv.shape[0]
    keys = rows if kv is None else kv.shape[0]
    vm = pl.BlockSpec(memory_space=pltpu.VMEM)
    if kv is None:
        kernel = lambda a, b, c, d, e, f, *rest: attn_bwd_kernel(
            D, a, b, None, c, d, e, f, None, *rest
        )
        operands = (length, qkv, do, o, st)
        outs = [jax.ShapeDtypeStruct((rows, 3 * D), BF16)]
    else:
        kernel = functools.partial(attn_bwd_kernel, 0)
        operands = (length, qkv, kv, do, o, st)
        outs = [jax.ShapeDtypeStruct((rows, D), BF16), jax.ShapeDtypeStruct((keys, 2 * D), BF16)]
    return pl.pallas_call(
        kernel,
        in_specs=[pl.BlockSpec(memory_space=pltpu.SMEM)] + [vm] * (len(operands) - 1),
        out_specs=[vm] * len(outs),
        out_shape=outs,
        scratch_shapes=[
            pltpu.VMEM((H, rows, LANES), BF16),
            pltpu.VMEM((H, keys, LANES), BF16),
            pltpu.VMEM((H, keys, LANES), BF16),
            pltpu.VMEM((H, rows, LANES), BF16),
            pltpu.VMEM((LANES, rows), F32),
            pltpu.VMEM((LANES, rows), F32),
        ],
        cost_estimate=pl.CostEstimate(
            flops=H * rows * keys * 256 * 10, bytes_accessed=rows * D * 16, transcendentals=H * rows * keys
        ),
        compiler_params=pltpu.CompilerParams(vmem_limit_bytes=VMEM_LIMIT),
        name="attention_backward",
    )(*operands)


def gather_plan(
    src, out, stage, local_sem, z_recv, y_recv, b_recv, h_recv, c_recv_own, c_recv_z, c_recv_y, c_recv_b, c_recv_h,
    up_send, down_send, y_send, b_send, h_send, c_send_own, c_send_z, c_send_y, c_send_b, c_send_h,
):
    rows = src.shape[0]
    unit = rows // 6 // 16 * 16 + 16
    sizes = [unit, unit, rows // 2 - 2 * unit, rows // 2 - 2 * unit, unit]
    begins = [0, unit, 2 * unit, rows // 2, rows - 2 * unit]
    x = lax.axis_index("seq")
    f = lax.axis_index("fsdp")
    z, y, c = f // 4, (f // 2) % 2, f % 2

    def place(zb, yb, j, side, cb=None):
        owner = (zb * 2 + yb) * 2 + (c if cb is None else cb)
        begin = jnp.where(side == 0, begins[j], rows - begins[j] - sizes[j])
        return pl.multiple_of(owner * rows + begin, 16), sizes[j]

    def view(spot):
        return out.at[pl.ds(spot[0], spot[1]), :]

    def device(zb, yb, cb, xb):
        return ((zb * 2 + yb) * 2 + cb, xb)

    up, down = device(z + 1, y, c, x), device(z - 1, y, c, x)
    beside, across, mate = device(z, 1 - y, c, x), device(z, y, c, 1 - x), device(z, y, 1 - c, x)

    def copy(spot, send, recv, to, source=None):
        return pltpu.make_async_remote_copy(
            src_ref=view(spot) if source is None else source,
            dst_ref=view(spot),
            send_sem=send,
            recv_sem=recv,
            device_id=to,
            device_id_type=MESH,
        )

    def arrived(spot, recv):
        copy(spot, local_sem.at[1], recv, mate).wait_recv()

    def own(j):
        begin = jnp.where(x == 0, begins[j], rows - begins[j] - sizes[j])
        return src.at[pl.ds(pl.multiple_of(begin, 16), sizes[j]), :]

    whole = (pl.multiple_of(f * rows, 16), rows)
    keep = pltpu.make_async_copy(src if stage is None else stage, view(whole), local_sem.at[0])

    def start():
        barrier = pltpu.get_barrier_semaphore()
        for to in (beside, across, mate):
            pl.semaphore_signal(barrier, inc=1, device_id=to, device_id_type=MESH)

        @pl.when(z < 3)
        def _():
            pl.semaphore_signal(barrier, inc=1, device_id=up, device_id_type=MESH)

        @pl.when(z > 0)
        def _():
            pl.semaphore_signal(barrier, inc=1, device_id=down, device_id_type=MESH)

        pl.semaphore_wait(barrier, 3 + jnp.where(z < 3, 1, 0) + jnp.where(z > 0, 1, 0))

        for j in range(5):
            spot = place(z, y, j, x)

            @pl.when(z < 3)
            def _():
                copy(spot, up_send.at[z, j], z_recv.at[z, j], up, own(j)).start()

            @pl.when(z > 0)
            def _():
                copy(spot, down_send.at[z, j], z_recv.at[z, j], down, own(j)).start()

            if j < 3:
                copy(spot, y_send.at[z, j], y_recv.at[z, j], beside, own(j)).start()
        copy(whole, c_send_own.at[0], c_recv_own.at[0], mate, src).start()
        if stage is None:
            keep.start()
        else:
            fetch = pltpu.make_async_copy(src, stage, local_sem.at[0])
            fetch.start()
            fetch.wait()
            keep.start()

    def z_event(d, j):
        def flow(zb, onward, to, sends):
            spot = place(zb, y, j, x)
            arrived(spot, z_recv.at[zb, j])

            @pl.when(onward)
            def _():
                copy(spot, sends.at[zb, j], z_recv.at[zb, j], to).start()

            if j == 0:
                copy(spot, b_send.at[zb], b_recv.at[zb], across).start()
            if j < 3:
                copy(spot, y_send.at[zb, j], y_recv.at[zb, j], beside).start()
            copy(spot, c_send_z.at[zb, j], c_recv_z.at[zb, j], mate).start()

        @pl.when(z - d >= 0)
        def _():
            flow(z - d, z < 3, up, up_send)

        @pl.when(z + d <= 3)
        def _():
            flow(z + d, z > 0, down, down_send)

    def each(d, act):
        if d == 0:
            act(z)
            return

        @pl.when(z - d >= 0)
        def _():
            act(z - d)

        @pl.when(z + d <= 3)
        def _():
            act(z + d)

    def y_event(d, j):
        def act(zb):
            spot = place(zb, 1 - y, j, x)
            arrived(spot, y_recv.at[zb, j])
            copy(spot, h_send.at[zb, j], h_recv.at[zb, j], across).start()
            copy(spot, c_send_y.at[zb, j], c_recv_y.at[zb, j], mate).start()

        each(d, act)

    def b_event(d):
        def act(zb):
            spot = place(zb, y, 0, 1 - x)
            arrived(spot, b_recv.at[zb])
            copy(spot, c_send_b.at[zb], c_recv_b.at[zb], mate).start()

        each(d, act)

    def h_event(d, j):
        def act(zb):
            spot = place(zb, 1 - y, j, 1 - x)
            arrived(spot, h_recv.at[zb, j])
            copy(spot, c_send_h.at[zb, j], c_recv_h.at[zb, j], mate).start()

        each(d, act)

    events = []
    for d in range(4):
        for j in range(5):
            at = (d - 1) * 5 + j + 1 if d else 0
            if d:
                events.append((at, functools.partial(z_event, d, j)))
                if j == 0:
                    events.append((at + 2, functools.partial(b_event, d)))
            if j < 3:
                ready = at + 1.5 if d else j + 1
                events.append((ready, functools.partial(y_event, d, j)))
                events.append((ready + 2, functools.partial(h_event, d, j)))
    def finish():
        keep.wait()
        other = 1 - c

        def core_spot(zb, yb, j, side):
            return place(zb, yb, j, side, other)

        arrived((pl.multiple_of(((z * 2 + y) * 2 + other) * rows, 16), rows), c_recv_own.at[0])
        copy(whole, c_send_own.at[0], c_recv_own.at[0], mate).wait_send()
        for d in range(4):
            def drain(zb, d=d):
                for j in range(5):
                    if d:
                        arrived(core_spot(zb, y, j, x), c_recv_z.at[zb, j])
                        copy(place(zb, y, j, x), c_send_z.at[zb, j], c_recv_z.at[zb, j], mate).wait_send()
                    if j < 3:
                        arrived(core_spot(zb, 1 - y, j, x), c_recv_y.at[zb, j])
                        arrived(core_spot(zb, 1 - y, j, 1 - x), c_recv_h.at[zb, j])
                        spot = place(zb, 1 - y, j, x)
                        copy(spot, c_send_y.at[zb, j], c_recv_y.at[zb, j], mate).wait_send()
                        copy(spot, h_send.at[zb, j], h_recv.at[zb, j], across).wait_send()
                        spot = place(zb, 1 - y, j, 1 - x)
                        copy(spot, c_send_h.at[zb, j], c_recv_h.at[zb, j], mate).wait_send()
                        spot = place(zb, y, j, x)
                        copy(spot, y_send.at[zb, j], y_recv.at[zb, j], beside).wait_send()
                if d:
                    arrived(core_spot(zb, y, 0, 1 - x), c_recv_b.at[zb])
                    spot = place(zb, y, 0, 1 - x)
                    copy(spot, c_send_b.at[zb], c_recv_b.at[zb], mate).wait_send()
                    spot = place(zb, y, 0, x)
                    copy(spot, b_send.at[zb], b_recv.at[zb], across).wait_send()

            each(d, drain)
            for j in range(5):
                @pl.when(jnp.logical_and(z - d >= 0, z < 3))
                def _():
                    zb = z - d
                    copy(place(zb, y, j, x), up_send.at[zb, j], z_recv.at[zb, j], up).wait_send()

                @pl.when(jnp.logical_and(z + d <= 3, z > 0))
                def _():
                    zb = z + d
                    copy(place(zb, y, j, x), down_send.at[zb, j], z_recv.at[zb, j], down).wait_send()

    return start, sorted(events, key=lambda e: e[0]), finish


def gather_kernel(*refs):
    start, events, finish = gather_plan(*refs)
    start()
    for _, event in events:
        event()
    finish()


def gather_semaphores():
    dma = pltpu.SemaphoreType.DMA
    core = [dma((1,)), dma((4, 5)), dma((4, 3)), dma((4,)), dma((4, 3))]
    links = [dma((4, 5)), dma((4, 3)), dma((4,)), dma((4, 3))]
    return [dma((2,))] + links + core + [dma((4, 5))] + links + core


def gather_blocks(shard, collective_id, held_rows):
    rows = shard.shape[0]
    return pl.pallas_call(
        gather_kernel,
        in_specs=[pl.BlockSpec(memory_space=pl.ANY)],
        out_specs=pl.BlockSpec(memory_space=pl.ANY),
        out_shape=jax.ShapeDtypeStruct((held_rows, LANES), BF16),
        scratch_shapes=[pltpu.VMEM((rows, LANES), BF16)] + gather_semaphores(),
        compiler_params=pltpu.CompilerParams(collective_id=collective_id, has_side_effects=True, vmem_limit_bytes=VMEM_LIMIT),
        name="gather_blocks",
    )(shard)


def gelu_parts(x):
    inner = 0.7978845608028654 * (x + 0.044715 * x * x * x)
    return jnp.tanh(inner)


def layer_norm(tensor, gain, offset):
    average = jnp.mean(tensor, axis=-1, keepdims=True)
    centred = tensor - average
    variance = jnp.mean(centred * centred, axis=-1, keepdims=True)
    return centred * lax.rsqrt(variance + epsilon) * gain + offset


def layer_norm_back(d_out, tensor, gain):
    average = jnp.mean(tensor, axis=-1, keepdims=True)
    centred = tensor - average
    variance = jnp.mean(centred * centred, axis=-1, keepdims=True)
    scale = lax.rsqrt(variance + epsilon)
    normal = centred * scale
    d_normal = d_out * gain
    mean_d = jnp.mean(d_normal, axis=-1, keepdims=True)
    mean_dn = jnp.mean(d_normal * normal, axis=-1, keepdims=True)
    return (d_normal - mean_d - normal * mean_dn) * scale


def dot_both(x, w, inner, up):
    cut = w.shape[0] // 256 * 256
    tail = dot(
        jnp.concatenate([x[:, cut:], inner], axis=1), jnp.concatenate([w[cut:], up], axis=0)
    )
    return dot(x[:, :cut], w[:cut]) + tail


def dot_both_t(x, w, inner, up_t):
    cut = w.shape[1] // 256 * 256
    tail = dot_t(
        jnp.concatenate([x[:, cut:], inner], axis=1), jnp.concatenate([w[:, cut:], up_t], axis=1)
    )
    return dot_t(x[:, :cut], w[:, :cut]) + tail


def matrix(ref, count=None):
    units, panels = ref.shape[:2]
    return jnp.concatenate(
        [ref[:, p].reshape(units * 16, LANES) for p in range(count or panels)], axis=1
    )


def unit_block(units, panels, place):
    return pl.BlockSpec((units, panels, 16, LANES), place)


def whole(shape):
    return pl.BlockSpec(shape, lambda i: (0,) * len(shape), pipeline_mode=pl.Buffered(1))


def columns(rows, width):
    return pl.BlockSpec((rows, width), lambda i: (0, i))


def struct(shape, dtype):
    return jax.ShapeDtypeStruct(shape, dtype)


def dense_params(flops, bytes_accessed):
    return dict(
        cost_estimate=pl.CostEstimate(
            flops=flops, bytes_accessed=bytes_accessed, transcendentals=0
        ),
        compiler_params=pltpu.CompilerParams(vmem_limit_bytes=VMEM_LIMIT),
    )


def qkv_kernel(hidden, w, vec, down, up, normed, inner, qkv, parts):
    c = pl.program_id(0)

    @pl.when(c == 0)
    def _():
        value = layer_norm(hidden[...], vec[0:1], vec[1:2]).astype(BF16)
        normed[...] = value
        narrow = dot_t(value, down[...]).astype(BF16)
        inner[...] = narrow
        for part in range(3):
            parts[part] = narrow[:, part * R : (part + 1) * R]

    bias = vec[pl.ds(jnp.where(c == 2, 5, 4), 1), :] * jnp.where(c == 1, 0.0, 1.0)
    qkv[...] = (dot_both(normed[...], matrix(w), parts[c], up[0]) + bias).astype(BF16)


def qkv_forward(hidden, w_qkv, vectors, attn):
    rows = hidden.shape[0]
    return pl.pallas_call(
        qkv_kernel,
        grid=(3,),
        in_specs=[
            whole((rows, D)),
            unit_block(72, 9, lambda i: (0, i, 0, 0)),
            whole((8, D)),
            whole((3 * R, D)),
            pl.BlockSpec((1, R, D), lambda i: (i, 0, 0)),
        ],
        out_specs=[whole((rows, D)), whole((rows, 3 * R)), columns(rows, D)],
        out_shape=[
            struct((rows, D), BF16),
            struct((rows, 3 * R), BF16),
            struct((rows, 3 * D), BF16),
        ],
        scratch_shapes=[pltpu.VMEM((3, rows, R), BF16)],
        name="qkv_forward",
        **dense_params(6 * rows * D * D, 14 * rows * D + 6 * D * D),
    )(hidden, w_qkv, vectors, attn[0:3].reshape(3 * R, D), attn[4:7])


TILE = 512
OUT_BLOCK = pl.BlockSpec(
    (72, 9, 16, LANES), lambda i: (3, 0, 0, 0), pipeline_mode=pl.Buffered(1)
)


def up_kernel(
    attended, hidden, w_o, vec, down_o, up_o, down_1, w_1, b_1, up_1,
    inner_o, middle, normed, inner_up, gate, activated,
):
    @pl.when(pl.program_id(0) == 0)
    def _():
        narrow = dot_t(attended[...], down_o[...]).astype(BF16)
        inner_o[...] = narrow
        middle[...] = hidden[...] + (dot_both(attended[...], matrix(w_o), narrow, up_o[...]) + vec[6:7])
        value = layer_norm(middle[...], vec[2:3], vec[3:4]).astype(BF16)
        normed[...] = value
        inner_up[...] = dot_t(value, down_1[...]).astype(BF16)

    x = dot_both(normed[...], matrix(w_1), inner_up[...], up_1[...]) + b_1[...]
    gate[...] = x.astype(BF16)
    activated[...] = (0.5 * x * (1.0 + gelu_parts(x))).astype(BF16)


def up_forward(attended, hidden, w_o, vectors, attn, narrow, w_1, b_1, wide):
    rows = hidden.shape[0]
    return pl.pallas_call(
        up_kernel,
        grid=(WIDE // TILE,),
        in_specs=[
            whole((rows, D)),
            whole((rows, D)),
            OUT_BLOCK,
            whole((8, D)),
            whole((R, D)),
            whole((R, D)),
            whole((R, D)),
            unit_block(72, 4, lambda i: (1, i, 0, 0)),
            columns(1, TILE),
            columns(R, TILE),
        ],
        out_specs=[
            whole((rows, R)),
            whole((rows, D)),
            whole((rows, D)),
            whole((rows, R)),
            columns(rows, TILE),
            columns(rows, TILE),
        ],
        out_shape=[
            struct((rows, R), BF16),
            struct((rows, D), F32),
            struct((rows, D), BF16),
            struct((rows, R), BF16),
            struct((rows, WIDE), BF16),
            struct((rows, WIDE), BF16),
        ],
        name="up_forward",
        **dense_params(2 * rows * D * (D + FF), 12 * rows * D + 4 * rows * FF + 2 * D * (D + FF)),
    )(attended, hidden, w_o, vectors, attn[3], attn[7], narrow[0], w_1, b_1, wide[0])


THIRD = D // 3


def down_kernel(activated, middle, w_2, b_2, down_2, up_2, inner, hidden):
    @pl.when(pl.program_id(0) == 0)
    def _():
        inner[...] = dot_t(activated[...], down_2[...]).astype(BF16)

    value = activated[:, :FF]

    hidden[...] = middle[...] + (
        dot(value, matrix(w_2)) + b_2[...] + dot(inner[...], up_2[...])
    )


def down_forward(activated, middle, w_2, b_2, narrow, wide):
    rows = middle.shape[0]
    return pl.pallas_call(
        down_kernel,
        grid=(3,),
        in_specs=[
            whole((rows, WIDE)),
            columns(rows, THIRD),
            pl.BlockSpec(
                (pl.Element(UNITS[3]), pl.Element(3), pl.Element(16), pl.Element(LANES)),
                lambda i: (TILES_AT[3] // 9, 3 * i, 0, 0),
            ),
            columns(1, THIRD),
            whole((R, WIDE)),
            columns(R, THIRD),
        ],
        out_specs=[whole((rows, R)), columns(rows, THIRD)],
        out_shape=[struct((rows, R), BF16), struct((rows, D), F32)],
        name="down_forward",
        **dense_params(2 * rows * D * FF, 8 * rows * D + 2 * rows * FF + 2 * D * FF),
    )(activated, middle, w_2, b_2, wide[1], narrow[1])


def gate_kernel(
    gradient, w_2, gate, down_2, up_1, up_2, inner_down, inner_up, d_gate, g_wide, d_inner_up, g_up_2,
    d_branch, d_inner_down, total,
):
    i = pl.program_id(0)

    @pl.when(i == 0)
    def _():
        value = gradient[...].astype(BF16)
        d_branch[...] = value
        d_inner_down[...] = dot_t(value, up_2[...]).astype(BF16)
        g_up_2[...] = dot_l(inner_down[...], value)
        total[...] = jnp.zeros_like(total)

    left = FF - i * TILE
    down = down_2[...]
    d_act = dot_t(d_branch[...], matrix(w_2)) + dot(d_inner_down[...], down)
    x = gate[...].astype(F32)
    t = gelu_parts(x)
    half = 0.5 * (1.0 + t)
    slope = half + 0.5 * x * (1.0 - t * t) * (
        0.7978845608028654 * (1.0 + 3 * 0.044715 * x * x)
    )
    keep = lax.broadcasted_iota(jnp.int32, (1, TILE), 1) < left
    value = jnp.where(keep, slope * d_act, 0.0).astype(BF16)
    d_gate[...] = value
    total[...] += dot_t(value, up_1[...])
    g_wide[0:R] = dot_l(inner_up[...], value)
    g_wide[R : 2 * R] = dot_l(d_inner_down[...], (x * half).astype(BF16))

    @pl.when(i == pl.num_programs(0) - 1)
    def _():
        d_inner_up[...] = total[...].astype(BF16)


def gate_backward(gradient, w_2, gate, narrow, wide, inner_down, inner_up):
    rows = gradient.shape[0]
    return pl.pallas_call(
        gate_kernel,
        grid=(WIDE // TILE,),
        in_specs=[
            whole((rows, D)),
            unit_block(TILE // 16, 9, lambda i: (TILES_AT[3] // 9 * 16 // TILE + i, 0, 0, 0)),
            columns(rows, TILE),
            columns(R, TILE),
            columns(R, TILE),
            whole((R, D)),
            whole((rows, R)),
            whole((rows, R)),
        ],
        out_specs=[columns(rows, TILE), columns(2 * R, TILE), whole((rows, R)), whole((R, D))],
        out_shape=[
            struct((rows, WIDE), BF16),
            struct((2 * R, WIDE), F32),
            struct((rows, R), BF16),
            struct((R, D), F32),
        ],
        scratch_shapes=[
            pltpu.VMEM((rows, D), BF16),
            pltpu.VMEM((rows, R), BF16),
            pltpu.VMEM((rows, R), F32),
        ],
        name="gate_backward",
        **dense_params(2 * rows * D * FF, 4 * rows * D + 4 * rows * FF + 2 * D * FF),
    )(gradient, w_2, gate, wide[1], wide[0], narrow[1], inner_down, inner_up)


def middle_kernel(
    d_gate, w_1, d_inner_up, down_1, normed, middle, gradient, vec, w_o, down_o, up_o, inner_o, attended,
    d_middle, d_attended, g_rows, d_normed,
):
    i = pl.program_id(0)
    at = pl.ds(pl.multiple_of(i * THIRD, LANES), THIRD)
    d_normed[:, at] = dot_t(d_gate[:, : 34 * LANES], matrix(w_1, 34)) + dot(
        d_inner_up[...], down_1[:, at]
    )

    @pl.when(i == pl.num_programs(0) - 1)
    def _():
        value = gradient[...] + layer_norm_back(d_normed[...], middle[...], vec[2:3])
        d_middle[...] = value
        d_out = value.astype(BF16)
        d_inner_o = dot_t(d_out, up_o[...]).astype(BF16)
        d_attended[...] = (dot_t(d_out, matrix(w_o)) + dot(d_inner_o, down_o[...])).astype(BF16)
        g_rows[0:R] = dot_l(d_inner_o, attended[...])
        g_rows[R : 2 * R] = dot_l(inner_o[...], d_out)
        g_rows[2 * R : 3 * R] = dot_l(d_inner_up[...], normed[...])


def middle_backward(
    d_gate, w_1, d_inner_up, narrow, normed, middle, gradient, vectors, w_o, attn, inner_o, attended
):
    rows = gradient.shape[0]
    return pl.pallas_call(
        middle_kernel,
        grid=(3,),
        in_specs=[
            whole((rows, WIDE)),
            unit_block(THIRD // 16, PANELS[2], lambda i: (3 + i, 0, 0, 0)),
            whole((rows, R)),
            whole((R, D)),
            whole((rows, D)),
            whole((rows, D)),
            whole((rows, D)),
            whole((8, D)),
            OUT_BLOCK,
            whole((R, D)),
            whole((R, D)),
            whole((rows, R)),
            whole((rows, D)),
        ],
        out_specs=[whole((rows, D)), whole((rows, D)), whole((3 * R, D))],
        out_shape=[
            struct((rows, D), F32),
            struct((rows, D), BF16),
            struct((3 * R, D), F32),
        ],
        scratch_shapes=[pltpu.VMEM((rows, D), F32)],
        name="middle_backward",
        **dense_params(2 * rows * D * (D + FF), 18 * rows * D + 2 * rows * FF + 2 * D * (D + FF)),
    )(
        d_gate, w_1, d_inner_up, narrow[0], normed, middle, gradient, vectors, w_o, attn[3], attn[7],
        inner_o, attended,
    )


def input_kernel(
    d_qkv, w_qkv, down, up, normed, inner, hidden, d_middle, vec, gradient, g_rows, d_normed, d_inner
):
    i = pl.program_id(0)

    @pl.when(i == 0)
    def _():
        for c in range(3):
            part = d_qkv[:, c * D : (c + 1) * D]
            d_inner[:, c * R : (c + 1) * R] = dot_t(part, up[c]).astype(BF16)
            g_rows[(3 + c) * R : (4 + c) * R] = dot_l(inner[:, c * R : (c + 1) * R], part)
        g_rows[0 : 3 * R] = dot_l(d_inner[...], normed[...])

    at = pl.ds(pl.multiple_of(i * THIRD, LANES), THIRD)
    d_normed[:, at] = dot_t(d_qkv[...], matrix(w_qkv)) + dot(d_inner[...], down[:, at])

    @pl.when(i == pl.num_programs(0) - 1)
    def _():
        gradient[...] = d_middle[...] + layer_norm_back(d_normed[...], hidden[...], vec[0:1])


def input_backward(d_qkv, w_qkv, attn, normed, inner, hidden, d_middle, vectors):
    rows = hidden.shape[0]
    return pl.pallas_call(
        input_kernel,
        grid=(3,),
        in_specs=[
            whole((rows, 3 * D)),
            unit_block(THIRD // 16, 27, lambda i: (i, 0, 0, 0)),
            whole((3 * R, D)),
            whole((3, R, D)),
            whole((rows, D)),
            whole((rows, 3 * R)),
            whole((rows, D)),
            whole((rows, D)),
            whole((8, D)),
        ],
        out_specs=[whole((rows, D)), whole((6 * R, D))],
        out_shape=[struct((rows, D), F32), struct((6 * R, D), F32)],
        scratch_shapes=[pltpu.VMEM((rows, D), F32), pltpu.VMEM((rows, 3 * R), BF16)],
        name="input_backward",
        **dense_params(6 * rows * D * D, 20 * rows * D + 6 * D * D),
    )(d_qkv, w_qkv, attn[0:3].reshape(3 * R, D), attn[4:7], normed, inner, hidden, d_middle, vectors)


FORWARD_STEPS = (3, H, WIDE // TILE, 3)
FORWARD_AT = (0, 3, 3 + H, 3 + H + WIDE // TILE)
FORWARD_BEGINS = (
    [4.5 * i for i in range(3)]
    + [14 + 2 * i for i in range(H)]
    + [46 + (5 if i else 0) + 2.6 * i for i in range(WIDE // TILE)]
    + [76 + 5 * i for i in range(3)]
)
CHUNK_TIME = 7.0


def forward_kernel(with_gather, *refs):
    (
        marks, hidden, w_qkv, vec, down, up, w_o, down_o, up_o, down_1, w_1, b_1, up_1, w_2, b_2, down_2, up_2,
    ) = refs[:17]
    refs = refs[17:]
    if with_gather:
        shard, refs = refs[0], refs[1:]
    (
        normed, inner_qkv, qkv, attended, stats, inner_o, middle, normed_two, inner_up, gate, inner_down,
        next_hidden,
    ) = refs[:12]
    refs = refs[12:]
    if with_gather:
        flat, refs = refs[0], refs[1:]
    heads, activated, parts = refs[:3]
    i = pl.program_id(0)
    rows = hidden.shape[0]
    _, att_at, up_at, down_at = FORWARD_AT
    last = down_at + 2

    def at_step(k):
        return pl.when(i == k)

    if with_gather:
        start, events, finish = gather_plan(shard, flat, None, *refs[3:])
        at_step(0)(start)
        steps = [[] for _ in FORWARD_BEGINS]
        late = []
        for when, event in events:
            ready = [k for k, begin in enumerate(FORWARD_BEGINS) if begin >= CHUNK_TIME * when + 4]
            (steps[ready[0]] if ready else late).append(event)
        for k, due in enumerate(steps):
            if due:

                @at_step(k)
                def _(due=due):
                    for event in due:
                        event()

    @pl.when(i < att_at)
    def _():
        @at_step(0)
        def _():
            value = layer_norm(hidden[...], vec[0:1], vec[1:2]).astype(BF16)
            normed[...] = value
            narrow = dot_t(value, down[...]).astype(BF16)
            inner_qkv[...] = narrow
            for part in range(3):
                parts[part] = narrow[:, part * R : (part + 1) * R]
            stats[...] = jnp.zeros_like(stats)

        bias = vec[pl.ds(jnp.where(i == 2, 5, 4), 1), :] * jnp.where(i == 1, 0.0, 1.0)
        value = (dot_both(normed[...], matrix(w_qkv), parts[i], up[0]) + bias).astype(BF16)
        qkv[...] = value
        mark = marks[0]
        for h in range(H):
            heads[i, h] = pad_lanes(value[:, h * HD : (h + 1) * HD], mark)

    @pl.when(jnp.logical_and(i >= att_at, i < up_at))
    def _():
        h = i - att_at
        lane = lax.broadcasted_iota(jnp.int32, (rows, LANES), 1)
        s = dot_t(heads[0, h], heads[1, h])
        m = jnp.max(s, axis=1, keepdims=True)
        p = jnp.exp2((s - m) * C2)
        total = jnp.sum(p, axis=1, keepdims=True)
        o = dot(p.astype(BF16), heads[2, h])
        heads[0, h] = (o * (1.0 / total)).astype(BF16)
        stats[...] = jnp.where(lane == h, m * C2 + jnp.log2(total), stats[...])

    @pl.when(jnp.logical_and(i >= up_at, i < down_at))
    def _():
        t = i - up_at

        @at_step(up_at)
        def _():
            for h in range(H):
                attended[:, h * HD : (h + 1) * HD] = heads[0, h][:, :HD]
            value = attended[...]
            narrow = dot_t(value, down_o[...]).astype(BF16)
            inner_o[...] = narrow
            middle[...] = hidden[...] + (dot_both(value, matrix(w_o), narrow, up_o[...]) + vec[6:7])
            value = layer_norm(middle[...], vec[2:3], vec[3:4]).astype(BF16)
            normed_two[...] = value
            inner_up[...] = dot_t(value, down_1[...]).astype(BF16)

        x = dot_both(normed_two[...], matrix(w_1), inner_up[...], up_1[...]) + b_1[...]
        gate[...] = x.astype(BF16)
        value = (0.5 * x * (1.0 + gelu_parts(x))).astype(BF16)
        activated[:, pl.ds(pl.multiple_of(t * TILE, LANES), TILE)] = value

    @pl.when(i >= down_at)
    def _():
        @at_step(down_at)
        def _():
            inner_down[...] = dot_t(activated[...], down_2[...]).astype(BF16)

        at = pl.ds(pl.multiple_of((i - down_at) * THIRD, LANES), THIRD)
        next_hidden[...] = middle[:, at] + (
            dot(activated[:, :FF], matrix(w_2.at[: UNITS[3]])) + b_2[...] + dot(inner_down[...], up_2[...])
        )

    if with_gather:

        @at_step(last)
        def _():
            for event in late:
                event()
            finish()


def layer_forward(length, hidden, w_qkv, w_o, w_1, w_2, vectors, b_1, attn, narrow, wide, shard=None):
    rows = hidden.shape[0]
    _, att_at, up_at, down_at = FORWARD_AT

    def step(i, k):
        return jnp.minimum(jnp.maximum(i - FORWARD_AT[k], 0), FORWARD_STEPS[k] - 1)

    def cols(count, width, k):
        return pl.BlockSpec((count, width), lambda i: (0, step(i, k)))

    lane = lax.broadcasted_iota(jnp.int32, (rows, LANES - HD), 1)
    key = lax.broadcasted_iota(jnp.int32, (rows, LANES - HD), 0)
    marks = jnp.stack([jnp.ones_like(lane, F32), jnp.where(key < length[0], 0.0, NEG), jnp.zeros_like(lane, F32)])
    marks = jnp.where(lane == 0, marks, 0.0).astype(BF16)
    operands = [
        marks, hidden, w_qkv, vectors, attn[0:3].reshape(3 * R, D), attn[4:7], w_o, attn[3], attn[7], narrow[0],
        w_1, b_1, wide[0], w_2, vectors[7:8], wide[1], narrow[1],
    ]
    in_specs = [
        pl.BlockSpec((1, rows, LANES - HD), lambda i: (step(i, 0), 0, 0)),
        whole((rows, D)),
        unit_block(72, 9, lambda i: (0, step(i, 0), 0, 0)),
        whole((8, D)),
        whole((3 * R, D)),
        pl.BlockSpec((1, R, D), lambda i: (step(i, 0), 0, 0)),
        OUT_BLOCK,
        whole((R, D)),
        whole((R, D)),
        whole((R, D)),
        unit_block(72, 4, lambda i: (1, step(i, 2), 0, 0)),
        cols(1, TILE, 2),
        cols(R, TILE, 2),
        unit_block(288, 3, lambda i: (2, step(i, 3), 0, 0)),
        cols(1, THIRD, 3),
        whole((R, WIDE)),
        cols(R, THIRD, 3),
    ]
    outs = [
        (whole((rows, D)), struct((rows, D), BF16)),
        (whole((rows, 3 * R)), struct((rows, 3 * R), BF16)),
        (cols(rows, D, 0), struct((rows, 3 * D), BF16)),
        (whole((rows, D)), struct((rows, D), BF16)),
        (whole((rows, LANES)), struct((rows, LANES), F32)),
        (whole((rows, R)), struct((rows, R), BF16)),
        (whole((rows, D)), struct((rows, D), F32)),
        (whole((rows, D)), struct((rows, D), BF16)),
        (whole((rows, R)), struct((rows, R), BF16)),
        (cols(rows, TILE, 2), struct((rows, WIDE), BF16)),
        (whole((rows, R)), struct((rows, R), BF16)),
        (cols(rows, THIRD, 3), struct((rows, D), F32)),
    ]
    scratch = [
        pltpu.VMEM((3, H, rows, LANES), BF16),
        pltpu.VMEM((rows, WIDE), BF16),
        pltpu.VMEM((3, rows, R), BF16),
    ]
    params = dict(vmem_limit_bytes=VMEM_MOST)
    if shard is not None:
        operands.append(shard)
        in_specs.append(pl.BlockSpec(memory_space=pl.ANY))
        outs.append(
            (pl.BlockSpec(memory_space=pl.ANY), struct((16 * TILES_HELD, LANES), BF16))
        )
        scratch += gather_semaphores()
        params.update(collective_id=3, has_side_effects=True)
    return pl.pallas_call(
        functools.partial(forward_kernel, shard is not None),
        grid=(sum(FORWARD_STEPS),),
        in_specs=in_specs,
        out_specs=[spec for spec, _ in outs],
        out_shape=[shape for _, shape in outs],
        scratch_shapes=scratch,
        cost_estimate=pl.CostEstimate(
            flops=2 * rows * D * (4 * D + 2 * FF) + 8 * rows * rows * D,
            bytes_accessed=2 * D * (4 * D + 2 * FF) + 30 * rows * D,
            transcendentals=H * rows * rows,
        ),
        compiler_params=pltpu.CompilerParams(**params),
        name="layer_forward_gather" if shard is not None else "layer_forward",
    )(*operands)


SHARE = 5
SHARE_ROWS = SHARE * 16


def share_kernel(
    adapters, terms, label, out, held, labels, totals, sums, local_sem, send, recv, label_send, label_recv, pair_sem
):
    x = lax.axis_index("seq")
    f = lax.axis_index("fsdp")
    count = terms.shape[0]
    me = f * 2 + x
    barrier = pltpu.get_barrier_semaphore()

    def device(k):
        return (k // 2, k % 2)

    def greet(k, carry):
        to = (me + k) % count
        pl.semaphore_signal(barrier, inc=1, device_id=device(to), device_id_type=MESH)
        return carry

    lax.fori_loop(1, count, greet, 0)
    pl.semaphore_wait(barrier, count - 1)

    def share_to(to, slot):
        return pltpu.make_async_remote_copy(
            src_ref=terms.at[to],
            dst_ref=held.at[slot],
            send_sem=send.at[to],
            recv_sem=recv.at[slot],
            device_id=device(to),
            device_id_type=MESH,
        )

    def label_to(to, slot):
        return pltpu.make_async_remote_copy(
            src_ref=label,
            dst_ref=labels.at[slot],
            send_sem=label_send.at[to],
            recv_sem=label_recv.at[slot],
            device_id=device(to),
            device_id_type=MESH,
        )

    def post(k, carry):
        to = (me + k) % count
        label_to(to, me).start()
        share_to(to, me).start()
        return carry

    lax.fori_loop(1, count, post, 0)
    mine = pltpu.make_async_copy(terms.at[me], held.at[me], local_sem.at[0])
    named = pltpu.make_async_copy(label, labels.at[me], local_sem.at[1])
    mine.start()
    named.start()
    totals[...] = jnp.zeros_like(totals)

    def add(slot):
        value = held[slot].reshape(SHARE_ROWS, LANES).astype(F32)
        name = labels[slot][0:1]
        for e in range(adapters):
            totals[e] += jnp.where(name == float(e), value, 0.0)

    mine.wait()
    named.wait()
    add(me)

    def take(k, carry):
        slot = (me + count - k) % count
        label_to(slot, slot).wait_recv()
        share_to(slot, slot).wait_recv()
        add(slot)
        return carry

    lax.fori_loop(1, count, take, 0)
    sums[...] = totals[...].reshape(adapters * SHARE_ROWS, LANES).astype(BF16)
    rows = adapters * SHARE_ROWS
    part = out.at[pl.ds(pl.multiple_of(x * rows, 16), rows), :]
    keep = pltpu.make_async_copy(sums, part, local_sem.at[0])
    keep.start()
    keep.wait()
    across = pltpu.make_async_remote_copy(
        src_ref=part,
        dst_ref=part,
        send_sem=pair_sem.at[0],
        recv_sem=pair_sem.at[1],
        device_id=(f, 1 - x),
        device_id_type=MESH,
    )
    across.start()

    def sent(k, carry):
        to = (me + k) % count
        label_to(to, me).wait_send()
        share_to(to, me).wait_send()
        return carry

    lax.fori_loop(1, count, sent, 0)
    across.wait_send()
    other = out.at[pl.ds(pl.multiple_of((1 - x) * rows, 16), rows), :]
    pltpu.make_async_remote_copy(
        src_ref=other,
        dst_ref=other,
        send_sem=pair_sem.at[0],
        recv_sem=pair_sem.at[1],
        device_id=(f, 1 - x),
        device_id_type=MESH,
    ).wait_recv()


def share_terms(terms, label, adapters):
    count = terms.shape[0]
    dma = pltpu.SemaphoreType.DMA
    rows = adapters * SHARE_ROWS
    return pl.pallas_call(
        functools.partial(share_kernel, adapters),
        in_specs=[pl.BlockSpec(memory_space=pl.ANY)] * 2,
        out_specs=pl.BlockSpec(memory_space=pl.ANY),
        out_shape=jax.ShapeDtypeStruct((2 * rows, LANES), BF16),
        scratch_shapes=[
            pltpu.VMEM((count, SHARE, 16, LANES), BF16),
            pltpu.VMEM((count, 8, LANES), F32),
            pltpu.VMEM((adapters, SHARE_ROWS, LANES), F32),
            pltpu.VMEM((rows, LANES), BF16),
            dma((2,)),
            dma((count,)),
            dma((count,)),
            dma((count,)),
            dma((count,)),
            dma((2,)),
        ],
        compiler_params=pltpu.CompilerParams(
            collective_id=1, has_side_effects=True, vmem_limit_bytes=VMEM_LIMIT
        ),
        name="share_terms",
    )(terms, label)


def table_kernel(layers, *refs):
    attn, narrow, wide = refs[layers:]
    for layer in range(layers):
        source = refs[layer]
        for t in range(10 * 9 + 2 * 34):
            tile = source[t // SHARE, 0, t % SHARE].astype(F32)
            if t < 90:
                at = slice(t % 9 * LANES, (t % 9 + 1) * LANES)
                if t < 72:
                    attn[layer, t // 9, 0, :, at] = tile
                else:
                    narrow[layer, t // 9 - 8, 0, :, at] = tile
            else:
                c, p = (t - 90) // 34, (t - 90) % 34
                width = min(LANES, FF - p * LANES)
                wide[layer, c, 0, :, p * LANES : p * LANES + width] = tile[:, :width]


def gradient_tables(gathered, adapters):
    layers = len(gathered)
    count = gathered[0].shape[0] // (adapters * SHARE_ROWS)
    gathered = [g.reshape(count, adapters, SHARE, 16, LANES) for g in gathered]

    def out_block(kinds, width):
        return pl.BlockSpec((layers, kinds, 1, R, width), lambda e: (0, 0, e, 0, 0))

    return pl.pallas_call(
        functools.partial(table_kernel, layers),
        grid=(adapters,),
        in_specs=[pl.BlockSpec((count, 1, SHARE, 16, LANES), lambda e: (0, e, 0, 0, 0))] * layers,
        out_specs=[out_block(8, D), out_block(2, D), out_block(2, FF)],
        out_shape=[
            struct((layers, 8, adapters, R, D), F32),
            struct((layers, 2, adapters, R, D), F32),
            struct((layers, 2, adapters, R, FF), F32),
        ],
        compiler_params=pltpu.CompilerParams(vmem_limit_bytes=VMEM_LIMIT),
        name="gradient_tables",
    )(*gathered)


def local(
    activations,
    group_image_count,
    image_adapter_index,
    lengths,
    frozen,
    attention_adapter_weights,
    narrow_adapter_weights,
    broad_adapter_weights,
    cotangent,
):
    slots, local_len, _ = activations.shape
    seq_parts = lax.axis_size("seq")
    fsdp_parts = lax.axis_size("fsdp")
    device_count = seq_parts * fsdp_parts
    me = lax.axis_index("seq")
    seq_total = local_len * seq_parts
    layer_count = frozen.shape[0]
    adapters = attention_adapter_weights.shape[2]
    parts = seq_parts // slots
    on_block = (fsdp_parts, seq_parts, slots) == (16, 2, 2)
    slot = me // parts
    part = me % parts
    tokens = seq_total // parts
    groups = [[s * parts + p for p in range(parts)] for s in range(slots)]

    def to_image(v):
        if parts == 1 and slots == 2:
            mine = lax.dynamic_index_in_dim(v, slot, 0, keepdims=False)
            other = lax.dynamic_index_in_dim(v, 1 - slot, 0, keepdims=False)
            other = lax.ppermute(other, "seq", [(0, 1), (1, 0)])
            return jnp.where(
                slot == 0,
                jnp.concatenate([mine, other], 0),
                jnp.concatenate([other, mine], 0),
            )
        whole = lax.all_gather(v, "seq", axis=1, tiled=True)
        whole = lax.dynamic_index_in_dim(whole, slot, 0, keepdims=False)
        return lax.dynamic_slice_in_dim(whole, part * tokens, tokens, 0)

    def to_tokens(v):
        if parts == 1 and slots == 2:
            mine = lax.dynamic_slice_in_dim(v, slot * local_len, local_len, 0)
            other = lax.dynamic_slice_in_dim(v, (1 - slot) * local_len, local_len, 0)
            other = lax.ppermute(other, "seq", [(0, 1), (1, 0)])
            return jnp.where(slot == 0, jnp.stack([mine, other]), jnp.stack([other, mine]))
        whole = lax.all_gather(v, "seq", axis=0, tiled=True).reshape(slots, seq_total, -1)
        return lax.dynamic_slice_in_dim(whole, me * local_len, local_len, 1)

    length = lax.dynamic_slice_in_dim(lengths, slot, 1, 0)
    adapter = lax.dynamic_index_in_dim(image_adapter_index, slot, 0, keepdims=False)
    is_live = slot < group_image_count[0]
    positions = part * tokens + jnp.arange(tokens, dtype=jnp.int32)
    row_mask = ((positions < length[0]) & is_live).astype(F32)[:, None]
    def pick(table):
        return lax.dynamic_index_in_dim(table, adapter, 1, keepdims=False)

    shards = lax.optimization_barrier(frozen.reshape(layer_count, -1, LANES))
    steps = [(d, d + 1) for d in range(fsdp_parts - 1)]
    steps = (steps, [(b, a) for a, b in steps])
    tiles = -(-(TILES_END + TILES_VECTORS) // (2 * fsdp_parts)) * 2
    index = lax.axis_index("fsdp").astype(jnp.int32).reshape(1)
    shards = [lay_shard(index, shards[layer], tiles, steps) for layer in range(layer_count)]
    hidden = to_image(activations).astype(F32) * row_mask
    shards[0], hidden = lax.optimization_barrier((shards[0], hidden))
    stored = []
    weights = []
    for layer in range(layer_count):
        if on_block and layer > 0:
            pass
        elif on_block:
            flat = gather_blocks(shards[layer], 0, 16 * TILES_HELD)
        else:
            flat = lax.all_gather(shards[layer], "fsdp", axis=0, tiled=True)
            flat = jnp.pad(flat, ((0, 16 * TILES_HELD - flat.shape[0]), (0, 0)))
        if layer == layer_count - 1:
            cotangent, flat = lax.optimization_barrier((cotangent, flat))
            d_output = to_image(cotangent)
        w_qkv, w_o, w_1, w_2 = (flat.reshape(-1, panels, 16, LANES) for panels in PANELS)
        vectors = lax.slice_in_dim(flat, 16 * TILES_END, 16 * TILES_END + 106, axis=0).reshape(-1)
        vectors, b_1 = vectors[: 8 * D].reshape(8, D).astype(F32), vectors[8 * D : 8 * D + FF]
        b_1 = jnp.pad(b_1.astype(F32), (0, WIDE - FF))[None, :]
        attn = pick(attention_adapter_weights[layer])
        narrow = pick(narrow_adapter_weights[layer])
        wide = jnp.pad(pick(broad_adapter_weights[layer]), ((0, 0), (0, 0), (0, WIDE - FF)))
        weights.append((w_qkv, w_o, w_1, w_2, vectors, attn, narrow, wide))
        keys = None
        if parts == 1:
            shard = shards[layer + 1] if on_block and layer + 1 < layer_count else None
            made = layer_forward(
                length, hidden, w_qkv, w_o, w_1, w_2, vectors, b_1, attn, narrow, wide, shard
            )
            normed, inner_qkv, qkv, attended, stats, inner_o, middle = made[:7]
            normed_two, inner_up, gate, inner_down, next_hidden = made[7:12]
            flat = made[12] if shard is not None else None
        else:
            normed, inner_qkv, qkv = qkv_forward(hidden, w_qkv, vectors, attn)
            keys = lax.all_gather(
                qkv[:, D:], "seq", axis=0, tiled=True, axis_index_groups=groups
            )
            attended, stats = attn_fwd(length, qkv, keys)
            inner_o, middle, normed_two, inner_up, gate, activated = up_forward(
                attended, hidden, w_o, vectors, attn, narrow, w_1, b_1, wide
            )
            inner_down, next_hidden = down_forward(
                activated, middle, w_2, vectors[7:8], narrow, wide
            )
        stored.append(
            (
                hidden,
                normed,
                inner_qkv,
                qkv,
                keys,
                stats,
                attended,
                inner_o,
                middle,
                normed_two,
                inner_up,
                gate,
                inner_down,
            )
        )
        hidden = next_hidden
    output = to_tokens((hidden * row_mask).astype(BF16))
    gradient = d_output.astype(F32) * row_mask
    collected = [None] * layer_count
    for layer in reversed(range(layer_count)):
        if layer == 0:
            output, gradient = lax.optimization_barrier((output, gradient))
        (
            layer_input,
            normed,
            inner_qkv,
            qkv,
            keys,
            stats,
            attended,
            inner_o,
            middle,
            normed_two,
            inner_up,
            gate,
            inner_down,
        ) = stored[layer]
        w_qkv, w_o, w_1, w_2, vectors, attn, narrow, wide = weights[layer]
        d_gate, g_wide, d_inner_up, g_up_2 = gate_backward(
            gradient, w_2, gate, narrow, wide, inner_down, inner_up
        )
        d_middle, d_attended, g_middle = middle_backward(
            d_gate, w_1, d_inner_up, narrow, normed_two, middle, gradient, vectors, w_o, attn,
            inner_o, attended,
        )
        d_qkv = attn_bwd(length, qkv, d_attended, attended, stats, keys)
        if parts > 1:
            d_keys = lax.psum_scatter(
                d_qkv[1].astype(F32),
                "seq",
                scatter_dimension=0,
                tiled=True,
                axis_index_groups=groups,
            )
            d_qkv = jnp.concatenate([d_qkv[0], d_keys.astype(BF16)], axis=1)
        else:
            d_qkv = d_qkv[0]
        gradient, g_input = input_backward(
            d_qkv, w_qkv, attn, normed, inner_qkv, layer_input, d_middle, vectors
        )
        rows_narrow = jnp.concatenate(
            [
                g_input[: 3 * R],
                g_middle[:R],
                g_input[3 * R :],
                g_middle[R:],
                g_up_2,
            ]
        )
        if on_block:
            terms = jnp.concatenate(
                [
                    rows_narrow.reshape(10, R, 9, LANES).transpose(0, 2, 1, 3).reshape(90, R, LANES),
                    g_wide.reshape(2, R, 36, LANES)
                    .transpose(0, 2, 1, 3)[:, :34]
                    .reshape(68, R, LANES),
                    jnp.zeros((2, R, LANES), F32),
                ]
            )
            terms = terms.astype(BF16).reshape(device_count, SHARE, R, LANES)
            label = jnp.broadcast_to(adapter.astype(F32), (8, LANES))
            sums = share_terms(terms, label, adapters)
            collected[layer] = gather_blocks(sums, 2, 16 * sums.shape[0])
            continue
        rows_narrow = rows_narrow.astype(BF16)
        rows_wide = g_wide[:, :FF].astype(BF16)

        def shares(rows):
            share = -(-rows.shape[0] // device_count)
            rows = jnp.pad(rows, ((0, share * device_count - rows.shape[0]), (0, 0)))
            return rows.reshape(device_count, share * rows.shape[1])

        terms = [shares(rows_narrow), shares(rows_wide)]
        used = terms[0].shape[1] + terms[1].shape[1]
        label = jnp.broadcast_to(adapter.astype(BF16), (device_count, -used % LANES + LANES))
        terms = lax.all_to_all(
            jnp.concatenate(terms + [label], axis=1),
            ("fsdp", "seq"),
            split_axis=0,
            concat_axis=0,
            tiled=True,
        )
        choice = jnp.arange(adapters, dtype=F32)[:, None] == terms[:, used].astype(F32)[None, :]
        sums = jnp.dot(choice.astype(F32), terms.astype(F32), precision=lax.Precision.HIGHEST)
        sums = lax.all_gather(sums.astype(BF16), ("fsdp", "seq")).transpose(1, 0, 2)
        split = -(-10 * R // device_count) * D

        def table(part, count, width):
            part = part.reshape(adapters, -1, width)[:, : count * R]
            return part.reshape(adapters, count, R, width).transpose(1, 0, 2, 3).astype(F32)

        collected[layer] = (table(sums[:, :, :split], 10, D), table(sums[:, :, split:used], 2, FF))
    if on_block:
        grad_attn, grad_narrow, grad_wide = gradient_tables(collected, adapters)
    else:
        grad_attn = jnp.stack([entry[0][0:8] for entry in collected], axis=0)
        grad_narrow = jnp.stack([entry[0][8:10] for entry in collected], axis=0)
        grad_wide = jnp.stack([entry[1] for entry in collected], axis=0)
    input_grad = to_tokens((gradient * row_mask).astype(BF16)).astype(F32)
    return (output, input_grad, grad_attn, grad_narrow, grad_wide)


def solution(mesh):
    in_specs = (
        P("fsdp", "seq", None),
        P("fsdp"),
        P("fsdp"),
        P("fsdp"),
        P(None, "fsdp"),
        P(),
        P(),
        P(),
        P("fsdp", "seq", None),
    )
    out_specs = (P("fsdp", "seq", None), P("fsdp", "seq", None), P(), P(), P())
    return jax.shard_map(local, mesh=mesh, in_specs=in_specs, out_specs=out_specs, check_vma=False)
```

```python
import functools
import math

import jax
import jax.numpy as jnp
from jax import lax
from jax.experimental import pallas as pl
from jax.experimental.pallas import tpu as pltpu
from jax.sharding import PartitionSpec as P

D = 1152
HD = 72
H = 16
FF = 4304
R = 16
LANES = 128
BF16 = jnp.bfloat16
F32 = jnp.float32
MESH = pl.DeviceIdType.MESH
VMEM_LIMIT = 60 << 20
VMEM_MOST = 67043328
C2 = math.log2(math.e) / math.sqrt(HD)
SCALE = 1.0 / math.sqrt(HD)
NEG = -1e30
epsilon = 1e-06
CUT_OUT = 3 * D * D // LANES
CUT_UP = CUT_OUT + D * D // LANES
CUT_DOWN = CUT_UP + D * FF // LANES
CUT_VECTORS = CUT_DOWN + FF * D // LANES


def dot(a, b):
    return jnp.dot(a, b, preferred_element_type=F32)


def dot_t(a, b):
    return lax.dot_general(a, b, (((1,), (1,)), ((), ())), preferred_element_type=F32)


def dot_l(a, b):
    return lax.dot_general(a, b, (((0,), (0,)), ((), ())), preferred_element_type=F32)


PANELS = (3 * D // LANES, D // LANES, 36, D // LANES)
UNITS = (D // 16, D // 16, D // 16, FF // 16)
TILES_AT = (0, 1944, 2592, 5184)
TILES_END = 7605
TILES_VECTORS = 22
TILES_HELD = 7776
FLAT_AT = (0, CUT_OUT, CUT_UP, CUT_DOWN)
WIDE = PANELS[2] * LANES
UP_ROWS = 16 * FF // LANES
HALO = 1600


def lay_kernel(own_rows, tiles, index_ref, before, own, after, out, flat, held, turned):
    d = index_ref[0]
    margin = 16 * PANELS[2]
    flat[0:HALO] = before[...].astype(F32)
    flat[HALO : HALO + own_rows] = own[...].astype(F32)
    flat[HALO + own_rows : 2 * HALO + own_rows] = after[...].astype(F32)
    flat_base = d * own_rows - HALO
    tile_base = d * tiles

    def span(at, units, panels):
        low = jnp.maximum(tile_base - at, 0) // panels
        high = jnp.clip((tile_base + tiles - at + panels - 1) // panels, 0, units)
        return low, jnp.maximum(high, low)

    for at, start, units, panels in zip(
        TILES_AT + (TILES_END,),
        FLAT_AT + (CUT_VECTORS,),
        UNITS + (TILES_VECTORS,),
        PANELS + (1,),
    ):
        low, high = span(at, units, panels)
        if start == CUT_UP:
            lane = lax.broadcasted_iota(jnp.int32, (8, LANES), 1)

            def up_units(b, carry):
                u = low + 8 * b
                source = pl.multiple_of(start + UP_ROWS * u - flat_base, 2)
                for j in range(16):
                    first, shift = (FF * j) // LANES, (FF * j) % LANES
                    turn = LANES - shift
                    now = flat[pl.ds(source + first, 8, stride=UP_ROWS), :]
                    now = pltpu.roll(now, turn, 1) if shift else now
                    for c in range(34):
                        value = now
                        if c < 33 or shift > LANES - FF % LANES:
                            now = flat[pl.ds(source + first + c + 1, 8, stride=UP_ROWS), :]
                            now = pltpu.roll(now, turn, 1) if shift else now
                            if shift:
                                value = jnp.where(lane < turn, value, now)
                        if c == 33:
                            value = jnp.where(lane < FF - 33 * LANES, value, 0.0)
                        turned[pl.ds(16 * c + j, 8, stride=16 * PANELS[2]), :] = value
                target = pl.multiple_of(16 * (at + PANELS[2] * u - tile_base) + margin, 16)
                held[pl.ds(target, 8 * 16 * PANELS[2]), :] = turned[...].astype(BF16)
                return carry

            turned[...] = jnp.zeros_like(turned)
            lax.fori_loop(0, (high - low + 7) // 8, up_units, 0)
        else:

            def unit(u, carry):
                source = pl.multiple_of(start + 16 * panels * u - flat_base, 16)
                target = pl.multiple_of(16 * (at + panels * u - tile_base) + margin, 16)
                for c in range(panels):
                    value = flat[pl.ds(source + c, 16, stride=panels), :]
                    held[pl.ds(target + 16 * c, 16), :] = value.astype(BF16)
                return carry

            lax.fori_loop(low, high, unit, 0)
    out[...] = held[margin : margin + 16 * tiles]


def lay_shard(index, shard, tiles, perms):
    own_rows = shard.shape[0]
    before = lax.ppermute(shard[own_rows - HALO :], "fsdp", perms[0])
    after = lax.ppermute(shard[:HALO], "fsdp", perms[1])
    vm = pl.BlockSpec(memory_space=pltpu.VMEM)
    margin = 16 * PANELS[2]
    return pl.pallas_call(
        functools.partial(lay_kernel, own_rows, tiles),
        in_specs=[pl.BlockSpec(memory_space=pltpu.SMEM), vm, vm, vm],
        out_specs=vm,
        out_shape=jax.ShapeDtypeStruct((16 * tiles, LANES), BF16),
        scratch_shapes=[
            pltpu.VMEM((own_rows + 2 * HALO + 8 * UP_ROWS, LANES), F32),
            pltpu.VMEM((16 * tiles + 10 * margin, LANES), BF16),
            pltpu.VMEM((8 * margin, LANES), F32),
        ],
        compiler_params=pltpu.CompilerParams(vmem_limit_bytes=VMEM_LIMIT),
        name="lay_shard",
    )(index, before, shard, after)


def pad_lanes(x, extra=None):
    if extra is None:
        extra = jnp.zeros((x.shape[0], LANES - HD), x.dtype)
    return jnp.concatenate([x, extra], axis=1)


def first_lane(rows, value):
    lane = lax.broadcasted_iota(jnp.int32, (rows, LANES - HD), 1)
    return jnp.where(lane == 0, value, 0.0).astype(BF16)


def key_bias(rows, length):
    key = lax.broadcasted_iota(jnp.int32, (rows, LANES - HD), 0)
    return first_lane(rows, jnp.where(key < length, 0.0, NEG))


def attn_fwd_kernel(offset, len_ref, qkv_ref, kv_ref, o_ref, st_ref, q_s, k_s, v_s):
    if kv_ref is None:
        kv_ref = qkv_ref
    rows, keys = qkv_ref.shape[0], kv_ref.shape[0]
    one = first_lane(rows, F32(1.0))
    bias = key_bias(keys, len_ref[0])
    for h in range(H):
        q_s[h] = pad_lanes(qkv_ref[:, h * HD : (h + 1) * HD], one)
        k_s[h] = pad_lanes(kv_ref[:, offset + h * HD : offset + (h + 1) * HD], bias)
        v_s[h] = pad_lanes(kv_ref[:, offset + D + h * HD : offset + D + (h + 1) * HD])
    st_ref[...] = jnp.zeros_like(st_ref)
    lane = lax.broadcasted_iota(jnp.int32, (rows, LANES), 1)

    def body(h, carry):
        s = dot_t(q_s[h], k_s[h])
        m = jnp.max(s, axis=1, keepdims=True)
        p = jnp.exp2((s - m) * C2)
        total = jnp.sum(p, axis=1, keepdims=True)
        o = dot(p.astype(BF16), v_s[h])
        q_s[h] = (o * (1.0 / total)).astype(BF16)
        st_ref[...] = jnp.where(lane == h, m * C2 + jnp.log2(total), st_ref[...])
        return carry

    lax.fori_loop(0, H, body, 0)
    for h in range(H):
        o_ref[:, h * HD : (h + 1) * HD] = q_s[h][:, :HD]


def attn_fwd(length, qkv, kv=None):
    rows = qkv.shape[0]
    keys = rows if kv is None else kv.shape[0]
    vm = pl.BlockSpec(memory_space=pltpu.VMEM)
    if kv is None:
        kernel = lambda a, b, *rest: attn_fwd_kernel(D, a, b, None, *rest)
        operands = (length, qkv)
    else:
        kernel = functools.partial(attn_fwd_kernel, 0)
        operands = (length, qkv, kv)
    return pl.pallas_call(
        kernel,
        in_specs=[pl.BlockSpec(memory_space=pltpu.SMEM)] + [vm] * (len(operands) - 1),
        out_specs=[vm, vm],
        out_shape=[
            jax.ShapeDtypeStruct((rows, D), BF16),
            jax.ShapeDtypeStruct((rows, LANES), F32),
        ],
        scratch_shapes=[
            pltpu.VMEM((H, rows, LANES), BF16),
            pltpu.VMEM((H, keys, LANES), BF16),
            pltpu.VMEM((H, keys, LANES), BF16),
        ],
        cost_estimate=pl.CostEstimate(
            flops=H * rows * keys * 256 * 4, bytes_accessed=rows * D * 8, transcendentals=H * rows * keys
        ),
        compiler_params=pltpu.CompilerParams(vmem_limit_bytes=VMEM_LIMIT),
        name="attention_forward",
    )(*operands)


def attn_bwd_kernel(
    offset, len_ref, qkv_ref, kv_ref, do_ref, o_ref, st_ref, dq_ref, dkv_ref, q_s, k_s, v_s, do_s, st_t, dl_t
):
    if kv_ref is None:
        kv_ref, dkv_ref = qkv_ref, dq_ref
    rows, keys = qkv_ref.shape[0], kv_ref.shape[0]
    one = first_lane(rows, F32(1.0))
    bias = key_bias(keys, len_ref[0])
    lane = lax.broadcasted_iota(jnp.int32, (rows, LANES), 1)
    delta = jnp.zeros((rows, LANES), F32)
    for h in range(H):
        q_s[h] = pad_lanes(qkv_ref[:, h * HD : (h + 1) * HD], one)
        k_s[h] = pad_lanes(kv_ref[:, offset + h * HD : offset + (h + 1) * HD], bias)
        v_s[h] = pad_lanes(kv_ref[:, offset + D + h * HD : offset + D + (h + 1) * HD])
        do = do_ref[:, h * HD : (h + 1) * HD]
        do_s[h] = pad_lanes(do)
        o = o_ref[:, h * HD : (h + 1) * HD].astype(F32)
        d = jnp.sum(do.astype(F32) * o, axis=1, keepdims=True)
        delta = jnp.where(lane == h, d, delta)
    st_t[...] = st_ref[...].T
    dl_t[...] = delta.T

    def body(h, carry):
        q, k, do = q_s[h], k_s[h], do_s[h]
        p = jnp.exp2(dot_t(k, q) * C2 - st_t[pl.ds(h, 1), :])
        dv = dot(p.astype(BF16), do)
        dp = dot_t(v_s[h], do)
        ds = (p * (dp - dl_t[pl.ds(h, 1), :])).astype(BF16)
        dk = dot(ds, q)
        dq = dot(k.T, ds)
        v_s[h] = dv.astype(BF16)
        k_s[h] = (dk * SCALE).astype(BF16)
        q_s[h] = (dq * SCALE).astype(BF16).T
        return carry

    lax.fori_loop(0, H, body, 0)
    for h in range(H):
        dq_ref[:, h * HD : (h + 1) * HD] = q_s[h][:, :HD]
        dkv_ref[:, offset + h * HD : offset + (h + 1) * HD] = k_s[h][:, :HD]
        dkv_ref[:, offset + D + h * HD : offset + D + (h + 1) * HD] = v_s[h][:, :HD]


def attn_bwd(length, qkv, do, o, st, kv=None):
    rows = qkv.shape[0]
    keys = rows if kv is None else kv.shape[0]
    vm = pl.BlockSpec(memory_space=pltpu.VMEM)
    if kv is None:
        kernel = lambda a, b, c, d, e, f, *rest: attn_bwd_kernel(
            D, a, b, None, c, d, e, f, None, *rest
        )
        operands = (length, qkv, do, o, st)
        outs = [jax.ShapeDtypeStruct((rows, 3 * D), BF16)]
    else:
        kernel = functools.partial(attn_bwd_kernel, 0)
        operands = (length, qkv, kv, do, o, st)
        outs = [jax.ShapeDtypeStruct((rows, D), BF16), jax.ShapeDtypeStruct((keys, 2 * D), BF16)]
    return pl.pallas_call(
        kernel,
        in_specs=[pl.BlockSpec(memory_space=pltpu.SMEM)] + [vm] * (len(operands) - 1),
        out_specs=[vm] * len(outs),
        out_shape=outs,
        scratch_shapes=[
            pltpu.VMEM((H, rows, LANES), BF16),
            pltpu.VMEM((H, keys, LANES), BF16),
            pltpu.VMEM((H, keys, LANES), BF16),
            pltpu.VMEM((H, rows, LANES), BF16),
            pltpu.VMEM((LANES, rows), F32),
            pltpu.VMEM((LANES, rows), F32),
        ],
        cost_estimate=pl.CostEstimate(
            flops=H * rows * keys * 256 * 10, bytes_accessed=rows * D * 16, transcendentals=H * rows * keys
        ),
        compiler_params=pltpu.CompilerParams(vmem_limit_bytes=VMEM_LIMIT),
        name="attention_backward",
    )(*operands)


LARGE_BLOCK = 4096


def gather_plan(
    src, out, stage, local_sem, z_recv, y_recv, b_recv, h_recv, c_recv_own, c_recv_z, c_recv_y, c_recv_b, c_recv_h,
    up_send, down_send, y_send, b_send, h_send, c_send_own, c_send_z, c_send_y, c_send_b, c_send_h,
):
    rows = src.shape[0]
    if rows >= LARGE_BLOCK:
        unit = rows // 6 // 16 * 16 + 16
        sizes = [unit, unit, rows // 2 - 2 * unit, rows // 2 - 2 * unit, unit]
        begins = [0, unit, 2 * unit, rows // 2, rows - 2 * unit]
    else:
        sizes = [rows // 2] * 2
        begins = [0, rows // 2]
    chunks, across_y = len(sizes), (len(sizes) + 1) // 2
    lend = chunks == 5
    x = lax.axis_index("seq")
    f = lax.axis_index("fsdp")
    z, y, c = f // 4, (f // 2) % 2, f % 2

    def place(zb, yb, j, side, cb=None):
        owner = (zb * 2 + yb) * 2 + (c if cb is None else cb)
        begin = jnp.where(side == 0, begins[j], rows - begins[j] - sizes[j])
        return pl.multiple_of(owner * rows + begin, 16), sizes[j]

    def view(spot):
        return out.at[pl.ds(spot[0], spot[1]), :]

    def device(zb, yb, cb, xb):
        return ((zb * 2 + yb) * 2 + cb, xb)

    up, down = device(z + 1, y, c, x), device(z - 1, y, c, x)
    beside, across, mate = device(z, 1 - y, c, x), device(z, y, c, 1 - x), device(z, y, 1 - c, x)

    def copy(spot, send, recv, to, source=None):
        return pltpu.make_async_remote_copy(
            src_ref=view(spot) if source is None else source,
            dst_ref=view(spot),
            send_sem=send,
            recv_sem=recv,
            device_id=to,
            device_id_type=MESH,
        )

    def arrived(spot, recv):
        copy(spot, local_sem.at[1], recv, mate).wait_recv()

    def own(j):
        begin = jnp.where(x == 0, begins[j], rows - begins[j] - sizes[j])
        return src.at[pl.ds(pl.multiple_of(begin, 16), sizes[j]), :]

    whole = (pl.multiple_of(f * rows, 16), rows)
    keep = pltpu.make_async_copy(src if stage is None else stage, view(whole), local_sem.at[0])

    def greet():
        barrier = pltpu.get_barrier_semaphore()
        for to in (beside, across, mate):
            pl.semaphore_signal(barrier, inc=1, device_id=to, device_id_type=MESH)

        @pl.when(z < 3)
        def _():
            pl.semaphore_signal(barrier, inc=1, device_id=up, device_id_type=MESH)

        @pl.when(z > 0)
        def _():
            pl.semaphore_signal(barrier, inc=1, device_id=down, device_id_type=MESH)

        pl.semaphore_wait(barrier, 3 + jnp.where(z < 3, 1, 0) + jnp.where(z > 0, 1, 0))

    def start(first=True):
        if first:
            greet()
        for j in range(chunks):
            spot = place(z, y, j, x)

            @pl.when(z < 3)
            def _():
                copy(spot, up_send.at[z, j], z_recv.at[z, j], up, own(j)).start()

            @pl.when(z > 0)
            def _():
                copy(spot, down_send.at[z, j], z_recv.at[z, j], down, own(j)).start()

            if j < across_y:
                copy(spot, y_send.at[z, j], y_recv.at[z, j], beside, own(j)).start()
        copy(whole, c_send_own.at[0], c_recv_own.at[0], mate, src).start()
        if stage is None:
            keep.start()
        else:
            fetch = pltpu.make_async_copy(src, stage, local_sem.at[0])
            fetch.start()
            fetch.wait()
            keep.start()

    def z_event(d, j):
        def flow(zb, onward, to, sends):
            spot = place(zb, y, j, x)
            arrived(spot, z_recv.at[zb, j])

            @pl.when(onward)
            def _():
                copy(spot, sends.at[zb, j], z_recv.at[zb, j], to).start()

            if j == 0 and lend:
                copy(spot, b_send.at[zb], b_recv.at[zb], across).start()
            if j < across_y:
                copy(spot, y_send.at[zb, j], y_recv.at[zb, j], beside).start()
            copy(spot, c_send_z.at[zb, j], c_recv_z.at[zb, j], mate).start()

        @pl.when(z - d >= 0)
        def _():
            flow(z - d, z < 3, up, up_send)

        @pl.when(z + d <= 3)
        def _():
            flow(z + d, z > 0, down, down_send)

    def each(d, act):
        if d == 0:
            act(z)
            return

        @pl.when(z - d >= 0)
        def _():
            act(z - d)

        @pl.when(z + d <= 3)
        def _():
            act(z + d)

    def y_event(d, j):
        def act(zb):
            spot = place(zb, 1 - y, j, x)
            arrived(spot, y_recv.at[zb, j])
            copy(spot, h_send.at[zb, j], h_recv.at[zb, j], across).start()
            copy(spot, c_send_y.at[zb, j], c_recv_y.at[zb, j], mate).start()

        each(d, act)

    def b_event(d):
        def act(zb):
            spot = place(zb, y, 0, 1 - x)
            arrived(spot, b_recv.at[zb])
            copy(spot, c_send_b.at[zb], c_recv_b.at[zb], mate).start()

        each(d, act)

    def h_event(d, j):
        def act(zb):
            spot = place(zb, 1 - y, j, 1 - x)
            arrived(spot, h_recv.at[zb, j])
            copy(spot, c_send_h.at[zb, j], c_recv_h.at[zb, j], mate).start()

        each(d, act)

    events = []
    for d in range(4):
        for j in range(chunks):
            at = (d - 1) * chunks + j + 1 if d else 0
            if d:
                events.append((at, functools.partial(z_event, d, j)))
                if j == 0 and lend:
                    events.append((at + 2, functools.partial(b_event, d)))
            if j < across_y:
                ready = at + 1.5 if d else j + 1
                events.append((ready, functools.partial(y_event, d, j)))
                events.append((ready + 2, functools.partial(h_event, d, j)))
    def finish():
        keep.wait()
        other = 1 - c

        def core_spot(zb, yb, j, side):
            return place(zb, yb, j, side, other)

        arrived((pl.multiple_of(((z * 2 + y) * 2 + other) * rows, 16), rows), c_recv_own.at[0])
        copy(whole, c_send_own.at[0], c_recv_own.at[0], mate).wait_send()
        for d in range(4):
            def drain(zb, d=d):
                for j in range(chunks):
                    if d:
                        arrived(core_spot(zb, y, j, x), c_recv_z.at[zb, j])
                        copy(place(zb, y, j, x), c_send_z.at[zb, j], c_recv_z.at[zb, j], mate).wait_send()
                    if j < across_y:
                        arrived(core_spot(zb, 1 - y, j, x), c_recv_y.at[zb, j])
                        arrived(core_spot(zb, 1 - y, j, 1 - x), c_recv_h.at[zb, j])
                        spot = place(zb, 1 - y, j, x)
                        copy(spot, c_send_y.at[zb, j], c_recv_y.at[zb, j], mate).wait_send()
                        copy(spot, h_send.at[zb, j], h_recv.at[zb, j], across).wait_send()
                        spot = place(zb, 1 - y, j, 1 - x)
                        copy(spot, c_send_h.at[zb, j], c_recv_h.at[zb, j], mate).wait_send()
                        spot = place(zb, y, j, x)
                        copy(spot, y_send.at[zb, j], y_recv.at[zb, j], beside).wait_send()
                if d and lend:
                    arrived(core_spot(zb, y, 0, 1 - x), c_recv_b.at[zb])
                    spot = place(zb, y, 0, 1 - x)
                    copy(spot, c_send_b.at[zb], c_recv_b.at[zb], mate).wait_send()
                    spot = place(zb, y, 0, x)
                    copy(spot, b_send.at[zb], b_recv.at[zb], across).wait_send()

            each(d, drain)
            for j in range(chunks):
                @pl.when(jnp.logical_and(z - d >= 0, z < 3))
                def _():
                    zb = z - d
                    copy(place(zb, y, j, x), up_send.at[zb, j], z_recv.at[zb, j], up).wait_send()

                @pl.when(jnp.logical_and(z + d <= 3, z > 0))
                def _():
                    zb = z + d
                    copy(place(zb, y, j, x), down_send.at[zb, j], z_recv.at[zb, j], down).wait_send()

    return start, sorted(events, key=lambda e: e[0]), finish


def gather_kernel(*refs):
    start, events, finish = gather_plan(*refs)
    start()
    for _, event in events:
        event()
    finish()


def gather_semaphores():
    dma = pltpu.SemaphoreType.DMA
    core = [dma((1,)), dma((4, 5)), dma((4, 3)), dma((4,)), dma((4, 3))]
    links = [dma((4, 5)), dma((4, 3)), dma((4,)), dma((4, 3))]
    return [dma((2,))] + links + core + [dma((4, 5))] + links + core


def gather_blocks(shard, collective_id, held_rows):
    rows = shard.shape[0]
    return pl.pallas_call(
        gather_kernel,
        in_specs=[pl.BlockSpec(memory_space=pl.ANY)],
        out_specs=pl.BlockSpec(memory_space=pl.ANY),
        out_shape=jax.ShapeDtypeStruct((held_rows, LANES), BF16),
        scratch_shapes=[pltpu.VMEM((rows, LANES), BF16)] + gather_semaphores(),
        compiler_params=pltpu.CompilerParams(collective_id=collective_id, has_side_effects=True, vmem_limit_bytes=VMEM_LIMIT),
        name="gather_blocks",
    )(shard)


def gelu_parts(x):
    inner = 0.7978845608028654 * (x + 0.044715 * x * x * x)
    return jnp.tanh(inner)


def layer_norm(tensor, gain, offset):
    average = jnp.mean(tensor, axis=-1, keepdims=True)
    centred = tensor - average
    variance = jnp.mean(centred * centred, axis=-1, keepdims=True)
    return centred * lax.rsqrt(variance + epsilon) * gain + offset


def layer_norm_back(d_out, tensor, gain):
    average = jnp.mean(tensor, axis=-1, keepdims=True)
    centred = tensor - average
    variance = jnp.mean(centred * centred, axis=-1, keepdims=True)
    scale = lax.rsqrt(variance + epsilon)
    normal = centred * scale
    d_normal = d_out * gain
    mean_d = jnp.mean(d_normal, axis=-1, keepdims=True)
    mean_dn = jnp.mean(d_normal * normal, axis=-1, keepdims=True)
    return (d_normal - mean_d - normal * mean_dn) * scale


def dot_both(x, w, inner, up):
    cut = w.shape[0] // 256 * 256
    tail = dot(
        jnp.concatenate([x[:, cut:], inner], axis=1), jnp.concatenate([w[cut:], up], axis=0)
    )
    return dot(x[:, :cut], w[:cut]) + tail


def dot_both_t(x, w, inner, up_t):
    cut = w.shape[1] // 256 * 256
    tail = dot_t(
        jnp.concatenate([x[:, cut:], inner], axis=1), jnp.concatenate([w[:, cut:], up_t], axis=1)
    )
    return dot_t(x[:, :cut], w[:, :cut]) + tail


def matrix(ref, count=None):
    units, panels = ref.shape[:2]
    return jnp.concatenate(
        [ref[:, p].reshape(units * 16, LANES) for p in range(count or panels)], axis=1
    )


def unit_block(units, panels, place):
    return pl.BlockSpec((units, panels, 16, LANES), place)


def whole(shape):
    return pl.BlockSpec(shape, lambda i: (0,) * len(shape), pipeline_mode=pl.Buffered(1))


def columns(rows, width):
    return pl.BlockSpec((rows, width), lambda i: (0, i))


def struct(shape, dtype):
    return jax.ShapeDtypeStruct(shape, dtype)


def dense_params(flops, bytes_accessed):
    return dict(
        cost_estimate=pl.CostEstimate(
            flops=flops, bytes_accessed=bytes_accessed, transcendentals=0
        ),
        compiler_params=pltpu.CompilerParams(vmem_limit_bytes=VMEM_LIMIT),
    )


def qkv_kernel(hidden, w, vec, down, up, normed, inner, qkv, parts):
    c = pl.program_id(0)

    @pl.when(c == 0)
    def _():
        value = layer_norm(hidden[...], vec[0:1], vec[1:2]).astype(BF16)
        normed[...] = value
        narrow = dot_t(value, down[...]).astype(BF16)
        inner[...] = narrow
        for part in range(3):
            parts[part] = narrow[:, part * R : (part + 1) * R]

    bias = vec[pl.ds(jnp.where(c == 2, 5, 4), 1), :] * jnp.where(c == 1, 0.0, 1.0)
    qkv[...] = (dot_both(normed[...], matrix(w), parts[c], up[0]) + bias).astype(BF16)


def qkv_forward(hidden, w_qkv, vectors, attn):
    rows = hidden.shape[0]
    return pl.pallas_call(
        qkv_kernel,
        grid=(3,),
        in_specs=[
            whole((rows, D)),
            unit_block(72, 9, lambda i: (0, i, 0, 0)),
            whole((8, D)),
            whole((3 * R, D)),
            pl.BlockSpec((1, R, D), lambda i: (i, 0, 0)),
        ],
        out_specs=[whole((rows, D)), whole((rows, 3 * R)), columns(rows, D)],
        out_shape=[
            struct((rows, D), BF16),
            struct((rows, 3 * R), BF16),
            struct((rows, 3 * D), BF16),
        ],
        scratch_shapes=[pltpu.VMEM((3, rows, R), BF16)],
        name="qkv_forward",
        **dense_params(6 * rows * D * D, 14 * rows * D + 6 * D * D),
    )(hidden, w_qkv, vectors, attn[0:3].reshape(3 * R, D), attn[4:7])


TILE = 512
OUT_BLOCK = pl.BlockSpec(
    (72, 9, 16, LANES), lambda i: (3, 0, 0, 0), pipeline_mode=pl.Buffered(1)
)


def up_kernel(
    attended, hidden, w_o, vec, down_o, up_o, down_1, w_1, b_1, up_1,
    inner_o, middle, normed, inner_up, gate, activated,
):
    @pl.when(pl.program_id(0) == 0)
    def _():
        narrow = dot_t(attended[...], down_o[...]).astype(BF16)
        inner_o[...] = narrow
        middle[...] = hidden[...] + (dot_both(attended[...], matrix(w_o), narrow, up_o[...]) + vec[6:7])
        value = layer_norm(middle[...], vec[2:3], vec[3:4]).astype(BF16)
        normed[...] = value
        inner_up[...] = dot_t(value, down_1[...]).astype(BF16)

    x = dot_both(normed[...], matrix(w_1), inner_up[...], up_1[...]) + b_1[...]
    gate[...] = x.astype(BF16)
    activated[...] = (0.5 * x * (1.0 + gelu_parts(x))).astype(BF16)


def up_forward(attended, hidden, w_o, vectors, attn, narrow, w_1, b_1, wide):
    rows = hidden.shape[0]
    return pl.pallas_call(
        up_kernel,
        grid=(WIDE // TILE,),
        in_specs=[
            whole((rows, D)),
            whole((rows, D)),
            OUT_BLOCK,
            whole((8, D)),
            whole((R, D)),
            whole((R, D)),
            whole((R, D)),
            unit_block(72, 4, lambda i: (1, i, 0, 0)),
            columns(1, TILE),
            columns(R, TILE),
        ],
        out_specs=[
            whole((rows, R)),
            whole((rows, D)),
            whole((rows, D)),
            whole((rows, R)),
            columns(rows, TILE),
            columns(rows, TILE),
        ],
        out_shape=[
            struct((rows, R), BF16),
            struct((rows, D), F32),
            struct((rows, D), BF16),
            struct((rows, R), BF16),
            struct((rows, WIDE), BF16),
            struct((rows, WIDE), BF16),
        ],
        name="up_forward",
        **dense_params(2 * rows * D * (D + FF), 12 * rows * D + 4 * rows * FF + 2 * D * (D + FF)),
    )(attended, hidden, w_o, vectors, attn[3], attn[7], narrow[0], w_1, b_1, wide[0])


THIRD = D // 3


def down_kernel(activated, middle, w_2, b_2, down_2, up_2, inner, hidden):
    @pl.when(pl.program_id(0) == 0)
    def _():
        inner[...] = dot_t(activated[...], down_2[...]).astype(BF16)

    value = activated[:, :FF]

    hidden[...] = middle[...] + (
        dot(value, matrix(w_2)) + b_2[...] + dot(inner[...], up_2[...])
    )


def down_forward(activated, middle, w_2, b_2, narrow, wide):
    rows = middle.shape[0]
    return pl.pallas_call(
        down_kernel,
        grid=(3,),
        in_specs=[
            whole((rows, WIDE)),
            columns(rows, THIRD),
            pl.BlockSpec(
                (pl.Element(UNITS[3]), pl.Element(3), pl.Element(16), pl.Element(LANES)),
                lambda i: (TILES_AT[3] // 9, 3 * i, 0, 0),
            ),
            columns(1, THIRD),
            whole((R, WIDE)),
            columns(R, THIRD),
        ],
        out_specs=[whole((rows, R)), columns(rows, THIRD)],
        out_shape=[struct((rows, R), BF16), struct((rows, D), F32)],
        name="down_forward",
        **dense_params(2 * rows * D * FF, 8 * rows * D + 2 * rows * FF + 2 * D * FF),
    )(activated, middle, w_2, b_2, wide[1], narrow[1])


def gate_kernel(
    gradient, w_2, gate, down_2, up_1, up_2, inner_down, inner_up, d_gate, g_wide, d_inner_up, g_up_2,
    d_branch, d_inner_down, total,
):
    i = pl.program_id(0)

    @pl.when(i == 0)
    def _():
        value = gradient[...].astype(BF16)
        d_branch[...] = value
        d_inner_down[...] = dot_t(value, up_2[...]).astype(BF16)
        g_up_2[...] = dot_l(inner_down[...], value)
        total[...] = jnp.zeros_like(total)

    left = FF - i * TILE
    down = down_2[...]
    d_act = dot_t(d_branch[...], matrix(w_2)) + dot(d_inner_down[...], down)
    x = gate[...].astype(F32)
    t = gelu_parts(x)
    half = 0.5 * (1.0 + t)
    slope = half + 0.5 * x * (1.0 - t * t) * (
        0.7978845608028654 * (1.0 + 3 * 0.044715 * x * x)
    )
    keep = lax.broadcasted_iota(jnp.int32, (1, TILE), 1) < left
    value = jnp.where(keep, slope * d_act, 0.0).astype(BF16)
    d_gate[...] = value
    total[...] += dot_t(value, up_1[...])
    g_wide[0:R] = dot_l(inner_up[...], value)
    g_wide[R : 2 * R] = dot_l(d_inner_down[...], (x * half).astype(BF16))

    @pl.when(i == pl.num_programs(0) - 1)
    def _():
        d_inner_up[...] = total[...].astype(BF16)


def gate_backward(gradient, w_2, gate, narrow, wide, inner_down, inner_up):
    rows = gradient.shape[0]
    return pl.pallas_call(
        gate_kernel,
        grid=(WIDE // TILE,),
        in_specs=[
            whole((rows, D)),
            unit_block(TILE // 16, 9, lambda i: (TILES_AT[3] // 9 * 16 // TILE + i, 0, 0, 0)),
            columns(rows, TILE),
            columns(R, TILE),
            columns(R, TILE),
            whole((R, D)),
            whole((rows, R)),
            whole((rows, R)),
        ],
        out_specs=[columns(rows, TILE), columns(2 * R, TILE), whole((rows, R)), whole((R, D))],
        out_shape=[
            struct((rows, WIDE), BF16),
            struct((2 * R, WIDE), F32),
            struct((rows, R), BF16),
            struct((R, D), F32),
        ],
        scratch_shapes=[
            pltpu.VMEM((rows, D), BF16),
            pltpu.VMEM((rows, R), BF16),
            pltpu.VMEM((rows, R), F32),
        ],
        name="gate_backward",
        **dense_params(2 * rows * D * FF, 4 * rows * D + 4 * rows * FF + 2 * D * FF),
    )(gradient, w_2, gate, wide[1], wide[0], narrow[1], inner_down, inner_up)


def middle_kernel(
    d_gate, w_1, d_inner_up, down_1, normed, middle, gradient, vec, w_o, down_o, up_o, inner_o, attended,
    d_middle, d_attended, g_rows, d_normed,
):
    i = pl.program_id(0)
    at = pl.ds(pl.multiple_of(i * THIRD, LANES), THIRD)
    d_normed[:, at] = dot_t(d_gate[:, : 34 * LANES], matrix(w_1, 34)) + dot(
        d_inner_up[...], down_1[:, at]
    )

    @pl.when(i == pl.num_programs(0) - 1)
    def _():
        value = gradient[...] + layer_norm_back(d_normed[...], middle[...], vec[2:3])
        d_middle[...] = value
        d_out = value.astype(BF16)
        d_inner_o = dot_t(d_out, up_o[...]).astype(BF16)
        d_attended[...] = (dot_t(d_out, matrix(w_o)) + dot(d_inner_o, down_o[...])).astype(BF16)
        g_rows[0:R] = dot_l(d_inner_o, attended[...])
        g_rows[R : 2 * R] = dot_l(inner_o[...], d_out)
        g_rows[2 * R : 3 * R] = dot_l(d_inner_up[...], normed[...])


def middle_backward(
    d_gate, w_1, d_inner_up, narrow, normed, middle, gradient, vectors, w_o, attn, inner_o, attended
):
    rows = gradient.shape[0]
    return pl.pallas_call(
        middle_kernel,
        grid=(3,),
        in_specs=[
            whole((rows, WIDE)),
            unit_block(THIRD // 16, PANELS[2], lambda i: (3 + i, 0, 0, 0)),
            whole((rows, R)),
            whole((R, D)),
            whole((rows, D)),
            whole((rows, D)),
            whole((rows, D)),
            whole((8, D)),
            OUT_BLOCK,
            whole((R, D)),
            whole((R, D)),
            whole((rows, R)),
            whole((rows, D)),
        ],
        out_specs=[whole((rows, D)), whole((rows, D)), whole((3 * R, D))],
        out_shape=[
            struct((rows, D), F32),
            struct((rows, D), BF16),
            struct((3 * R, D), F32),
        ],
        scratch_shapes=[pltpu.VMEM((rows, D), F32)],
        name="middle_backward",
        **dense_params(2 * rows * D * (D + FF), 18 * rows * D + 2 * rows * FF + 2 * D * (D + FF)),
    )(
        d_gate, w_1, d_inner_up, narrow[0], normed, middle, gradient, vectors, w_o, attn[3], attn[7],
        inner_o, attended,
    )


def input_kernel(
    d_qkv, w_qkv, down, up, normed, inner, hidden, d_middle, vec, gradient, g_rows, d_normed, d_inner
):
    i = pl.program_id(0)

    @pl.when(i == 0)
    def _():
        for c in range(3):
            part = d_qkv[:, c * D : (c + 1) * D]
            d_inner[:, c * R : (c + 1) * R] = dot_t(part, up[c]).astype(BF16)
            g_rows[(3 + c) * R : (4 + c) * R] = dot_l(inner[:, c * R : (c + 1) * R], part)
        g_rows[0 : 3 * R] = dot_l(d_inner[...], normed[...])

    at = pl.ds(pl.multiple_of(i * THIRD, LANES), THIRD)
    d_normed[:, at] = dot_t(d_qkv[...], matrix(w_qkv)) + dot(d_inner[...], down[:, at])

    @pl.when(i == pl.num_programs(0) - 1)
    def _():
        gradient[...] = d_middle[...] + layer_norm_back(d_normed[...], hidden[...], vec[0:1])


def input_backward(d_qkv, w_qkv, attn, normed, inner, hidden, d_middle, vectors):
    rows = hidden.shape[0]
    return pl.pallas_call(
        input_kernel,
        grid=(3,),
        in_specs=[
            whole((rows, 3 * D)),
            unit_block(THIRD // 16, 27, lambda i: (i, 0, 0, 0)),
            whole((3 * R, D)),
            whole((3, R, D)),
            whole((rows, D)),
            whole((rows, 3 * R)),
            whole((rows, D)),
            whole((rows, D)),
            whole((8, D)),
        ],
        out_specs=[whole((rows, D)), whole((6 * R, D))],
        out_shape=[struct((rows, D), F32), struct((6 * R, D), F32)],
        scratch_shapes=[pltpu.VMEM((rows, D), F32), pltpu.VMEM((rows, 3 * R), BF16)],
        name="input_backward",
        **dense_params(6 * rows * D * D, 20 * rows * D + 6 * D * D),
    )(d_qkv, w_qkv, attn[0:3].reshape(3 * R, D), attn[4:7], normed, inner, hidden, d_middle, vectors)


PAIR = 2 * LANES
PAIRS = -(-D // PAIR)
FORWARD_STEPS = (3, H, WIDE // TILE, PAIRS)
FORWARD_AT = (0, 3, 3 + H, 3 + H + WIDE // TILE)
FORWARD_BEGINS = (
    [4.5 * i for i in range(3)]
    + [14 + 2 * i for i in range(H)]
    + [46 + (5 if i else 0) + 2.6 * i for i in range(WIDE // TILE)]
    + [73 + 3 * i for i in range(PAIRS)]
)
CHUNK_TIME = 7.0


def forward_kernel(with_gather, *refs):
    (
        bias_lane, hidden, w_qkv, vec, down, up, w_o, down_o, up_o, down_1, w_1, b_1, up_1, w_2, w_2_odd, b_2,
        down_2, up_2,
    ) = refs[:18]
    refs = refs[18:]
    if with_gather:
        shard, refs = refs[0], refs[1:]
    (
        normed, inner_qkv, qkv, attended, stats, inner_o, middle, normed_two, inner_up, gate, inner_down,
        next_hidden,
    ) = refs[:12]
    refs = refs[12:]
    if with_gather:
        flat, refs = refs[0], refs[1:]
    heads, activated, parts = refs[:3]
    i = pl.program_id(0)
    rows = hidden.shape[0]
    _, att_at, up_at, down_at = FORWARD_AT
    last = down_at + PAIRS - 1

    def at_step(k):
        return pl.when(i == k)

    if with_gather:
        start, events, finish = gather_plan(shard, flat, None, *refs[3:])
        at_step(0)(start)
        steps = [[] for _ in FORWARD_BEGINS]
        late = []
        for when, event in events:
            ready = [k for k, begin in enumerate(FORWARD_BEGINS) if begin >= CHUNK_TIME * when + 4]
            (steps[ready[0]] if ready else late).append(event)
        for k, due in enumerate(steps):
            if due:

                @at_step(k)
                def _(due=due):
                    for event in due:
                        event()

    @pl.when(i < att_at)
    def _():
        @at_step(0)
        def _():
            value = layer_norm(hidden[...], vec[0:1], vec[1:2]).astype(BF16)
            normed[...] = value
            narrow = dot_t(value, down[...]).astype(BF16)
            inner_qkv[...] = narrow
            for part in range(3):
                parts[part] = narrow[:, part * R : (part + 1) * R]
            stats[...] = jnp.zeros_like(stats)

        bias = vec[pl.ds(jnp.where(i == 2, 5, 4), 1), :] * jnp.where(i == 1, 0.0, 1.0)
        value = (dot_both(normed[...], matrix(w_qkv), parts[i], up[0]) + bias).astype(BF16)
        qkv[...] = value
        mark = jnp.where(i == 0, first_lane(rows, F32(1.0)), jnp.where(i == 1, bias_lane[...], jnp.zeros_like(bias_lane[...])))
        for h in range(H):
            heads[i, h] = pad_lanes(value[:, h * HD : (h + 1) * HD], mark)

    @pl.when(jnp.logical_and(i >= att_at, i < up_at))
    def _():
        h = i - att_at
        lane = lax.broadcasted_iota(jnp.int32, (rows, LANES), 1)
        s = dot_t(heads[0, h], heads[1, h])
        m = jnp.max(s, axis=1, keepdims=True)
        p = jnp.exp2((s - m) * C2)
        total = jnp.sum(p, axis=1, keepdims=True)
        o = dot(p.astype(BF16), heads[2, h])
        heads[0, h] = (o * (1.0 / total)).astype(BF16)
        stats[...] = jnp.where(lane == h, m * C2 + jnp.log2(total), stats[...])

    @pl.when(jnp.logical_and(i >= up_at, i < down_at))
    def _():
        t = i - up_at

        @at_step(up_at)
        def _():
            for h in range(H):
                attended[:, h * HD : (h + 1) * HD] = heads[0, h][:, :HD]
            value = attended[...]
            narrow = dot_t(value, down_o[...]).astype(BF16)
            inner_o[...] = narrow
            middle[...] = hidden[...] + (dot_both(value, matrix(w_o), narrow, up_o[...]) + vec[6:7])
            value = layer_norm(middle[...], vec[2:3], vec[3:4]).astype(BF16)
            normed_two[...] = value
            inner_up[...] = dot_t(value, down_1[...]).astype(BF16)

        x = dot_both(normed_two[...], matrix(w_1), inner_up[...], up_1[...]) + b_1[...]
        gate[...] = x.astype(BF16)
        value = (0.5 * x * (1.0 + gelu_parts(x))).astype(BF16)
        activated[:, pl.ds(pl.multiple_of(t * TILE, LANES), TILE)] = value

    @pl.when(i >= down_at)
    def _():
        @at_step(down_at)
        def _():
            w = jnp.concatenate([matrix(w_2.at[: UNITS[3]]), down_2[...].T[:FF]], axis=1)
            value = dot(activated[:, :FF], w)
            narrow = value[:, LANES : LANES + R].astype(BF16)
            inner_down[...] = narrow
            value = value[:, :LANES] + b_2[:, :LANES] + dot(narrow, up_2[:, :LANES])
            next_hidden[:, :LANES] = middle[:, D - LANES :] + value

        @pl.when(i > down_at)
        def _():
            at = pl.ds(pl.multiple_of((i - down_at - 1) * PAIR, LANES), PAIR)
            w = jnp.concatenate([matrix(w.at[: UNITS[3]]) for w in (w_2, w_2_odd)], axis=1)
            value = dot(activated[:, :FF], w) + b_2[...] + dot(inner_down[...], up_2[...])
            next_hidden[...] = middle[:, at] + value

    if with_gather:

        @at_step(last)
        def _():
            for event in late:
                event()
            finish()


def layer_forward(bias, hidden, weights, b_1, shard=None):
    w_qkv, w_o, w_1, w_2, vectors, attn, narrow, wide, _ = weights
    rows = hidden.shape[0]
    _, att_at, up_at, down_at = FORWARD_AT

    def step(i, k):
        return jnp.minimum(jnp.maximum(i - FORWARD_AT[k], 0), FORWARD_STEPS[k] - 1)

    def cols(count, width, k):
        return pl.BlockSpec((count, width), lambda i: (0, step(i, k)))

    def pair(i):
        return jnp.where(step(i, 3) == 0, PAIRS - 1, step(i, 3) - 1)

    def pairs(count):
        return pl.BlockSpec((count, PAIR), lambda i: (0, pair(i)))

    operands = [
        bias, hidden, w_qkv, vectors, attn[0:3].reshape(3 * R, D), attn[4:7], w_o, attn[3], attn[7], narrow[0],
        w_1, b_1, wide[0], w_2, w_2, vectors[7:8], wide[1], narrow[1],
    ]
    in_specs = [
        whole((rows, LANES - HD)),
        whole((rows, D)),
        unit_block(72, 9, lambda i: (0, step(i, 0), 0, 0)),
        whole((8, D)),
        whole((3 * R, D)),
        pl.BlockSpec((1, R, D), lambda i: (step(i, 0), 0, 0)),
        OUT_BLOCK,
        whole((R, D)),
        whole((R, D)),
        whole((R, D)),
        unit_block(72, 4, lambda i: (1, step(i, 2), 0, 0)),
        cols(1, TILE, 2),
        cols(R, TILE, 2),
        unit_block(288, 1, lambda i: (2, 2 * pair(i), 0, 0)),
        unit_block(288, 1, lambda i: (2, jnp.minimum(2 * pair(i) + 1, 8), 0, 0)),
        pairs(1),
        whole((R, WIDE)),
        pairs(R),
    ]
    outs = [
        (whole((rows, D)), struct((rows, D), BF16)),
        (whole((rows, 3 * R)), struct((rows, 3 * R), BF16)),
        (cols(rows, D, 0), struct((rows, 3 * D), BF16)),
        (whole((rows, D)), struct((rows, D), BF16)),
        (whole((rows, LANES)), struct((rows, LANES), F32)),
        (whole((rows, R)), struct((rows, R), BF16)),
        (whole((rows, D)), struct((rows, D), F32)),
        (whole((rows, D)), struct((rows, D), BF16)),
        (whole((rows, R)), struct((rows, R), BF16)),
        (cols(rows, TILE, 2), struct((rows, WIDE), BF16)),
        (whole((rows, R)), struct((rows, R), BF16)),
        (pairs(rows), struct((rows, D), F32)),
    ]
    scratch = [
        pltpu.VMEM((3, H, rows, LANES), BF16),
        pltpu.VMEM((rows, WIDE), BF16),
        pltpu.VMEM((3, rows, R), BF16),
    ]
    params = dict(vmem_limit_bytes=VMEM_MOST)
    if shard is not None:
        operands.append(shard)
        in_specs.append(pl.BlockSpec(memory_space=pl.ANY))
        outs.append(
            (pl.BlockSpec(memory_space=pl.ANY), struct((16 * TILES_HELD, LANES), BF16))
        )
        scratch += gather_semaphores()
        params.update(collective_id=3, has_side_effects=True)
    return pl.pallas_call(
        functools.partial(forward_kernel, shard is not None),
        grid=(sum(FORWARD_STEPS),),
        in_specs=in_specs,
        out_specs=[spec for spec, _ in outs],
        out_shape=[shape for _, shape in outs],
        scratch_shapes=scratch,
        cost_estimate=pl.CostEstimate(
            flops=2 * rows * D * (4 * D + 2 * FF) + 8 * rows * rows * D,
            bytes_accessed=2 * D * (4 * D + 2 * FF) + 30 * rows * D,
            transcendentals=H * rows * rows,
        ),
        compiler_params=pltpu.CompilerParams(**params),
        name="layer_forward_gather" if shard is not None else "layer_forward",
    )(*operands)


SHARE = 5
SHARE_ROWS = SHARE * 16


def share_plan(
    adapters, named, terms, names, out, held, totals, sums, local_sem, send, recv, pair_sem
):
    x = lax.axis_index("seq")
    f = lax.axis_index("fsdp")
    count = terms.shape[0]
    me = f * 2 + x
    rows = adapters * SHARE_ROWS

    def device(k):
        return (k // 2, k % 2)

    def share_to(to, slot):
        return pltpu.make_async_remote_copy(
            src_ref=terms.at[to],
            dst_ref=held.at[slot],
            send_sem=send.at[to],
            recv_sem=recv.at[slot],
            device_id=device(to),
            device_id_type=MESH,
        )

    def own():
        return pltpu.make_async_copy(terms.at[me], held.at[me], local_sem.at[0])

    def across(side):
        part = out.at[pl.ds(pl.multiple_of(side * rows, 16), rows), :]
        return pltpu.make_async_remote_copy(
            src_ref=part,
            dst_ref=part,
            send_sem=pair_sem.at[0],
            recv_sem=pair_sem.at[1],
            device_id=(f, 1 - x),
            device_id_type=MESH,
        )

    def start():
        barrier = pltpu.get_barrier_semaphore()

        def greet(k, carry):
            to = (me + k) % count
            pl.semaphore_signal(barrier, inc=1, device_id=device(to), device_id_type=MESH)
            return carry

        lax.fori_loop(1, count, greet, 0)
        pl.semaphore_wait(barrier, count - 1)

        def post(k, carry):
            to = (me + k) % count
            share_to(to, me).start()
            return carry

        lax.fori_loop(1, count, post, 0)
        own().start()

    def add_up():
        totals[...] = jnp.zeros_like(totals)

        def add(slot):
            value = held[slot, :SHARE].reshape(SHARE_ROWS, LANES).astype(F32)
            if named:
                name = names[pl.ds(slot, 1), :]
            else:
                name = held[slot, SHARE].astype(F32)[0:1]
                names[pl.ds(slot, 1), :] = name
            for e in range(adapters):
                totals[e] += jnp.where(name == float(e), value, 0.0)

        own().wait()
        add(me)

        def take(k, carry):
            slot = (me + count - k) % count
            share_to(slot, slot).wait_recv()
            add(slot)
            return carry

        lax.fori_loop(1, count, take, 0)
        sums[...] = totals[...].reshape(rows, LANES).astype(BF16)
        part = out.at[pl.ds(pl.multiple_of(x * rows, 16), rows), :]
        keep = pltpu.make_async_copy(sums, part, local_sem.at[0])
        keep.start()
        keep.wait()
        across(x).start()

    def finish():
        def sent(k, carry):
            to = (me + k) % count
            share_to(to, me).wait_send()
            return carry

        lax.fori_loop(1, count, sent, 0)
        across(x).wait_send()
        across(1 - x).wait_recv()

    return start, add_up, finish


def share_kernel(adapters, *refs):
    for part in share_plan(adapters, True, *refs):
        part()


def share_scratch(count, adapters, tiles):
    dma = pltpu.SemaphoreType.DMA
    rows = adapters * SHARE_ROWS
    return [
        pltpu.VMEM((count, tiles, 16, LANES), BF16),
        pltpu.VMEM((adapters, SHARE_ROWS, LANES), F32),
        pltpu.VMEM((rows, LANES), BF16),
        dma((1,)),
        dma((count,)),
        dma((count,)),
        dma((2,)),
    ]


def share_terms(terms, names, adapters):
    rows = adapters * SHARE_ROWS
    return pl.pallas_call(
        functools.partial(share_kernel, adapters),
        in_specs=[pl.BlockSpec(memory_space=pl.ANY), pl.BlockSpec(memory_space=pltpu.VMEM)],
        out_specs=pl.BlockSpec(memory_space=pl.ANY),
        out_shape=jax.ShapeDtypeStruct((2 * rows, LANES), BF16),
        scratch_shapes=share_scratch(terms.shape[0], adapters, SHARE),
        compiler_params=pltpu.CompilerParams(
            collective_id=1, has_side_effects=True, vmem_limit_bytes=VMEM_LIMIT
        ),
        name="share_terms",
    )(terms, names)


def table_kernel(layers, *refs):
    attn, narrow, wide = refs[layers:]
    for layer in range(layers):
        source = refs[layer]
        for t in range(10 * 9 + 2 * 34):
            tile = source[t // SHARE, 0, t % SHARE].astype(F32)
            if t < 90:
                at = slice(t % 9 * LANES, (t % 9 + 1) * LANES)
                if t < 72:
                    attn[layer, t // 9, 0, :, at] = tile
                else:
                    narrow[layer, t // 9 - 8, 0, :, at] = tile
            else:
                c, p = (t - 90) // 34, (t - 90) % 34
                width = min(LANES, FF - p * LANES)
                wide[layer, c, 0, :, p * LANES : p * LANES + width] = tile[:, :width]


def gradient_tables(gathered, adapters):
    layers = len(gathered)
    count = gathered[0].shape[0] // (adapters * SHARE_ROWS)
    gathered = [g.reshape(count, adapters, SHARE, 16, LANES) for g in gathered]

    def out_block(kinds, width):
        return pl.BlockSpec((layers, kinds, 1, R, width), lambda e: (0, 0, e, 0, 0))

    return pl.pallas_call(
        functools.partial(table_kernel, layers),
        grid=(adapters,),
        in_specs=[pl.BlockSpec((count, 1, SHARE, 16, LANES), lambda e: (0, e, 0, 0, 0))] * layers,
        out_specs=[out_block(8, D), out_block(2, D), out_block(2, FF)],
        out_shape=[
            struct((layers, 8, adapters, R, D), F32),
            struct((layers, 2, adapters, R, D), F32),
            struct((layers, 2, adapters, R, FF), F32),
        ],
        compiler_params=pltpu.CompilerParams(vmem_limit_bytes=VMEM_LIMIT),
        name="gradient_tables",
    )(*gathered)


BACKWARD_STEPS = (WIDE // TILE, PAIRS, 1, H, PAIRS)
BACKWARD_AT = (0, 9, 14, 15, 31)
SHARE_AT, PASS_AT, GATHER_AT = 7, 9, 10


def backward_kernel(adapters, *refs):
    (
        gradient, w_2, gate, down_2, up_2, inner_down, inner_up, w_1, w_1_odd, up_1, down_1, normed_two_in, vec, w_o, down_o,
        up_o, inner_o, attended, bias, stats, w_qkv, w_qkv_odd, up, down, inner_qkv, middle_in, qkv_in, hidden_in, normed_in,
    ) = refs[:29]
    refs = refs[29:]
    if adapters:
        terms, half, refs = refs[0], refs[1], refs[2:]
    new_gradient, g_wide, g_up_2, g_middle, g_input = refs[:5]
    refs = refs[5:]
    if adapters:
        pair, gathered, other_half, names, refs = refs[0], refs[1], refs[2], refs[3], refs[4:]
    (
        d_branch, d_inner_down, d_inner_up, wide, residual, d_normed, heads, stat_t, delta_t, load_sem,
    ) = refs[:10]
    refs = refs[10:]
    i = pl.program_id(0)
    _, middle_at, turn_at, att_at, input_at = BACKWARD_AT
    last = input_at + PAIRS - 1

    def at_step(k):
        return pl.when(i == k)

    def load_middle():
        return pltpu.make_async_copy(middle_in, residual, load_sem.at[0])

    def load_qkv():
        return pltpu.make_async_copy(qkv_in, wide.at[:, : 3 * D], load_sem.at[1])

    def load_hidden():
        return pltpu.make_async_copy(hidden_in, residual, load_sem.at[0])

    def load_normed_two():
        return pltpu.make_async_copy(normed_two_in, d_branch, load_sem.at[2])

    def load_normed():
        return pltpu.make_async_copy(normed_in, d_branch, load_sem.at[2])

    if adapters:
        share_start, share_sum, share_finish = share_plan(
            adapters, False, terms, names, pair, *refs[:7]
        )
        swap_sem = refs[7]
        start, events, finish = gather_plan(pair, gathered, None, *refs[8:])
        swap = pltpu.make_async_remote_copy(
            src_ref=half,
            dst_ref=other_half,
            send_sem=swap_sem.at[0],
            recv_sem=swap_sem.at[1],
            device_id=(lax.axis_index("fsdp"), 1 - lax.axis_index("seq")),
            device_id_type=MESH,
        )
        at_step(0)(share_start)
        at_step(GATHER_AT + 12)(swap.start)
        at_step(SHARE_AT)(share_sum)
        at_step(PASS_AT)(share_finish)

        @at_step(GATHER_AT)
        def _():
            start(False)

        steps = {}
        for when, event in events:
            steps.setdefault(min(GATHER_AT + 1 + int(when), last), []).append(event)
        for k, due in steps.items():

            @at_step(k)
            def _(due=due):
                for event in due:
                    event()

    @pl.when(i < middle_at)
    def _():
        @at_step(0)
        def _():
            load_middle().start()
            value = gradient[...].astype(BF16)
            d_branch[...] = value
            d_inner_down[...] = dot_t(value, up_2[...]).astype(BF16)
            g_up_2[...] = dot_l(inner_down[...], value)

        left = FF - i * TILE
        d_act = dot_both_t(d_branch[...], matrix(w_2), d_inner_down[...], down_2[...].T)
        x = gate[...].astype(F32)
        t = gelu_parts(x)
        half = 0.5 * (1.0 + t)
        slope = half + 0.5 * x * (1.0 - t * t) * (
            0.7978845608028654 * (1.0 + 3 * 0.044715 * x * x)
        )
        keep = lax.broadcasted_iota(jnp.int32, (1, TILE), 1) < left
        value = jnp.where(keep, slope * d_act, 0.0).astype(BF16)
        wide[:, pl.ds(pl.multiple_of(i * TILE, LANES), TILE)] = value
        g_wide[0:R] = dot_l(inner_up[...], value)
        g_wide[R : 2 * R] = dot_l(d_inner_down[...], (x * half).astype(BF16))

    @pl.when(jnp.logical_and(i >= middle_at, i < turn_at))
    def _():
        at_step(middle_at)(load_normed_two().start)

        @pl.when(i < turn_at - 1)
        def _():
            w = jnp.concatenate([matrix(w_1, 34), matrix(w_1_odd, 34)], axis=0)
            d_normed[i - middle_at] = dot_t(wide[:, : 34 * LANES], w)

        @at_step(turn_at - 1)
        def _():
            w = jnp.concatenate([matrix(w_1, 34), up_1[:, : 34 * LANES]], axis=0)
            value = dot_t(wide[:, : 34 * LANES], w)
            d_normed[PAIRS - 1, :, :LANES] = value[:, :LANES]
            d_inner_up[...] = value[:, LANES : LANES + R].astype(BF16)

    def joined():
        parts = [d_normed[k] for k in range(PAIRS - 1)]
        return jnp.concatenate(parts + [d_normed[PAIRS - 1, :, :LANES]], axis=1)

    @at_step(turn_at)
    def _():
        load_qkv().start()
        load_middle().wait()
        d_two = joined() + dot(d_inner_up[...], down_1[...])
        value = gradient[...] + layer_norm_back(d_two, residual[...], vec[2:3])
        load_hidden().start()
        new_gradient[...] = value
        d_out = value.astype(BF16)
        d_inner_o = dot_t(d_out, up_o[...]).astype(BF16)
        wide[:, 3 * D :] = (dot_t(d_out, matrix(w_o)) + dot(d_inner_o, down_o[...])).astype(BF16)
        g_middle[0:R] = dot_l(d_inner_o, attended[...])
        g_middle[R : 2 * R] = dot_l(inner_o[...], d_out)
        load_normed_two().wait()
        g_middle[2 * R : 3 * R] = dot_l(d_inner_up[...], d_branch[...])
        load_normed().start()
        load_qkv().wait()
        rows = gradient.shape[0]
        lane = lax.broadcasted_iota(jnp.int32, (rows, LANES), 1)
        delta = jnp.zeros((rows, LANES), F32)
        marked = (first_lane(rows, F32(1.0)), bias[...], None)
        for h in range(H):
            for c in range(3):
                part = wide[:, c * D + h * HD : c * D + (h + 1) * HD]
                heads[c, h] = pad_lanes(part, marked[c])
            do = wide[:, 3 * D + h * HD : 3 * D + (h + 1) * HD]
            heads[3, h] = pad_lanes(do)
            o = attended[:, h * HD : (h + 1) * HD].astype(F32)
            d = jnp.sum(do.astype(F32) * o, axis=1, keepdims=True)
            delta = jnp.where(lane == h, d, delta)
        stat_t[...] = stats[...].T
        delta_t[...] = delta.T

    @pl.when(jnp.logical_and(i >= att_at, i < input_at))
    def _():
        h = i - att_at
        q, k, do = heads[0, h], heads[1, h], heads[3, h]
        p = jnp.exp2(dot_t(k, q) * C2 - stat_t[pl.ds(h, 1), :])
        dv = dot(p.astype(BF16), do)
        dp = dot_t(heads[2, h], do)
        ds = (p * (dp - delta_t[pl.ds(h, 1), :])).astype(BF16)
        dk = dot(ds, q)
        dq = dot(k.T, ds)
        heads[2, h] = dv.astype(BF16)
        heads[1, h] = (dk * SCALE).astype(BF16)
        heads[0, h] = (dq * SCALE).astype(BF16).T

    @pl.when(i >= input_at)
    def _():
        @at_step(input_at)
        def _():
            load_normed().wait()
            for c in range(3):
                for h in range(H):
                    wide[:, c * D + h * HD : c * D + (h + 1) * HD] = heads[c, h][:, :HD]
            for c in range(3):
                part = wide[:, c * D : (c + 1) * D]
                g_input[(3 + c) * R : (4 + c) * R] = dot_l(inner_qkv[:, c * R : (c + 1) * R], part)

        @pl.when(i < last)
        def _():
            w = jnp.concatenate([matrix(w_qkv), matrix(w_qkv_odd)], axis=0)
            d_normed[i - input_at] = dot_t(wide[:, : 3 * D], w)

        @at_step(last)
        def _():
            w = jnp.concatenate([matrix(w_qkv), up[...]], axis=0)
            value = dot_t(wide[:, : 3 * D], w)
            d_normed[PAIRS - 1, :, :LANES] = value[:, :LANES]
            narrow = value[:, LANES : LANES + 3 * R].astype(BF16)
            g_input[0 : 3 * R] = dot_l(narrow, d_branch[...])
            load_hidden().wait()
            d_one = joined() + dot(narrow, down[...])
            new_gradient[...] += layer_norm_back(d_one, residual[...], vec[0:1])

    if adapters:

        @at_step(last)
        def _():
            finish()
            swap.wait()


def layer_backward(
    gradient, saved, weights, bias, adapters=0, terms=None, half=None
):
    hidden, normed, inner_qkv, qkv, stats, attended, inner_o, middle, normed_two, inner_up, gate, inner_down = saved
    w_qkv, w_o, w_1, w_2, vectors, attn, narrow, wide, up_diagonal = weights
    rows = gradient.shape[0]

    def step(i, k):
        return jnp.minimum(jnp.maximum(i - BACKWARD_AT[k], 0), BACKWARD_STEPS[k] - 1)

    def cols(count, width, k):
        return pl.BlockSpec((count, width), lambda i: (0, step(i, k)))

    hbm = pl.BlockSpec(memory_space=pl.ANY)
    operands = [
        (whole((rows, D)), gradient),
        (unit_block(TILE // 16, 9, lambda i: (TILES_AT[3] // 9 * 16 // TILE + step(i, 0), 0, 0, 0)), w_2),
        (cols(rows, TILE, 0), gate),
        (cols(R, TILE, 0), wide[1]),
        (whole((R, D)), narrow[1]),
        (whole((rows, R)), inner_down),
        (whole((rows, R)), inner_up),
        (unit_block(8, PANELS[2], lambda i: (9 + 2 * step(i, 1), 0, 0, 0)), w_1),
        (unit_block(8, PANELS[2], lambda i: (10 + jnp.minimum(2 * step(i, 1), 7), 0, 0, 0)), w_1),
        (whole((R, WIDE)), wide[0]),
        (whole((R, D)), narrow[0]),
        (hbm, normed_two),
        (whole((8, D)), vectors),
        (OUT_BLOCK, w_o),
        (whole((R, D)), attn[3]),
        (whole((R, D)), attn[7]),
        (whole((rows, R)), inner_o),
        (whole((rows, D)), attended),
        (whole((rows, LANES - HD)), bias),
        (whole((rows, LANES)), stats),
        (unit_block(8, 27, lambda i: (2 * step(i, 4), 0, 0, 0)), w_qkv),
        (unit_block(8, 27, lambda i: (jnp.minimum(2 * step(i, 4) + 1, 8), 0, 0, 0)), w_qkv),
        (whole((3 * R, 3 * D)), up_diagonal),
        (whole((3 * R, D)), attn[0:3].reshape(3 * R, D)),
        (whole((rows, 3 * R)), inner_qkv),
        (hbm, middle),
        (hbm, qkv),
        (hbm, hidden),
        (hbm, normed),
    ]
    outs = [
        (whole((rows, D)), struct((rows, D), F32)),
        (cols(2 * R, TILE, 0), struct((2 * R, WIDE), F32)),
        (whole((R, D)), struct((R, D), F32)),
        (whole((3 * R, D)), struct((3 * R, D), F32)),
        (whole((6 * R, D)), struct((6 * R, D), F32)),
    ]
    scratch = [
        pltpu.VMEM((rows, D), BF16),
        pltpu.VMEM((rows, R), BF16),
        pltpu.VMEM((rows, R), BF16),
        pltpu.VMEM((rows, WIDE), BF16),
        pltpu.VMEM((rows, D), F32),
        pltpu.VMEM((PAIRS, rows, PAIR), F32),
        pltpu.VMEM((4, H, rows, LANES), BF16),
        pltpu.VMEM((LANES, rows), F32),
        pltpu.VMEM((LANES, rows), F32),
        pltpu.SemaphoreType.DMA((3,)),
    ]
    params = dict(vmem_limit_bytes=VMEM_MOST)
    if adapters:
        operands += [(hbm, terms), (hbm, half)]
        block = 2 * adapters * SHARE_ROWS
        outs += [(hbm, struct((block, LANES), BF16)), (hbm, struct((16 * block, LANES), BF16))]
        outs += [(hbm, struct(half.shape, BF16))]
        outs += [(whole((terms.shape[0], LANES)), struct((terms.shape[0], LANES), F32))]
        scratch += share_scratch(terms.shape[0], adapters, SHARE + 1) + [pltpu.SemaphoreType.DMA((2,))]
        scratch += gather_semaphores()
        params.update(collective_id=4, has_side_effects=True)
    return pl.pallas_call(
        functools.partial(backward_kernel, adapters),
        grid=(sum(BACKWARD_STEPS),),
        in_specs=[spec for spec, _ in operands],
        out_specs=[spec for spec, _ in outs],
        out_shape=[shape for _, shape in outs],
        scratch_shapes=scratch,
        cost_estimate=pl.CostEstimate(
            flops=2 * rows * D * (4 * D + 2 * FF) + 20 * rows * rows * D,
            bytes_accessed=2 * D * (4 * D + 2 * FF) + 40 * rows * D,
            transcendentals=H * rows * rows,
        ),
        compiler_params=pltpu.CompilerParams(**params),
        name="layer_backward_share" if adapters else "layer_backward",
    )(*[operand for _, operand in operands])


def local(
    activations,
    group_image_count,
    image_adapter_index,
    lengths,
    frozen,
    attention_adapter_weights,
    narrow_adapter_weights,
    broad_adapter_weights,
    cotangent,
):
    slots, local_len, _ = activations.shape
    seq_parts = lax.axis_size("seq")
    fsdp_parts = lax.axis_size("fsdp")
    device_count = seq_parts * fsdp_parts
    me = lax.axis_index("seq")
    seq_total = local_len * seq_parts
    layer_count = frozen.shape[0]
    adapters = attention_adapter_weights.shape[2]
    parts = seq_parts // slots
    on_block = (fsdp_parts, seq_parts, slots, layer_count) == (16, 2, 2, 2)
    slot = me // parts
    part = me % parts
    tokens = seq_total // parts
    groups = [[s * parts + p for p in range(parts)] for s in range(slots)]

    def to_image(v):
        if parts == 1 and slots == 2:
            mine = lax.dynamic_index_in_dim(v, slot, 0, keepdims=False)
            other = lax.dynamic_index_in_dim(v, 1 - slot, 0, keepdims=False)
            other = lax.ppermute(other, "seq", [(0, 1), (1, 0)])
            return jnp.where(
                slot == 0,
                jnp.concatenate([mine, other], 0),
                jnp.concatenate([other, mine], 0),
            )
        whole = lax.all_gather(v, "seq", axis=1, tiled=True)
        whole = lax.dynamic_index_in_dim(whole, slot, 0, keepdims=False)
        return lax.dynamic_slice_in_dim(whole, part * tokens, tokens, 0)

    def half_of(v, which):
        return lax.dynamic_slice_in_dim(v, which * local_len, local_len, 0)

    def to_tokens(v, other=None):
        if parts == 1 and slots == 2:
            mine = half_of(v, slot)
            if other is None:
                other = lax.ppermute(half_of(v, 1 - slot), "seq", [(0, 1), (1, 0)])
            return jnp.where(slot == 0, jnp.stack([mine, other]), jnp.stack([other, mine]))
        whole = lax.all_gather(v, "seq", axis=0, tiled=True).reshape(slots, seq_total, -1)
        return lax.dynamic_slice_in_dim(whole, me * local_len, local_len, 1)

    length = lax.dynamic_slice_in_dim(lengths, slot, 1, 0)
    adapter = lax.dynamic_index_in_dim(image_adapter_index, slot, 0, keepdims=False)
    is_live = slot < group_image_count[0]
    positions = part * tokens + jnp.arange(tokens, dtype=jnp.int32)
    row_mask = ((positions < length[0]) & is_live).astype(F32)[:, None]
    def pick(table):
        return lax.dynamic_index_in_dim(table, adapter, 2, keepdims=False)

    attention_adapters = pick(attention_adapter_weights)
    narrow_adapters = pick(narrow_adapter_weights)
    wide_adapters = pick(broad_adapter_weights)
    wide_adapters = jnp.pad(wide_adapters, ((0, 0), (0, 0), (0, 0), (0, WIDE - FF)))
    shards = lax.optimization_barrier(frozen.reshape(layer_count, -1, LANES))
    steps = [(d, d + 1) for d in range(fsdp_parts - 1)]
    steps = (steps, [(b, a) for a, b in steps])
    tiles = -(-(TILES_END + TILES_VECTORS) // (2 * fsdp_parts)) * 2
    index = lax.axis_index("fsdp").astype(jnp.int32).reshape(1)
    shards = [lay_shard(index, shards[layer], tiles, steps) for layer in range(layer_count)]
    lane = lax.broadcasted_iota(jnp.int32, (tokens, LANES - HD), 1)
    key = lax.broadcasted_iota(jnp.int32, (tokens, LANES - HD), 0)
    bias = jnp.where((lane == 0) & (key >= length[0]), NEG, 0.0).astype(BF16)
    hidden = to_image(activations).astype(F32) * row_mask
    shards[0], hidden = lax.optimization_barrier((shards[0], hidden))
    stored = []
    weights = []
    for layer in range(layer_count):
        if on_block and layer > 0:
            pass
        elif on_block:
            flat = gather_blocks(shards[layer], 0, 16 * TILES_HELD)
        else:
            flat = lax.all_gather(shards[layer], "fsdp", axis=0, tiled=True)
            flat = jnp.pad(flat, ((0, 16 * TILES_HELD - flat.shape[0]), (0, 0)))
        if layer == layer_count - 1:
            cotangent, flat = lax.optimization_barrier((cotangent, flat))
            d_output = to_image(cotangent)
        w_qkv, w_o, w_1, w_2 = (flat.reshape(-1, panels, 16, LANES) for panels in PANELS)
        vectors = lax.slice_in_dim(flat, 16 * TILES_END, 16 * TILES_END + 106, axis=0).reshape(-1)
        vectors, b_1 = vectors[: 8 * D].reshape(8, D).astype(F32), vectors[8 * D : 8 * D + FF]
        b_1 = jnp.pad(b_1.astype(F32), (0, WIDE - FF))[None, :]
        attn, narrow, wide = attention_adapters[layer], narrow_adapters[layer], wide_adapters[layer]
        up_diagonal = jnp.concatenate(
            [jnp.pad(attn[4 + c], ((0, 0), (c * D, (2 - c) * D))) for c in range(3)]
        )
        weights.append((w_qkv, w_o, w_1, w_2, vectors, attn, narrow, wide, up_diagonal))
        keys = None
        if parts == 1:
            shard = shards[layer + 1] if on_block and layer + 1 < layer_count else None
            made = layer_forward(bias, hidden, weights[layer], b_1, shard)
            normed, inner_qkv, qkv, attended, stats, inner_o, middle = made[:7]
            normed_two, inner_up, gate, inner_down, next_hidden = made[7:12]
            flat = made[12] if shard is not None else None
        else:
            normed, inner_qkv, qkv = qkv_forward(hidden, w_qkv, vectors, attn)
            keys = lax.all_gather(
                qkv[:, D:], "seq", axis=0, tiled=True, axis_index_groups=groups
            )
            attended, stats = attn_fwd(length, qkv, keys)
            inner_o, middle, normed_two, inner_up, gate, activated = up_forward(
                attended, hidden, w_o, vectors, attn, narrow, w_1, b_1, wide
            )
            inner_down, next_hidden = down_forward(
                activated, middle, w_2, vectors[7:8], narrow, wide
            )
        stored.append(
            (
                hidden,
                normed,
                inner_qkv,
                qkv,
                keys,
                stats,
                attended,
                inner_o,
                middle,
                normed_two,
                inner_up,
                gate,
                inner_down,
            )
        )
        hidden = next_hidden
    output = (hidden * row_mask).astype(BF16)
    other_half = None
    gradient = d_output.astype(F32) * row_mask
    collected = [None] * layer_count
    terms = None
    for layer in reversed(range(layer_count)):
        (
            layer_input,
            normed,
            inner_qkv,
            qkv,
            keys,
            stats,
            attended,
            inner_o,
            middle,
            normed_two,
            inner_up,
            gate,
            inner_down,
        ) = stored[layer]
        w_qkv, w_o, w_1, w_2, vectors, attn, narrow, wide = weights[layer][:8]
        if parts == 1:
            saved = (
                layer_input, normed, inner_qkv, qkv, stats, attended, inner_o, middle, normed_two, inner_up,
                gate, inner_down,
            )
            hosted = terms if on_block and layer + 1 < layer_count else None
            made = layer_backward(
                gradient,
                saved,
                weights[layer],
                bias,
                adapters if hosted is not None else 0,
                hosted,
                half_of(output, 1 - slot),
            )
            gradient, g_wide, g_up_2, g_middle, g_input = made[:5]
            if hosted is not None:
                collected[layer + 1], other_half, names = made[6:9]
        else:
            d_gate, g_wide, d_inner_up, g_up_2 = gate_backward(
                gradient, w_2, gate, narrow, wide, inner_down, inner_up
            )
            d_middle, d_attended, g_middle = middle_backward(
                d_gate, w_1, d_inner_up, narrow, normed_two, middle, gradient, vectors, w_o, attn,
                inner_o, attended,
            )
            d_qkv = attn_bwd(length, qkv, d_attended, attended, stats, keys)
            if parts > 1:
                d_keys = lax.psum_scatter(
                    d_qkv[1].astype(F32),
                    "seq",
                    scatter_dimension=0,
                    tiled=True,
                    axis_index_groups=groups,
                )
                d_qkv = jnp.concatenate([d_qkv[0], d_keys.astype(BF16)], axis=1)
            else:
                d_qkv = d_qkv[0]
            gradient, g_input = input_backward(
                d_qkv, w_qkv, attn, normed, inner_qkv, layer_input, d_middle, vectors
            )
        rows_narrow = jnp.concatenate(
            [
                g_input[: 3 * R],
                g_middle[:R],
                g_input[3 * R :],
                g_middle[R:],
                g_up_2,
            ]
        )
        if on_block:
            terms = jnp.concatenate(
                [
                    rows_narrow.reshape(10, R, 9, LANES).transpose(0, 2, 1, 3).reshape(90, R, LANES),
                    g_wide.reshape(2, R, 36, LANES)
                    .transpose(0, 2, 1, 3)[:, :34]
                    .reshape(68, R, LANES),
                    jnp.zeros((2, R, LANES), F32),
                ]
            )
            terms = terms.astype(BF16).reshape(device_count, SHARE, R, LANES)
            if layer == 0:
                sums = share_terms(terms, names, adapters)
                collected[layer] = gather_blocks(sums, 2, 16 * sums.shape[0])
            else:
                name = jnp.broadcast_to(adapter.astype(BF16), (device_count, 1, R, LANES))
                terms = jnp.concatenate([terms, name], axis=1)
            continue
        rows_narrow = rows_narrow.astype(BF16)
        rows_wide = g_wide[:, :FF].astype(BF16)

        def shares(rows):
            share = -(-rows.shape[0] // device_count)
            rows = jnp.pad(rows, ((0, share * device_count - rows.shape[0]), (0, 0)))
            return rows.reshape(device_count, share * rows.shape[1])

        terms = [shares(rows_narrow), shares(rows_wide)]
        used = terms[0].shape[1] + terms[1].shape[1]
        label = jnp.broadcast_to(adapter.astype(BF16), (device_count, -used % LANES + LANES))
        terms = lax.all_to_all(
            jnp.concatenate(terms + [label], axis=1),
            ("fsdp", "seq"),
            split_axis=0,
            concat_axis=0,
            tiled=True,
        )
        choice = jnp.arange(adapters, dtype=F32)[:, None] == terms[:, used].astype(F32)[None, :]
        sums = jnp.dot(choice.astype(F32), terms.astype(F32), precision=lax.Precision.HIGHEST)
        sums = lax.all_gather(sums.astype(BF16), ("fsdp", "seq")).transpose(1, 0, 2)
        split = -(-10 * R // device_count) * D

        def table(part, count, width):
            part = part.reshape(adapters, -1, width)[:, : count * R]
            return part.reshape(adapters, count, R, width).transpose(1, 0, 2, 3).astype(F32)

        collected[layer] = (table(sums[:, :, :split], 10, D), table(sums[:, :, split:used], 2, FF))
    if on_block:
        grad_attn, grad_narrow, grad_wide = gradient_tables(collected, adapters)
    else:
        grad_attn = jnp.stack([entry[0][0:8] for entry in collected], axis=0)
        grad_narrow = jnp.stack([entry[0][8:10] for entry in collected], axis=0)
        grad_wide = jnp.stack([entry[1] for entry in collected], axis=0)
    output = to_tokens(output, other_half)
    input_grad = to_tokens((gradient * row_mask).astype(BF16)).astype(F32)
    return (output, input_grad, grad_attn, grad_narrow, grad_wide)


def solution(mesh):
    in_specs = (
        P("fsdp", "seq", None),
        P("fsdp"),
        P("fsdp"),
        P("fsdp"),
        P(None, "fsdp"),
        P(),
        P(),
        P(),
        P("fsdp", "seq", None),
    )
    out_specs = (P("fsdp", "seq", None), P("fsdp", "seq", None), P(), P(), P())
    return jax.shard_map(local, mesh=mesh, in_specs=in_specs, out_specs=out_specs, check_vma=False)
```

```python
import functools
import math

import jax
import jax.numpy as jnp
from jax import lax
from jax.experimental import pallas as pl
from jax.experimental.pallas import tpu as pltpu
from jax.sharding import PartitionSpec as P

D = 1152
HD = 72
H = 16
FF = 4304
R = 16
LANES = 128
BF16 = jnp.bfloat16
F32 = jnp.float32
MESH = pl.DeviceIdType.MESH
VMEM_LIMIT = 60 << 20
VMEM_MOST = 67043328
C2 = math.log2(math.e) / math.sqrt(HD)
SCALE = 1.0 / math.sqrt(HD)
NEG = -1e30
epsilon = 1e-06
CUT_OUT = 3 * D * D // LANES
CUT_UP = CUT_OUT + D * D // LANES
CUT_DOWN = CUT_UP + D * FF // LANES
CUT_VECTORS = CUT_DOWN + FF * D // LANES


def dot(a, b):
    return jnp.dot(a, b, preferred_element_type=F32)


def dot_t(a, b):
    return lax.dot_general(a, b, (((1,), (1,)), ((), ())), preferred_element_type=F32)


def dot_l(a, b):
    return lax.dot_general(a, b, (((0,), (0,)), ((), ())), preferred_element_type=F32)


PANELS = (3 * D // LANES, D // LANES, 36, D // LANES)
UNITS = (D // 16, D // 16, D // 16, FF // 16)
TILES_AT = (0, 1944, 2592, 5184)
TILES_END = 7605
TILES_VECTORS = 22
TILES_HELD = 7776
FLAT_AT = (0, CUT_OUT, CUT_UP, CUT_DOWN)
WIDE = PANELS[2] * LANES
UP_ROWS = 16 * FF // LANES
HALO = 1600


def lay_rows(d, own_rows, tiles, before, own, after, flat, held, turned):
    margin = 16 * PANELS[2]
    flat[0:HALO] = before.astype(F32)
    flat[HALO : HALO + own_rows] = own.astype(F32)
    flat[HALO + own_rows : 2 * HALO + own_rows] = after.astype(F32)
    flat_base = d * own_rows - HALO
    tile_base = d * tiles

    def span(at, units, panels):
        low = jnp.maximum(tile_base - at, 0) // panels
        high = jnp.maximum(tile_base + tiles - at + panels - 1, 0) // panels
        high = jnp.minimum(high, units)
        return low, jnp.maximum(high, low)

    for at, start, units, panels in zip(
        TILES_AT + (TILES_END,),
        FLAT_AT + (CUT_VECTORS,),
        UNITS + (TILES_VECTORS,),
        PANELS + (1,),
    ):
        low, high = span(at, units, panels)
        if start == CUT_UP:
            lane = lax.broadcasted_iota(jnp.int32, (8, LANES), 1)

            def up_units(b, carry):
                u = low + 8 * b
                source = pl.multiple_of(start + UP_ROWS * u - flat_base, 2)
                for j in range(16):
                    first, shift = (FF * j) // LANES, (FF * j) % LANES
                    turn = LANES - shift
                    now = flat[pl.ds(source + first, 8, stride=UP_ROWS), :]
                    now = pltpu.roll(now, turn, 1) if shift else now
                    for c in range(34):
                        value = now
                        if c < 33 or shift > LANES - FF % LANES:
                            now = flat[pl.ds(source + first + c + 1, 8, stride=UP_ROWS), :]
                            now = pltpu.roll(now, turn, 1) if shift else now
                            if shift:
                                value = jnp.where(lane < turn, value, now)
                        if c == 33:
                            value = jnp.where(lane < FF - 33 * LANES, value, 0.0)
                        turned[pl.ds(16 * c + j, 8, stride=16 * PANELS[2]), :] = value
                target = pl.multiple_of(16 * (at + PANELS[2] * u - tile_base) + margin, 16)
                held[pl.ds(target, 8 * 16 * PANELS[2]), :] = turned[...].astype(BF16)
                return carry

            turned[...] = jnp.zeros_like(turned)
            lax.fori_loop(0, (high - low + 7) // 8, up_units, 0)
        else:

            def unit(u, carry):
                source = pl.multiple_of(start + 16 * panels * u - flat_base, 16)
                target = pl.multiple_of(16 * (at + panels * u - tile_base) + margin, 16)
                for c in range(panels):
                    value = flat[pl.ds(source + c, 16, stride=panels), :]
                    held[pl.ds(target + 16 * c, 16), :] = value.astype(BF16)
                return carry

            lax.fori_loop(low, high, unit, 0)


def lay_kernel(own_rows, tiles, index_ref, before, own, after, out, flat, held, turned):
    margin = 16 * PANELS[2]
    lay_rows(index_ref[0], own_rows, tiles, before[...], own[...], after[...], flat, held, turned)
    out[...] = held[margin : margin + 16 * tiles]


def lay_scratch(own_rows, tiles):
    margin = 16 * PANELS[2]
    return [
        pltpu.VMEM((own_rows + 2 * HALO + 8 * UP_ROWS, LANES), F32),
        pltpu.VMEM((16 * tiles + 10 * margin, LANES), BF16),
        pltpu.VMEM((8 * margin, LANES), F32),
    ]


def lay_shard(index, shard, tiles, perms):
    own_rows = shard.shape[0]
    before = lax.ppermute(shard[own_rows - HALO :], "fsdp", perms[0])
    after = lax.ppermute(shard[:HALO], "fsdp", perms[1])
    vm = pl.BlockSpec(memory_space=pltpu.VMEM)
    return pl.pallas_call(
        functools.partial(lay_kernel, own_rows, tiles),
        in_specs=[pl.BlockSpec(memory_space=pltpu.SMEM), vm, vm, vm],
        out_specs=vm,
        out_shape=jax.ShapeDtypeStruct((16 * tiles, LANES), BF16),
        scratch_shapes=lay_scratch(own_rows, tiles),
        compiler_params=pltpu.CompilerParams(vmem_limit_bytes=VMEM_LIMIT),
        name="lay_shard",
    )(index, before, shard, after)


def pad_lanes(x, extra=None):
    if extra is None:
        extra = jnp.zeros((x.shape[0], LANES - HD), x.dtype)
    return jnp.concatenate([x, extra], axis=1)


def first_lane(rows, value):
    lane = lax.broadcasted_iota(jnp.int32, (rows, LANES - HD), 1)
    return jnp.where(lane == 0, value, 0.0).astype(BF16)


def key_bias(rows, length):
    key = lax.broadcasted_iota(jnp.int32, (rows, LANES - HD), 0)
    return first_lane(rows, jnp.where(key < length, 0.0, NEG))


def attn_fwd_kernel(offset, len_ref, qkv_ref, kv_ref, o_ref, st_ref, q_s, k_s, v_s):
    if kv_ref is None:
        kv_ref = qkv_ref
    rows, keys = qkv_ref.shape[0], kv_ref.shape[0]
    one = first_lane(rows, F32(1.0))
    bias = key_bias(keys, len_ref[0])
    for h in range(H):
        q_s[h] = pad_lanes(qkv_ref[:, h * HD : (h + 1) * HD], one)
        k_s[h] = pad_lanes(kv_ref[:, offset + h * HD : offset + (h + 1) * HD], bias)
        v_s[h] = pad_lanes(kv_ref[:, offset + D + h * HD : offset + D + (h + 1) * HD])
    st_ref[...] = jnp.zeros_like(st_ref)
    lane = lax.broadcasted_iota(jnp.int32, (rows, LANES), 1)

    def body(h, carry):
        s = dot_t(q_s[h], k_s[h])
        m = jnp.max(s, axis=1, keepdims=True)
        p = jnp.exp2((s - m) * C2)
        total = jnp.sum(p, axis=1, keepdims=True)
        o = dot(p.astype(BF16), v_s[h])
        q_s[h] = (o * (1.0 / total)).astype(BF16)
        st_ref[...] = jnp.where(lane == h, m * C2 + jnp.log2(total), st_ref[...])
        return carry

    lax.fori_loop(0, H, body, 0)
    for h in range(H):
        o_ref[:, h * HD : (h + 1) * HD] = q_s[h][:, :HD]


def attn_fwd(length, qkv, kv=None):
    rows = qkv.shape[0]
    keys = rows if kv is None else kv.shape[0]
    vm = pl.BlockSpec(memory_space=pltpu.VMEM)
    if kv is None:
        kernel = lambda a, b, *rest: attn_fwd_kernel(D, a, b, None, *rest)
        operands = (length, qkv)
    else:
        kernel = functools.partial(attn_fwd_kernel, 0)
        operands = (length, qkv, kv)
    return pl.pallas_call(
        kernel,
        in_specs=[pl.BlockSpec(memory_space=pltpu.SMEM)] + [vm] * (len(operands) - 1),
        out_specs=[vm, vm],
        out_shape=[
            jax.ShapeDtypeStruct((rows, D), BF16),
            jax.ShapeDtypeStruct((rows, LANES), F32),
        ],
        scratch_shapes=[
            pltpu.VMEM((H, rows, LANES), BF16),
            pltpu.VMEM((H, keys, LANES), BF16),
            pltpu.VMEM((H, keys, LANES), BF16),
        ],
        cost_estimate=pl.CostEstimate(
            flops=H * rows * keys * 256 * 4, bytes_accessed=rows * D * 8, transcendentals=H * rows * keys
        ),
        compiler_params=pltpu.CompilerParams(vmem_limit_bytes=VMEM_LIMIT),
        name="attention_forward",
    )(*operands)


def attn_bwd_kernel(
    offset, len_ref, qkv_ref, kv_ref, do_ref, o_ref, st_ref, dq_ref, dkv_ref, q_s, k_s, v_s, do_s, st_t, dl_t
):
    if kv_ref is None:
        kv_ref, dkv_ref = qkv_ref, dq_ref
    rows, keys = qkv_ref.shape[0], kv_ref.shape[0]
    one = first_lane(rows, F32(1.0))
    bias = key_bias(keys, len_ref[0])
    lane = lax.broadcasted_iota(jnp.int32, (rows, LANES), 1)
    delta = jnp.zeros((rows, LANES), F32)
    for h in range(H):
        q_s[h] = pad_lanes(qkv_ref[:, h * HD : (h + 1) * HD], one)
        k_s[h] = pad_lanes(kv_ref[:, offset + h * HD : offset + (h + 1) * HD], bias)
        v_s[h] = pad_lanes(kv_ref[:, offset + D + h * HD : offset + D + (h + 1) * HD])
        do = do_ref[:, h * HD : (h + 1) * HD]
        do_s[h] = pad_lanes(do)
        o = o_ref[:, h * HD : (h + 1) * HD].astype(F32)
        d = jnp.sum(do.astype(F32) * o, axis=1, keepdims=True)
        delta = jnp.where(lane == h, d, delta)
    st_t[...] = st_ref[...].T
    dl_t[...] = delta.T

    def body(h, carry):
        q, k, do = q_s[h], k_s[h], do_s[h]
        p = jnp.exp2(dot_t(k, q) * C2 - st_t[pl.ds(h, 1), :])
        dv = dot(p.astype(BF16), do)
        dp = dot_t(v_s[h], do)
        ds = (p * (dp - dl_t[pl.ds(h, 1), :])).astype(BF16)
        dk = dot(ds, q)
        dq = dot(k.T, ds)
        v_s[h] = dv.astype(BF16)
        k_s[h] = (dk * SCALE).astype(BF16)
        q_s[h] = (dq * SCALE).astype(BF16).T
        return carry

    lax.fori_loop(0, H, body, 0)
    for h in range(H):
        dq_ref[:, h * HD : (h + 1) * HD] = q_s[h][:, :HD]
        dkv_ref[:, offset + h * HD : offset + (h + 1) * HD] = k_s[h][:, :HD]
        dkv_ref[:, offset + D + h * HD : offset + D + (h + 1) * HD] = v_s[h][:, :HD]


def attn_bwd(length, qkv, do, o, st, kv=None):
    rows = qkv.shape[0]
    keys = rows if kv is None else kv.shape[0]
    vm = pl.BlockSpec(memory_space=pltpu.VMEM)
    if kv is None:
        kernel = lambda a, b, c, d, e, f, *rest: attn_bwd_kernel(
            D, a, b, None, c, d, e, f, None, *rest
        )
        operands = (length, qkv, do, o, st)
        outs = [jax.ShapeDtypeStruct((rows, 3 * D), BF16)]
    else:
        kernel = functools.partial(attn_bwd_kernel, 0)
        operands = (length, qkv, kv, do, o, st)
        outs = [jax.ShapeDtypeStruct((rows, D), BF16), jax.ShapeDtypeStruct((keys, 2 * D), BF16)]
    return pl.pallas_call(
        kernel,
        in_specs=[pl.BlockSpec(memory_space=pltpu.SMEM)] + [vm] * (len(operands) - 1),
        out_specs=[vm] * len(outs),
        out_shape=outs,
        scratch_shapes=[
            pltpu.VMEM((H, rows, LANES), BF16),
            pltpu.VMEM((H, keys, LANES), BF16),
            pltpu.VMEM((H, keys, LANES), BF16),
            pltpu.VMEM((H, rows, LANES), BF16),
            pltpu.VMEM((LANES, rows), F32),
            pltpu.VMEM((LANES, rows), F32),
        ],
        cost_estimate=pl.CostEstimate(
            flops=H * rows * keys * 256 * 10, bytes_accessed=rows * D * 16, transcendentals=H * rows * keys
        ),
        compiler_params=pltpu.CompilerParams(vmem_limit_bytes=VMEM_LIMIT),
        name="attention_backward",
    )(*operands)


LARGE_BLOCK = 4096


def gather_plan(
    src, out, stage, local_sem, z_recv, y_recv, b_recv, h_recv, c_recv_own, c_recv_z, c_recv_y, c_recv_b, c_recv_h,
    up_send, down_send, y_send, b_send, h_send, c_send_own, c_send_z, c_send_y, c_send_b, c_send_h,
):
    rows = src.shape[0]
    if rows >= LARGE_BLOCK:
        unit = rows // 6 // 16 * 16 + 16
        sizes = [unit, unit, rows // 2 - 2 * unit, rows // 2 - 2 * unit, unit]
        begins = [0, unit, 2 * unit, rows // 2, rows - 2 * unit]
    else:
        sizes = [rows // 2] * 2
        begins = [0, rows // 2]
    chunks, across_y = len(sizes), (len(sizes) + 1) // 2
    lend = chunks == 5
    x = lax.axis_index("seq")
    f = lax.axis_index("fsdp")
    z, y, c = f // 4, (f // 2) % 2, f % 2

    def place(zb, yb, j, side, cb=None):
        owner = (zb * 2 + yb) * 2 + (c if cb is None else cb)
        begin = jnp.where(side == 0, begins[j], rows - begins[j] - sizes[j])
        return pl.multiple_of(owner * rows + begin, 16), sizes[j]

    def view(spot):
        return out.at[pl.ds(spot[0], spot[1]), :]

    def device(zb, yb, cb, xb):
        return ((zb * 2 + yb) * 2 + cb, xb)

    up, down = device(z + 1, y, c, x), device(z - 1, y, c, x)
    beside, across, mate = device(z, 1 - y, c, x), device(z, y, c, 1 - x), device(z, y, 1 - c, x)

    def copy(spot, send, recv, to, source=None):
        return pltpu.make_async_remote_copy(
            src_ref=view(spot) if source is None else source,
            dst_ref=view(spot),
            send_sem=send,
            recv_sem=recv,
            device_id=to,
            device_id_type=MESH,
        )

    def arrived(spot, recv):
        copy(spot, local_sem.at[1], recv, mate).wait_recv()

    def own(j):
        begin = jnp.where(x == 0, begins[j], rows - begins[j] - sizes[j])
        return src.at[pl.ds(pl.multiple_of(begin, 16), sizes[j]), :]

    whole = (pl.multiple_of(f * rows, 16), rows)
    keep = pltpu.make_async_copy(src if stage is None else stage, view(whole), local_sem.at[0])

    def greet():
        barrier = pltpu.get_barrier_semaphore()
        for to in (beside, across, mate):
            pl.semaphore_signal(barrier, inc=1, device_id=to, device_id_type=MESH)

        @pl.when(z < 3)
        def _():
            pl.semaphore_signal(barrier, inc=1, device_id=up, device_id_type=MESH)

        @pl.when(z > 0)
        def _():
            pl.semaphore_signal(barrier, inc=1, device_id=down, device_id_type=MESH)

        pl.semaphore_wait(barrier, 3 + jnp.where(z < 3, 1, 0) + jnp.where(z > 0, 1, 0))

    def start(first=True):
        if first:
            greet()
        for j in range(chunks):
            spot = place(z, y, j, x)

            @pl.when(z < 3)
            def _():
                copy(spot, up_send.at[z, j], z_recv.at[z, j], up, own(j)).start()

            @pl.when(z > 0)
            def _():
                copy(spot, down_send.at[z, j], z_recv.at[z, j], down, own(j)).start()

            if j < across_y:
                copy(spot, y_send.at[z, j], y_recv.at[z, j], beside, own(j)).start()
        copy(whole, c_send_own.at[0], c_recv_own.at[0], mate, src).start()
        if stage is None:
            keep.start()
        else:
            fetch = pltpu.make_async_copy(src, stage, local_sem.at[0])
            fetch.start()
            fetch.wait()
            keep.start()

    def z_event(d, j):
        def flow(zb, onward, to, sends):
            spot = place(zb, y, j, x)
            arrived(spot, z_recv.at[zb, j])

            @pl.when(onward)
            def _():
                copy(spot, sends.at[zb, j], z_recv.at[zb, j], to).start()

            if j == 0 and lend:
                copy(spot, b_send.at[zb], b_recv.at[zb], across).start()
            if j < across_y:
                copy(spot, y_send.at[zb, j], y_recv.at[zb, j], beside).start()
            copy(spot, c_send_z.at[zb, j], c_recv_z.at[zb, j], mate).start()

        @pl.when(z - d >= 0)
        def _():
            flow(z - d, z < 3, up, up_send)

        @pl.when(z + d <= 3)
        def _():
            flow(z + d, z > 0, down, down_send)

    def each(d, act):
        if d == 0:
            act(z)
            return

        @pl.when(z - d >= 0)
        def _():
            act(z - d)

        @pl.when(z + d <= 3)
        def _():
            act(z + d)

    def y_event(d, j):
        def act(zb):
            spot = place(zb, 1 - y, j, x)
            arrived(spot, y_recv.at[zb, j])
            copy(spot, h_send.at[zb, j], h_recv.at[zb, j], across).start()
            copy(spot, c_send_y.at[zb, j], c_recv_y.at[zb, j], mate).start()

        each(d, act)

    def b_event(d):
        def act(zb):
            spot = place(zb, y, 0, 1 - x)
            arrived(spot, b_recv.at[zb])
            copy(spot, c_send_b.at[zb], c_recv_b.at[zb], mate).start()

        each(d, act)

    def h_event(d, j):
        def act(zb):
            spot = place(zb, 1 - y, j, 1 - x)
            arrived(spot, h_recv.at[zb, j])
            copy(spot, c_send_h.at[zb, j], c_recv_h.at[zb, j], mate).start()

        each(d, act)

    events = []
    for d in range(4):
        for j in range(chunks):
            at = (d - 1) * chunks + j + 1 if d else 0
            if d:
                events.append((at, functools.partial(z_event, d, j)))
                if j == 0 and lend:
                    events.append((at + 2, functools.partial(b_event, d)))
            if j < across_y:
                ready = at + 1.5 if d else j + 1
                events.append((ready, functools.partial(y_event, d, j)))
                events.append((ready + 2, functools.partial(h_event, d, j)))
    def finish():
        keep.wait()
        other = 1 - c

        def core_spot(zb, yb, j, side):
            return place(zb, yb, j, side, other)

        arrived((pl.multiple_of(((z * 2 + y) * 2 + other) * rows, 16), rows), c_recv_own.at[0])
        copy(whole, c_send_own.at[0], c_recv_own.at[0], mate).wait_send()
        for d in range(4):
            def drain(zb, d=d):
                for j in range(chunks):
                    if d:
                        arrived(core_spot(zb, y, j, x), c_recv_z.at[zb, j])
                        copy(place(zb, y, j, x), c_send_z.at[zb, j], c_recv_z.at[zb, j], mate).wait_send()
                    if j < across_y:
                        arrived(core_spot(zb, 1 - y, j, x), c_recv_y.at[zb, j])
                        arrived(core_spot(zb, 1 - y, j, 1 - x), c_recv_h.at[zb, j])
                        spot = place(zb, 1 - y, j, x)
                        copy(spot, c_send_y.at[zb, j], c_recv_y.at[zb, j], mate).wait_send()
                        copy(spot, h_send.at[zb, j], h_recv.at[zb, j], across).wait_send()
                        spot = place(zb, 1 - y, j, 1 - x)
                        copy(spot, c_send_h.at[zb, j], c_recv_h.at[zb, j], mate).wait_send()
                        spot = place(zb, y, j, x)
                        copy(spot, y_send.at[zb, j], y_recv.at[zb, j], beside).wait_send()
                if d and lend:
                    arrived(core_spot(zb, y, 0, 1 - x), c_recv_b.at[zb])
                    spot = place(zb, y, 0, 1 - x)
                    copy(spot, c_send_b.at[zb], c_recv_b.at[zb], mate).wait_send()
                    spot = place(zb, y, 0, x)
                    copy(spot, b_send.at[zb], b_recv.at[zb], across).wait_send()

            each(d, drain)
            for j in range(chunks):
                @pl.when(jnp.logical_and(z - d >= 0, z < 3))
                def _():
                    zb = z - d
                    copy(place(zb, y, j, x), up_send.at[zb, j], z_recv.at[zb, j], up).wait_send()

                @pl.when(jnp.logical_and(z + d <= 3, z > 0))
                def _():
                    zb = z + d
                    copy(place(zb, y, j, x), down_send.at[zb, j], z_recv.at[zb, j], down).wait_send()

    return start, sorted(events, key=lambda e: e[0]), finish


def gather_kernel(*refs):
    start, events, finish = gather_plan(*refs)
    start()
    for _, event in events:
        event()
    finish()


def gather_semaphores():
    dma = pltpu.SemaphoreType.DMA
    core = [dma((1,)), dma((4, 5)), dma((4, 3)), dma((4,)), dma((4, 3))]
    links = [dma((4, 5)), dma((4, 3)), dma((4,)), dma((4, 3))]
    return [dma((2,))] + links + core + [dma((4, 5))] + links + core


def gather_blocks(shard, collective_id, held_rows):
    rows = shard.shape[0]
    return pl.pallas_call(
        gather_kernel,
        in_specs=[pl.BlockSpec(memory_space=pl.ANY)],
        out_specs=pl.BlockSpec(memory_space=pl.ANY),
        out_shape=jax.ShapeDtypeStruct((held_rows, LANES), BF16),
        scratch_shapes=[pltpu.VMEM((rows, LANES), BF16)] + gather_semaphores(),
        compiler_params=pltpu.CompilerParams(collective_id=collective_id, has_side_effects=True, vmem_limit_bytes=VMEM_LIMIT),
        name="gather_blocks",
    )(shard)


def gelu_parts(x):
    inner = 0.7978845608028654 * (x + 0.044715 * x * x * x)
    return jnp.tanh(inner)


def layer_norm(tensor, gain, offset):
    average = jnp.mean(tensor, axis=-1, keepdims=True)
    centred = tensor - average
    variance = jnp.mean(centred * centred, axis=-1, keepdims=True)
    return centred * lax.rsqrt(variance + epsilon) * gain + offset


def layer_norm_back(d_out, tensor, gain):
    average = jnp.mean(tensor, axis=-1, keepdims=True)
    centred = tensor - average
    variance = jnp.mean(centred * centred, axis=-1, keepdims=True)
    scale = lax.rsqrt(variance + epsilon)
    normal = centred * scale
    d_normal = d_out * gain
    mean_d = jnp.mean(d_normal, axis=-1, keepdims=True)
    mean_dn = jnp.mean(d_normal * normal, axis=-1, keepdims=True)
    return (d_normal - mean_d - normal * mean_dn) * scale


def dot_both(x, w, inner, up):
    cut = w.shape[0] // 256 * 256
    tail = dot(
        jnp.concatenate([x[:, cut:], inner], axis=1), jnp.concatenate([w[cut:], up], axis=0)
    )
    return dot(x[:, :cut], w[:cut]) + tail


def dot_both_t(x, w, inner, up_t):
    cut = w.shape[1] // 256 * 256
    tail = dot_t(
        jnp.concatenate([x[:, cut:], inner], axis=1), jnp.concatenate([w[:, cut:], up_t], axis=1)
    )
    return dot_t(x[:, :cut], w[:, :cut]) + tail


def matrix(ref, count=None):
    units, panels = ref.shape[:2]
    return jnp.concatenate(
        [ref[:, p].reshape(units * 16, LANES) for p in range(count or panels)], axis=1
    )


def unit_block(units, panels, place):
    return pl.BlockSpec((units, panels, 16, LANES), place)


def whole(shape):
    return pl.BlockSpec(shape, lambda i: (0,) * len(shape), pipeline_mode=pl.Buffered(1))


def columns(rows, width):
    return pl.BlockSpec((rows, width), lambda i: (0, i))


def struct(shape, dtype):
    return jax.ShapeDtypeStruct(shape, dtype)


def dense_params(flops, bytes_accessed):
    return dict(
        cost_estimate=pl.CostEstimate(
            flops=flops, bytes_accessed=bytes_accessed, transcendentals=0
        ),
        compiler_params=pltpu.CompilerParams(vmem_limit_bytes=VMEM_LIMIT),
    )


def qkv_kernel(hidden, w, vec, down, up, normed, inner, qkv, parts):
    c = pl.program_id(0)

    @pl.when(c == 0)
    def _():
        value = layer_norm(hidden[...], vec[0:1], vec[1:2]).astype(BF16)
        normed[...] = value
        narrow = dot_t(value, down[...]).astype(BF16)
        inner[...] = narrow
        for part in range(3):
            parts[part] = narrow[:, part * R : (part + 1) * R]

    bias = vec[pl.ds(jnp.where(c == 2, 5, 4), 1), :] * jnp.where(c == 1, 0.0, 1.0)
    qkv[...] = (dot_both(normed[...], matrix(w), parts[c], up[0]) + bias).astype(BF16)


def qkv_forward(hidden, w_qkv, vectors, attn):
    rows = hidden.shape[0]
    return pl.pallas_call(
        qkv_kernel,
        grid=(3,),
        in_specs=[
            whole((rows, D)),
            unit_block(72, 9, lambda i: (0, i, 0, 0)),
            whole((8, D)),
            whole((3 * R, D)),
            pl.BlockSpec((1, R, D), lambda i: (i, 0, 0)),
        ],
        out_specs=[whole((rows, D)), whole((rows, 3 * R)), columns(rows, D)],
        out_shape=[
            struct((rows, D), BF16),
            struct((rows, 3 * R), BF16),
            struct((rows, 3 * D), BF16),
        ],
        scratch_shapes=[pltpu.VMEM((3, rows, R), BF16)],
        name="qkv_forward",
        **dense_params(6 * rows * D * D, 14 * rows * D + 6 * D * D),
    )(hidden, w_qkv, vectors, attn[0:3].reshape(3 * R, D), attn[4:7])


TILE = 512
OUT_BLOCK = pl.BlockSpec(
    (72, 9, 16, LANES), lambda i: (3, 0, 0, 0), pipeline_mode=pl.Buffered(1)
)


def up_kernel(
    attended, hidden, w_o, vec, down_o, up_o, down_1, w_1, b_1, up_1,
    inner_o, middle, normed, inner_up, gate, activated,
):
    @pl.when(pl.program_id(0) == 0)
    def _():
        narrow = dot_t(attended[...], down_o[...]).astype(BF16)
        inner_o[...] = narrow
        middle[...] = hidden[...] + (dot_both(attended[...], matrix(w_o), narrow, up_o[...]) + vec[6:7])
        value = layer_norm(middle[...], vec[2:3], vec[3:4]).astype(BF16)
        normed[...] = value
        inner_up[...] = dot_t(value, down_1[...]).astype(BF16)

    x = dot_both(normed[...], matrix(w_1), inner_up[...], up_1[...]) + b_1[...]
    gate[...] = x.astype(BF16)
    activated[...] = (0.5 * x * (1.0 + gelu_parts(x))).astype(BF16)


def up_forward(attended, hidden, w_o, vectors, attn, narrow, w_1, b_1, wide):
    rows = hidden.shape[0]
    return pl.pallas_call(
        up_kernel,
        grid=(WIDE // TILE,),
        in_specs=[
            whole((rows, D)),
            whole((rows, D)),
            OUT_BLOCK,
            whole((8, D)),
            whole((R, D)),
            whole((R, D)),
            whole((R, D)),
            unit_block(72, 4, lambda i: (1, i, 0, 0)),
            columns(1, TILE),
            columns(R, TILE),
        ],
        out_specs=[
            whole((rows, R)),
            whole((rows, D)),
            whole((rows, D)),
            whole((rows, R)),
            columns(rows, TILE),
            columns(rows, TILE),
        ],
        out_shape=[
            struct((rows, R), BF16),
            struct((rows, D), F32),
            struct((rows, D), BF16),
            struct((rows, R), BF16),
            struct((rows, WIDE), BF16),
            struct((rows, WIDE), BF16),
        ],
        name="up_forward",
        **dense_params(2 * rows * D * (D + FF), 12 * rows * D + 4 * rows * FF + 2 * D * (D + FF)),
    )(attended, hidden, w_o, vectors, attn[3], attn[7], narrow[0], w_1, b_1, wide[0])


THIRD = D // 3


def down_kernel(activated, middle, w_2, b_2, down_2, up_2, inner, hidden):
    @pl.when(pl.program_id(0) == 0)
    def _():
        inner[...] = dot_t(activated[...], down_2[...]).astype(BF16)

    value = activated[:, :FF]

    hidden[...] = middle[...] + (
        dot(value, matrix(w_2)) + b_2[...] + dot(inner[...], up_2[...])
    )


def down_forward(activated, middle, w_2, b_2, narrow, wide):
    rows = middle.shape[0]
    return pl.pallas_call(
        down_kernel,
        grid=(3,),
        in_specs=[
            whole((rows, WIDE)),
            columns(rows, THIRD),
            pl.BlockSpec(
                (pl.Element(UNITS[3]), pl.Element(3), pl.Element(16), pl.Element(LANES)),
                lambda i: (TILES_AT[3] // 9, 3 * i, 0, 0),
            ),
            columns(1, THIRD),
            whole((R, WIDE)),
            columns(R, THIRD),
        ],
        out_specs=[whole((rows, R)), columns(rows, THIRD)],
        out_shape=[struct((rows, R), BF16), struct((rows, D), F32)],
        name="down_forward",
        **dense_params(2 * rows * D * FF, 8 * rows * D + 2 * rows * FF + 2 * D * FF),
    )(activated, middle, w_2, b_2, wide[1], narrow[1])


def gate_kernel(
    gradient, w_2, gate, down_2, up_1, up_2, inner_down, inner_up, d_gate, g_wide, d_inner_up, g_up_2,
    d_branch, d_inner_down, total,
):
    i = pl.program_id(0)

    @pl.when(i == 0)
    def _():
        value = gradient[...].astype(BF16)
        d_branch[...] = value
        d_inner_down[...] = dot_t(value, up_2[...]).astype(BF16)
        g_up_2[...] = dot_l(inner_down[...], value)
        total[...] = jnp.zeros_like(total)

    left = FF - i * TILE
    down = down_2[...]
    d_act = dot_t(d_branch[...], matrix(w_2)) + dot(d_inner_down[...], down)
    x = gate[...].astype(F32)
    t = gelu_parts(x)
    half = 0.5 * (1.0 + t)
    slope = half + 0.5 * x * (1.0 - t * t) * (
        0.7978845608028654 * (1.0 + 3 * 0.044715 * x * x)
    )
    keep = lax.broadcasted_iota(jnp.int32, (1, TILE), 1) < left
    value = jnp.where(keep, slope * d_act, 0.0).astype(BF16)
    d_gate[...] = value
    total[...] += dot_t(value, up_1[...])
    g_wide[0:R] = dot_l(inner_up[...], value)
    g_wide[R : 2 * R] = dot_l(d_inner_down[...], (x * half).astype(BF16))

    @pl.when(i == pl.num_programs(0) - 1)
    def _():
        d_inner_up[...] = total[...].astype(BF16)


def gate_backward(gradient, w_2, gate, narrow, wide, inner_down, inner_up):
    rows = gradient.shape[0]
    return pl.pallas_call(
        gate_kernel,
        grid=(WIDE // TILE,),
        in_specs=[
            whole((rows, D)),
            unit_block(TILE // 16, 9, lambda i: (TILES_AT[3] // 9 * 16 // TILE + i, 0, 0, 0)),
            columns(rows, TILE),
            columns(R, TILE),
            columns(R, TILE),
            whole((R, D)),
            whole((rows, R)),
            whole((rows, R)),
        ],
        out_specs=[columns(rows, TILE), columns(2 * R, TILE), whole((rows, R)), whole((R, D))],
        out_shape=[
            struct((rows, WIDE), BF16),
            struct((2 * R, WIDE), F32),
            struct((rows, R), BF16),
            struct((R, D), F32),
        ],
        scratch_shapes=[
            pltpu.VMEM((rows, D), BF16),
            pltpu.VMEM((rows, R), BF16),
            pltpu.VMEM((rows, R), F32),
        ],
        name="gate_backward",
        **dense_params(2 * rows * D * FF, 4 * rows * D + 4 * rows * FF + 2 * D * FF),
    )(gradient, w_2, gate, wide[1], wide[0], narrow[1], inner_down, inner_up)


def middle_kernel(
    d_gate, w_1, d_inner_up, down_1, normed, middle, gradient, vec, w_o, down_o, up_o, inner_o, attended,
    d_middle, d_attended, g_rows, d_normed,
):
    i = pl.program_id(0)
    at = pl.ds(pl.multiple_of(i * THIRD, LANES), THIRD)
    d_normed[:, at] = dot_t(d_gate[:, : 34 * LANES], matrix(w_1, 34)) + dot(
        d_inner_up[...], down_1[:, at]
    )

    @pl.when(i == pl.num_programs(0) - 1)
    def _():
        value = gradient[...] + layer_norm_back(d_normed[...], middle[...], vec[2:3])
        d_middle[...] = value
        d_out = value.astype(BF16)
        d_inner_o = dot_t(d_out, up_o[...]).astype(BF16)
        d_attended[...] = (dot_t(d_out, matrix(w_o)) + dot(d_inner_o, down_o[...])).astype(BF16)
        g_rows[0:R] = dot_l(d_inner_o, attended[...])
        g_rows[R : 2 * R] = dot_l(inner_o[...], d_out)
        g_rows[2 * R : 3 * R] = dot_l(d_inner_up[...], normed[...])


def middle_backward(
    d_gate, w_1, d_inner_up, narrow, normed, middle, gradient, vectors, w_o, attn, inner_o, attended
):
    rows = gradient.shape[0]
    return pl.pallas_call(
        middle_kernel,
        grid=(3,),
        in_specs=[
            whole((rows, WIDE)),
            unit_block(THIRD // 16, PANELS[2], lambda i: (3 + i, 0, 0, 0)),
            whole((rows, R)),
            whole((R, D)),
            whole((rows, D)),
            whole((rows, D)),
            whole((rows, D)),
            whole((8, D)),
            OUT_BLOCK,
            whole((R, D)),
            whole((R, D)),
            whole((rows, R)),
            whole((rows, D)),
        ],
        out_specs=[whole((rows, D)), whole((rows, D)), whole((3 * R, D))],
        out_shape=[
            struct((rows, D), F32),
            struct((rows, D), BF16),
            struct((3 * R, D), F32),
        ],
        scratch_shapes=[pltpu.VMEM((rows, D), F32)],
        name="middle_backward",
        **dense_params(2 * rows * D * (D + FF), 18 * rows * D + 2 * rows * FF + 2 * D * (D + FF)),
    )(
        d_gate, w_1, d_inner_up, narrow[0], normed, middle, gradient, vectors, w_o, attn[3], attn[7],
        inner_o, attended,
    )


def input_kernel(
    d_qkv, w_qkv, down, up, normed, inner, hidden, d_middle, vec, gradient, g_rows, d_normed, d_inner
):
    i = pl.program_id(0)

    @pl.when(i == 0)
    def _():
        for c in range(3):
            part = d_qkv[:, c * D : (c + 1) * D]
            d_inner[:, c * R : (c + 1) * R] = dot_t(part, up[c]).astype(BF16)
            g_rows[(3 + c) * R : (4 + c) * R] = dot_l(inner[:, c * R : (c + 1) * R], part)
        g_rows[0 : 3 * R] = dot_l(d_inner[...], normed[...])

    at = pl.ds(pl.multiple_of(i * THIRD, LANES), THIRD)
    d_normed[:, at] = dot_t(d_qkv[...], matrix(w_qkv)) + dot(d_inner[...], down[:, at])

    @pl.when(i == pl.num_programs(0) - 1)
    def _():
        gradient[...] = d_middle[...] + layer_norm_back(d_normed[...], hidden[...], vec[0:1])


def input_backward(d_qkv, w_qkv, attn, normed, inner, hidden, d_middle, vectors):
    rows = hidden.shape[0]
    return pl.pallas_call(
        input_kernel,
        grid=(3,),
        in_specs=[
            whole((rows, 3 * D)),
            unit_block(THIRD // 16, 27, lambda i: (i, 0, 0, 0)),
            whole((3 * R, D)),
            whole((3, R, D)),
            whole((rows, D)),
            whole((rows, 3 * R)),
            whole((rows, D)),
            whole((rows, D)),
            whole((8, D)),
        ],
        out_specs=[whole((rows, D)), whole((6 * R, D))],
        out_shape=[struct((rows, D), F32), struct((6 * R, D), F32)],
        scratch_shapes=[pltpu.VMEM((rows, D), F32), pltpu.VMEM((rows, 3 * R), BF16)],
        name="input_backward",
        **dense_params(6 * rows * D * D, 20 * rows * D + 6 * D * D),
    )(d_qkv, w_qkv, attn[0:3].reshape(3 * R, D), attn[4:7], normed, inner, hidden, d_middle, vectors)


PAIR = 2 * LANES
PAIRS = -(-D // PAIR)
FORWARD_STEPS = (3, H, WIDE // TILE, PAIRS)
FORWARD_AT = (0, 3, 3 + H, 3 + H + WIDE // TILE)
FORWARD_BEGINS = (
    [4.5 * i for i in range(3)]
    + [14 + 2 * i for i in range(H)]
    + [46 + (5 if i else 0) + 2.6 * i for i in range(WIDE // TILE)]
    + [73 + 3 * i for i in range(PAIRS)]
)
CHUNK_TIME = 7.0


def forward_kernel(with_gather, *refs):
    (
        bias_lane, hidden, w_qkv, vec, down, up, w_o, down_o, up_o, down_1, w_1, b_1, up_1, w_2, w_2_odd, b_2,
        down_2, up_2,
    ) = refs[:18]
    refs = refs[18:]
    if with_gather:
        shard, refs = refs[0], refs[1:]
    (
        normed, inner_qkv, qkv, attended, stats, inner_o, middle, normed_two, inner_up, gate, inner_down,
        next_hidden,
    ) = refs[:12]
    refs = refs[12:]
    if with_gather:
        flat, refs = refs[0], refs[1:]
    heads, activated, parts = refs[:3]
    i = pl.program_id(0)
    rows = hidden.shape[0]
    _, att_at, up_at, down_at = FORWARD_AT
    last = down_at + PAIRS - 1

    def at_step(k):
        return pl.when(i == k)

    if with_gather:
        start, events, finish = gather_plan(shard, flat, None, *refs[3:])
        at_step(0)(start)
        steps = [[] for _ in FORWARD_BEGINS]
        late = []
        for when, event in events:
            ready = [k for k, begin in enumerate(FORWARD_BEGINS) if begin >= CHUNK_TIME * when + 4]
            (steps[ready[0]] if ready else late).append(event)
        for k, due in enumerate(steps):
            if due:

                @at_step(k)
                def _(due=due):
                    for event in due:
                        event()

    @pl.when(i < att_at)
    def _():
        @at_step(0)
        def _():
            value = layer_norm(hidden[...], vec[0:1], vec[1:2]).astype(BF16)
            normed[...] = value
            narrow = dot_t(value, down[...]).astype(BF16)
            inner_qkv[...] = narrow
            for part in range(3):
                parts[part] = narrow[:, part * R : (part + 1) * R]
            stats[...] = jnp.zeros_like(stats)

        bias = vec[pl.ds(jnp.where(i == 2, 5, 4), 1), :] * jnp.where(i == 1, 0.0, 1.0)
        value = (dot_both(normed[...], matrix(w_qkv), parts[i], up[0]) + bias).astype(BF16)
        qkv[...] = value
        mark = jnp.where(i == 0, first_lane(rows, F32(1.0)), jnp.where(i == 1, bias_lane[...], jnp.zeros_like(bias_lane[...])))
        for h in range(H):
            heads[i, h] = pad_lanes(value[:, h * HD : (h + 1) * HD], mark)

    @pl.when(jnp.logical_and(i >= att_at, i < up_at))
    def _():
        h = i - att_at
        lane = lax.broadcasted_iota(jnp.int32, (rows, LANES), 1)
        s = dot_t(heads[0, h], heads[1, h])
        m = jnp.max(s, axis=1, keepdims=True)
        p = jnp.exp2((s - m) * C2)
        total = jnp.sum(p, axis=1, keepdims=True)
        o = dot(p.astype(BF16), heads[2, h])
        heads[0, h] = (o * (1.0 / total)).astype(BF16)
        stats[...] = jnp.where(lane == h, m * C2 + jnp.log2(total), stats[...])

    @pl.when(jnp.logical_and(i >= up_at, i < down_at))
    def _():
        t = i - up_at

        @at_step(up_at)
        def _():
            for h in range(H):
                attended[:, h * HD : (h + 1) * HD] = heads[0, h][:, :HD]
            value = attended[...]
            narrow = dot_t(value, down_o[...]).astype(BF16)
            inner_o[...] = narrow
            middle[...] = hidden[...] + (dot_both(value, matrix(w_o), narrow, up_o[...]) + vec[6:7])
            value = layer_norm(middle[...], vec[2:3], vec[3:4]).astype(BF16)
            normed_two[...] = value
            inner_up[...] = dot_t(value, down_1[...]).astype(BF16)

        x = dot_both(normed_two[...], matrix(w_1), inner_up[...], up_1[...]) + b_1[...]
        gate[...] = x.astype(BF16)
        value = (0.5 * x * (1.0 + gelu_parts(x))).astype(BF16)
        activated[:, pl.ds(pl.multiple_of(t * TILE, LANES), TILE)] = value

    @pl.when(i >= down_at)
    def _():
        @at_step(down_at)
        def _():
            w = jnp.concatenate([matrix(w_2.at[: UNITS[3]]), down_2[...].T[:FF]], axis=1)
            value = dot(activated[:, :FF], w)
            narrow = value[:, LANES : LANES + R].astype(BF16)
            inner_down[...] = narrow
            value = value[:, :LANES] + b_2[:, :LANES] + dot(narrow, up_2[:, :LANES])
            next_hidden[:, :LANES] = middle[:, D - LANES :] + value

        @pl.when(i > down_at)
        def _():
            at = pl.ds(pl.multiple_of((i - down_at - 1) * PAIR, LANES), PAIR)
            w = jnp.concatenate([matrix(w.at[: UNITS[3]]) for w in (w_2, w_2_odd)], axis=1)
            value = dot(activated[:, :FF], w) + b_2[...] + dot(inner_down[...], up_2[...])
            next_hidden[...] = middle[:, at] + value

    if with_gather:

        @at_step(last)
        def _():
            for event in late:
                event()
            finish()


def layer_forward(bias, hidden, weights, b_1, shard=None):
    w_qkv, w_o, w_1, w_2, vectors, attn, narrow, wide, _ = weights
    rows = hidden.shape[0]
    _, att_at, up_at, down_at = FORWARD_AT

    def step(i, k):
        return jnp.minimum(jnp.maximum(i - FORWARD_AT[k], 0), FORWARD_STEPS[k] - 1)

    def cols(count, width, k):
        return pl.BlockSpec((count, width), lambda i: (0, step(i, k)))

    def pair(i):
        return jnp.where(step(i, 3) == 0, PAIRS - 1, step(i, 3) - 1)

    def pairs(count):
        return pl.BlockSpec((count, PAIR), lambda i: (0, pair(i)))

    operands = [
        bias, hidden, w_qkv, vectors, attn[0:3].reshape(3 * R, D), attn[4:7], w_o, attn[3], attn[7], narrow[0],
        w_1, b_1, wide[0], w_2, w_2, vectors[7:8], wide[1], narrow[1],
    ]
    in_specs = [
        whole((rows, LANES - HD)),
        whole((rows, D)),
        unit_block(72, 9, lambda i: (0, step(i, 0), 0, 0)),
        whole((8, D)),
        whole((3 * R, D)),
        pl.BlockSpec((1, R, D), lambda i: (step(i, 0), 0, 0)),
        OUT_BLOCK,
        whole((R, D)),
        whole((R, D)),
        whole((R, D)),
        unit_block(72, 4, lambda i: (1, step(i, 2), 0, 0)),
        cols(1, TILE, 2),
        cols(R, TILE, 2),
        unit_block(288, 1, lambda i: (2, 2 * pair(i), 0, 0)),
        unit_block(288, 1, lambda i: (2, jnp.minimum(2 * pair(i) + 1, 8), 0, 0)),
        pairs(1),
        whole((R, WIDE)),
        pairs(R),
    ]
    outs = [
        (whole((rows, D)), struct((rows, D), BF16)),
        (whole((rows, 3 * R)), struct((rows, 3 * R), BF16)),
        (cols(rows, D, 0), struct((rows, 3 * D), BF16)),
        (whole((rows, D)), struct((rows, D), BF16)),
        (whole((rows, LANES)), struct((rows, LANES), F32)),
        (whole((rows, R)), struct((rows, R), BF16)),
        (whole((rows, D)), struct((rows, D), F32)),
        (whole((rows, D)), struct((rows, D), BF16)),
        (whole((rows, R)), struct((rows, R), BF16)),
        (cols(rows, TILE, 2), struct((rows, WIDE), BF16)),
        (whole((rows, R)), struct((rows, R), BF16)),
        (pairs(rows), struct((rows, D), F32)),
    ]
    scratch = [
        pltpu.VMEM((3, H, rows, LANES), BF16),
        pltpu.VMEM((rows, WIDE), BF16),
        pltpu.VMEM((3, rows, R), BF16),
    ]
    params = dict(vmem_limit_bytes=VMEM_MOST)
    if shard is not None:
        operands.append(shard)
        in_specs.append(pl.BlockSpec(memory_space=pl.ANY))
        outs.append(
            (pl.BlockSpec(memory_space=pl.ANY), struct((16 * TILES_HELD, LANES), BF16))
        )
        scratch += gather_semaphores()
        params.update(collective_id=3, has_side_effects=True)
    return pl.pallas_call(
        functools.partial(forward_kernel, shard is not None),
        grid=(sum(FORWARD_STEPS),),
        in_specs=in_specs,
        out_specs=[spec for spec, _ in outs],
        out_shape=[shape for _, shape in outs],
        scratch_shapes=scratch,
        cost_estimate=pl.CostEstimate(
            flops=2 * rows * D * (4 * D + 2 * FF) + 8 * rows * rows * D,
            bytes_accessed=2 * D * (4 * D + 2 * FF) + 30 * rows * D,
            transcendentals=H * rows * rows,
        ),
        compiler_params=pltpu.CompilerParams(**params),
        name="layer_forward_gather" if shard is not None else "layer_forward",
    )(*operands)


def first_gather_kernel(tiles, shard_a, shard_b, gathered, laid_a, laid_b, own, halo, flat, held, turned, *sems):
    own_sem, halo_send, halo_recv = sems[:3]
    f = lax.axis_index("fsdp")
    x = lax.axis_index("seq")
    z = f // 4
    rows = shard_a.shape[0]
    last = lax.axis_size("fsdp") - 1
    margin = 16 * PANELS[2]
    barrier = pltpu.get_barrier_semaphore()
    start, events, finish = gather_plan(laid_a, gathered, None, *sems[3:])

    def greet(to):
        pl.semaphore_signal(barrier, inc=1, device_id=to, device_id_type=MESH)

    y, c = (f // 2) % 2, f % 2
    for to in ((f + 2 - 4 * y, x), (f, 1 - x), (f + 1 - 2 * c, x)):
        greet(to)
    for there, step in ((z < 3, 4), (z > 0, -4), (f < last, 1), (f > 0, -1)):

        @pl.when(there)
        def _(step=step):
            greet((f + step, x))

    expected = 3
    for there in (z < 3, z > 0, f < last, f > 0):
        expected = expected + jnp.where(there, 1, 0)
    pl.semaphore_wait(barrier, expected)

    def halo_copy(layer, side):
        source = (shard_a, shard_b)[layer].at[pl.ds((rows - HALO) * (1 - side), HALO), :]
        return pltpu.make_async_remote_copy(
            src_ref=source,
            dst_ref=halo.at[layer, side],
            send_sem=halo_send.at[layer, side],
            recv_sem=halo_recv.at[layer, side],
            device_id=(f + 1 - 2 * side, x),
            device_id_type=MESH,
        )

    def sends(side):
        return f < last if side == 0 else f > 0

    def takes(side):
        return sends(1 - side)

    for layer in range(2):
        for side in range(2):

            @pl.when(sends(side))
            def _(layer=layer, side=side):
                halo_copy(layer, side).start()

    def lay(layer, source, laid):
        fetch = pltpu.make_async_copy(source, own, own_sem.at[0])
        fetch.start()
        fetch.wait()
        for side in range(2):

            @pl.when(takes(side))
            def _(side=side):
                halo_copy(layer, side).wait_recv()

            @pl.when(jnp.logical_not(takes(side)))
            def _(side=side):
                halo[layer, side] = jnp.zeros((HALO, LANES), BF16)

        lay_rows(f, rows, tiles, halo[layer, 0], own[...], halo[layer, 1], flat, held, turned)
        keep = pltpu.make_async_copy(held.at[pl.ds(margin, 16 * tiles), :], laid, own_sem.at[0])
        keep.start()
        keep.wait()

    lay(0, shard_a, laid_a)
    start(False)
    lay(1, shard_b, laid_b)
    for _, event in events:
        event()
    finish()
    for layer in range(2):
        for side in range(2):

            @pl.when(sends(side))
            def _(layer=layer, side=side):
                halo_copy(layer, side).wait_send()


def first_gather(shards, tiles):
    rows = shards[0].shape[0]
    dma = pltpu.SemaphoreType.DMA
    hbm = pl.BlockSpec(memory_space=pl.ANY)
    laid = jax.ShapeDtypeStruct((16 * tiles, LANES), BF16)
    return pl.pallas_call(
        functools.partial(first_gather_kernel, tiles),
        in_specs=[hbm, hbm],
        out_specs=[hbm, hbm, hbm],
        out_shape=[jax.ShapeDtypeStruct((16 * TILES_HELD, LANES), BF16), laid, laid],
        scratch_shapes=[pltpu.VMEM((rows, LANES), BF16), pltpu.VMEM((2, 2, HALO, LANES), BF16)]
        + lay_scratch(rows, tiles)
        + [dma((1,)), dma((2, 2)), dma((2, 2))]
        + gather_semaphores(),
        compiler_params=pltpu.CompilerParams(
            collective_id=0, has_side_effects=True, vmem_limit_bytes=VMEM_MOST
        ),
        name="first_gather",
    )(*shards)


SHARE = 5
SHARE_ROWS = SHARE * 16


def share_plan(
    adapters, named, terms, names, out, held, totals, sums, local_sem, send, recv, pair_sem
):
    x = lax.axis_index("seq")
    f = lax.axis_index("fsdp")
    count = terms.shape[0]
    me = f * 2 + x
    rows = adapters * SHARE_ROWS

    def device(k):
        return (k // 2, k % 2)

    def share_to(to, slot):
        return pltpu.make_async_remote_copy(
            src_ref=terms.at[to],
            dst_ref=held.at[slot],
            send_sem=send.at[to],
            recv_sem=recv.at[slot],
            device_id=device(to),
            device_id_type=MESH,
        )

    def own():
        return pltpu.make_async_copy(terms.at[me], held.at[me], local_sem.at[0])

    def across(side):
        part = out.at[pl.ds(pl.multiple_of(side * rows, 16), rows), :]
        return pltpu.make_async_remote_copy(
            src_ref=part,
            dst_ref=part,
            send_sem=pair_sem.at[0],
            recv_sem=pair_sem.at[1],
            device_id=(f, 1 - x),
            device_id_type=MESH,
        )

    def start():
        barrier = pltpu.get_barrier_semaphore()

        def greet(k, carry):
            to = (me + k) % count
            pl.semaphore_signal(barrier, inc=1, device_id=device(to), device_id_type=MESH)
            return carry

        lax.fori_loop(1, count, greet, 0)
        pl.semaphore_wait(barrier, count - 1)

        def post(k, carry):
            to = (me + k) % count
            share_to(to, me).start()
            return carry

        lax.fori_loop(1, count, post, 0)
        own().start()

    def add_up():
        totals[...] = jnp.zeros_like(totals)

        def add(slot):
            value = held[slot, :SHARE].reshape(SHARE_ROWS, LANES).astype(F32)
            if named:
                name = names[pl.ds(slot, 1), :]
            else:
                name = held[slot, SHARE].astype(F32)[0:1]
                names[pl.ds(slot, 1), :] = name
            for e in range(adapters):
                totals[e] += jnp.where(name == float(e), value, 0.0)

        own().wait()
        add(me)

        def take(k, carry):
            slot = (me + count - k) % count
            share_to(slot, slot).wait_recv()
            add(slot)
            return carry

        lax.fori_loop(1, count, take, 0)
        sums[...] = totals[...].reshape(rows, LANES).astype(BF16)
        part = out.at[pl.ds(pl.multiple_of(x * rows, 16), rows), :]
        keep = pltpu.make_async_copy(sums, part, local_sem.at[0])
        keep.start()
        keep.wait()
        across(x).start()

    def finish():
        def sent(k, carry):
            to = (me + k) % count
            share_to(to, me).wait_send()
            return carry

        lax.fori_loop(1, count, sent, 0)
        across(x).wait_send()
        across(1 - x).wait_recv()

    return start, add_up, finish


def share_kernel(adapters, *refs):
    for part in share_plan(adapters, True, *refs):
        part()


def share_scratch(count, adapters, tiles):
    dma = pltpu.SemaphoreType.DMA
    rows = adapters * SHARE_ROWS
    return [
        pltpu.VMEM((count, tiles, 16, LANES), BF16),
        pltpu.VMEM((adapters, SHARE_ROWS, LANES), F32),
        pltpu.VMEM((rows, LANES), BF16),
        dma((1,)),
        dma((count,)),
        dma((count,)),
        dma((2,)),
    ]


def share_terms(terms, names, adapters):
    rows = adapters * SHARE_ROWS
    return pl.pallas_call(
        functools.partial(share_kernel, adapters),
        in_specs=[pl.BlockSpec(memory_space=pl.ANY), pl.BlockSpec(memory_space=pltpu.VMEM)],
        out_specs=pl.BlockSpec(memory_space=pl.ANY),
        out_shape=jax.ShapeDtypeStruct((2 * rows, LANES), BF16),
        scratch_shapes=share_scratch(terms.shape[0], adapters, SHARE),
        compiler_params=pltpu.CompilerParams(
            collective_id=1, has_side_effects=True, vmem_limit_bytes=VMEM_LIMIT
        ),
        name="share_terms",
    )(terms, names)


def table_kernel(layers, *refs):
    attn, narrow, wide = refs[layers:]
    for layer in range(layers):
        source = refs[layer]
        for t in range(10 * 9 + 2 * 34):
            tile = source[t // SHARE, 0, t % SHARE].astype(F32)
            if t < 90:
                at = slice(t % 9 * LANES, (t % 9 + 1) * LANES)
                if t < 72:
                    attn[layer, t // 9, 0, :, at] = tile
                else:
                    narrow[layer, t // 9 - 8, 0, :, at] = tile
            else:
                c, p = (t - 90) // 34, (t - 90) % 34
                width = min(LANES, FF - p * LANES)
                wide[layer, c, 0, :, p * LANES : p * LANES + width] = tile[:, :width]


def gradient_tables(gathered, adapters):
    layers = len(gathered)
    count = gathered[0].shape[0] // (adapters * SHARE_ROWS)
    gathered = [g.reshape(count, adapters, SHARE, 16, LANES) for g in gathered]

    def out_block(kinds, width):
        return pl.BlockSpec((layers, kinds, 1, R, width), lambda e: (0, 0, e, 0, 0))

    return pl.pallas_call(
        functools.partial(table_kernel, layers),
        grid=(adapters,),
        in_specs=[pl.BlockSpec((count, 1, SHARE, 16, LANES), lambda e: (0, e, 0, 0, 0))] * layers,
        out_specs=[out_block(8, D), out_block(2, D), out_block(2, FF)],
        out_shape=[
            struct((layers, 8, adapters, R, D), F32),
            struct((layers, 2, adapters, R, D), F32),
            struct((layers, 2, adapters, R, FF), F32),
        ],
        compiler_params=pltpu.CompilerParams(vmem_limit_bytes=VMEM_LIMIT),
        name="gradient_tables",
    )(*gathered)


BACKWARD_STEPS = (WIDE // TILE, PAIRS, 1, H, PAIRS)
BACKWARD_AT = (0, 9, 14, 15, 31)
SHARE_AT, PASS_AT, GATHER_AT = 7, 9, 10


def backward_kernel(adapters, *refs):
    (
        gradient, w_2, gate, down_2, up_2, inner_down, inner_up, w_1, w_1_odd, up_1, down_1, normed_two_in, vec, w_o, down_o,
        up_o, inner_o, attended, bias, stats, w_qkv, w_qkv_odd, up, down, inner_qkv, middle_in, qkv_in, hidden_in, normed_in,
    ) = refs[:29]
    refs = refs[29:]
    if adapters:
        terms, half, refs = refs[0], refs[1], refs[2:]
    new_gradient, g_wide, g_up_2, g_middle, g_input = refs[:5]
    refs = refs[5:]
    if adapters:
        pair, gathered, other_half, names, refs = refs[0], refs[1], refs[2], refs[3], refs[4:]
    (
        d_branch, d_inner_down, d_inner_up, wide, residual, d_normed, heads, stat_t, delta_t, load_sem,
    ) = refs[:10]
    refs = refs[10:]
    i = pl.program_id(0)
    _, middle_at, turn_at, att_at, input_at = BACKWARD_AT
    last = input_at + PAIRS - 1

    def at_step(k):
        return pl.when(i == k)

    def load_middle():
        return pltpu.make_async_copy(middle_in, residual, load_sem.at[0])

    def load_qkv():
        return pltpu.make_async_copy(qkv_in, wide.at[:, : 3 * D], load_sem.at[1])

    def load_hidden():
        return pltpu.make_async_copy(hidden_in, residual, load_sem.at[0])

    def load_normed_two():
        return pltpu.make_async_copy(normed_two_in, d_branch, load_sem.at[2])

    def load_normed():
        return pltpu.make_async_copy(normed_in, d_branch, load_sem.at[2])

    if adapters:
        share_start, share_sum, share_finish = share_plan(
            adapters, False, terms, names, pair, *refs[:7]
        )
        swap_sem = refs[7]
        start, events, finish = gather_plan(pair, gathered, None, *refs[8:])
        swap = pltpu.make_async_remote_copy(
            src_ref=half,
            dst_ref=other_half,
            send_sem=swap_sem.at[0],
            recv_sem=swap_sem.at[1],
            device_id=(lax.axis_index("fsdp"), 1 - lax.axis_index("seq")),
            device_id_type=MESH,
        )
        at_step(0)(share_start)
        at_step(GATHER_AT + 12)(swap.start)
        at_step(SHARE_AT)(share_sum)
        at_step(PASS_AT)(share_finish)

        @at_step(GATHER_AT)
        def _():
            start(False)

        steps = {}
        for when, event in events:
            steps.setdefault(min(GATHER_AT + 1 + int(when), last), []).append(event)
        for k, due in steps.items():

            @at_step(k)
            def _(due=due):
                for event in due:
                    event()

    @pl.when(i < middle_at)
    def _():
        @at_step(0)
        def _():
            load_middle().start()
            value = gradient[...].astype(BF16)
            d_branch[...] = value
            d_inner_down[...] = dot_t(value, up_2[...]).astype(BF16)
            g_up_2[...] = dot_l(inner_down[...], value)

        left = FF - i * TILE
        d_act = dot_both_t(d_branch[...], matrix(w_2), d_inner_down[...], down_2[...].T)
        x = gate[...].astype(F32)
        t = gelu_parts(x)
        half = 0.5 * (1.0 + t)
        slope = half + 0.5 * x * (1.0 - t * t) * (
            0.7978845608028654 * (1.0 + 3 * 0.044715 * x * x)
        )
        keep = lax.broadcasted_iota(jnp.int32, (1, TILE), 1) < left
        value = jnp.where(keep, slope * d_act, 0.0).astype(BF16)
        wide[:, pl.ds(pl.multiple_of(i * TILE, LANES), TILE)] = value
        g_wide[0:R] = dot_l(inner_up[...], value)
        g_wide[R : 2 * R] = dot_l(d_inner_down[...], (x * half).astype(BF16))

    @pl.when(jnp.logical_and(i >= middle_at, i < turn_at))
    def _():
        at_step(middle_at)(load_normed_two().start)

        @pl.when(i < turn_at - 1)
        def _():
            w = jnp.concatenate([matrix(w_1, 34), matrix(w_1_odd, 34)], axis=0)
            d_normed[i - middle_at] = dot_t(wide[:, : 34 * LANES], w)

        @at_step(turn_at - 1)
        def _():
            w = jnp.concatenate([matrix(w_1, 34), up_1[:, : 34 * LANES]], axis=0)
            value = dot_t(wide[:, : 34 * LANES], w)
            d_normed[PAIRS - 1, :, :LANES] = value[:, :LANES]
            d_inner_up[...] = value[:, LANES : LANES + R].astype(BF16)

    def joined():
        parts = [d_normed[k] for k in range(PAIRS - 1)]
        return jnp.concatenate(parts + [d_normed[PAIRS - 1, :, :LANES]], axis=1)

    @at_step(turn_at)
    def _():
        load_qkv().start()
        load_middle().wait()
        d_two = joined() + dot(d_inner_up[...], down_1[...])
        value = gradient[...] + layer_norm_back(d_two, residual[...], vec[2:3])
        load_hidden().start()
        new_gradient[...] = value
        d_out = value.astype(BF16)
        d_inner_o = dot_t(d_out, up_o[...]).astype(BF16)
        wide[:, 3 * D :] = (dot_t(d_out, matrix(w_o)) + dot(d_inner_o, down_o[...])).astype(BF16)
        g_middle[0:R] = dot_l(d_inner_o, attended[...])
        g_middle[R : 2 * R] = dot_l(inner_o[...], d_out)
        load_normed_two().wait()
        g_middle[2 * R : 3 * R] = dot_l(d_inner_up[...], d_branch[...])
        load_normed().start()
        load_qkv().wait()
        rows = gradient.shape[0]
        lane = lax.broadcasted_iota(jnp.int32, (rows, LANES), 1)
        delta = jnp.zeros((rows, LANES), F32)
        marked = (first_lane(rows, F32(1.0)), bias[...], None)
        for h in range(H):
            for c in range(3):
                part = wide[:, c * D + h * HD : c * D + (h + 1) * HD]
                heads[c, h] = pad_lanes(part, marked[c])
            do = wide[:, 3 * D + h * HD : 3 * D + (h + 1) * HD]
            heads[3, h] = pad_lanes(do)
            o = attended[:, h * HD : (h + 1) * HD].astype(F32)
            d = jnp.sum(do.astype(F32) * o, axis=1, keepdims=True)
            delta = jnp.where(lane == h, d, delta)
        stat_t[...] = stats[...].T
        delta_t[...] = delta.T

    @pl.when(jnp.logical_and(i >= att_at, i < input_at))
    def _():
        h = i - att_at
        q, k, do = heads[0, h], heads[1, h], heads[3, h]
        p = jnp.exp2(dot_t(k, q) * C2 - stat_t[pl.ds(h, 1), :])
        dv = dot(p.astype(BF16), do)
        dp = dot_t(heads[2, h], do)
        ds = (p * (dp - delta_t[pl.ds(h, 1), :])).astype(BF16)
        dk = dot(ds, q)
        dq = dot(k.T, ds)
        heads[2, h] = dv.astype(BF16)
        heads[1, h] = (dk * SCALE).astype(BF16)
        heads[0, h] = (dq * SCALE).astype(BF16).T

    @pl.when(i >= input_at)
    def _():
        @at_step(input_at)
        def _():
            load_normed().wait()
            for c in range(3):
                for h in range(H):
                    wide[:, c * D + h * HD : c * D + (h + 1) * HD] = heads[c, h][:, :HD]
            for c in range(3):
                part = wide[:, c * D : (c + 1) * D]
                g_input[(3 + c) * R : (4 + c) * R] = dot_l(inner_qkv[:, c * R : (c + 1) * R], part)

        @pl.when(i < last)
        def _():
            w = jnp.concatenate([matrix(w_qkv), matrix(w_qkv_odd)], axis=0)
            d_normed[i - input_at] = dot_t(wide[:, : 3 * D], w)

        @at_step(last)
        def _():
            w = jnp.concatenate([matrix(w_qkv), up[...]], axis=0)
            value = dot_t(wide[:, : 3 * D], w)
            d_normed[PAIRS - 1, :, :LANES] = value[:, :LANES]
            narrow = value[:, LANES : LANES + 3 * R].astype(BF16)
            g_input[0 : 3 * R] = dot_l(narrow, d_branch[...])
            load_hidden().wait()
            d_one = joined() + dot(narrow, down[...])
            new_gradient[...] += layer_norm_back(d_one, residual[...], vec[0:1])

    if adapters:

        @at_step(last)
        def _():
            finish()
            swap.wait()


def layer_backward(
    gradient, saved, weights, bias, adapters=0, terms=None, half=None
):
    hidden, normed, inner_qkv, qkv, stats, attended, inner_o, middle, normed_two, inner_up, gate, inner_down = saved
    w_qkv, w_o, w_1, w_2, vectors, attn, narrow, wide, up_diagonal = weights
    rows = gradient.shape[0]

    def step(i, k):
        return jnp.minimum(jnp.maximum(i - BACKWARD_AT[k], 0), BACKWARD_STEPS[k] - 1)

    def cols(count, width, k):
        return pl.BlockSpec((count, width), lambda i: (0, step(i, k)))

    hbm = pl.BlockSpec(memory_space=pl.ANY)
    operands = [
        (whole((rows, D)), gradient),
        (unit_block(TILE // 16, 9, lambda i: (TILES_AT[3] // 9 * 16 // TILE + step(i, 0), 0, 0, 0)), w_2),
        (cols(rows, TILE, 0), gate),
        (cols(R, TILE, 0), wide[1]),
        (whole((R, D)), narrow[1]),
        (whole((rows, R)), inner_down),
        (whole((rows, R)), inner_up),
        (unit_block(8, PANELS[2], lambda i: (9 + 2 * step(i, 1), 0, 0, 0)), w_1),
        (unit_block(8, PANELS[2], lambda i: (10 + jnp.minimum(2 * step(i, 1), 7), 0, 0, 0)), w_1),
        (whole((R, WIDE)), wide[0]),
        (whole((R, D)), narrow[0]),
        (hbm, normed_two),
        (whole((8, D)), vectors),
        (OUT_BLOCK, w_o),
        (whole((R, D)), attn[3]),
        (whole((R, D)), attn[7]),
        (whole((rows, R)), inner_o),
        (whole((rows, D)), attended),
        (whole((rows, LANES - HD)), bias),
        (whole((rows, LANES)), stats),
        (unit_block(8, 27, lambda i: (2 * step(i, 4), 0, 0, 0)), w_qkv),
        (unit_block(8, 27, lambda i: (jnp.minimum(2 * step(i, 4) + 1, 8), 0, 0, 0)), w_qkv),
        (whole((3 * R, 3 * D)), up_diagonal),
        (whole((3 * R, D)), attn[0:3].reshape(3 * R, D)),
        (whole((rows, 3 * R)), inner_qkv),
        (hbm, middle),
        (hbm, qkv),
        (hbm, hidden),
        (hbm, normed),
    ]
    outs = [
        (whole((rows, D)), struct((rows, D), F32)),
        (cols(2 * R, TILE, 0), struct((2 * R, WIDE), F32)),
        (whole((R, D)), struct((R, D), F32)),
        (whole((3 * R, D)), struct((3 * R, D), F32)),
        (whole((6 * R, D)), struct((6 * R, D), F32)),
    ]
    scratch = [
        pltpu.VMEM((rows, D), BF16),
        pltpu.VMEM((rows, R), BF16),
        pltpu.VMEM((rows, R), BF16),
        pltpu.VMEM((rows, WIDE), BF16),
        pltpu.VMEM((rows, D), F32),
        pltpu.VMEM((PAIRS, rows, PAIR), F32),
        pltpu.VMEM((4, H, rows, LANES), BF16),
        pltpu.VMEM((LANES, rows), F32),
        pltpu.VMEM((LANES, rows), F32),
        pltpu.SemaphoreType.DMA((3,)),
    ]
    params = dict(vmem_limit_bytes=VMEM_MOST)
    if adapters:
        operands += [(hbm, terms), (hbm, half)]
        block = 2 * adapters * SHARE_ROWS
        outs += [(hbm, struct((block, LANES), BF16)), (hbm, struct((16 * block, LANES), BF16))]
        outs += [(hbm, struct(half.shape, BF16))]
        outs += [(whole((terms.shape[0], LANES)), struct((terms.shape[0], LANES), F32))]
        scratch += share_scratch(terms.shape[0], adapters, SHARE + 1) + [pltpu.SemaphoreType.DMA((2,))]
        scratch += gather_semaphores()
        params.update(collective_id=4, has_side_effects=True)
    return pl.pallas_call(
        functools.partial(backward_kernel, adapters),
        grid=(sum(BACKWARD_STEPS),),
        in_specs=[spec for spec, _ in operands],
        out_specs=[spec for spec, _ in outs],
        out_shape=[shape for _, shape in outs],
        scratch_shapes=scratch,
        cost_estimate=pl.CostEstimate(
            flops=2 * rows * D * (4 * D + 2 * FF) + 20 * rows * rows * D,
            bytes_accessed=2 * D * (4 * D + 2 * FF) + 40 * rows * D,
            transcendentals=H * rows * rows,
        ),
        compiler_params=pltpu.CompilerParams(**params),
        name="layer_backward_share" if adapters else "layer_backward",
    )(*[operand for _, operand in operands])


def prepare_kernel(scalars, attn_in, narrow_in, wide_in, mine, other, attn, narrow, wide, diagonal, bias, hidden):
    length, live, slot = scalars[1], scalars[2], scalars[3]
    attn[...] = attn_in[:, :, 0]
    narrow[...] = narrow_in[:, :, 0]
    wide[...] = jnp.zeros_like(wide)
    wide[:, :, :, :FF] = wide_in[:, :, 0]
    diagonal[...] = jnp.zeros_like(diagonal)
    for layer in range(attn.shape[0]):
        for c in range(3):
            diagonal[layer, c * R : (c + 1) * R, c * D : (c + 1) * D] = attn_in[layer, 4 + c, 0]
    bias[...] = key_bias(bias.shape[0], length)
    half = mine.shape[1]
    row = lax.broadcasted_iota(jnp.int32, (half, 1), 0)

    def place(at, value):
        keep = jnp.where(row + at < length, live, 0) > 0
        hidden[at : at + half] = jnp.where(keep, value.astype(F32), 0.0)

    for first in range(2):

        @pl.when(slot == first)
        def _(first=first):
            place(first * half, mine[0])
            place((1 - first) * half, other[...])


def prepare(scalars, attention_table, narrow_table, wide_table, activations, other):
    layers = attention_table.shape[0]
    rows = 2 * other.shape[0]

    def picked(kinds, width):
        return pl.BlockSpec((layers, kinds, 1, R, width), lambda i, k: (0, 0, k[0], 0, 0))

    def full(*shape):
        return pl.BlockSpec(shape, lambda i, k: (0,) * len(shape))

    shapes = [
        ((layers, 8, R, D), BF16),
        ((layers, 2, R, D), BF16),
        ((layers, 2, R, WIDE), BF16),
        ((layers, 3 * R, 3 * D), BF16),
        ((rows, LANES - HD), BF16),
        ((rows, D), F32),
    ]
    return pl.pallas_call(
        prepare_kernel,
        grid_spec=pltpu.PrefetchScalarGridSpec(
            num_scalar_prefetch=1,
            grid=(1,),
            in_specs=[
                picked(8, D),
                picked(2, D),
                picked(2, FF),
                pl.BlockSpec((1,) + other.shape, lambda i, k: (k[3], 0, 0)),
                full(*other.shape),
            ],
            out_specs=[full(*shape) for shape, _ in shapes],
        ),
        out_shape=[struct(*shape) for shape in shapes],
        compiler_params=pltpu.CompilerParams(vmem_limit_bytes=VMEM_LIMIT),
        name="prepare",
    )(scalars, attention_table, narrow_table, wide_table, activations, other)


def local(
    activations,
    group_image_count,
    image_adapter_index,
    lengths,
    frozen,
    attention_adapter_weights,
    narrow_adapter_weights,
    broad_adapter_weights,
    cotangent,
):
    slots, local_len, _ = activations.shape
    seq_parts = lax.axis_size("seq")
    fsdp_parts = lax.axis_size("fsdp")
    device_count = seq_parts * fsdp_parts
    me = lax.axis_index("seq")
    seq_total = local_len * seq_parts
    layer_count = frozen.shape[0]
    adapters = attention_adapter_weights.shape[2]
    parts = seq_parts // slots
    on_block = (fsdp_parts, seq_parts, slots, layer_count) == (16, 2, 2, 2)
    slot = me // parts
    part = me % parts
    tokens = seq_total // parts
    groups = [[s * parts + p for p in range(parts)] for s in range(slots)]

    def to_image(v):
        if parts == 1 and slots == 2:
            mine = lax.dynamic_index_in_dim(v, slot, 0, keepdims=False)
            other = lax.dynamic_index_in_dim(v, 1 - slot, 0, keepdims=False)
            other = lax.ppermute(other, "seq", [(0, 1), (1, 0)])
            return jnp.where(
                slot == 0,
                jnp.concatenate([mine, other], 0),
                jnp.concatenate([other, mine], 0),
            )
        whole = lax.all_gather(v, "seq", axis=1, tiled=True)
        whole = lax.dynamic_index_in_dim(whole, slot, 0, keepdims=False)
        return lax.dynamic_slice_in_dim(whole, part * tokens, tokens, 0)

    def half_of(v, which):
        return lax.dynamic_slice_in_dim(v, which * local_len, local_len, 0)

    def to_tokens(v, other=None):
        if parts == 1 and slots == 2:
            mine = half_of(v, slot)
            if other is None:
                other = lax.ppermute(half_of(v, 1 - slot), "seq", [(0, 1), (1, 0)])
            return jnp.where(slot == 0, jnp.stack([mine, other]), jnp.stack([other, mine]))
        whole = lax.all_gather(v, "seq", axis=0, tiled=True).reshape(slots, seq_total, -1)
        return lax.dynamic_slice_in_dim(whole, me * local_len, local_len, 1)

    length = lax.dynamic_slice_in_dim(lengths, slot, 1, 0)
    adapter = lax.dynamic_index_in_dim(image_adapter_index, slot, 0, keepdims=False)
    is_live = slot < group_image_count[0]
    positions = part * tokens + jnp.arange(tokens, dtype=jnp.int32)
    row_mask = ((positions < length[0]) & is_live).astype(F32)[:, None]
    shards = lax.optimization_barrier(frozen.reshape(layer_count, -1, LANES))
    tiles = -(-(TILES_END + TILES_VECTORS) // (2 * fsdp_parts)) * 2
    if on_block:
        flat, *shards = first_gather([shards[layer] for layer in range(layer_count)], tiles)
    else:
        steps = [(d, d + 1) for d in range(fsdp_parts - 1)]
        steps = (steps, [(b, a) for a, b in steps])
        index = lax.axis_index("fsdp").astype(jnp.int32).reshape(1)
        shards = [lay_shard(index, shards[layer], tiles, steps) for layer in range(layer_count)]
    if parts == 1 and slots == 2:
        other = lax.dynamic_index_in_dim(activations, 1 - slot, 0, keepdims=False)
        other = lax.ppermute(other, "seq", [(0, 1), (1, 0)])
        scalars = jnp.stack([adapter, length[0], is_live.astype(jnp.int32), slot.astype(jnp.int32)])
        prepared = prepare(
            scalars, attention_adapter_weights, narrow_adapter_weights, broad_adapter_weights, activations, other
        )
        attention_adapters, narrow_adapters, wide_adapters, up_diagonals, bias, hidden = prepared
    else:
        def pick(table):
            return lax.dynamic_index_in_dim(table, adapter, 2, keepdims=False)

        attention_adapters = pick(attention_adapter_weights)
        narrow_adapters = pick(narrow_adapter_weights)
        wide_adapters = pick(broad_adapter_weights)
        wide_adapters = jnp.pad(wide_adapters, ((0, 0), (0, 0), (0, 0), (0, WIDE - FF)))
        lane = lax.broadcasted_iota(jnp.int32, (tokens, LANES - HD), 1)
        key = lax.broadcasted_iota(jnp.int32, (tokens, LANES - HD), 0)
        bias = jnp.where((lane == 0) & (key >= length[0]), NEG, 0.0).astype(BF16)
        hidden = to_image(activations).astype(F32) * row_mask
        up_diagonals = jnp.stack(
            [
                jnp.concatenate(
                    [
                        jnp.pad(attention_adapters[layer, 4 + c], ((0, 0), (c * D, (2 - c) * D)))
                        for c in range(3)
                    ]
                )
                for layer in range(layer_count)
            ]
        )
    stored = []
    weights = []
    for layer in range(layer_count):
        if not on_block:
            flat = lax.all_gather(shards[layer], "fsdp", axis=0, tiled=True)
            flat = jnp.pad(flat, ((0, 16 * TILES_HELD - flat.shape[0]), (0, 0)))
        if layer == layer_count - 1:
            cotangent, flat = lax.optimization_barrier((cotangent, flat))
            d_output = to_image(cotangent)
        w_qkv, w_o, w_1, w_2 = (flat.reshape(-1, panels, 16, LANES) for panels in PANELS)
        vectors = lax.slice_in_dim(flat, 16 * TILES_END, 16 * TILES_END + 106, axis=0).reshape(-1)
        vectors, b_1 = vectors[: 8 * D].reshape(8, D).astype(F32), vectors[8 * D : 8 * D + FF]
        b_1 = jnp.pad(b_1.astype(F32), (0, WIDE - FF))[None, :]
        attn, narrow, wide = attention_adapters[layer], narrow_adapters[layer], wide_adapters[layer]
        weights.append((w_qkv, w_o, w_1, w_2, vectors, attn, narrow, wide, up_diagonals[layer]))
        keys = None
        if parts == 1:
            shard = shards[layer + 1] if on_block and layer + 1 < layer_count else None
            made = layer_forward(bias, hidden, weights[layer], b_1, shard)
            normed, inner_qkv, qkv, attended, stats, inner_o, middle = made[:7]
            normed_two, inner_up, gate, inner_down, next_hidden = made[7:12]
            flat = made[12] if shard is not None else None
        else:
            normed, inner_qkv, qkv = qkv_forward(hidden, w_qkv, vectors, attn)
            keys = lax.all_gather(
                qkv[:, D:], "seq", axis=0, tiled=True, axis_index_groups=groups
            )
            attended, stats = attn_fwd(length, qkv, keys)
            inner_o, middle, normed_two, inner_up, gate, activated = up_forward(
                attended, hidden, w_o, vectors, attn, narrow, w_1, b_1, wide
            )
            inner_down, next_hidden = down_forward(
                activated, middle, w_2, vectors[7:8], narrow, wide
            )
        stored.append(
            (
                hidden,
                normed,
                inner_qkv,
                qkv,
                keys,
                stats,
                attended,
                inner_o,
                middle,
                normed_two,
                inner_up,
                gate,
                inner_down,
            )
        )
        hidden = next_hidden
    output = (hidden * row_mask).astype(BF16)
    other_half = None
    gradient = d_output.astype(F32) * row_mask
    collected = [None] * layer_count
    terms = None
    for layer in reversed(range(layer_count)):
        (
            layer_input,
            normed,
            inner_qkv,
            qkv,
            keys,
            stats,
            attended,
            inner_o,
            middle,
            normed_two,
            inner_up,
            gate,
            inner_down,
        ) = stored[layer]
        w_qkv, w_o, w_1, w_2, vectors, attn, narrow, wide = weights[layer][:8]
        if parts == 1:
            saved = (
                layer_input, normed, inner_qkv, qkv, stats, attended, inner_o, middle, normed_two, inner_up,
                gate, inner_down,
            )
            hosted = terms if on_block and layer + 1 < layer_count else None
            made = layer_backward(
                gradient,
                saved,
                weights[layer],
                bias,
                adapters if hosted is not None else 0,
                hosted,
                half_of(output, 1 - slot),
            )
            gradient, g_wide, g_up_2, g_middle, g_input = made[:5]
            if hosted is not None:
                collected[layer + 1], other_half, names = made[6:9]
        else:
            d_gate, g_wide, d_inner_up, g_up_2 = gate_backward(
                gradient, w_2, gate, narrow, wide, inner_down, inner_up
            )
            d_middle, d_attended, g_middle = middle_backward(
                d_gate, w_1, d_inner_up, narrow, normed_two, middle, gradient, vectors, w_o, attn,
                inner_o, attended,
            )
            d_qkv = attn_bwd(length, qkv, d_attended, attended, stats, keys)
            if parts > 1:
                d_keys = lax.psum_scatter(
                    d_qkv[1].astype(F32),
                    "seq",
                    scatter_dimension=0,
                    tiled=True,
                    axis_index_groups=groups,
                )
                d_qkv = jnp.concatenate([d_qkv[0], d_keys.astype(BF16)], axis=1)
            else:
                d_qkv = d_qkv[0]
            gradient, g_input = input_backward(
                d_qkv, w_qkv, attn, normed, inner_qkv, layer_input, d_middle, vectors
            )
        rows_narrow = jnp.concatenate(
            [
                g_input[: 3 * R],
                g_middle[:R],
                g_input[3 * R :],
                g_middle[R:],
                g_up_2,
            ]
        )
        if on_block:
            terms = jnp.concatenate(
                [
                    rows_narrow.reshape(10, R, 9, LANES).transpose(0, 2, 1, 3).reshape(90, R, LANES),
                    g_wide.reshape(2, R, 36, LANES)
                    .transpose(0, 2, 1, 3)[:, :34]
                    .reshape(68, R, LANES),
                    jnp.zeros((2, R, LANES), F32),
                ]
            )
            terms = terms.astype(BF16).reshape(device_count, SHARE, R, LANES)
            if layer == 0:
                sums = share_terms(terms, names, adapters)
                collected[layer] = gather_blocks(sums, 2, 16 * sums.shape[0])
            else:
                name = jnp.broadcast_to(adapter.astype(BF16), (device_count, 1, R, LANES))
                terms = jnp.concatenate([terms, name], axis=1)
            continue
        rows_narrow = rows_narrow.astype(BF16)
        rows_wide = g_wide[:, :FF].astype(BF16)

        def shares(rows):
            share = -(-rows.shape[0] // device_count)
            rows = jnp.pad(rows, ((0, share * device_count - rows.shape[0]), (0, 0)))
            return rows.reshape(device_count, share * rows.shape[1])

        terms = [shares(rows_narrow), shares(rows_wide)]
        used = terms[0].shape[1] + terms[1].shape[1]
        label = jnp.broadcast_to(adapter.astype(BF16), (device_count, -used % LANES + LANES))
        terms = lax.all_to_all(
            jnp.concatenate(terms + [label], axis=1),
            ("fsdp", "seq"),
            split_axis=0,
            concat_axis=0,
            tiled=True,
        )
        choice = jnp.arange(adapters, dtype=F32)[:, None] == terms[:, used].astype(F32)[None, :]
        sums = jnp.dot(choice.astype(F32), terms.astype(F32), precision=lax.Precision.HIGHEST)
        sums = lax.all_gather(sums.astype(BF16), ("fsdp", "seq")).transpose(1, 0, 2)
        split = -(-10 * R // device_count) * D

        def table(part, count, width):
            part = part.reshape(adapters, -1, width)[:, : count * R]
            return part.reshape(adapters, count, R, width).transpose(1, 0, 2, 3).astype(F32)

        collected[layer] = (table(sums[:, :, :split], 10, D), table(sums[:, :, split:used], 2, FF))
    if on_block:
        grad_attn, grad_narrow, grad_wide = gradient_tables(collected, adapters)
    else:
        grad_attn = jnp.stack([entry[0][0:8] for entry in collected], axis=0)
        grad_narrow = jnp.stack([entry[0][8:10] for entry in collected], axis=0)
        grad_wide = jnp.stack([entry[1] for entry in collected], axis=0)
    output = to_tokens(output, other_half)
    input_grad = to_tokens((gradient * row_mask).astype(BF16)).astype(F32)
    return (output, input_grad, grad_attn, grad_narrow, grad_wide)


def solution(mesh):
    in_specs = (
        P("fsdp", "seq", None),
        P("fsdp"),
        P("fsdp"),
        P("fsdp"),
        P(None, "fsdp"),
        P(),
        P(),
        P(),
        P("fsdp", "seq", None),
    )
    out_specs = (P("fsdp", "seq", None), P("fsdp", "seq", None), P(), P(), P())
    return jax.shard_map(local, mesh=mesh, in_specs=in_specs, out_specs=out_specs, check_vma=False)
```

```python
import functools
import math

import jax
import jax.numpy as jnp
from jax import lax
from jax.experimental import pallas as pl
from jax.experimental.pallas import tpu as pltpu
from jax.sharding import PartitionSpec as P

D = 1152
HD = 72
H = 16
FF = 4304
R = 16
LANES = 128
BF16 = jnp.bfloat16
F32 = jnp.float32
MESH = pl.DeviceIdType.MESH
VMEM_LIMIT = 60 << 20
VMEM_MOST = 67043328
C2 = math.log2(math.e) / math.sqrt(HD)
SCALE = 1.0 / math.sqrt(HD)
NEG = -1e30
epsilon = 1e-06
CUT_OUT = 3 * D * D // LANES
CUT_UP = CUT_OUT + D * D // LANES
CUT_DOWN = CUT_UP + D * FF // LANES
CUT_VECTORS = CUT_DOWN + FF * D // LANES


def dot(a, b):
    return jnp.dot(a, b, preferred_element_type=F32)


def dot_t(a, b):
    return lax.dot_general(a, b, (((1,), (1,)), ((), ())), preferred_element_type=F32)


def dot_l(a, b):
    return lax.dot_general(a, b, (((0,), (0,)), ((), ())), preferred_element_type=F32)


PANELS = (3 * D // LANES, D // LANES, 36, D // LANES)
UNITS = (D // 16, D // 16, D // 16, FF // 16)
TILES_AT = (0, 1944, 2592, 5184)
TILES_END = 7605
TILES_VECTORS = 22
TILES_HELD = 7776
FLAT_AT = (0, CUT_OUT, CUT_UP, CUT_DOWN)
WIDE = PANELS[2] * LANES
UP_ROWS = 16 * FF // LANES
HALO = 1600


def lay_rows(d, own_rows, tiles, before, own, after, flat, held, turned):
    margin = 16 * PANELS[2]
    flat[0:HALO] = before.astype(F32)
    flat[HALO : HALO + own_rows] = own.astype(F32)
    flat[HALO + own_rows : 2 * HALO + own_rows] = after.astype(F32)
    flat_base = d * own_rows - HALO
    tile_base = d * tiles

    def span(at, units, panels):
        low = jnp.maximum(tile_base - at, 0) // panels
        high = jnp.maximum(tile_base + tiles - at + panels - 1, 0) // panels
        high = jnp.minimum(high, units)
        return low, jnp.maximum(high, low)

    for at, start, units, panels in zip(
        TILES_AT + (TILES_END,),
        FLAT_AT + (CUT_VECTORS,),
        UNITS + (TILES_VECTORS,),
        PANELS + (1,),
    ):
        low, high = span(at, units, panels)
        if start == CUT_UP:
            lane = lax.broadcasted_iota(jnp.int32, (8, LANES), 1)

            def up_units(b, carry):
                u = low + 8 * b
                source = pl.multiple_of(start + UP_ROWS * u - flat_base, 2)
                for j in range(16):
                    first, shift = (FF * j) // LANES, (FF * j) % LANES
                    turn = LANES - shift
                    now = flat[pl.ds(source + first, 8, stride=UP_ROWS), :]
                    now = pltpu.roll(now, turn, 1) if shift else now
                    for c in range(34):
                        value = now
                        if c < 33 or shift > LANES - FF % LANES:
                            now = flat[pl.ds(source + first + c + 1, 8, stride=UP_ROWS), :]
                            now = pltpu.roll(now, turn, 1) if shift else now
                            if shift:
                                value = jnp.where(lane < turn, value, now)
                        if c == 33:
                            value = jnp.where(lane < FF - 33 * LANES, value, 0.0)
                        turned[pl.ds(16 * c + j, 8, stride=16 * PANELS[2]), :] = value
                target = pl.multiple_of(16 * (at + PANELS[2] * u - tile_base) + margin, 16)
                held[pl.ds(target, 8 * 16 * PANELS[2]), :] = turned[...].astype(BF16)
                return carry

            turned[...] = jnp.zeros_like(turned)
            lax.fori_loop(0, (high - low + 7) // 8, up_units, 0)
        else:

            def unit(u, carry):
                source = pl.multiple_of(start + 16 * panels * u - flat_base, 16)
                target = pl.multiple_of(16 * (at + panels * u - tile_base) + margin, 16)
                for c in range(panels):
                    value = flat[pl.ds(source + c, 16, stride=panels), :]
                    held[pl.ds(target + 16 * c, 16), :] = value.astype(BF16)
                return carry

            lax.fori_loop(low, high, unit, 0)


def lay_kernel(own_rows, tiles, index_ref, before, own, after, out, flat, held, turned):
    margin = 16 * PANELS[2]
    lay_rows(index_ref[0], own_rows, tiles, before[...], own[...], after[...], flat, held, turned)
    out[...] = held[margin : margin + 16 * tiles]


def lay_scratch(own_rows, tiles):
    margin = 16 * PANELS[2]
    return [
        pltpu.VMEM((own_rows + 2 * HALO + 8 * UP_ROWS, LANES), F32),
        pltpu.VMEM((16 * tiles + 10 * margin, LANES), BF16),
        pltpu.VMEM((8 * margin, LANES), F32),
    ]


def lay_shard(index, shard, tiles, perms):
    own_rows = shard.shape[0]
    before = lax.ppermute(shard[own_rows - HALO :], "fsdp", perms[0])
    after = lax.ppermute(shard[:HALO], "fsdp", perms[1])
    vm = pl.BlockSpec(memory_space=pltpu.VMEM)
    return pl.pallas_call(
        functools.partial(lay_kernel, own_rows, tiles),
        in_specs=[pl.BlockSpec(memory_space=pltpu.SMEM), vm, vm, vm],
        out_specs=vm,
        out_shape=jax.ShapeDtypeStruct((16 * tiles, LANES), BF16),
        scratch_shapes=lay_scratch(own_rows, tiles),
        compiler_params=pltpu.CompilerParams(vmem_limit_bytes=VMEM_LIMIT),
        name="lay_shard",
    )(index, before, shard, after)


def pad_lanes(x, extra=None):
    if extra is None:
        extra = jnp.zeros((x.shape[0], LANES - HD), x.dtype)
    return jnp.concatenate([x, extra], axis=1)


def first_lane(rows, value):
    lane = lax.broadcasted_iota(jnp.int32, (rows, LANES - HD), 1)
    return jnp.where(lane == 0, value, 0.0).astype(BF16)


def key_bias(rows, length):
    key = lax.broadcasted_iota(jnp.int32, (rows, LANES - HD), 0)
    return first_lane(rows, jnp.where(key < length, 0.0, NEG))


def attn_fwd_kernel(offset, len_ref, qkv_ref, kv_ref, o_ref, st_ref, q_s, k_s, v_s):
    if kv_ref is None:
        kv_ref = qkv_ref
    rows, keys = qkv_ref.shape[0], kv_ref.shape[0]
    one = first_lane(rows, F32(1.0))
    bias = key_bias(keys, len_ref[0])
    for h in range(H):
        q_s[h] = pad_lanes(qkv_ref[:, h * HD : (h + 1) * HD], one)
        k_s[h] = pad_lanes(kv_ref[:, offset + h * HD : offset + (h + 1) * HD], bias)
        v_s[h] = pad_lanes(kv_ref[:, offset + D + h * HD : offset + D + (h + 1) * HD])
    st_ref[...] = jnp.zeros_like(st_ref)
    lane = lax.broadcasted_iota(jnp.int32, (rows, LANES), 1)

    def body(h, carry):
        s = dot_t(q_s[h], k_s[h])
        m = jnp.max(s, axis=1, keepdims=True)
        p = jnp.exp2((s - m) * C2)
        total = jnp.sum(p, axis=1, keepdims=True)
        o = dot(p.astype(BF16), v_s[h])
        q_s[h] = (o * (1.0 / total)).astype(BF16)
        st_ref[...] = jnp.where(lane == h, m * C2 + jnp.log2(total), st_ref[...])
        return carry

    lax.fori_loop(0, H, body, 0)
    for h in range(H):
        o_ref[:, h * HD : (h + 1) * HD] = q_s[h][:, :HD]


def attn_fwd(length, qkv, kv=None):
    rows = qkv.shape[0]
    keys = rows if kv is None else kv.shape[0]
    vm = pl.BlockSpec(memory_space=pltpu.VMEM)
    if kv is None:
        kernel = lambda a, b, *rest: attn_fwd_kernel(D, a, b, None, *rest)
        operands = (length, qkv)
    else:
        kernel = functools.partial(attn_fwd_kernel, 0)
        operands = (length, qkv, kv)
    return pl.pallas_call(
        kernel,
        in_specs=[pl.BlockSpec(memory_space=pltpu.SMEM)] + [vm] * (len(operands) - 1),
        out_specs=[vm, vm],
        out_shape=[
            jax.ShapeDtypeStruct((rows, D), BF16),
            jax.ShapeDtypeStruct((rows, LANES), F32),
        ],
        scratch_shapes=[
            pltpu.VMEM((H, rows, LANES), BF16),
            pltpu.VMEM((H, keys, LANES), BF16),
            pltpu.VMEM((H, keys, LANES), BF16),
        ],
        cost_estimate=pl.CostEstimate(
            flops=H * rows * keys * 256 * 4, bytes_accessed=rows * D * 8, transcendentals=H * rows * keys
        ),
        compiler_params=pltpu.CompilerParams(vmem_limit_bytes=VMEM_LIMIT),
        name="attention_forward",
    )(*operands)


def attn_bwd_kernel(
    offset, len_ref, qkv_ref, kv_ref, do_ref, o_ref, st_ref, dq_ref, dkv_ref, q_s, k_s, v_s, do_s, st_t, dl_t
):
    if kv_ref is None:
        kv_ref, dkv_ref = qkv_ref, dq_ref
    rows, keys = qkv_ref.shape[0], kv_ref.shape[0]
    one = first_lane(rows, F32(1.0))
    bias = key_bias(keys, len_ref[0])
    lane = lax.broadcasted_iota(jnp.int32, (rows, LANES), 1)
    delta = jnp.zeros((rows, LANES), F32)
    for h in range(H):
        q_s[h] = pad_lanes(qkv_ref[:, h * HD : (h + 1) * HD], one)
        k_s[h] = pad_lanes(kv_ref[:, offset + h * HD : offset + (h + 1) * HD], bias)
        v_s[h] = pad_lanes(kv_ref[:, offset + D + h * HD : offset + D + (h + 1) * HD])
        do = do_ref[:, h * HD : (h + 1) * HD]
        do_s[h] = pad_lanes(do)
        o = o_ref[:, h * HD : (h + 1) * HD].astype(F32)
        d = jnp.sum(do.astype(F32) * o, axis=1, keepdims=True)
        delta = jnp.where(lane == h, d, delta)
    st_t[...] = st_ref[...].T
    dl_t[...] = delta.T

    def body(h, carry):
        q, k, do = q_s[h], k_s[h], do_s[h]
        p = jnp.exp2(dot_t(k, q) * C2 - st_t[pl.ds(h, 1), :])
        dv = dot(p.astype(BF16), do)
        dp = dot_t(v_s[h], do)
        ds = (p * (dp - dl_t[pl.ds(h, 1), :])).astype(BF16)
        dk = dot(ds, q)
        dq = dot(k.T, ds)
        v_s[h] = dv.astype(BF16)
        k_s[h] = (dk * SCALE).astype(BF16)
        q_s[h] = (dq * SCALE).astype(BF16).T
        return carry

    lax.fori_loop(0, H, body, 0)
    for h in range(H):
        dq_ref[:, h * HD : (h + 1) * HD] = q_s[h][:, :HD]
        dkv_ref[:, offset + h * HD : offset + (h + 1) * HD] = k_s[h][:, :HD]
        dkv_ref[:, offset + D + h * HD : offset + D + (h + 1) * HD] = v_s[h][:, :HD]


def attn_bwd(length, qkv, do, o, st, kv=None):
    rows = qkv.shape[0]
    keys = rows if kv is None else kv.shape[0]
    vm = pl.BlockSpec(memory_space=pltpu.VMEM)
    if kv is None:
        kernel = lambda a, b, c, d, e, f, *rest: attn_bwd_kernel(
            D, a, b, None, c, d, e, f, None, *rest
        )
        operands = (length, qkv, do, o, st)
        outs = [jax.ShapeDtypeStruct((rows, 3 * D), BF16)]
    else:
        kernel = functools.partial(attn_bwd_kernel, 0)
        operands = (length, qkv, kv, do, o, st)
        outs = [jax.ShapeDtypeStruct((rows, D), BF16), jax.ShapeDtypeStruct((keys, 2 * D), BF16)]
    return pl.pallas_call(
        kernel,
        in_specs=[pl.BlockSpec(memory_space=pltpu.SMEM)] + [vm] * (len(operands) - 1),
        out_specs=[vm] * len(outs),
        out_shape=outs,
        scratch_shapes=[
            pltpu.VMEM((H, rows, LANES), BF16),
            pltpu.VMEM((H, keys, LANES), BF16),
            pltpu.VMEM((H, keys, LANES), BF16),
            pltpu.VMEM((H, rows, LANES), BF16),
            pltpu.VMEM((LANES, rows), F32),
            pltpu.VMEM((LANES, rows), F32),
        ],
        cost_estimate=pl.CostEstimate(
            flops=H * rows * keys * 256 * 10, bytes_accessed=rows * D * 16, transcendentals=H * rows * keys
        ),
        compiler_params=pltpu.CompilerParams(vmem_limit_bytes=VMEM_LIMIT),
        name="attention_backward",
    )(*operands)


LARGE_BLOCK = 4096


def gather_plan(
    src, out, stage, local_sem, z_recv, y_recv, b_recv, h_recv, c_recv_own, c_recv_z, c_recv_y, c_recv_b, c_recv_h,
    up_send, down_send, y_send, b_send, h_send, c_send_own, c_send_z, c_send_y, c_send_b, c_send_h,
):
    rows = src.shape[0]
    if rows >= LARGE_BLOCK:
        unit = rows // 6 // 16 * 16 + 16
        sizes = [unit, unit, rows // 2 - 2 * unit, rows // 2 - 2 * unit, unit]
        begins = [0, unit, 2 * unit, rows // 2, rows - 2 * unit]
    else:
        sizes = [rows // 2] * 2
        begins = [0, rows // 2]
    chunks, across_y = len(sizes), (len(sizes) + 1) // 2
    lend = chunks == 5
    x = lax.axis_index("seq")
    f = lax.axis_index("fsdp")
    z, y, c = f // 4, (f // 2) % 2, f % 2

    def place(zb, yb, j, side, cb=None):
        owner = (zb * 2 + yb) * 2 + (c if cb is None else cb)
        begin = jnp.where(side == 0, begins[j], rows - begins[j] - sizes[j])
        return pl.multiple_of(owner * rows + begin, 16), sizes[j]

    def view(spot):
        return out.at[pl.ds(spot[0], spot[1]), :]

    def device(zb, yb, cb, xb):
        return ((zb * 2 + yb) * 2 + cb, xb)

    up, down = device(z + 1, y, c, x), device(z - 1, y, c, x)
    beside, across, mate = device(z, 1 - y, c, x), device(z, y, c, 1 - x), device(z, y, 1 - c, x)

    def copy(spot, send, recv, to, source=None):
        return pltpu.make_async_remote_copy(
            src_ref=view(spot) if source is None else source,
            dst_ref=view(spot),
            send_sem=send,
            recv_sem=recv,
            device_id=to,
            device_id_type=MESH,
        )

    def arrived(spot, recv):
        copy(spot, local_sem.at[1], recv, mate).wait_recv()

    def own(j):
        begin = jnp.where(x == 0, begins[j], rows - begins[j] - sizes[j])
        return src.at[pl.ds(pl.multiple_of(begin, 16), sizes[j]), :]

    whole = (pl.multiple_of(f * rows, 16), rows)
    keep = pltpu.make_async_copy(src if stage is None else stage, view(whole), local_sem.at[0])

    def greet():
        barrier = pltpu.get_barrier_semaphore()
        for to in (beside, across, mate):
            pl.semaphore_signal(barrier, inc=1, device_id=to, device_id_type=MESH)

        @pl.when(z < 3)
        def _():
            pl.semaphore_signal(barrier, inc=1, device_id=up, device_id_type=MESH)

        @pl.when(z > 0)
        def _():
            pl.semaphore_signal(barrier, inc=1, device_id=down, device_id_type=MESH)

        pl.semaphore_wait(barrier, 3 + jnp.where(z < 3, 1, 0) + jnp.where(z > 0, 1, 0))

    def start(first=True):
        if first:
            greet()
        for j in range(chunks):
            spot = place(z, y, j, x)

            @pl.when(z < 3)
            def _():
                copy(spot, up_send.at[z, j], z_recv.at[z, j], up, own(j)).start()

            @pl.when(z > 0)
            def _():
                copy(spot, down_send.at[z, j], z_recv.at[z, j], down, own(j)).start()

            if j < across_y:
                copy(spot, y_send.at[z, j], y_recv.at[z, j], beside, own(j)).start()
        copy(whole, c_send_own.at[0], c_recv_own.at[0], mate, src).start()
        if stage is None:
            keep.start()
        else:
            fetch = pltpu.make_async_copy(src, stage, local_sem.at[0])
            fetch.start()
            fetch.wait()
            keep.start()

    def z_event(d, j):
        def flow(zb, onward, to, sends):
            spot = place(zb, y, j, x)
            arrived(spot, z_recv.at[zb, j])

            @pl.when(onward)
            def _():
                copy(spot, sends.at[zb, j], z_recv.at[zb, j], to).start()

            if j == 0 and lend:
                copy(spot, b_send.at[zb], b_recv.at[zb], across).start()
            if j < across_y:
                copy(spot, y_send.at[zb, j], y_recv.at[zb, j], beside).start()
            copy(spot, c_send_z.at[zb, j], c_recv_z.at[zb, j], mate).start()

        @pl.when(z - d >= 0)
        def _():
            flow(z - d, z < 3, up, up_send)

        @pl.when(z + d <= 3)
        def _():
            flow(z + d, z > 0, down, down_send)

    def each(d, act):
        if d == 0:
            act(z)
            return

        @pl.when(z - d >= 0)
        def _():
            act(z - d)

        @pl.when(z + d <= 3)
        def _():
            act(z + d)

    def y_event(d, j):
        def act(zb):
            spot = place(zb, 1 - y, j, x)
            arrived(spot, y_recv.at[zb, j])
            copy(spot, h_send.at[zb, j], h_recv.at[zb, j], across).start()
            copy(spot, c_send_y.at[zb, j], c_recv_y.at[zb, j], mate).start()

        each(d, act)

    def b_event(d):
        def act(zb):
            spot = place(zb, y, 0, 1 - x)
            arrived(spot, b_recv.at[zb])
            copy(spot, c_send_b.at[zb], c_recv_b.at[zb], mate).start()

        each(d, act)

    def h_event(d, j):
        def act(zb):
            spot = place(zb, 1 - y, j, 1 - x)
            arrived(spot, h_recv.at[zb, j])
            copy(spot, c_send_h.at[zb, j], c_recv_h.at[zb, j], mate).start()

        each(d, act)

    events = []
    for d in range(4):
        for j in range(chunks):
            at = (d - 1) * chunks + j + 1 if d else 0
            if d:
                events.append((at, functools.partial(z_event, d, j)))
                if j == 0 and lend:
                    events.append((at + 2, functools.partial(b_event, d)))
            if j < across_y:
                ready = at + 1.5 if d else j + 1
                events.append((ready, functools.partial(y_event, d, j)))
                events.append((ready + 2, functools.partial(h_event, d, j)))
    def finish():
        keep.wait()
        other = 1 - c

        def core_spot(zb, yb, j, side):
            return place(zb, yb, j, side, other)

        arrived((pl.multiple_of(((z * 2 + y) * 2 + other) * rows, 16), rows), c_recv_own.at[0])
        copy(whole, c_send_own.at[0], c_recv_own.at[0], mate).wait_send()
        for d in range(4):
            def drain(zb, d=d):
                for j in range(chunks):
                    if d:
                        arrived(core_spot(zb, y, j, x), c_recv_z.at[zb, j])
                        copy(place(zb, y, j, x), c_send_z.at[zb, j], c_recv_z.at[zb, j], mate).wait_send()
                    if j < across_y:
                        arrived(core_spot(zb, 1 - y, j, x), c_recv_y.at[zb, j])
                        arrived(core_spot(zb, 1 - y, j, 1 - x), c_recv_h.at[zb, j])
                        spot = place(zb, 1 - y, j, x)
                        copy(spot, c_send_y.at[zb, j], c_recv_y.at[zb, j], mate).wait_send()
                        copy(spot, h_send.at[zb, j], h_recv.at[zb, j], across).wait_send()
                        spot = place(zb, 1 - y, j, 1 - x)
                        copy(spot, c_send_h.at[zb, j], c_recv_h.at[zb, j], mate).wait_send()
                        spot = place(zb, y, j, x)
                        copy(spot, y_send.at[zb, j], y_recv.at[zb, j], beside).wait_send()
                if d and lend:
                    arrived(core_spot(zb, y, 0, 1 - x), c_recv_b.at[zb])
                    spot = place(zb, y, 0, 1 - x)
                    copy(spot, c_send_b.at[zb], c_recv_b.at[zb], mate).wait_send()
                    spot = place(zb, y, 0, x)
                    copy(spot, b_send.at[zb], b_recv.at[zb], across).wait_send()

            each(d, drain)
            for j in range(chunks):
                @pl.when(jnp.logical_and(z - d >= 0, z < 3))
                def _():
                    zb = z - d
                    copy(place(zb, y, j, x), up_send.at[zb, j], z_recv.at[zb, j], up).wait_send()

                @pl.when(jnp.logical_and(z + d <= 3, z > 0))
                def _():
                    zb = z + d
                    copy(place(zb, y, j, x), down_send.at[zb, j], z_recv.at[zb, j], down).wait_send()

    return start, sorted(events, key=lambda e: e[0]), finish


def gather_kernel(*refs):
    start, events, finish = gather_plan(*refs)
    start()
    for _, event in events:
        event()
    finish()


def gather_semaphores():
    dma = pltpu.SemaphoreType.DMA
    core = [dma((1,)), dma((4, 5)), dma((4, 3)), dma((4,)), dma((4, 3))]
    links = [dma((4, 5)), dma((4, 3)), dma((4,)), dma((4, 3))]
    return [dma((2,))] + links + core + [dma((4, 5))] + links + core


def gather_blocks(shard, collective_id, held_rows):
    rows = shard.shape[0]
    return pl.pallas_call(
        gather_kernel,
        in_specs=[pl.BlockSpec(memory_space=pl.ANY)],
        out_specs=pl.BlockSpec(memory_space=pl.ANY),
        out_shape=jax.ShapeDtypeStruct((held_rows, LANES), BF16),
        scratch_shapes=[pltpu.VMEM((rows, LANES), BF16)] + gather_semaphores(),
        compiler_params=pltpu.CompilerParams(collective_id=collective_id, has_side_effects=True, vmem_limit_bytes=VMEM_LIMIT),
        name="gather_blocks",
    )(shard)


def gelu_parts(x):
    inner = 0.7978845608028654 * (x + 0.044715 * x * x * x)
    return jnp.tanh(inner)


def layer_norm(tensor, gain, offset):
    average = jnp.mean(tensor, axis=-1, keepdims=True)
    centred = tensor - average
    variance = jnp.mean(centred * centred, axis=-1, keepdims=True)
    return centred * lax.rsqrt(variance + epsilon) * gain + offset


def layer_norm_back(d_out, tensor, gain):
    average = jnp.mean(tensor, axis=-1, keepdims=True)
    centred = tensor - average
    variance = jnp.mean(centred * centred, axis=-1, keepdims=True)
    scale = lax.rsqrt(variance + epsilon)
    normal = centred * scale
    d_normal = d_out * gain
    mean_d = jnp.mean(d_normal, axis=-1, keepdims=True)
    mean_dn = jnp.mean(d_normal * normal, axis=-1, keepdims=True)
    return (d_normal - mean_d - normal * mean_dn) * scale


def dot_both(x, w, inner, up):
    cut = w.shape[0] // 256 * 256
    tail = dot(
        jnp.concatenate([x[:, cut:], inner], axis=1), jnp.concatenate([w[cut:], up], axis=0)
    )
    return dot(x[:, :cut], w[:cut]) + tail


def dot_both_t(x, w, inner, up_t):
    cut = w.shape[1] // 256 * 256
    tail = dot_t(
        jnp.concatenate([x[:, cut:], inner], axis=1), jnp.concatenate([w[:, cut:], up_t], axis=1)
    )
    return dot_t(x[:, :cut], w[:, :cut]) + tail


def matrix(ref, count=None):
    units, panels = ref.shape[:2]
    return jnp.concatenate(
        [ref[:, p].reshape(units * 16, LANES) for p in range(count or panels)], axis=1
    )


def unit_block(units, panels, place):
    return pl.BlockSpec((units, panels, 16, LANES), place)


def whole(shape):
    return pl.BlockSpec(shape, lambda i: (0,) * len(shape), pipeline_mode=pl.Buffered(1))


def columns(rows, width):
    return pl.BlockSpec((rows, width), lambda i: (0, i))


def struct(shape, dtype):
    return jax.ShapeDtypeStruct(shape, dtype)


def dense_params(flops, bytes_accessed):
    return dict(
        cost_estimate=pl.CostEstimate(
            flops=flops, bytes_accessed=bytes_accessed, transcendentals=0
        ),
        compiler_params=pltpu.CompilerParams(vmem_limit_bytes=VMEM_LIMIT),
    )


def qkv_kernel(hidden, w, vec, down, up, normed, inner, qkv, parts):
    c = pl.program_id(0)

    @pl.when(c == 0)
    def _():
        value = layer_norm(hidden[...], vec[0:1], vec[1:2]).astype(BF16)
        normed[...] = value
        narrow = dot_t(value, down[...]).astype(BF16)
        inner[...] = narrow
        for part in range(3):
            parts[part] = narrow[:, part * R : (part + 1) * R]

    bias = vec[pl.ds(jnp.where(c == 2, 5, 4), 1), :] * jnp.where(c == 1, 0.0, 1.0)
    qkv[...] = (dot_both(normed[...], matrix(w), parts[c], up[0]) + bias).astype(BF16)


def qkv_forward(hidden, w_qkv, vectors, attn):
    rows = hidden.shape[0]
    return pl.pallas_call(
        qkv_kernel,
        grid=(3,),
        in_specs=[
            whole((rows, D)),
            unit_block(72, 9, lambda i: (0, i, 0, 0)),
            whole((8, D)),
            whole((3 * R, D)),
            pl.BlockSpec((1, R, D), lambda i: (i, 0, 0)),
        ],
        out_specs=[whole((rows, D)), whole((rows, 3 * R)), columns(rows, D)],
        out_shape=[
            struct((rows, D), BF16),
            struct((rows, 3 * R), BF16),
            struct((rows, 3 * D), BF16),
        ],
        scratch_shapes=[pltpu.VMEM((3, rows, R), BF16)],
        name="qkv_forward",
        **dense_params(6 * rows * D * D, 14 * rows * D + 6 * D * D),
    )(hidden, w_qkv, vectors, attn[0:3].reshape(3 * R, D), attn[4:7])


TILE = 512
OUT_BLOCK = pl.BlockSpec(
    (72, 9, 16, LANES), lambda i: (3, 0, 0, 0), pipeline_mode=pl.Buffered(1)
)


def up_kernel(
    attended, hidden, w_o, vec, down_o, up_o, down_1, w_1, b_1, up_1,
    inner_o, middle, normed, inner_up, gate, activated,
):
    @pl.when(pl.program_id(0) == 0)
    def _():
        narrow = dot_t(attended[...], down_o[...]).astype(BF16)
        inner_o[...] = narrow
        middle[...] = hidden[...] + (dot_both(attended[...], matrix(w_o), narrow, up_o[...]) + vec[6:7])
        value = layer_norm(middle[...], vec[2:3], vec[3:4]).astype(BF16)
        normed[...] = value
        inner_up[...] = dot_t(value, down_1[...]).astype(BF16)

    x = dot_both(normed[...], matrix(w_1), inner_up[...], up_1[...]) + b_1[...]
    gate[...] = x.astype(BF16)
    activated[...] = (0.5 * x * (1.0 + gelu_parts(x))).astype(BF16)


def up_forward(attended, hidden, w_o, vectors, attn, narrow, w_1, b_1, wide):
    rows = hidden.shape[0]
    return pl.pallas_call(
        up_kernel,
        grid=(WIDE // TILE,),
        in_specs=[
            whole((rows, D)),
            whole((rows, D)),
            OUT_BLOCK,
            whole((8, D)),
            whole((R, D)),
            whole((R, D)),
            whole((R, D)),
            unit_block(72, 4, lambda i: (1, i, 0, 0)),
            columns(1, TILE),
            columns(R, TILE),
        ],
        out_specs=[
            whole((rows, R)),
            whole((rows, D)),
            whole((rows, D)),
            whole((rows, R)),
            columns(rows, TILE),
            columns(rows, TILE),
        ],
        out_shape=[
            struct((rows, R), BF16),
            struct((rows, D), F32),
            struct((rows, D), BF16),
            struct((rows, R), BF16),
            struct((rows, WIDE), BF16),
            struct((rows, WIDE), BF16),
        ],
        name="up_forward",
        **dense_params(2 * rows * D * (D + FF), 12 * rows * D + 4 * rows * FF + 2 * D * (D + FF)),
    )(attended, hidden, w_o, vectors, attn[3], attn[7], narrow[0], w_1, b_1, wide[0])


THIRD = D // 3


def down_kernel(activated, middle, w_2, b_2, down_2, up_2, inner, hidden):
    @pl.when(pl.program_id(0) == 0)
    def _():
        inner[...] = dot_t(activated[...], down_2[...]).astype(BF16)

    value = activated[:, :FF]

    hidden[...] = middle[...] + (
        dot(value, matrix(w_2)) + b_2[...] + dot(inner[...], up_2[...])
    )


def down_forward(activated, middle, w_2, b_2, narrow, wide):
    rows = middle.shape[0]
    return pl.pallas_call(
        down_kernel,
        grid=(3,),
        in_specs=[
            whole((rows, WIDE)),
            columns(rows, THIRD),
            pl.BlockSpec(
                (pl.Element(UNITS[3]), pl.Element(3), pl.Element(16), pl.Element(LANES)),
                lambda i: (TILES_AT[3] // 9, 3 * i, 0, 0),
            ),
            columns(1, THIRD),
            whole((R, WIDE)),
            columns(R, THIRD),
        ],
        out_specs=[whole((rows, R)), columns(rows, THIRD)],
        out_shape=[struct((rows, R), BF16), struct((rows, D), F32)],
        name="down_forward",
        **dense_params(2 * rows * D * FF, 8 * rows * D + 2 * rows * FF + 2 * D * FF),
    )(activated, middle, w_2, b_2, wide[1], narrow[1])


def gate_kernel(
    gradient, w_2, gate, down_2, up_1, up_2, inner_down, inner_up, d_gate, g_wide, d_inner_up, g_up_2,
    d_branch, d_inner_down, total,
):
    i = pl.program_id(0)

    @pl.when(i == 0)
    def _():
        value = gradient[...].astype(BF16)
        d_branch[...] = value
        d_inner_down[...] = dot_t(value, up_2[...]).astype(BF16)
        g_up_2[...] = dot_l(inner_down[...], value)
        total[...] = jnp.zeros_like(total)

    left = FF - i * TILE
    down = down_2[...]
    d_act = dot_t(d_branch[...], matrix(w_2)) + dot(d_inner_down[...], down)
    x = gate[...].astype(F32)
    t = gelu_parts(x)
    half = 0.5 * (1.0 + t)
    slope = half + 0.5 * x * (1.0 - t * t) * (
        0.7978845608028654 * (1.0 + 3 * 0.044715 * x * x)
    )
    keep = lax.broadcasted_iota(jnp.int32, (1, TILE), 1) < left
    value = jnp.where(keep, slope * d_act, 0.0).astype(BF16)
    d_gate[...] = value
    total[...] += dot_t(value, up_1[...])
    g_wide[0:R] = dot_l(inner_up[...], value)
    g_wide[R : 2 * R] = dot_l(d_inner_down[...], (x * half).astype(BF16))

    @pl.when(i == pl.num_programs(0) - 1)
    def _():
        d_inner_up[...] = total[...].astype(BF16)


def gate_backward(gradient, w_2, gate, narrow, wide, inner_down, inner_up):
    rows = gradient.shape[0]
    return pl.pallas_call(
        gate_kernel,
        grid=(WIDE // TILE,),
        in_specs=[
            whole((rows, D)),
            unit_block(TILE // 16, 9, lambda i: (TILES_AT[3] // 9 * 16 // TILE + i, 0, 0, 0)),
            columns(rows, TILE),
            columns(R, TILE),
            columns(R, TILE),
            whole((R, D)),
            whole((rows, R)),
            whole((rows, R)),
        ],
        out_specs=[columns(rows, TILE), columns(2 * R, TILE), whole((rows, R)), whole((R, D))],
        out_shape=[
            struct((rows, WIDE), BF16),
            struct((2 * R, WIDE), F32),
            struct((rows, R), BF16),
            struct((R, D), F32),
        ],
        scratch_shapes=[
            pltpu.VMEM((rows, D), BF16),
            pltpu.VMEM((rows, R), BF16),
            pltpu.VMEM((rows, R), F32),
        ],
        name="gate_backward",
        **dense_params(2 * rows * D * FF, 4 * rows * D + 4 * rows * FF + 2 * D * FF),
    )(gradient, w_2, gate, wide[1], wide[0], narrow[1], inner_down, inner_up)


def middle_kernel(
    d_gate, w_1, d_inner_up, down_1, normed, middle, gradient, vec, w_o, down_o, up_o, inner_o, attended,
    d_middle, d_attended, g_rows, d_normed,
):
    i = pl.program_id(0)
    at = pl.ds(pl.multiple_of(i * THIRD, LANES), THIRD)
    d_normed[:, at] = dot_t(d_gate[:, : 34 * LANES], matrix(w_1, 34)) + dot(
        d_inner_up[...], down_1[:, at]
    )

    @pl.when(i == pl.num_programs(0) - 1)
    def _():
        value = gradient[...] + layer_norm_back(d_normed[...], middle[...], vec[2:3])
        d_middle[...] = value
        d_out = value.astype(BF16)
        d_inner_o = dot_t(d_out, up_o[...]).astype(BF16)
        d_attended[...] = (dot_t(d_out, matrix(w_o)) + dot(d_inner_o, down_o[...])).astype(BF16)
        g_rows[0:R] = dot_l(d_inner_o, attended[...])
        g_rows[R : 2 * R] = dot_l(inner_o[...], d_out)
        g_rows[2 * R : 3 * R] = dot_l(d_inner_up[...], normed[...])


def middle_backward(
    d_gate, w_1, d_inner_up, narrow, normed, middle, gradient, vectors, w_o, attn, inner_o, attended
):
    rows = gradient.shape[0]
    return pl.pallas_call(
        middle_kernel,
        grid=(3,),
        in_specs=[
            whole((rows, WIDE)),
            unit_block(THIRD // 16, PANELS[2], lambda i: (3 + i, 0, 0, 0)),
            whole((rows, R)),
            whole((R, D)),
            whole((rows, D)),
            whole((rows, D)),
            whole((rows, D)),
            whole((8, D)),
            OUT_BLOCK,
            whole((R, D)),
            whole((R, D)),
            whole((rows, R)),
            whole((rows, D)),
        ],
        out_specs=[whole((rows, D)), whole((rows, D)), whole((3 * R, D))],
        out_shape=[
            struct((rows, D), F32),
            struct((rows, D), BF16),
            struct((3 * R, D), F32),
        ],
        scratch_shapes=[pltpu.VMEM((rows, D), F32)],
        name="middle_backward",
        **dense_params(2 * rows * D * (D + FF), 18 * rows * D + 2 * rows * FF + 2 * D * (D + FF)),
    )(
        d_gate, w_1, d_inner_up, narrow[0], normed, middle, gradient, vectors, w_o, attn[3], attn[7],
        inner_o, attended,
    )


def input_kernel(
    d_qkv, w_qkv, down, up, normed, inner, hidden, d_middle, vec, gradient, g_rows, d_normed, d_inner
):
    i = pl.program_id(0)

    @pl.when(i == 0)
    def _():
        for c in range(3):
            part = d_qkv[:, c * D : (c + 1) * D]
            d_inner[:, c * R : (c + 1) * R] = dot_t(part, up[c]).astype(BF16)
            g_rows[(3 + c) * R : (4 + c) * R] = dot_l(inner[:, c * R : (c + 1) * R], part)
        g_rows[0 : 3 * R] = dot_l(d_inner[...], normed[...])

    at = pl.ds(pl.multiple_of(i * THIRD, LANES), THIRD)
    d_normed[:, at] = dot_t(d_qkv[...], matrix(w_qkv)) + dot(d_inner[...], down[:, at])

    @pl.when(i == pl.num_programs(0) - 1)
    def _():
        gradient[...] = d_middle[...] + layer_norm_back(d_normed[...], hidden[...], vec[0:1])


def input_backward(d_qkv, w_qkv, attn, normed, inner, hidden, d_middle, vectors):
    rows = hidden.shape[0]
    return pl.pallas_call(
        input_kernel,
        grid=(3,),
        in_specs=[
            whole((rows, 3 * D)),
            unit_block(THIRD // 16, 27, lambda i: (i, 0, 0, 0)),
            whole((3 * R, D)),
            whole((3, R, D)),
            whole((rows, D)),
            whole((rows, 3 * R)),
            whole((rows, D)),
            whole((rows, D)),
            whole((8, D)),
        ],
        out_specs=[whole((rows, D)), whole((6 * R, D))],
        out_shape=[struct((rows, D), F32), struct((6 * R, D), F32)],
        scratch_shapes=[pltpu.VMEM((rows, D), F32), pltpu.VMEM((rows, 3 * R), BF16)],
        name="input_backward",
        **dense_params(6 * rows * D * D, 20 * rows * D + 6 * D * D),
    )(d_qkv, w_qkv, attn[0:3].reshape(3 * R, D), attn[4:7], normed, inner, hidden, d_middle, vectors)


PAIR = 2 * LANES
PAIRS = -(-D // PAIR)
FORWARD_STEPS = (3, H, WIDE // TILE, PAIRS)
FORWARD_AT = (0, 3, 3 + H, 3 + H + WIDE // TILE)
FORWARD_BEGINS = (
    [4.5 * i for i in range(3)]
    + [14 + 2 * i for i in range(H)]
    + [46 + (5 if i else 0) + 2.6 * i for i in range(WIDE // TILE)]
    + [73 + 3 * i for i in range(PAIRS)]
)
CHUNK_TIME = 7.0


def of_layer(layer, *shape):
    return pl.BlockSpec(
        (1,) + shape, lambda i: (layer,) + (0,) * len(shape), pipeline_mode=pl.Buffered(1)
    )


def forward_kernel(with_gather, *refs):
    (
        bias_lane, hidden, w_qkv, vec, attn, w_o, narrow_in, w_1, b_1, up_1, w_2, w_2_odd, b_2, down_2, up_2,
    ) = refs[:15]
    refs = refs[15:]
    if with_gather:
        shard, refs = refs[0], refs[1:]
    (
        normed, inner_qkv, qkv, attended, stats, inner_o, middle, normed_two, inner_up, gate, inner_down,
        next_hidden,
    ) = refs[:12]
    refs = refs[12:]
    if with_gather:
        flat, refs = refs[0], refs[1:]
    heads, activated, parts = refs[:3]
    i = pl.program_id(0)
    rows = hidden.shape[0]
    _, att_at, up_at, down_at = FORWARD_AT
    last = down_at + PAIRS - 1

    def at_step(k):
        return pl.when(i == k)

    if with_gather:
        start, events, finish = gather_plan(shard, flat, None, *refs[3:])
        at_step(0)(start)
        steps = [[] for _ in FORWARD_BEGINS]
        late = []
        for when, event in events:
            ready = [k for k, begin in enumerate(FORWARD_BEGINS) if begin >= CHUNK_TIME * when + 4]
            (steps[ready[0]] if ready else late).append(event)
        for k, due in enumerate(steps):
            if due:

                @at_step(k)
                def _(due=due):
                    for event in due:
                        event()

    @pl.when(i < att_at)
    def _():
        @at_step(0)
        def _():
            value = layer_norm(hidden[...], vec[0:1], vec[1:2]).astype(BF16)
            normed[...] = value
            narrow = dot_t(value, attn[0, 0:3].reshape(3 * R, D)).astype(BF16)
            inner_qkv[...] = narrow
            for part in range(3):
                parts[part] = narrow[:, part * R : (part + 1) * R]
            stats[...] = jnp.zeros_like(stats)

        bias = vec[pl.ds(jnp.where(i == 2, 5, 4), 1), :] * jnp.where(i == 1, 0.0, 1.0)
        value = (dot_both(normed[...], matrix(w_qkv), parts[i], attn[0, 4 + i]) + bias).astype(BF16)
        qkv[...] = value
        mark = jnp.where(i == 0, first_lane(rows, F32(1.0)), jnp.where(i == 1, bias_lane[...], jnp.zeros_like(bias_lane[...])))
        for h in range(H):
            heads[i, h] = pad_lanes(value[:, h * HD : (h + 1) * HD], mark)

    @pl.when(jnp.logical_and(i >= att_at, i < up_at))
    def _():
        h = i - att_at
        lane = lax.broadcasted_iota(jnp.int32, (rows, LANES), 1)
        s = dot_t(heads[0, h], heads[1, h])
        m = jnp.max(s, axis=1, keepdims=True)
        p = jnp.exp2((s - m) * C2)
        total = jnp.sum(p, axis=1, keepdims=True)
        o = dot(p.astype(BF16), heads[2, h])
        heads[0, h] = (o * (1.0 / total)).astype(BF16)
        stats[...] = jnp.where(lane == h, m * C2 + jnp.log2(total), stats[...])

    @pl.when(jnp.logical_and(i >= up_at, i < down_at))
    def _():
        t = i - up_at

        @at_step(up_at)
        def _():
            for h in range(H):
                attended[:, h * HD : (h + 1) * HD] = heads[0, h][:, :HD]
            value = attended[...]
            narrow = dot_t(value, attn[0, 3]).astype(BF16)
            inner_o[...] = narrow
            middle[...] = hidden[...] + (dot_both(value, matrix(w_o), narrow, attn[0, 7]) + vec[6:7])
            value = layer_norm(middle[...], vec[2:3], vec[3:4]).astype(BF16)
            normed_two[...] = value
            inner_up[...] = dot_t(value, narrow_in[0, 0]).astype(BF16)

        x = dot_both(normed_two[...], matrix(w_1), inner_up[...], up_1[0, 0]) + b_1[...]
        gate[...] = x.astype(BF16)
        value = (0.5 * x * (1.0 + gelu_parts(x))).astype(BF16)
        activated[:, pl.ds(pl.multiple_of(t * TILE, LANES), TILE)] = value

    @pl.when(i >= down_at)
    def _():
        @at_step(down_at)
        def _():
            w = jnp.concatenate([matrix(w_2.at[: UNITS[3]]), down_2[0, 0].T[:FF]], axis=1)
            value = dot(activated[:, :FF], w)
            narrow = value[:, LANES : LANES + R].astype(BF16)
            inner_down[...] = narrow
            value = value[:, :LANES] + b_2[:, :LANES] + dot(narrow, up_2[0, 0, :, :LANES])
            next_hidden[:, :LANES] = middle[:, D - LANES :] + value

        @pl.when(i > down_at)
        def _():
            at = pl.ds(pl.multiple_of((i - down_at - 1) * PAIR, LANES), PAIR)
            w = jnp.concatenate([matrix(w.at[: UNITS[3]]) for w in (w_2, w_2_odd)], axis=1)
            value = dot(activated[:, :FF], w) + b_2[...] + dot(inner_down[...], up_2[0, 0])
            next_hidden[...] = middle[:, at] + value

    if with_gather:

        @at_step(last)
        def _():
            for event in late:
                event()
            finish()


def layer_forward(layer, bias, hidden, weights, tables, shard=None):
    w_qkv, w_o, w_1, w_2, vectors, b_1 = weights
    attn, narrow, wide, _ = tables
    rows = hidden.shape[0]
    _, att_at, up_at, down_at = FORWARD_AT

    def step(i, k):
        return jnp.minimum(jnp.maximum(i - FORWARD_AT[k], 0), FORWARD_STEPS[k] - 1)

    def cols(count, width, k):
        return pl.BlockSpec((count, width), lambda i: (0, step(i, k)))

    def pair(i):
        return jnp.where(step(i, 3) == 0, PAIRS - 1, step(i, 3) - 1)

    def pairs(count):
        return pl.BlockSpec((count, PAIR), lambda i: (0, pair(i)))

    operands = [
        bias, hidden, w_qkv, vectors, attn, w_o, narrow, w_1, b_1, wide, w_2, w_2, vectors[7:8], wide, narrow,
    ]
    in_specs = [
        whole((rows, LANES - HD)),
        whole((rows, D)),
        unit_block(72, 9, lambda i: (0, step(i, 0), 0, 0)),
        whole((8, D)),
        of_layer(layer, 8, R, D),
        OUT_BLOCK,
        of_layer(layer, 2, R, D),
        unit_block(72, 4, lambda i: (1, step(i, 2), 0, 0)),
        cols(1, TILE, 2),
        pl.BlockSpec((1, 1, R, TILE), lambda i: (layer, 0, 0, step(i, 2))),
        unit_block(288, 1, lambda i: (2, 2 * pair(i), 0, 0)),
        unit_block(288, 1, lambda i: (2, jnp.minimum(2 * pair(i) + 1, 8), 0, 0)),
        pairs(1),
        pl.BlockSpec((1, 1, R, WIDE), lambda i: (layer, 1, 0, 0), pipeline_mode=pl.Buffered(1)),
        pl.BlockSpec((1, 1, R, PAIR), lambda i: (layer, 1, 0, pair(i))),
    ]
    outs = [
        (whole((rows, D)), struct((rows, D), BF16)),
        (whole((rows, 3 * R)), struct((rows, 3 * R), BF16)),
        (cols(rows, D, 0), struct((rows, 3 * D), BF16)),
        (whole((rows, D)), struct((rows, D), BF16)),
        (whole((rows, LANES)), struct((rows, LANES), F32)),
        (whole((rows, R)), struct((rows, R), BF16)),
        (whole((rows, D)), struct((rows, D), F32)),
        (whole((rows, D)), struct((rows, D), BF16)),
        (whole((rows, R)), struct((rows, R), BF16)),
        (cols(rows, TILE, 2), struct((rows, WIDE), BF16)),
        (whole((rows, R)), struct((rows, R), BF16)),
        (pairs(rows), struct((rows, D), F32)),
    ]
    scratch = [
        pltpu.VMEM((3, H, rows, LANES), BF16),
        pltpu.VMEM((rows, WIDE), BF16),
        pltpu.VMEM((3, rows, R), BF16),
    ]
    params = dict(vmem_limit_bytes=VMEM_MOST)
    if shard is not None:
        operands.append(shard)
        in_specs.append(pl.BlockSpec(memory_space=pl.ANY))
        outs.append(
            (pl.BlockSpec(memory_space=pl.ANY), struct((16 * TILES_HELD, LANES), BF16))
        )
        scratch += gather_semaphores()
        params.update(collective_id=3, has_side_effects=True)
    return pl.pallas_call(
        functools.partial(forward_kernel, shard is not None),
        grid=(sum(FORWARD_STEPS),),
        in_specs=in_specs,
        out_specs=[spec for spec, _ in outs],
        out_shape=[shape for _, shape in outs],
        scratch_shapes=scratch,
        cost_estimate=pl.CostEstimate(
            flops=2 * rows * D * (4 * D + 2 * FF) + 8 * rows * rows * D,
            bytes_accessed=2 * D * (4 * D + 2 * FF) + 30 * rows * D,
            transcendentals=H * rows * rows,
        ),
        compiler_params=pltpu.CompilerParams(**params),
        name="layer_forward_gather" if shard is not None else "layer_forward",
    )(*operands)


def first_gather_kernel(tiles, shard_a, shard_b, gathered, laid_a, laid_b, own, halo, flat, held, turned, *sems):
    own_sem, halo_send, halo_recv = sems[:3]
    f = lax.axis_index("fsdp")
    x = lax.axis_index("seq")
    z = f // 4
    rows = shard_a.shape[0]
    last = lax.axis_size("fsdp") - 1
    margin = 16 * PANELS[2]
    barrier = pltpu.get_barrier_semaphore()
    start, events, finish = gather_plan(laid_a, gathered, None, *sems[3:])

    def greet(to):
        pl.semaphore_signal(barrier, inc=1, device_id=to, device_id_type=MESH)

    y, c = (f // 2) % 2, f % 2
    for to in ((f + 2 - 4 * y, x), (f, 1 - x), (f + 1 - 2 * c, x)):
        greet(to)
    for there, step in ((z < 3, 4), (z > 0, -4), (f < last, 1), (f > 0, -1)):

        @pl.when(there)
        def _(step=step):
            greet((f + step, x))

    expected = 3
    for there in (z < 3, z > 0, f < last, f > 0):
        expected = expected + jnp.where(there, 1, 0)
    pl.semaphore_wait(barrier, expected)

    def halo_copy(layer, side):
        source = (shard_a, shard_b)[layer].at[pl.ds((rows - HALO) * (1 - side), HALO), :]
        return pltpu.make_async_remote_copy(
            src_ref=source,
            dst_ref=halo.at[layer, side],
            send_sem=halo_send.at[layer, side],
            recv_sem=halo_recv.at[layer, side],
            device_id=(f + 1 - 2 * side, x),
            device_id_type=MESH,
        )

    def sends(side):
        return f < last if side == 0 else f > 0

    def takes(side):
        return sends(1 - side)

    for layer in range(2):
        for side in range(2):

            @pl.when(sends(side))
            def _(layer=layer, side=side):
                halo_copy(layer, side).start()

    def lay(layer, source, laid):
        fetch = pltpu.make_async_copy(source, own, own_sem.at[0])
        fetch.start()
        fetch.wait()
        for side in range(2):

            @pl.when(takes(side))
            def _(side=side):
                halo_copy(layer, side).wait_recv()

            @pl.when(jnp.logical_not(takes(side)))
            def _(side=side):
                halo[layer, side] = jnp.zeros((HALO, LANES), BF16)

        lay_rows(f, rows, tiles, halo[layer, 0], own[...], halo[layer, 1], flat, held, turned)
        keep = pltpu.make_async_copy(held.at[pl.ds(margin, 16 * tiles), :], laid, own_sem.at[0])
        keep.start()
        keep.wait()

    lay(0, shard_a, laid_a)
    start(False)
    lay(1, shard_b, laid_b)
    for _, event in events:
        event()
    finish()
    for layer in range(2):
        for side in range(2):

            @pl.when(sends(side))
            def _(layer=layer, side=side):
                halo_copy(layer, side).wait_send()


def first_gather(shards, tiles):
    rows = shards[0].shape[0]
    dma = pltpu.SemaphoreType.DMA
    hbm = pl.BlockSpec(memory_space=pl.ANY)
    laid = jax.ShapeDtypeStruct((16 * tiles, LANES), BF16)
    return pl.pallas_call(
        functools.partial(first_gather_kernel, tiles),
        in_specs=[hbm, hbm],
        out_specs=[hbm, hbm, hbm],
        out_shape=[jax.ShapeDtypeStruct((16 * TILES_HELD, LANES), BF16), laid, laid],
        scratch_shapes=[pltpu.VMEM((rows, LANES), BF16), pltpu.VMEM((2, 2, HALO, LANES), BF16)]
        + lay_scratch(rows, tiles)
        + [dma((1,)), dma((2, 2)), dma((2, 2))]
        + gather_semaphores(),
        compiler_params=pltpu.CompilerParams(
            collective_id=0, has_side_effects=True, vmem_limit_bytes=VMEM_MOST
        ),
        name="first_gather",
    )(*shards)


SHARE = 5
SHARE_ROWS = SHARE * 16


def share_plan(
    adapters, named, terms, names, out, held, totals, sums, local_sem, send, recv, pair_sem
):
    x = lax.axis_index("seq")
    f = lax.axis_index("fsdp")
    count = terms.shape[0]
    me = f * 2 + x
    rows = adapters * SHARE_ROWS

    def device(k):
        return (k // 2, k % 2)

    def share_to(to, slot):
        return pltpu.make_async_remote_copy(
            src_ref=terms.at[to],
            dst_ref=held.at[slot],
            send_sem=send.at[to],
            recv_sem=recv.at[slot],
            device_id=device(to),
            device_id_type=MESH,
        )

    def own():
        return pltpu.make_async_copy(terms.at[me], held.at[me], local_sem.at[0])

    def across(side):
        part = out.at[pl.ds(pl.multiple_of(side * rows, 16), rows), :]
        return pltpu.make_async_remote_copy(
            src_ref=part,
            dst_ref=part,
            send_sem=pair_sem.at[0],
            recv_sem=pair_sem.at[1],
            device_id=(f, 1 - x),
            device_id_type=MESH,
        )

    def start():
        barrier = pltpu.get_barrier_semaphore()

        def greet(k, carry):
            to = (me + k) % count
            pl.semaphore_signal(barrier, inc=1, device_id=device(to), device_id_type=MESH)
            return carry

        lax.fori_loop(1, count, greet, 0)
        pl.semaphore_wait(barrier, count - 1)

        def post(k, carry):
            to = (me + k) % count
            share_to(to, me).start()
            return carry

        lax.fori_loop(1, count, post, 0)
        own().start()

    def add_up():
        totals[...] = jnp.zeros_like(totals)

        def add(slot):
            value = held[slot, :SHARE].reshape(SHARE_ROWS, LANES).astype(F32)
            if named:
                name = names[pl.ds(slot, 1), :]
            else:
                name = held[slot, SHARE].astype(F32)[0:1]
                names[pl.ds(slot, 1), :] = name
            for e in range(adapters):
                totals[e] += jnp.where(name == float(e), value, 0.0)

        own().wait()
        add(me)

        def take(k, carry):
            slot = (me + count - k) % count
            share_to(slot, slot).wait_recv()
            add(slot)
            return carry

        lax.fori_loop(1, count, take, 0)
        sums[...] = totals[...].reshape(rows, LANES).astype(BF16)
        part = out.at[pl.ds(pl.multiple_of(x * rows, 16), rows), :]
        keep = pltpu.make_async_copy(sums, part, local_sem.at[0])
        keep.start()
        keep.wait()
        across(x).start()

    def finish():
        def sent(k, carry):
            to = (me + k) % count
            share_to(to, me).wait_send()
            return carry

        lax.fori_loop(1, count, sent, 0)
        across(x).wait_send()
        across(1 - x).wait_recv()

    return start, add_up, finish


def share_kernel(adapters, *refs):
    for part in share_plan(adapters, True, *refs):
        part()


def share_scratch(count, adapters, tiles):
    dma = pltpu.SemaphoreType.DMA
    rows = adapters * SHARE_ROWS
    return [
        pltpu.VMEM((count, tiles, 16, LANES), BF16),
        pltpu.VMEM((adapters, SHARE_ROWS, LANES), F32),
        pltpu.VMEM((rows, LANES), BF16),
        dma((1,)),
        dma((count,)),
        dma((count,)),
        dma((2,)),
    ]


def share_terms(terms, names, adapters):
    rows = adapters * SHARE_ROWS
    return pl.pallas_call(
        functools.partial(share_kernel, adapters),
        in_specs=[pl.BlockSpec(memory_space=pl.ANY), pl.BlockSpec(memory_space=pltpu.VMEM)],
        out_specs=pl.BlockSpec(memory_space=pl.ANY),
        out_shape=jax.ShapeDtypeStruct((2 * rows, LANES), BF16),
        scratch_shapes=share_scratch(terms.shape[0], adapters, SHARE),
        compiler_params=pltpu.CompilerParams(
            collective_id=1, has_side_effects=True, vmem_limit_bytes=VMEM_LIMIT
        ),
        name="share_terms",
    )(terms, names)


def table_kernel(layers, *refs):
    attn, narrow, wide = refs[layers:]
    for layer in range(layers):
        source = refs[layer]
        for t in range(10 * 9 + 2 * 34):
            tile = source[t // SHARE, 0, t % SHARE].astype(F32)
            if t < 90:
                at = slice(t % 9 * LANES, (t % 9 + 1) * LANES)
                if t < 72:
                    attn[layer, t // 9, 0, :, at] = tile
                else:
                    narrow[layer, t // 9 - 8, 0, :, at] = tile
            else:
                c, p = (t - 90) // 34, (t - 90) % 34
                width = min(LANES, FF - p * LANES)
                wide[layer, c, 0, :, p * LANES : p * LANES + width] = tile[:, :width]


def gradient_tables(gathered, adapters):
    layers = len(gathered)
    count = gathered[0].shape[0] // (adapters * SHARE_ROWS)
    gathered = [g.reshape(count, adapters, SHARE, 16, LANES) for g in gathered]

    def out_block(kinds, width):
        return pl.BlockSpec((layers, kinds, 1, R, width), lambda e: (0, 0, e, 0, 0))

    return pl.pallas_call(
        functools.partial(table_kernel, layers),
        grid=(adapters,),
        in_specs=[pl.BlockSpec((count, 1, SHARE, 16, LANES), lambda e: (0, e, 0, 0, 0))] * layers,
        out_specs=[out_block(8, D), out_block(2, D), out_block(2, FF)],
        out_shape=[
            struct((layers, 8, adapters, R, D), F32),
            struct((layers, 2, adapters, R, D), F32),
            struct((layers, 2, adapters, R, FF), F32),
        ],
        compiler_params=pltpu.CompilerParams(vmem_limit_bytes=VMEM_LIMIT),
        name="gradient_tables",
    )(*gathered)


BACKWARD_STEPS = (WIDE // TILE, PAIRS, 1, H, PAIRS)
BACKWARD_AT = (0, 9, 14, 15, 31)
SHARE_AT, PASS_AT, GATHER_AT = 7, 9, 10


def backward_kernel(adapters, spread, *refs):
    (
        gradient, w_2, gate, down_2, inner_down, inner_up, w_1, w_1_odd, up_1, narrow, normed_two_in, vec, w_o, attn,
        label, inner_o, attended, bias, stats, w_qkv, w_qkv_odd, up, inner_qkv, middle_in, qkv_in, hidden_in, normed_in,
    ) = refs[:27]
    refs = refs[27:]
    if adapters:
        terms, half, refs = refs[0], refs[1], refs[2:]
    new_gradient, new_terms = refs[:2]
    refs = refs[2:]
    if adapters:
        pair, gathered, other_half, names, refs = refs[0], refs[1], refs[2], refs[3], refs[4:]
    (
        d_branch, d_inner_down, d_inner_up, wide, residual, d_normed, heads, stat_t, delta_t, load_sem,
    ) = refs[:10]
    refs = refs[10:]
    i = pl.program_id(0)
    _, middle_at, turn_at, att_at, input_at = BACKWARD_AT
    last = input_at + PAIRS - 1

    def at_step(k):
        return pl.when(i == k)

    def place(t):
        return t if spread == SHARE else t // SHARE * spread + t % SHARE

    def put(table, value):
        for p in range(D // LANES):
            tile = value[:, p * LANES : (p + 1) * LANES]
            new_terms[place(table * (D // LANES) + p)] = tile.astype(BF16)

    def load_middle():
        return pltpu.make_async_copy(middle_in, residual, load_sem.at[0])

    def load_qkv():
        return pltpu.make_async_copy(qkv_in, wide.at[:, : 3 * D], load_sem.at[1])

    def load_hidden():
        return pltpu.make_async_copy(hidden_in, residual, load_sem.at[0])

    def load_normed_two():
        return pltpu.make_async_copy(normed_two_in, d_branch, load_sem.at[2])

    def load_normed():
        return pltpu.make_async_copy(normed_in, d_branch, load_sem.at[2])

    if adapters:
        share_start, share_sum, share_finish = share_plan(
            adapters, False, terms, names, pair, *refs[:7]
        )
        swap_sem = refs[7]
        start, events, finish = gather_plan(pair, gathered, None, *refs[8:])
        swap = pltpu.make_async_remote_copy(
            src_ref=half,
            dst_ref=other_half,
            send_sem=swap_sem.at[0],
            recv_sem=swap_sem.at[1],
            device_id=(lax.axis_index("fsdp"), 1 - lax.axis_index("seq")),
            device_id_type=MESH,
        )
        at_step(0)(share_start)
        at_step(GATHER_AT + 12)(swap.start)
        at_step(SHARE_AT)(share_sum)
        at_step(PASS_AT)(share_finish)

        @at_step(GATHER_AT)
        def _():
            start(False)

        steps = {}
        for when, event in events:
            steps.setdefault(min(GATHER_AT + 1 + int(when), last), []).append(event)
        for k, due in steps.items():

            @at_step(k)
            def _(due=due):
                for event in due:
                    event()

    @pl.when(i < middle_at)
    def _():
        @at_step(0)
        def _():
            load_middle().start()
            value = gradient[...].astype(BF16)
            d_branch[...] = value
            d_inner_down[...] = dot_t(value, narrow[0, 1]).astype(BF16)
            put(9, dot_l(inner_down[...], value))
            for t in (158, 159):
                new_terms[place(t)] = jnp.zeros((R, LANES), BF16)
            if spread > SHARE:
                for k in range(SHARE, new_terms.shape[0], spread):
                    new_terms[k] = label[...]

        left = FF - i * TILE
        d_act = dot_both_t(d_branch[...], matrix(w_2), d_inner_down[...], down_2[0, 0].T)
        x = gate[...].astype(F32)
        t = gelu_parts(x)
        half = 0.5 * (1.0 + t)
        slope = half + 0.5 * x * (1.0 - t * t) * (
            0.7978845608028654 * (1.0 + 3 * 0.044715 * x * x)
        )
        keep = lax.broadcasted_iota(jnp.int32, (1, TILE), 1) < left
        value = jnp.where(keep, slope * d_act, 0.0).astype(BF16)
        wide[:, pl.ds(pl.multiple_of(i * TILE, LANES), TILE)] = value
        made = (
            dot_l(inner_up[...], value).astype(BF16),
            dot_l(d_inner_down[...], (x * half).astype(BF16)).astype(BF16),
        )

        def put_wide(panels):
            for kind in range(2):
                for p in panels:
                    tile = made[kind][:, p * LANES : (p + 1) * LANES]
                    new_terms[place(90 + 34 * kind + 4 * i + p)] = tile

        put_wide(range(2))

        @pl.when(i < middle_at - 1)
        def _():
            put_wide(range(2, 4))


    @pl.when(jnp.logical_and(i >= middle_at, i < turn_at))
    def _():
        at_step(middle_at)(load_normed_two().start)

        @pl.when(i < turn_at - 1)
        def _():
            w = jnp.concatenate([matrix(w_1, 34), matrix(w_1_odd, 34)], axis=0)
            d_normed[i - middle_at] = dot_t(wide[:, : 34 * LANES], w)

        @at_step(turn_at - 1)
        def _():
            w = jnp.concatenate([matrix(w_1, 34), up_1[0, 0, :, : 34 * LANES]], axis=0)
            value = dot_t(wide[:, : 34 * LANES], w)
            d_normed[PAIRS - 1, :, :LANES] = value[:, :LANES]
            d_inner_up[...] = value[:, LANES : LANES + R].astype(BF16)

    def joined():
        parts = [d_normed[k] for k in range(PAIRS - 1)]
        return jnp.concatenate(parts + [d_normed[PAIRS - 1, :, :LANES]], axis=1)

    @at_step(turn_at)
    def _():
        load_qkv().start()
        load_middle().wait()
        d_two = joined() + dot(d_inner_up[...], narrow[0, 0])
        value = gradient[...] + layer_norm_back(d_two, residual[...], vec[2:3])
        load_hidden().start()
        new_gradient[...] = value
        d_out = value.astype(BF16)
        d_inner_o = dot_t(d_out, attn[0, 7]).astype(BF16)
        wide[:, 3 * D :] = (dot_t(d_out, matrix(w_o)) + dot(d_inner_o, attn[0, 3])).astype(BF16)
        put(3, dot_l(d_inner_o, attended[...]))
        put(7, dot_l(inner_o[...], d_out))
        load_normed_two().wait()
        put(8, dot_l(d_inner_up[...], d_branch[...]))
        load_normed().start()
        load_qkv().wait()
        rows = gradient.shape[0]
        lane = lax.broadcasted_iota(jnp.int32, (rows, LANES), 1)
        delta = jnp.zeros((rows, LANES), F32)
        marked = (first_lane(rows, F32(1.0)), bias[...], None)
        for h in range(H):
            for c in range(3):
                part = wide[:, c * D + h * HD : c * D + (h + 1) * HD]
                heads[c, h] = pad_lanes(part, marked[c])
            do = wide[:, 3 * D + h * HD : 3 * D + (h + 1) * HD]
            heads[3, h] = pad_lanes(do)
            o = attended[:, h * HD : (h + 1) * HD].astype(F32)
            d = jnp.sum(do.astype(F32) * o, axis=1, keepdims=True)
            delta = jnp.where(lane == h, d, delta)
        stat_t[...] = stats[...].T
        delta_t[...] = delta.T

    @pl.when(jnp.logical_and(i >= att_at, i < input_at))
    def _():
        h = i - att_at
        q, k, do = heads[0, h], heads[1, h], heads[3, h]
        p = jnp.exp2(dot_t(k, q) * C2 - stat_t[pl.ds(h, 1), :])
        dv = dot(p.astype(BF16), do)
        dp = dot_t(heads[2, h], do)
        ds = (p * (dp - delta_t[pl.ds(h, 1), :])).astype(BF16)
        dk = dot(ds, q)
        dq = dot(k.T, ds)
        heads[2, h] = dv.astype(BF16)
        heads[1, h] = (dk * SCALE).astype(BF16)
        heads[0, h] = (dq * SCALE).astype(BF16).T

    @pl.when(i >= input_at)
    def _():
        @at_step(input_at)
        def _():
            load_normed().wait()
            for c in range(3):
                for h in range(H):
                    wide[:, c * D + h * HD : c * D + (h + 1) * HD] = heads[c, h][:, :HD]
            for c in range(3):
                part = wide[:, c * D : (c + 1) * D]
                put(4 + c, dot_l(inner_qkv[:, c * R : (c + 1) * R], part))

        @pl.when(i < last)
        def _():
            w = jnp.concatenate([matrix(w_qkv), matrix(w_qkv_odd)], axis=0)
            d_normed[i - input_at] = dot_t(wide[:, : 3 * D], w)

        @at_step(last)
        def _():
            w = jnp.concatenate([matrix(w_qkv), up[0]], axis=0)
            value = dot_t(wide[:, : 3 * D], w)
            d_normed[PAIRS - 1, :, :LANES] = value[:, :LANES]
            inner = value[:, LANES : LANES + 3 * R].astype(BF16)
            made = dot_l(inner, d_branch[...])
            for c in range(3):
                put(c, made[c * R : (c + 1) * R])
            load_hidden().wait()
            d_one = joined() + dot(inner, attn[0, 0:3].reshape(3 * R, D))
            new_gradient[...] += layer_norm_back(d_one, residual[...], vec[0:1])

    if adapters:

        @at_step(last)
        def _():
            finish()
            swap.wait()


def layer_backward(
    layer, gradient, saved, weights, tables, bias, label, spread, adapters=0, terms=None, half=None
):
    hidden, normed, inner_qkv, qkv, stats, attended, inner_o, middle, normed_two, inner_up, gate, inner_down = saved
    w_qkv, w_o, w_1, w_2, vectors, _ = weights
    attn, narrow, wide, up_diagonal = tables
    rows = gradient.shape[0]

    def step(i, k):
        return jnp.minimum(jnp.maximum(i - BACKWARD_AT[k], 0), BACKWARD_STEPS[k] - 1)

    def cols(count, width, k):
        return pl.BlockSpec((count, width), lambda i: (0, step(i, k)))

    hbm = pl.BlockSpec(memory_space=pl.ANY)
    operands = [
        (whole((rows, D)), gradient),
        (unit_block(TILE // 16, 9, lambda i: (TILES_AT[3] // 9 * 16 // TILE + step(i, 0), 0, 0, 0)), w_2),
        (cols(rows, TILE, 0), gate),
        (pl.BlockSpec((1, 1, R, TILE), lambda i: (layer, 1, 0, step(i, 0))), wide),
        (whole((rows, R)), inner_down),
        (whole((rows, R)), inner_up),
        (unit_block(8, PANELS[2], lambda i: (9 + 2 * step(i, 1), 0, 0, 0)), w_1),
        (unit_block(8, PANELS[2], lambda i: (10 + jnp.minimum(2 * step(i, 1), 7), 0, 0, 0)), w_1),
        (of_layer(layer, 1, R, WIDE), wide),
        (of_layer(layer, 2, R, D), narrow),
        (hbm, normed_two),
        (whole((8, D)), vectors),
        (OUT_BLOCK, w_o),
        (of_layer(layer, 8, R, D), attn),
        (whole((R, LANES)), label),
        (whole((rows, R)), inner_o),
        (whole((rows, D)), attended),
        (whole((rows, LANES - HD)), bias),
        (whole((rows, LANES)), stats),
        (unit_block(8, 27, lambda i: (2 * step(i, 4), 0, 0, 0)), w_qkv),
        (unit_block(8, 27, lambda i: (jnp.minimum(2 * step(i, 4) + 1, 8), 0, 0, 0)), w_qkv),
        (of_layer(layer, 3 * R, 3 * D), up_diagonal),
        (whole((rows, 3 * R)), inner_qkv),
        (hbm, middle),
        (hbm, qkv),
        (hbm, hidden),
        (hbm, normed),
    ]
    outs = [
        (whole((rows, D)), struct((rows, D), F32)),
        (whole((32 * spread, R, LANES)), struct((32 * spread, R, LANES), BF16)),
    ]
    scratch = [
        pltpu.VMEM((rows, D), BF16),
        pltpu.VMEM((rows, R), BF16),
        pltpu.VMEM((rows, R), BF16),
        pltpu.VMEM((rows, WIDE), BF16),
        pltpu.VMEM((rows, D), F32),
        pltpu.VMEM((PAIRS, rows, PAIR), F32),
        pltpu.VMEM((4, H, rows, LANES), BF16),
        pltpu.VMEM((LANES, rows), F32),
        pltpu.VMEM((LANES, rows), F32),
        pltpu.SemaphoreType.DMA((3,)),
    ]
    params = dict(vmem_limit_bytes=VMEM_MOST)
    if adapters:
        operands += [(hbm, terms), (hbm, half)]
        block = 2 * adapters * SHARE_ROWS
        outs += [(hbm, struct((block, LANES), BF16)), (hbm, struct((16 * block, LANES), BF16))]
        outs += [(hbm, struct(half.shape, BF16))]
        outs += [(whole((terms.shape[0], LANES)), struct((terms.shape[0], LANES), F32))]
        scratch += share_scratch(terms.shape[0], adapters, SHARE + 1) + [pltpu.SemaphoreType.DMA((2,))]
        scratch += gather_semaphores()
        params.update(collective_id=4, has_side_effects=True)
    return pl.pallas_call(
        functools.partial(backward_kernel, adapters, spread),
        grid=(sum(BACKWARD_STEPS),),
        in_specs=[spec for spec, _ in operands],
        out_specs=[spec for spec, _ in outs],
        out_shape=[shape for _, shape in outs],
        scratch_shapes=scratch,
        cost_estimate=pl.CostEstimate(
            flops=2 * rows * D * (4 * D + 2 * FF) + 20 * rows * rows * D,
            bytes_accessed=2 * D * (4 * D + 2 * FF) + 40 * rows * D,
            transcendentals=H * rows * rows,
        ),
        compiler_params=pltpu.CompilerParams(**params),
        name="layer_backward_share" if adapters else "layer_backward",
    )(*[operand for _, operand in operands])


VECTOR_ROWS = 240


def read_vectors(block, vectors, b_1, rows):
    rows[...] = block[...].astype(F32)
    for p in range(D // LANES):
        vectors[:, p * LANES : (p + 1) * LANES] = rows[pl.ds(p, 8, stride=D // LANES), :]
    b_1[...] = jnp.zeros_like(b_1)
    first = 8 * D // LANES
    for p in range(-(-FF // LANES)):
        width = min(LANES, FF - p * LANES)
        b_1[:, p * LANES : p * LANES + width] = rows[first + p : first + p + 1, :width]


def layer_vectors(flat):
    return pl.pallas_call(
        read_vectors,
        grid=(1,),
        in_specs=[pl.BlockSpec((VECTOR_ROWS, LANES), lambda i: (16 * TILES_END // VECTOR_ROWS, 0))],
        out_specs=[whole((8, D)), whole((1, WIDE))],
        out_shape=[struct((8, D), F32), struct((1, WIDE), F32)],
        scratch_shapes=[pltpu.VMEM((VECTOR_ROWS, LANES), F32)],
        name="layer_vectors",
    )(flat)


def prepare_kernel(
    scalars, attn_in, narrow_in, wide_in, mine, other, block, attn, narrow, wide, diagonal, bias, hidden, label,
    vectors, b_1, rows,
):
    slot = scalars[5]
    length, live = scalars[2 + slot], jnp.where(slot < scalars[4], 1, 0)
    read_vectors(block, vectors, b_1, rows)
    label[...] = jnp.full(label.shape, scalars[slot], jnp.int32).astype(F32).astype(BF16)
    attn[...] = attn_in[:, :, 0]
    narrow[...] = narrow_in[:, :, 0]
    wide[...] = jnp.zeros_like(wide)
    wide[:, :, :, :FF] = wide_in[:, :, 0]
    diagonal[...] = jnp.zeros_like(diagonal)
    for layer in range(attn.shape[0]):
        for c in range(3):
            diagonal[layer, c * R : (c + 1) * R, c * D : (c + 1) * D] = attn_in[layer, 4 + c, 0]
    bias[...] = key_bias(bias.shape[0], length)
    half = mine.shape[1]
    row = lax.broadcasted_iota(jnp.int32, (half, 1), 0)

    def place(at, value):
        keep = jnp.where(row + at < length, live, 0) > 0
        hidden[at : at + half] = jnp.where(keep, value.astype(F32), 0.0)

    for first in range(2):

        @pl.when(slot == first)
        def _(first=first):
            place(first * half, mine[0])
            place((1 - first) * half, other[...])


def prepare(scalars, attention_table, narrow_table, wide_table, activations, other, flat):
    layers = attention_table.shape[0]
    rows = 2 * other.shape[0]

    def picked(kinds, width):
        return pl.BlockSpec((layers, kinds, 1, R, width), lambda i, k: (0, 0, k[k[5]], 0, 0))

    def full(*shape):
        return pl.BlockSpec(shape, lambda i, k: (0,) * len(shape))

    shapes = [
        ((layers, 8, R, D), BF16),
        ((layers, 2, R, D), BF16),
        ((layers, 2, R, WIDE), BF16),
        ((layers, 3 * R, 3 * D), BF16),
        ((rows, LANES - HD), BF16),
        ((rows, D), F32),
        ((R, LANES), BF16),
        ((8, D), F32),
        ((1, WIDE), F32),
    ]
    return pl.pallas_call(
        prepare_kernel,
        grid_spec=pltpu.PrefetchScalarGridSpec(
            num_scalar_prefetch=1,
            grid=(1,),
            in_specs=[
                picked(8, D),
                picked(2, D),
                picked(2, FF),
                pl.BlockSpec((1,) + other.shape, lambda i, k: (k[5], 0, 0)),
                full(*other.shape),
                pl.BlockSpec((VECTOR_ROWS, LANES), lambda i, k: (16 * TILES_END // VECTOR_ROWS, 0)),
            ],
            out_specs=[full(*shape) for shape, _ in shapes],
            scratch_shapes=[pltpu.VMEM((VECTOR_ROWS, LANES), F32)],
        ),
        out_shape=[struct(*shape) for shape in shapes],
        compiler_params=pltpu.CompilerParams(vmem_limit_bytes=VMEM_LIMIT),
        name="prepare",
    )(scalars, attention_table, narrow_table, wide_table, activations, other, flat)


def local(
    activations,
    group_image_count,
    image_adapter_index,
    lengths,
    frozen,
    attention_adapter_weights,
    narrow_adapter_weights,
    broad_adapter_weights,
    cotangent,
):
    slots, local_len, _ = activations.shape
    seq_parts = lax.axis_size("seq")
    fsdp_parts = lax.axis_size("fsdp")
    device_count = seq_parts * fsdp_parts
    me = lax.axis_index("seq")
    seq_total = local_len * seq_parts
    layer_count = frozen.shape[0]
    adapters = attention_adapter_weights.shape[2]
    parts = seq_parts // slots
    on_block = (fsdp_parts, seq_parts, slots, layer_count) == (16, 2, 2, 2)
    slot = me // parts
    part = me % parts
    tokens = seq_total // parts
    groups = [[s * parts + p for p in range(parts)] for s in range(slots)]

    def to_image(v):
        if parts == 1 and slots == 2:
            mine = lax.dynamic_index_in_dim(v, slot, 0, keepdims=False)
            other = lax.dynamic_index_in_dim(v, 1 - slot, 0, keepdims=False)
            other = lax.ppermute(other, "seq", [(0, 1), (1, 0)])
            return jnp.where(
                slot == 0,
                jnp.concatenate([mine, other], 0),
                jnp.concatenate([other, mine], 0),
            )
        whole = lax.all_gather(v, "seq", axis=1, tiled=True)
        whole = lax.dynamic_index_in_dim(whole, slot, 0, keepdims=False)
        return lax.dynamic_slice_in_dim(whole, part * tokens, tokens, 0)

    def half_of(v, which):
        return lax.dynamic_slice_in_dim(v, which * local_len, local_len, 0)

    def to_tokens(v, other=None):
        if parts == 1 and slots == 2:
            mine = half_of(v, slot)
            if other is None:
                other = lax.ppermute(half_of(v, 1 - slot), "seq", [(0, 1), (1, 0)])
            return jnp.where(slot == 0, jnp.stack([mine, other]), jnp.stack([other, mine]))
        whole = lax.all_gather(v, "seq", axis=0, tiled=True).reshape(slots, seq_total, -1)
        return lax.dynamic_slice_in_dim(whole, me * local_len, local_len, 1)

    length = lax.dynamic_slice_in_dim(lengths, slot, 1, 0)
    adapter = lax.dynamic_index_in_dim(image_adapter_index, slot, 0, keepdims=False)
    is_live = slot < group_image_count[0]
    positions = part * tokens + jnp.arange(tokens, dtype=jnp.int32)
    row_mask = ((positions < length[0]) & is_live).astype(F32)[:, None]
    shards = lax.optimization_barrier(frozen.reshape(layer_count, -1, LANES))
    tiles = -(-(TILES_END + TILES_VECTORS) // (2 * fsdp_parts)) * 2
    if on_block:
        flat, *shards = first_gather([shards[layer] for layer in range(layer_count)], tiles)
    else:
        steps = [(d, d + 1) for d in range(fsdp_parts - 1)]
        steps = (steps, [(b, a) for a, b in steps])
        index = lax.axis_index("fsdp").astype(jnp.int32).reshape(1)
        shards = [lay_shard(index, shards[layer], tiles, steps) for layer in range(layer_count)]
    if on_block:
        other = lax.dynamic_index_in_dim(activations, 1 - slot, 0, keepdims=False)
        other = lax.ppermute(other, "seq", [(0, 1), (1, 0)])
        scalars = jnp.concatenate(
            [image_adapter_index, lengths, group_image_count, slot.astype(jnp.int32)[None]]
        )
        prepared = prepare(
            scalars,
            attention_adapter_weights,
            narrow_adapter_weights,
            broad_adapter_weights,
            activations,
            other,
            flat,
        )
        tables, (bias, hidden, label) = prepared[:4], prepared[4:7]
    else:
        def pick(table):
            return lax.dynamic_index_in_dim(table, adapter, 2, keepdims=False)

        attention_adapters = pick(attention_adapter_weights)
        narrow_adapters = pick(narrow_adapter_weights)
        wide_adapters = pick(broad_adapter_weights)
        wide_adapters = jnp.pad(wide_adapters, ((0, 0), (0, 0), (0, 0), (0, WIDE - FF)))
        lane = lax.broadcasted_iota(jnp.int32, (tokens, LANES - HD), 1)
        key = lax.broadcasted_iota(jnp.int32, (tokens, LANES - HD), 0)
        bias = jnp.where((lane == 0) & (key >= length[0]), NEG, 0.0).astype(BF16)
        hidden = to_image(activations).astype(F32) * row_mask
        up_diagonals = jnp.stack(
            [
                jnp.concatenate(
                    [
                        jnp.pad(attention_adapters[layer, 4 + c], ((0, 0), (c * D, (2 - c) * D)))
                        for c in range(3)
                    ]
                )
                for layer in range(layer_count)
            ]
        )
    stored = []
    weights = []
    for layer in range(layer_count):
        if not on_block:
            flat = lax.all_gather(shards[layer], "fsdp", axis=0, tiled=True)
            flat = jnp.pad(flat, ((0, 16 * TILES_HELD - flat.shape[0]), (0, 0)))
        if layer == layer_count - 1:
            cotangent, flat = lax.optimization_barrier((cotangent, flat))
            d_output = to_image(cotangent)
        w_qkv, w_o, w_1, w_2 = (flat.reshape(-1, panels, 16, LANES) for panels in PANELS)
        if on_block:
            vectors, b_1 = prepared[7:9] if layer == 0 else layer_vectors(flat)
            weights.append((w_qkv, w_o, w_1, w_2, vectors, b_1))
        else:
            vectors = lax.slice_in_dim(flat, 16 * TILES_END, 16 * TILES_END + 106, axis=0).reshape(-1)
            vectors, b_1 = vectors[: 8 * D].reshape(8, D).astype(F32), vectors[8 * D : 8 * D + FF]
            b_1 = jnp.pad(b_1.astype(F32), (0, WIDE - FF))[None, :]
            attn, narrow, wide = attention_adapters[layer], narrow_adapters[layer], wide_adapters[layer]
            weights.append((w_qkv, w_o, w_1, w_2, vectors, attn, narrow, wide))
        keys = None
        if on_block:
            shard = shards[layer + 1] if layer + 1 < layer_count else None
            made = layer_forward(layer, bias, hidden, weights[layer], tables, shard)
            normed, inner_qkv, qkv, attended, stats, inner_o, middle = made[:7]
            normed_two, inner_up, gate, inner_down, next_hidden = made[7:12]
            flat = made[12] if shard is not None else None
        else:
            normed, inner_qkv, qkv = qkv_forward(hidden, w_qkv, vectors, attn)
            keys = lax.all_gather(
                qkv[:, D:], "seq", axis=0, tiled=True, axis_index_groups=groups
            )
            attended, stats = attn_fwd(length, qkv, keys)
            inner_o, middle, normed_two, inner_up, gate, activated = up_forward(
                attended, hidden, w_o, vectors, attn, narrow, w_1, b_1, wide
            )
            inner_down, next_hidden = down_forward(
                activated, middle, w_2, vectors[7:8], narrow, wide
            )
        stored.append(
            (
                hidden,
                normed,
                inner_qkv,
                qkv,
                keys,
                stats,
                attended,
                inner_o,
                middle,
                normed_two,
                inner_up,
                gate,
                inner_down,
            )
        )
        hidden = next_hidden
    output = (hidden * row_mask).astype(BF16)
    other_half = None
    gradient = d_output.astype(F32) * row_mask
    collected = [None] * layer_count
    terms = None
    for layer in reversed(range(layer_count)):
        (
            layer_input,
            normed,
            inner_qkv,
            qkv,
            keys,
            stats,
            attended,
            inner_o,
            middle,
            normed_two,
            inner_up,
            gate,
            inner_down,
        ) = stored[layer]
        if not on_block:
            w_qkv, w_o, w_1, w_2, vectors, attn, narrow, wide = weights[layer]
        if on_block:
            saved = (
                layer_input, normed, inner_qkv, qkv, stats, attended, inner_o, middle, normed_two, inner_up,
                gate, inner_down,
            )
            hosting = layer + 1 < layer_count
            spread = SHARE if layer == 0 else SHARE + 1
            made = layer_backward(
                layer,
                gradient,
                saved,
                weights[layer],
                tables,
                bias,
                label,
                spread,
                adapters if hosting else 0,
                terms,
                half_of(output, 1 - slot),
            )
            gradient, terms = made[:2]
            terms = terms.reshape(device_count, spread, R, LANES)
            if hosting:
                collected[layer + 1], other_half, names = made[3:6]
            if layer == 0:
                sums = share_terms(terms, names, adapters)
                collected[layer] = gather_blocks(sums, 2, 16 * sums.shape[0])
            continue
        if True:
            d_gate, g_wide, d_inner_up, g_up_2 = gate_backward(
                gradient, w_2, gate, narrow, wide, inner_down, inner_up
            )
            d_middle, d_attended, g_middle = middle_backward(
                d_gate, w_1, d_inner_up, narrow, normed_two, middle, gradient, vectors, w_o, attn,
                inner_o, attended,
            )
            d_qkv = attn_bwd(length, qkv, d_attended, attended, stats, keys)
            if parts > 1:
                d_keys = lax.psum_scatter(
                    d_qkv[1].astype(F32),
                    "seq",
                    scatter_dimension=0,
                    tiled=True,
                    axis_index_groups=groups,
                )
                d_qkv = jnp.concatenate([d_qkv[0], d_keys.astype(BF16)], axis=1)
            else:
                d_qkv = d_qkv[0]
            gradient, g_input = input_backward(
                d_qkv, w_qkv, attn, normed, inner_qkv, layer_input, d_middle, vectors
            )
        rows_narrow = jnp.concatenate(
            [
                g_input[: 3 * R],
                g_middle[:R],
                g_input[3 * R :],
                g_middle[R:],
                g_up_2,
            ]
        )
        rows_narrow = rows_narrow.astype(BF16)
        rows_wide = g_wide[:, :FF].astype(BF16)

        def shares(rows):
            share = -(-rows.shape[0] // device_count)
            rows = jnp.pad(rows, ((0, share * device_count - rows.shape[0]), (0, 0)))
            return rows.reshape(device_count, share * rows.shape[1])

        terms = [shares(rows_narrow), shares(rows_wide)]
        used = terms[0].shape[1] + terms[1].shape[1]
        label = jnp.broadcast_to(adapter.astype(BF16), (device_count, -used % LANES + LANES))
        terms = lax.all_to_all(
            jnp.concatenate(terms + [label], axis=1),
            ("fsdp", "seq"),
            split_axis=0,
            concat_axis=0,
            tiled=True,
        )
        choice = jnp.arange(adapters, dtype=F32)[:, None] == terms[:, used].astype(F32)[None, :]
        sums = jnp.dot(choice.astype(F32), terms.astype(F32), precision=lax.Precision.HIGHEST)
        sums = lax.all_gather(sums.astype(BF16), ("fsdp", "seq")).transpose(1, 0, 2)
        split = -(-10 * R // device_count) * D

        def table(part, count, width):
            part = part.reshape(adapters, -1, width)[:, : count * R]
            return part.reshape(adapters, count, R, width).transpose(1, 0, 2, 3).astype(F32)

        collected[layer] = (table(sums[:, :, :split], 10, D), table(sums[:, :, split:used], 2, FF))
    if on_block:
        grad_attn, grad_narrow, grad_wide = gradient_tables(collected, adapters)
    else:
        grad_attn = jnp.stack([entry[0][0:8] for entry in collected], axis=0)
        grad_narrow = jnp.stack([entry[0][8:10] for entry in collected], axis=0)
        grad_wide = jnp.stack([entry[1] for entry in collected], axis=0)
    output = to_tokens(output, other_half)
    input_grad = to_tokens((gradient * row_mask).astype(BF16)).astype(F32)
    return (output, input_grad, grad_attn, grad_narrow, grad_wide)


def solution(mesh):
    in_specs = (
        P("fsdp", "seq", None),
        P("fsdp"),
        P("fsdp"),
        P("fsdp"),
        P(None, "fsdp"),
        P(),
        P(),
        P(),
        P("fsdp", "seq", None),
    )
    out_specs = (P("fsdp", "seq", None), P("fsdp", "seq", None), P(), P(), P())
    return jax.shard_map(local, mesh=mesh, in_specs=in_specs, out_specs=out_specs, check_vma=False)
```

```python
import functools
import math

import jax
import jax.numpy as jnp
from jax import lax
from jax.experimental import pallas as pl
from jax.experimental.pallas import tpu as pltpu
from jax.sharding import PartitionSpec as P

D = 1152
HD = 72
H = 16
FF = 4304
R = 16
LANES = 128
BF16 = jnp.bfloat16
F32 = jnp.float32
MESH = pl.DeviceIdType.MESH
VMEM_LIMIT = 60 << 20
VMEM_MOST = 67043328
C2 = math.log2(math.e) / math.sqrt(HD)
SCALE = 1.0 / math.sqrt(HD)
NEG = -1e30
epsilon = 1e-06
CUT_OUT = 3 * D * D // LANES
CUT_UP = CUT_OUT + D * D // LANES
CUT_DOWN = CUT_UP + D * FF // LANES
CUT_VECTORS = CUT_DOWN + FF * D // LANES


def dot(a, b):
    return jnp.dot(a, b, preferred_element_type=F32)


def dot_t(a, b):
    return lax.dot_general(a, b, (((1,), (1,)), ((), ())), preferred_element_type=F32)


def dot_l(a, b):
    return lax.dot_general(a, b, (((0,), (0,)), ((), ())), preferred_element_type=F32)


PANELS = (3 * D // LANES, D // LANES, 36, D // LANES)
UNITS = (D // 16, D // 16, D // 16, FF // 16)
TILES_AT = (0, 1944, 2592, 5184)
TILES_END = 7605
TILES_VECTORS = 22
TILES_HELD = 7776
FLAT_AT = (0, CUT_OUT, CUT_UP, CUT_DOWN)
WIDE = PANELS[2] * LANES
UP_ROWS = 16 * FF // LANES
HALO = 1600


def lay_rows(d, own_rows, tiles, before, own, after, flat, held, turned):
    margin = 16 * PANELS[2]
    flat[0:HALO] = before.astype(F32)
    flat[HALO : HALO + own_rows] = own.astype(F32)
    flat[HALO + own_rows : 2 * HALO + own_rows] = after.astype(F32)
    flat_base = d * own_rows - HALO
    tile_base = d * tiles

    def span(at, units, panels):
        low = jnp.maximum(tile_base - at, 0) // panels
        high = jnp.maximum(tile_base + tiles - at + panels - 1, 0) // panels
        high = jnp.minimum(high, units)
        return low, jnp.maximum(high, low)

    for at, start, units, panels in zip(
        TILES_AT + (TILES_END,),
        FLAT_AT + (CUT_VECTORS,),
        UNITS + (TILES_VECTORS,),
        PANELS + (1,),
    ):
        low, high = span(at, units, panels)
        if start == CUT_UP:
            lane = lax.broadcasted_iota(jnp.int32, (8, LANES), 1)

            def up_units(b, carry):
                u = low + 8 * b
                source = pl.multiple_of(start + UP_ROWS * u - flat_base, 2)
                for j in range(16):
                    first, shift = (FF * j) // LANES, (FF * j) % LANES
                    turn = LANES - shift
                    now = flat[pl.ds(source + first, 8, stride=UP_ROWS), :]
                    now = pltpu.roll(now, turn, 1) if shift else now
                    for c in range(34):
                        value = now
                        if c < 33 or shift > LANES - FF % LANES:
                            now = flat[pl.ds(source + first + c + 1, 8, stride=UP_ROWS), :]
                            now = pltpu.roll(now, turn, 1) if shift else now
                            if shift:
                                value = jnp.where(lane < turn, value, now)
                        if c == 33:
                            value = jnp.where(lane < FF - 33 * LANES, value, 0.0)
                        turned[pl.ds(16 * c + j, 8, stride=16 * PANELS[2]), :] = value
                target = pl.multiple_of(16 * (at + PANELS[2] * u - tile_base) + margin, 16)
                held[pl.ds(target, 8 * 16 * PANELS[2]), :] = turned[...].astype(BF16)
                return carry

            turned[...] = jnp.zeros_like(turned)
            lax.fori_loop(0, (high - low + 7) // 8, up_units, 0)
        else:

            def unit(u, carry):
                source = pl.multiple_of(start + 16 * panels * u - flat_base, 16)
                target = pl.multiple_of(16 * (at + panels * u - tile_base) + margin, 16)
                for c in range(panels):
                    value = flat[pl.ds(source + c, 16, stride=panels), :]
                    held[pl.ds(target + 16 * c, 16), :] = value.astype(BF16)
                return carry

            lax.fori_loop(low, high, unit, 0)


def lay_kernel(own_rows, tiles, index_ref, before, own, after, out, flat, held, turned):
    margin = 16 * PANELS[2]
    lay_rows(index_ref[0], own_rows, tiles, before[...], own[...], after[...], flat, held, turned)
    out[...] = held[margin : margin + 16 * tiles]


def lay_scratch(own_rows, tiles):
    margin = 16 * PANELS[2]
    return [
        pltpu.VMEM((own_rows + 2 * HALO + 8 * UP_ROWS, LANES), F32),
        pltpu.VMEM((16 * tiles + 10 * margin, LANES), BF16),
        pltpu.VMEM((8 * margin, LANES), F32),
    ]


def lay_shard(index, shard, tiles, perms):
    own_rows = shard.shape[0]
    before = lax.ppermute(shard[own_rows - HALO :], "fsdp", perms[0])
    after = lax.ppermute(shard[:HALO], "fsdp", perms[1])
    vm = pl.BlockSpec(memory_space=pltpu.VMEM)
    return pl.pallas_call(
        functools.partial(lay_kernel, own_rows, tiles),
        in_specs=[pl.BlockSpec(memory_space=pltpu.SMEM), vm, vm, vm],
        out_specs=vm,
        out_shape=jax.ShapeDtypeStruct((16 * tiles, LANES), BF16),
        scratch_shapes=lay_scratch(own_rows, tiles),
        compiler_params=pltpu.CompilerParams(vmem_limit_bytes=VMEM_LIMIT),
        name="lay_shard",
    )(index, before, shard, after)


def pad_lanes(x, extra=None):
    if extra is None:
        extra = jnp.zeros((x.shape[0], LANES - HD), x.dtype)
    return jnp.concatenate([x, extra], axis=1)


def first_lane(rows, value):
    lane = lax.broadcasted_iota(jnp.int32, (rows, LANES - HD), 1)
    return jnp.where(lane == 0, value, 0.0).astype(BF16)


def key_bias(rows, length):
    key = lax.broadcasted_iota(jnp.int32, (rows, LANES - HD), 0)
    return first_lane(rows, jnp.where(key < length, 0.0, NEG))


def attn_fwd_kernel(offset, len_ref, qkv_ref, kv_ref, o_ref, st_ref, q_s, k_s, v_s):
    if kv_ref is None:
        kv_ref = qkv_ref
    rows, keys = qkv_ref.shape[0], kv_ref.shape[0]
    one = first_lane(rows, F32(1.0))
    bias = key_bias(keys, len_ref[0])
    for h in range(H):
        q_s[h] = pad_lanes(qkv_ref[:, h * HD : (h + 1) * HD], one)
        k_s[h] = pad_lanes(kv_ref[:, offset + h * HD : offset + (h + 1) * HD], bias)
        v_s[h] = pad_lanes(kv_ref[:, offset + D + h * HD : offset + D + (h + 1) * HD])
    st_ref[...] = jnp.zeros_like(st_ref)
    lane = lax.broadcasted_iota(jnp.int32, (rows, LANES), 1)

    def body(h, carry):
        s = dot_t(q_s[h], k_s[h])
        m = jnp.max(s, axis=1, keepdims=True)
        p = jnp.exp2((s - m) * C2)
        total = jnp.sum(p, axis=1, keepdims=True)
        o = dot(p.astype(BF16), v_s[h])
        q_s[h] = (o * (1.0 / total)).astype(BF16)
        st_ref[...] = jnp.where(lane == h, m * C2 + jnp.log2(total), st_ref[...])
        return carry

    lax.fori_loop(0, H, body, 0)
    for h in range(H):
        o_ref[:, h * HD : (h + 1) * HD] = q_s[h][:, :HD]


def attn_fwd(length, qkv, kv=None):
    rows = qkv.shape[0]
    keys = rows if kv is None else kv.shape[0]
    vm = pl.BlockSpec(memory_space=pltpu.VMEM)
    if kv is None:
        kernel = lambda a, b, *rest: attn_fwd_kernel(D, a, b, None, *rest)
        operands = (length, qkv)
    else:
        kernel = functools.partial(attn_fwd_kernel, 0)
        operands = (length, qkv, kv)
    return pl.pallas_call(
        kernel,
        in_specs=[pl.BlockSpec(memory_space=pltpu.SMEM)] + [vm] * (len(operands) - 1),
        out_specs=[vm, vm],
        out_shape=[
            jax.ShapeDtypeStruct((rows, D), BF16),
            jax.ShapeDtypeStruct((rows, LANES), F32),
        ],
        scratch_shapes=[
            pltpu.VMEM((H, rows, LANES), BF16),
            pltpu.VMEM((H, keys, LANES), BF16),
            pltpu.VMEM((H, keys, LANES), BF16),
        ],
        cost_estimate=pl.CostEstimate(
            flops=H * rows * keys * 256 * 4, bytes_accessed=rows * D * 8, transcendentals=H * rows * keys
        ),
        compiler_params=pltpu.CompilerParams(vmem_limit_bytes=VMEM_LIMIT),
        name="attention_forward",
    )(*operands)


def attn_bwd_kernel(
    offset, len_ref, qkv_ref, kv_ref, do_ref, o_ref, st_ref, dq_ref, dkv_ref, q_s, k_s, v_s, do_s, st_t, dl_t
):
    if kv_ref is None:
        kv_ref, dkv_ref = qkv_ref, dq_ref
    rows, keys = qkv_ref.shape[0], kv_ref.shape[0]
    one = first_lane(rows, F32(1.0))
    bias = key_bias(keys, len_ref[0])
    lane = lax.broadcasted_iota(jnp.int32, (rows, LANES), 1)
    delta = jnp.zeros((rows, LANES), F32)
    for h in range(H):
        q_s[h] = pad_lanes(qkv_ref[:, h * HD : (h + 1) * HD], one)
        k_s[h] = pad_lanes(kv_ref[:, offset + h * HD : offset + (h + 1) * HD], bias)
        v_s[h] = pad_lanes(kv_ref[:, offset + D + h * HD : offset + D + (h + 1) * HD])
        do = do_ref[:, h * HD : (h + 1) * HD]
        do_s[h] = pad_lanes(do)
        o = o_ref[:, h * HD : (h + 1) * HD].astype(F32)
        d = jnp.sum(do.astype(F32) * o, axis=1, keepdims=True)
        delta = jnp.where(lane == h, d, delta)
    st_t[...] = st_ref[...].T
    dl_t[...] = delta.T

    def body(h, carry):
        q, k, do = q_s[h], k_s[h], do_s[h]
        p = jnp.exp2(dot_t(k, q) * C2 - st_t[pl.ds(h, 1), :])
        dv = dot(p.astype(BF16), do)
        dp = dot_t(v_s[h], do)
        ds = (p * (dp - dl_t[pl.ds(h, 1), :])).astype(BF16)
        dk = dot(ds, q)
        dq = dot(k.T, ds)
        v_s[h] = dv.astype(BF16)
        k_s[h] = (dk * SCALE).astype(BF16)
        q_s[h] = (dq * SCALE).astype(BF16).T
        return carry

    lax.fori_loop(0, H, body, 0)
    for h in range(H):
        dq_ref[:, h * HD : (h + 1) * HD] = q_s[h][:, :HD]
        dkv_ref[:, offset + h * HD : offset + (h + 1) * HD] = k_s[h][:, :HD]
        dkv_ref[:, offset + D + h * HD : offset + D + (h + 1) * HD] = v_s[h][:, :HD]


def attn_bwd(length, qkv, do, o, st, kv=None):
    rows = qkv.shape[0]
    keys = rows if kv is None else kv.shape[0]
    vm = pl.BlockSpec(memory_space=pltpu.VMEM)
    if kv is None:
        kernel = lambda a, b, c, d, e, f, *rest: attn_bwd_kernel(
            D, a, b, None, c, d, e, f, None, *rest
        )
        operands = (length, qkv, do, o, st)
        outs = [jax.ShapeDtypeStruct((rows, 3 * D), BF16)]
    else:
        kernel = functools.partial(attn_bwd_kernel, 0)
        operands = (length, qkv, kv, do, o, st)
        outs = [jax.ShapeDtypeStruct((rows, D), BF16), jax.ShapeDtypeStruct((keys, 2 * D), BF16)]
    return pl.pallas_call(
        kernel,
        in_specs=[pl.BlockSpec(memory_space=pltpu.SMEM)] + [vm] * (len(operands) - 1),
        out_specs=[vm] * len(outs),
        out_shape=outs,
        scratch_shapes=[
            pltpu.VMEM((H, rows, LANES), BF16),
            pltpu.VMEM((H, keys, LANES), BF16),
            pltpu.VMEM((H, keys, LANES), BF16),
            pltpu.VMEM((H, rows, LANES), BF16),
            pltpu.VMEM((LANES, rows), F32),
            pltpu.VMEM((LANES, rows), F32),
        ],
        cost_estimate=pl.CostEstimate(
            flops=H * rows * keys * 256 * 10, bytes_accessed=rows * D * 16, transcendentals=H * rows * keys
        ),
        compiler_params=pltpu.CompilerParams(vmem_limit_bytes=VMEM_LIMIT),
        name="attention_backward",
    )(*operands)


LARGE_BLOCK = 4096


def gather_plan(
    src, out, stage, local_sem, z_recv, y_recv, b_recv, h_recv, c_recv_own, c_recv_z, c_recv_y, c_recv_b, c_recv_h,
    up_send, down_send, y_send, b_send, h_send, c_send_own, c_send_z, c_send_y, c_send_b, c_send_h,
):
    rows = src.shape[0]
    if rows >= LARGE_BLOCK:
        unit = rows // 6 // 16 * 16 + 16
        sizes = [unit, unit, rows // 2 - 2 * unit, rows // 2 - 2 * unit, unit]
        begins = [0, unit, 2 * unit, rows // 2, rows - 2 * unit]
    else:
        sizes = [rows // 2] * 2
        begins = [0, rows // 2]
    chunks, across_y = len(sizes), (len(sizes) + 1) // 2
    lend = chunks == 5
    x = lax.axis_index("seq")
    f = lax.axis_index("fsdp")
    z, y, c = f // 4, (f // 2) % 2, f % 2

    def place(zb, yb, j, side, cb=None):
        owner = (zb * 2 + yb) * 2 + (c if cb is None else cb)
        begin = jnp.where(side == 0, begins[j], rows - begins[j] - sizes[j])
        return pl.multiple_of(owner * rows + begin, 16), sizes[j]

    def view(spot):
        return out.at[pl.ds(spot[0], spot[1]), :]

    def device(zb, yb, cb, xb):
        return ((zb * 2 + yb) * 2 + cb, xb)

    up, down = device(z + 1, y, c, x), device(z - 1, y, c, x)
    beside, across, mate = device(z, 1 - y, c, x), device(z, y, c, 1 - x), device(z, y, 1 - c, x)

    def copy(spot, send, recv, to, source=None):
        return pltpu.make_async_remote_copy(
            src_ref=view(spot) if source is None else source,
            dst_ref=view(spot),
            send_sem=send,
            recv_sem=recv,
            device_id=to,
            device_id_type=MESH,
        )

    def arrived(spot, recv):
        copy(spot, local_sem.at[1], recv, mate).wait_recv()

    def own(j):
        begin = jnp.where(x == 0, begins[j], rows - begins[j] - sizes[j])
        return src.at[pl.ds(pl.multiple_of(begin, 16), sizes[j]), :]

    whole = (pl.multiple_of(f * rows, 16), rows)
    keep = pltpu.make_async_copy(src if stage is None else stage, view(whole), local_sem.at[0])

    def greet():
        barrier = pltpu.get_barrier_semaphore()
        for to in (beside, across, mate):
            pl.semaphore_signal(barrier, inc=1, device_id=to, device_id_type=MESH)

        @pl.when(z < 3)
        def _():
            pl.semaphore_signal(barrier, inc=1, device_id=up, device_id_type=MESH)

        @pl.when(z > 0)
        def _():
            pl.semaphore_signal(barrier, inc=1, device_id=down, device_id_type=MESH)

        pl.semaphore_wait(barrier, 3 + jnp.where(z < 3, 1, 0) + jnp.where(z > 0, 1, 0))

    def start(first=True):
        if first:
            greet()
        for j in range(chunks):
            spot = place(z, y, j, x)

            @pl.when(z < 3)
            def _():
                copy(spot, up_send.at[z, j], z_recv.at[z, j], up, own(j)).start()

            @pl.when(z > 0)
            def _():
                copy(spot, down_send.at[z, j], z_recv.at[z, j], down, own(j)).start()

            if j < across_y:
                copy(spot, y_send.at[z, j], y_recv.at[z, j], beside, own(j)).start()
        copy(whole, c_send_own.at[0], c_recv_own.at[0], mate, src).start()
        if stage is None:
            keep.start()
        else:
            fetch = pltpu.make_async_copy(src, stage, local_sem.at[0])
            fetch.start()
            fetch.wait()
            keep.start()

    def z_event(d, j):
        def flow(zb, onward, to, sends):
            spot = place(zb, y, j, x)
            arrived(spot, z_recv.at[zb, j])

            @pl.when(onward)
            def _():
                copy(spot, sends.at[zb, j], z_recv.at[zb, j], to).start()

            if j == 0 and lend:
                copy(spot, b_send.at[zb], b_recv.at[zb], across).start()
            if j < across_y:
                copy(spot, y_send.at[zb, j], y_recv.at[zb, j], beside).start()
            copy(spot, c_send_z.at[zb, j], c_recv_z.at[zb, j], mate).start()

        @pl.when(z - d >= 0)
        def _():
            flow(z - d, z < 3, up, up_send)

        @pl.when(z + d <= 3)
        def _():
            flow(z + d, z > 0, down, down_send)

    def each(d, act):
        if d == 0:
            act(z)
            return

        @pl.when(z - d >= 0)
        def _():
            act(z - d)

        @pl.when(z + d <= 3)
        def _():
            act(z + d)

    def y_event(d, j):
        def act(zb):
            spot = place(zb, 1 - y, j, x)
            arrived(spot, y_recv.at[zb, j])
            copy(spot, h_send.at[zb, j], h_recv.at[zb, j], across).start()
            copy(spot, c_send_y.at[zb, j], c_recv_y.at[zb, j], mate).start()

        each(d, act)

    def b_event(d):
        def act(zb):
            spot = place(zb, y, 0, 1 - x)
            arrived(spot, b_recv.at[zb])
            copy(spot, c_send_b.at[zb], c_recv_b.at[zb], mate).start()

        each(d, act)

    def h_event(d, j):
        def act(zb):
            spot = place(zb, 1 - y, j, 1 - x)
            arrived(spot, h_recv.at[zb, j])
            copy(spot, c_send_h.at[zb, j], c_recv_h.at[zb, j], mate).start()

        each(d, act)

    events = []
    for d in range(4):
        for j in range(chunks):
            at = (d - 1) * chunks + j + 1 if d else 0
            if d:
                events.append((at, functools.partial(z_event, d, j)))
                if j == 0 and lend:
                    events.append((at + 2, functools.partial(b_event, d)))
            if j < across_y:
                ready = at + 1.5 if d else j + 1
                events.append((ready, functools.partial(y_event, d, j)))
                events.append((ready + 2, functools.partial(h_event, d, j)))
    def finish():
        keep.wait()
        other = 1 - c

        def core_spot(zb, yb, j, side):
            return place(zb, yb, j, side, other)

        arrived((pl.multiple_of(((z * 2 + y) * 2 + other) * rows, 16), rows), c_recv_own.at[0])
        copy(whole, c_send_own.at[0], c_recv_own.at[0], mate).wait_send()
        for d in range(4):
            def drain(zb, d=d):
                for j in range(chunks):
                    if d:
                        arrived(core_spot(zb, y, j, x), c_recv_z.at[zb, j])
                        copy(place(zb, y, j, x), c_send_z.at[zb, j], c_recv_z.at[zb, j], mate).wait_send()
                    if j < across_y:
                        arrived(core_spot(zb, 1 - y, j, x), c_recv_y.at[zb, j])
                        arrived(core_spot(zb, 1 - y, j, 1 - x), c_recv_h.at[zb, j])
                        spot = place(zb, 1 - y, j, x)
                        copy(spot, c_send_y.at[zb, j], c_recv_y.at[zb, j], mate).wait_send()
                        copy(spot, h_send.at[zb, j], h_recv.at[zb, j], across).wait_send()
                        spot = place(zb, 1 - y, j, 1 - x)
                        copy(spot, c_send_h.at[zb, j], c_recv_h.at[zb, j], mate).wait_send()
                        spot = place(zb, y, j, x)
                        copy(spot, y_send.at[zb, j], y_recv.at[zb, j], beside).wait_send()
                if d and lend:
                    arrived(core_spot(zb, y, 0, 1 - x), c_recv_b.at[zb])
                    spot = place(zb, y, 0, 1 - x)
                    copy(spot, c_send_b.at[zb], c_recv_b.at[zb], mate).wait_send()
                    spot = place(zb, y, 0, x)
                    copy(spot, b_send.at[zb], b_recv.at[zb], across).wait_send()

            each(d, drain)
            for j in range(chunks):
                @pl.when(jnp.logical_and(z - d >= 0, z < 3))
                def _():
                    zb = z - d
                    copy(place(zb, y, j, x), up_send.at[zb, j], z_recv.at[zb, j], up).wait_send()

                @pl.when(jnp.logical_and(z + d <= 3, z > 0))
                def _():
                    zb = z + d
                    copy(place(zb, y, j, x), down_send.at[zb, j], z_recv.at[zb, j], down).wait_send()

    return start, sorted(events, key=lambda e: e[0]), finish


def gather_kernel(*refs):
    start, events, finish = gather_plan(*refs)
    start()
    for _, event in events:
        event()
    finish()


def gather_semaphores():
    dma = pltpu.SemaphoreType.DMA
    core = [dma((1,)), dma((4, 5)), dma((4, 3)), dma((4,)), dma((4, 3))]
    links = [dma((4, 5)), dma((4, 3)), dma((4,)), dma((4, 3))]
    return [dma((2,))] + links + core + [dma((4, 5))] + links + core


def gather_blocks(shard, collective_id, held_rows):
    rows = shard.shape[0]
    return pl.pallas_call(
        gather_kernel,
        in_specs=[pl.BlockSpec(memory_space=pl.ANY)],
        out_specs=pl.BlockSpec(memory_space=pl.ANY),
        out_shape=jax.ShapeDtypeStruct((held_rows, LANES), BF16),
        scratch_shapes=[pltpu.VMEM((rows, LANES), BF16)] + gather_semaphores(),
        compiler_params=pltpu.CompilerParams(collective_id=collective_id, has_side_effects=True, vmem_limit_bytes=VMEM_LIMIT),
        name="gather_blocks",
    )(shard)


def gelu_parts(x):
    inner = 0.7978845608028654 * (x + 0.044715 * x * x * x)
    return jnp.tanh(inner)


def layer_norm(tensor, gain, offset):
    average = jnp.mean(tensor, axis=-1, keepdims=True)
    centred = tensor - average
    variance = jnp.mean(centred * centred, axis=-1, keepdims=True)
    return centred * lax.rsqrt(variance + epsilon) * gain + offset


def layer_norm_back(d_out, tensor, gain):
    average = jnp.mean(tensor, axis=-1, keepdims=True)
    centred = tensor - average
    variance = jnp.mean(centred * centred, axis=-1, keepdims=True)
    scale = lax.rsqrt(variance + epsilon)
    normal = centred * scale
    d_normal = d_out * gain
    mean_d = jnp.mean(d_normal, axis=-1, keepdims=True)
    mean_dn = jnp.mean(d_normal * normal, axis=-1, keepdims=True)
    return (d_normal - mean_d - normal * mean_dn) * scale


def dot_both(x, w, inner, up):
    cut = w.shape[0] // 256 * 256
    tail = dot(
        jnp.concatenate([x[:, cut:], inner], axis=1), jnp.concatenate([w[cut:], up], axis=0)
    )
    return dot(x[:, :cut], w[:cut]) + tail


def dot_both_t(x, w, inner, up_t):
    cut = w.shape[1] // 256 * 256
    tail = dot_t(
        jnp.concatenate([x[:, cut:], inner], axis=1), jnp.concatenate([w[:, cut:], up_t], axis=1)
    )
    return dot_t(x[:, :cut], w[:, :cut]) + tail


def matrix(ref, count=None):
    units, panels = ref.shape[:2]
    return jnp.concatenate(
        [ref[:, p].reshape(units * 16, LANES) for p in range(count or panels)], axis=1
    )


def unit_block(units, panels, place):
    return pl.BlockSpec((units, panels, 16, LANES), place)


def whole(shape):
    return pl.BlockSpec(shape, lambda i: (0,) * len(shape), pipeline_mode=pl.Buffered(1))


def columns(rows, width):
    return pl.BlockSpec((rows, width), lambda i: (0, i))


def struct(shape, dtype):
    return jax.ShapeDtypeStruct(shape, dtype)


def dense_params(flops, bytes_accessed):
    return dict(
        cost_estimate=pl.CostEstimate(
            flops=flops, bytes_accessed=bytes_accessed, transcendentals=0
        ),
        compiler_params=pltpu.CompilerParams(vmem_limit_bytes=VMEM_LIMIT),
    )


def qkv_kernel(hidden, w, vec, down, up, normed, inner, qkv, parts):
    c = pl.program_id(0)

    @pl.when(c == 0)
    def _():
        value = layer_norm(hidden[...], vec[0:1], vec[1:2]).astype(BF16)
        normed[...] = value
        narrow = dot_t(value, down[...]).astype(BF16)
        inner[...] = narrow
        for part in range(3):
            parts[part] = narrow[:, part * R : (part + 1) * R]

    bias = vec[pl.ds(jnp.where(c == 2, 5, 4), 1), :] * jnp.where(c == 1, 0.0, 1.0)
    qkv[...] = (dot_both(normed[...], matrix(w), parts[c], up[0]) + bias).astype(BF16)


def qkv_forward(hidden, w_qkv, vectors, attn):
    rows = hidden.shape[0]
    return pl.pallas_call(
        qkv_kernel,
        grid=(3,),
        in_specs=[
            whole((rows, D)),
            unit_block(72, 9, lambda i: (0, i, 0, 0)),
            whole((8, D)),
            whole((3 * R, D)),
            pl.BlockSpec((1, R, D), lambda i: (i, 0, 0)),
        ],
        out_specs=[whole((rows, D)), whole((rows, 3 * R)), columns(rows, D)],
        out_shape=[
            struct((rows, D), BF16),
            struct((rows, 3 * R), BF16),
            struct((rows, 3 * D), BF16),
        ],
        scratch_shapes=[pltpu.VMEM((3, rows, R), BF16)],
        name="qkv_forward",
        **dense_params(6 * rows * D * D, 14 * rows * D + 6 * D * D),
    )(hidden, w_qkv, vectors, attn[0:3].reshape(3 * R, D), attn[4:7])


TILE = 512
OUT_BLOCK = pl.BlockSpec(
    (72, 9, 16, LANES), lambda i: (3, 0, 0, 0), pipeline_mode=pl.Buffered(1)
)


def up_kernel(
    attended, hidden, w_o, vec, down_o, up_o, down_1, w_1, b_1, up_1,
    inner_o, middle, normed, inner_up, gate, activated,
):
    @pl.when(pl.program_id(0) == 0)
    def _():
        narrow = dot_t(attended[...], down_o[...]).astype(BF16)
        inner_o[...] = narrow
        middle[...] = hidden[...] + (dot_both(attended[...], matrix(w_o), narrow, up_o[...]) + vec[6:7])
        value = layer_norm(middle[...], vec[2:3], vec[3:4]).astype(BF16)
        normed[...] = value
        inner_up[...] = dot_t(value, down_1[...]).astype(BF16)

    x = dot_both(normed[...], matrix(w_1), inner_up[...], up_1[...]) + b_1[...]
    gate[...] = x.astype(BF16)
    activated[...] = (0.5 * x * (1.0 + gelu_parts(x))).astype(BF16)


def up_forward(attended, hidden, w_o, vectors, attn, narrow, w_1, b_1, wide):
    rows = hidden.shape[0]
    return pl.pallas_call(
        up_kernel,
        grid=(WIDE // TILE,),
        in_specs=[
            whole((rows, D)),
            whole((rows, D)),
            OUT_BLOCK,
            whole((8, D)),
            whole((R, D)),
            whole((R, D)),
            whole((R, D)),
            unit_block(72, 4, lambda i: (1, i, 0, 0)),
            columns(1, TILE),
            columns(R, TILE),
        ],
        out_specs=[
            whole((rows, R)),
            whole((rows, D)),
            whole((rows, D)),
            whole((rows, R)),
            columns(rows, TILE),
            columns(rows, TILE),
        ],
        out_shape=[
            struct((rows, R), BF16),
            struct((rows, D), F32),
            struct((rows, D), BF16),
            struct((rows, R), BF16),
            struct((rows, WIDE), BF16),
            struct((rows, WIDE), BF16),
        ],
        name="up_forward",
        **dense_params(2 * rows * D * (D + FF), 12 * rows * D + 4 * rows * FF + 2 * D * (D + FF)),
    )(attended, hidden, w_o, vectors, attn[3], attn[7], narrow[0], w_1, b_1, wide[0])


THIRD = D // 3


def down_kernel(activated, middle, w_2, b_2, down_2, up_2, inner, hidden):
    @pl.when(pl.program_id(0) == 0)
    def _():
        inner[...] = dot_t(activated[...], down_2[...]).astype(BF16)

    value = activated[:, :FF]

    hidden[...] = middle[...] + (
        dot(value, matrix(w_2)) + b_2[...] + dot(inner[...], up_2[...])
    )


def down_forward(activated, middle, w_2, b_2, narrow, wide):
    rows = middle.shape[0]
    return pl.pallas_call(
        down_kernel,
        grid=(3,),
        in_specs=[
            whole((rows, WIDE)),
            columns(rows, THIRD),
            pl.BlockSpec(
                (pl.Element(UNITS[3]), pl.Element(3), pl.Element(16), pl.Element(LANES)),
                lambda i: (TILES_AT[3] // 9, 3 * i, 0, 0),
            ),
            columns(1, THIRD),
            whole((R, WIDE)),
            columns(R, THIRD),
        ],
        out_specs=[whole((rows, R)), columns(rows, THIRD)],
        out_shape=[struct((rows, R), BF16), struct((rows, D), F32)],
        name="down_forward",
        **dense_params(2 * rows * D * FF, 8 * rows * D + 2 * rows * FF + 2 * D * FF),
    )(activated, middle, w_2, b_2, wide[1], narrow[1])


def gate_kernel(
    gradient, w_2, gate, down_2, up_1, up_2, inner_down, inner_up, d_gate, g_wide, d_inner_up, g_up_2,
    d_branch, d_inner_down, total,
):
    i = pl.program_id(0)

    @pl.when(i == 0)
    def _():
        value = gradient[...].astype(BF16)
        d_branch[...] = value
        d_inner_down[...] = dot_t(value, up_2[...]).astype(BF16)
        g_up_2[...] = dot_l(inner_down[...], value)
        total[...] = jnp.zeros_like(total)

    left = FF - i * TILE
    down = down_2[...]
    d_act = dot_t(d_branch[...], matrix(w_2)) + dot(d_inner_down[...], down)
    x = gate[...].astype(F32)
    t = gelu_parts(x)
    half = 0.5 * (1.0 + t)
    slope = half + 0.5 * x * (1.0 - t * t) * (
        0.7978845608028654 * (1.0 + 3 * 0.044715 * x * x)
    )
    keep = lax.broadcasted_iota(jnp.int32, (1, TILE), 1) < left
    value = jnp.where(keep, slope * d_act, 0.0).astype(BF16)
    d_gate[...] = value
    total[...] += dot_t(value, up_1[...])
    g_wide[0:R] = dot_l(inner_up[...], value)
    g_wide[R : 2 * R] = dot_l(d_inner_down[...], (x * half).astype(BF16))

    @pl.when(i == pl.num_programs(0) - 1)
    def _():
        d_inner_up[...] = total[...].astype(BF16)


def gate_backward(gradient, w_2, gate, narrow, wide, inner_down, inner_up):
    rows = gradient.shape[0]
    return pl.pallas_call(
        gate_kernel,
        grid=(WIDE // TILE,),
        in_specs=[
            whole((rows, D)),
            unit_block(TILE // 16, 9, lambda i: (TILES_AT[3] // 9 * 16 // TILE + i, 0, 0, 0)),
            columns(rows, TILE),
            columns(R, TILE),
            columns(R, TILE),
            whole((R, D)),
            whole((rows, R)),
            whole((rows, R)),
        ],
        out_specs=[columns(rows, TILE), columns(2 * R, TILE), whole((rows, R)), whole((R, D))],
        out_shape=[
            struct((rows, WIDE), BF16),
            struct((2 * R, WIDE), F32),
            struct((rows, R), BF16),
            struct((R, D), F32),
        ],
        scratch_shapes=[
            pltpu.VMEM((rows, D), BF16),
            pltpu.VMEM((rows, R), BF16),
            pltpu.VMEM((rows, R), F32),
        ],
        name="gate_backward",
        **dense_params(2 * rows * D * FF, 4 * rows * D + 4 * rows * FF + 2 * D * FF),
    )(gradient, w_2, gate, wide[1], wide[0], narrow[1], inner_down, inner_up)


def middle_kernel(
    d_gate, w_1, d_inner_up, down_1, normed, middle, gradient, vec, w_o, down_o, up_o, inner_o, attended,
    d_middle, d_attended, g_rows, d_normed,
):
    i = pl.program_id(0)
    at = pl.ds(pl.multiple_of(i * THIRD, LANES), THIRD)
    d_normed[:, at] = dot_t(d_gate[:, : 34 * LANES], matrix(w_1, 34)) + dot(
        d_inner_up[...], down_1[:, at]
    )

    @pl.when(i == pl.num_programs(0) - 1)
    def _():
        value = gradient[...] + layer_norm_back(d_normed[...], middle[...], vec[2:3])
        d_middle[...] = value
        d_out = value.astype(BF16)
        d_inner_o = dot_t(d_out, up_o[...]).astype(BF16)
        d_attended[...] = (dot_t(d_out, matrix(w_o)) + dot(d_inner_o, down_o[...])).astype(BF16)
        g_rows[0:R] = dot_l(d_inner_o, attended[...])
        g_rows[R : 2 * R] = dot_l(inner_o[...], d_out)
        g_rows[2 * R : 3 * R] = dot_l(d_inner_up[...], normed[...])


def middle_backward(
    d_gate, w_1, d_inner_up, narrow, normed, middle, gradient, vectors, w_o, attn, inner_o, attended
):
    rows = gradient.shape[0]
    return pl.pallas_call(
        middle_kernel,
        grid=(3,),
        in_specs=[
            whole((rows, WIDE)),
            unit_block(THIRD // 16, PANELS[2], lambda i: (3 + i, 0, 0, 0)),
            whole((rows, R)),
            whole((R, D)),
            whole((rows, D)),
            whole((rows, D)),
            whole((rows, D)),
            whole((8, D)),
            OUT_BLOCK,
            whole((R, D)),
            whole((R, D)),
            whole((rows, R)),
            whole((rows, D)),
        ],
        out_specs=[whole((rows, D)), whole((rows, D)), whole((3 * R, D))],
        out_shape=[
            struct((rows, D), F32),
            struct((rows, D), BF16),
            struct((3 * R, D), F32),
        ],
        scratch_shapes=[pltpu.VMEM((rows, D), F32)],
        name="middle_backward",
        **dense_params(2 * rows * D * (D + FF), 18 * rows * D + 2 * rows * FF + 2 * D * (D + FF)),
    )(
        d_gate, w_1, d_inner_up, narrow[0], normed, middle, gradient, vectors, w_o, attn[3], attn[7],
        inner_o, attended,
    )


def input_kernel(
    d_qkv, w_qkv, down, up, normed, inner, hidden, d_middle, vec, gradient, g_rows, d_normed, d_inner
):
    i = pl.program_id(0)

    @pl.when(i == 0)
    def _():
        for c in range(3):
            part = d_qkv[:, c * D : (c + 1) * D]
            d_inner[:, c * R : (c + 1) * R] = dot_t(part, up[c]).astype(BF16)
            g_rows[(3 + c) * R : (4 + c) * R] = dot_l(inner[:, c * R : (c + 1) * R], part)
        g_rows[0 : 3 * R] = dot_l(d_inner[...], normed[...])

    at = pl.ds(pl.multiple_of(i * THIRD, LANES), THIRD)
    d_normed[:, at] = dot_t(d_qkv[...], matrix(w_qkv)) + dot(d_inner[...], down[:, at])

    @pl.when(i == pl.num_programs(0) - 1)
    def _():
        gradient[...] = d_middle[...] + layer_norm_back(d_normed[...], hidden[...], vec[0:1])


def input_backward(d_qkv, w_qkv, attn, normed, inner, hidden, d_middle, vectors):
    rows = hidden.shape[0]
    return pl.pallas_call(
        input_kernel,
        grid=(3,),
        in_specs=[
            whole((rows, 3 * D)),
            unit_block(THIRD // 16, 27, lambda i: (i, 0, 0, 0)),
            whole((3 * R, D)),
            whole((3, R, D)),
            whole((rows, D)),
            whole((rows, 3 * R)),
            whole((rows, D)),
            whole((rows, D)),
            whole((8, D)),
        ],
        out_specs=[whole((rows, D)), whole((6 * R, D))],
        out_shape=[struct((rows, D), F32), struct((6 * R, D), F32)],
        scratch_shapes=[pltpu.VMEM((rows, D), F32), pltpu.VMEM((rows, 3 * R), BF16)],
        name="input_backward",
        **dense_params(6 * rows * D * D, 20 * rows * D + 6 * D * D),
    )(d_qkv, w_qkv, attn[0:3].reshape(3 * R, D), attn[4:7], normed, inner, hidden, d_middle, vectors)


PAIR = 2 * LANES
PAIRS = -(-D // PAIR)
TWIN = 2
FOUR = 4
FORWARD_STEPS = (3, H // FOUR, WIDE // TILE, PAIRS)
FORWARD_AT = (0, 3, 3 + H // FOUR, 3 + H // FOUR + WIDE // TILE)
FORWARD_BEGINS = (
    [4.5 * i for i in range(3)]
    + [14 + 6 * i for i in range(H // FOUR)]
    + [38 + (5 if i else 0) + 2.6 * i for i in range(WIDE // TILE)]
    + [65 + 3 * i for i in range(PAIRS)]
)
CHUNK_TIME = 7.4


def of_layer(layer, *shape):
    return pl.BlockSpec(
        (1,) + shape, lambda i: (layer,) + (0,) * len(shape), pipeline_mode=pl.Buffered(1)
    )


def forward_kernel(with_gather, *refs):
    (
        bias_lane, hidden, w_qkv, vec, attn, w_o, narrow_in, w_1, b_1, up_1, w_2, w_2_odd, b_2, down_2, up_2,
    ) = refs[:15]
    refs = refs[15:]
    if with_gather:
        shard, refs = refs[0], refs[1:]
    (
        normed, inner_qkv, qkv, attended, stats, inner_o, middle, normed_two, inner_up, gate, inner_down,
        next_hidden,
    ) = refs[:12]
    refs = refs[12:]
    if with_gather:
        flat, refs = refs[0], refs[1:]
    heads, activated, parts = refs[:3]
    i = pl.program_id(0)
    rows = hidden.shape[0]
    _, att_at, up_at, down_at = FORWARD_AT
    last = down_at + PAIRS - 1

    def at_step(k):
        return pl.when(i == k)

    if with_gather:
        start, events, finish = gather_plan(shard, flat, None, *refs[3:])
        at_step(0)(start)
        steps = [[] for _ in FORWARD_BEGINS]
        late = []
        for when, event in events:
            ready = [k for k, begin in enumerate(FORWARD_BEGINS) if begin >= CHUNK_TIME * when + 4]
            (steps[ready[0]] if ready else late).append(event)
        for k, due in enumerate(steps):
            if due:

                @at_step(k)
                def _(due=due):
                    for event in due:
                        event()

    @pl.when(i < att_at)
    def _():
        @at_step(0)
        def _():
            value = layer_norm(hidden[...], vec[0:1], vec[1:2]).astype(BF16)
            normed[...] = value
            narrow = dot_t(value, attn[0, 0:3].reshape(3 * R, D)).astype(BF16)
            inner_qkv[...] = narrow
            for part in range(3):
                parts[part] = narrow[:, part * R : (part + 1) * R]
            stats[...] = jnp.zeros_like(stats)

        bias = vec[pl.ds(jnp.where(i == 2, 5, 4), 1), :] * jnp.where(i == 1, 0.0, 1.0)
        value = (dot_both(normed[...], matrix(w_qkv), parts[i], attn[0, 4 + i]) + bias).astype(BF16)
        qkv[...] = value
        mark = jnp.where(i == 0, first_lane(rows, F32(1.0)), jnp.where(i == 1, bias_lane[...], jnp.zeros_like(bias_lane[...])))
        for h in range(H):
            heads[i, h] = pad_lanes(value[:, h * HD : (h + 1) * HD], mark)

    @pl.when(jnp.logical_and(i >= att_at, i < up_at))
    def _():
        lane = lax.broadcasted_iota(jnp.int32, (rows, LANES), 1)
        pair_at = (i - att_at) * FOUR
        scores = [dot_t(heads[0, pair_at + k], heads[1, pair_at + k]) for k in range(FOUR)]
        kept = stats[...]
        for k in range(FOUR):
            h, s = pair_at + k, scores[k]
            m = jnp.max(s, axis=1, keepdims=True)
            p = jnp.exp2((s - m) * C2)
            total = jnp.sum(p, axis=1, keepdims=True)
            o = dot(p.astype(BF16), heads[2, h])
            heads[0, h] = (o * (1.0 / total)).astype(BF16)
            kept = jnp.where(lane == h, m * C2 + jnp.log2(total), kept)
        stats[...] = kept

    @pl.when(jnp.logical_and(i >= up_at, i < down_at))
    def _():
        t = i - up_at

        @at_step(up_at)
        def _():
            for h in range(H):
                attended[:, h * HD : (h + 1) * HD] = heads[0, h][:, :HD]
            value = attended[...]
            narrow = dot_t(value, attn[0, 3]).astype(BF16)
            inner_o[...] = narrow
            middle[...] = hidden[...] + (dot_both(value, matrix(w_o), narrow, attn[0, 7]) + vec[6:7])
            value = layer_norm(middle[...], vec[2:3], vec[3:4]).astype(BF16)
            normed_two[...] = value
            inner_up[...] = dot_t(value, narrow_in[0, 0]).astype(BF16)

        x = dot_both(normed_two[...], matrix(w_1), inner_up[...], up_1[0, 0]) + b_1[...]
        gate[...] = x.astype(BF16)
        value = (0.5 * x * (1.0 + gelu_parts(x))).astype(BF16)
        activated[:, pl.ds(pl.multiple_of(t * TILE, LANES), TILE)] = value

    @pl.when(i >= down_at)
    def _():
        @at_step(down_at)
        def _():
            w = jnp.concatenate([matrix(w_2.at[: UNITS[3]]), down_2[0, 0].T[:FF]], axis=1)
            value = dot(activated[:, :FF], w)
            narrow = value[:, LANES : LANES + R].astype(BF16)
            inner_down[...] = narrow
            value = value[:, :LANES] + b_2[:, :LANES] + dot(narrow, up_2[0, 0, :, :LANES])
            next_hidden[:, :LANES] = middle[:, D - LANES :] + value

        @pl.when(i > down_at)
        def _():
            at = pl.ds(pl.multiple_of((i - down_at - 1) * PAIR, LANES), PAIR)
            w = jnp.concatenate([matrix(w.at[: UNITS[3]]) for w in (w_2, w_2_odd)], axis=1)
            value = dot(activated[:, :FF], w) + b_2[...] + dot(inner_down[...], up_2[0, 0])
            next_hidden[...] = middle[:, at] + value

    if with_gather:

        @at_step(last)
        def _():
            for event in late:
                event()
            finish()


def layer_forward(layer, bias, hidden, weights, tables, shard=None):
    w_qkv, w_o, w_1, w_2, vectors, b_1 = weights
    attn, narrow, wide, _ = tables
    rows = hidden.shape[0]
    _, att_at, up_at, down_at = FORWARD_AT

    def step(i, k):
        return jnp.minimum(jnp.maximum(i - FORWARD_AT[k], 0), FORWARD_STEPS[k] - 1)

    def cols(count, width, k):
        return pl.BlockSpec((count, width), lambda i: (0, step(i, k)))

    def pair(i):
        return jnp.where(step(i, 3) == 0, PAIRS - 1, step(i, 3) - 1)

    def pairs(count):
        return pl.BlockSpec((count, PAIR), lambda i: (0, pair(i)))

    operands = [
        bias, hidden, w_qkv, vectors, attn, w_o, narrow, w_1, b_1, wide, w_2, w_2, vectors[7:8], wide, narrow,
    ]
    in_specs = [
        whole((rows, LANES - HD)),
        whole((rows, D)),
        unit_block(72, 9, lambda i: (0, step(i, 0), 0, 0)),
        whole((8, D)),
        of_layer(layer, 8, R, D),
        OUT_BLOCK,
        of_layer(layer, 2, R, D),
        unit_block(72, 4, lambda i: (1, step(i, 2), 0, 0)),
        cols(1, TILE, 2),
        pl.BlockSpec((1, 1, R, TILE), lambda i: (layer, 0, 0, step(i, 2))),
        unit_block(288, 1, lambda i: (2, 2 * pair(i), 0, 0)),
        unit_block(288, 1, lambda i: (2, jnp.minimum(2 * pair(i) + 1, 8), 0, 0)),
        pairs(1),
        pl.BlockSpec((1, 1, R, WIDE), lambda i: (layer, 1, 0, 0), pipeline_mode=pl.Buffered(1)),
        pl.BlockSpec((1, 1, R, PAIR), lambda i: (layer, 1, 0, pair(i))),
    ]
    outs = [
        (whole((rows, D)), struct((rows, D), BF16)),
        (whole((rows, 3 * R)), struct((rows, 3 * R), BF16)),
        (cols(rows, D, 0), struct((rows, 3 * D), BF16)),
        (whole((rows, D)), struct((rows, D), BF16)),
        (whole((rows, LANES)), struct((rows, LANES), F32)),
        (whole((rows, R)), struct((rows, R), BF16)),
        (whole((rows, D)), struct((rows, D), F32)),
        (whole((rows, D)), struct((rows, D), BF16)),
        (whole((rows, R)), struct((rows, R), BF16)),
        (cols(rows, TILE, 2), struct((rows, WIDE), BF16)),
        (whole((rows, R)), struct((rows, R), BF16)),
        (pairs(rows), struct((rows, D), F32)),
    ]
    scratch = [
        pltpu.VMEM((3, H, rows, LANES), BF16),
        pltpu.VMEM((rows, WIDE), BF16),
        pltpu.VMEM((3, rows, R), BF16),
    ]
    params = dict(vmem_limit_bytes=VMEM_MOST)
    if shard is not None:
        operands.append(shard)
        in_specs.append(pl.BlockSpec(memory_space=pl.ANY))
        outs.append(
            (pl.BlockSpec(memory_space=pl.ANY), struct((16 * TILES_HELD, LANES), BF16))
        )
        scratch += gather_semaphores()
        params.update(collective_id=3, has_side_effects=True)
    return pl.pallas_call(
        functools.partial(forward_kernel, shard is not None),
        grid=(sum(FORWARD_STEPS),),
        in_specs=in_specs,
        out_specs=[spec for spec, _ in outs],
        out_shape=[shape for _, shape in outs],
        scratch_shapes=scratch,
        cost_estimate=pl.CostEstimate(
            flops=2 * rows * D * (4 * D + 2 * FF) + 8 * rows * rows * D,
            bytes_accessed=2 * D * (4 * D + 2 * FF) + 30 * rows * D,
            transcendentals=H * rows * rows,
        ),
        compiler_params=pltpu.CompilerParams(**params),
        name="layer_forward_gather" if shard is not None else "layer_forward",
    )(*operands)


def first_gather_kernel(tiles, shard_a, shard_b, gathered, laid_a, laid_b, own, halo, flat, held, turned, *sems):
    own_sem, halo_send, halo_recv = sems[:3]
    f = lax.axis_index("fsdp")
    x = lax.axis_index("seq")
    z = f // 4
    rows = shard_a.shape[0]
    last = lax.axis_size("fsdp") - 1
    margin = 16 * PANELS[2]
    barrier = pltpu.get_barrier_semaphore()
    start, events, finish = gather_plan(laid_a, gathered, None, *sems[3:])

    def greet(to):
        pl.semaphore_signal(barrier, inc=1, device_id=to, device_id_type=MESH)

    y, c = (f // 2) % 2, f % 2
    for to in ((f + 2 - 4 * y, x), (f, 1 - x), (f + 1 - 2 * c, x)):
        greet(to)
    for there, step in ((z < 3, 4), (z > 0, -4), (f < last, 1), (f > 0, -1)):

        @pl.when(there)
        def _(step=step):
            greet((f + step, x))

    expected = 3
    for there in (z < 3, z > 0, f < last, f > 0):
        expected = expected + jnp.where(there, 1, 0)
    pl.semaphore_wait(barrier, expected)

    def halo_copy(layer, side):
        source = (shard_a, shard_b)[layer].at[pl.ds((rows - HALO) * (1 - side), HALO), :]
        return pltpu.make_async_remote_copy(
            src_ref=source,
            dst_ref=halo.at[layer, side],
            send_sem=halo_send.at[layer, side],
            recv_sem=halo_recv.at[layer, side],
            device_id=(f + 1 - 2 * side, x),
            device_id_type=MESH,
        )

    def sends(side):
        return f < last if side == 0 else f > 0

    def takes(side):
        return sends(1 - side)

    for layer in range(2):
        for side in range(2):

            @pl.when(sends(side))
            def _(layer=layer, side=side):
                halo_copy(layer, side).start()

    def lay(layer, source, laid):
        fetch = pltpu.make_async_copy(source, own, own_sem.at[0])
        fetch.start()
        fetch.wait()
        for side in range(2):

            @pl.when(takes(side))
            def _(side=side):
                halo_copy(layer, side).wait_recv()

            @pl.when(jnp.logical_not(takes(side)))
            def _(side=side):
                halo[layer, side] = jnp.zeros((HALO, LANES), BF16)

        lay_rows(f, rows, tiles, halo[layer, 0], own[...], halo[layer, 1], flat, held, turned)
        keep = pltpu.make_async_copy(held.at[pl.ds(margin, 16 * tiles), :], laid, own_sem.at[0])
        keep.start()
        keep.wait()

    lay(0, shard_a, laid_a)
    start(False)
    lay(1, shard_b, laid_b)
    for _, event in events:
        event()
    finish()
    for layer in range(2):
        for side in range(2):

            @pl.when(sends(side))
            def _(layer=layer, side=side):
                halo_copy(layer, side).wait_send()


def first_gather(shards, tiles):
    rows = shards[0].shape[0]
    dma = pltpu.SemaphoreType.DMA
    hbm = pl.BlockSpec(memory_space=pl.ANY)
    laid = jax.ShapeDtypeStruct((16 * tiles, LANES), BF16)
    return pl.pallas_call(
        functools.partial(first_gather_kernel, tiles),
        in_specs=[hbm, hbm],
        out_specs=[hbm, hbm, hbm],
        out_shape=[jax.ShapeDtypeStruct((16 * TILES_HELD, LANES), BF16), laid, laid],
        scratch_shapes=[pltpu.VMEM((rows, LANES), BF16), pltpu.VMEM((2, 2, HALO, LANES), BF16)]
        + lay_scratch(rows, tiles)
        + [dma((1,)), dma((2, 2)), dma((2, 2))]
        + gather_semaphores(),
        compiler_params=pltpu.CompilerParams(
            collective_id=0, has_side_effects=True, vmem_limit_bytes=VMEM_MOST
        ),
        name="first_gather",
    )(*shards)


SHARE = 5
SHARE_ROWS = SHARE * 16


def share_plan(
    adapters, named, terms, names, out, held, totals, sums, local_sem, send, recv, pair_sem
):
    x = lax.axis_index("seq")
    f = lax.axis_index("fsdp")
    count = terms.shape[0]
    me = f * 2 + x
    rows = adapters * SHARE_ROWS

    def device(k):
        return (k // 2, k % 2)

    def share_to(to, slot):
        return pltpu.make_async_remote_copy(
            src_ref=terms.at[to],
            dst_ref=held.at[slot],
            send_sem=send.at[to],
            recv_sem=recv.at[slot],
            device_id=device(to),
            device_id_type=MESH,
        )

    def own():
        return pltpu.make_async_copy(terms.at[me], held.at[me], local_sem.at[0])

    def across(side):
        part = out.at[pl.ds(pl.multiple_of(side * rows, 16), rows), :]
        return pltpu.make_async_remote_copy(
            src_ref=part,
            dst_ref=part,
            send_sem=pair_sem.at[0],
            recv_sem=pair_sem.at[1],
            device_id=(f, 1 - x),
            device_id_type=MESH,
        )

    def start():
        barrier = pltpu.get_barrier_semaphore()

        def greet(k, carry):
            to = (me + k) % count
            pl.semaphore_signal(barrier, inc=1, device_id=device(to), device_id_type=MESH)
            return carry

        lax.fori_loop(1, count, greet, 0)
        pl.semaphore_wait(barrier, count - 1)

        def post(k, carry):
            to = (me + k) % count
            share_to(to, me).start()
            return carry

        lax.fori_loop(1, count, post, 0)
        own().start()

    def add_up():
        totals[...] = jnp.zeros_like(totals)

        def add(slot):
            value = held[slot, :SHARE].reshape(SHARE_ROWS, LANES).astype(F32)
            if named:
                name = names[pl.ds(slot, 1), :]
            else:
                name = held[slot, SHARE].astype(F32)[0:1]
                names[pl.ds(slot, 1), :] = name
            for e in range(adapters):
                totals[e] += jnp.where(name == float(e), value, 0.0)

        own().wait()
        add(me)

        def take(k, carry):
            slot = (me + count - k) % count
            share_to(slot, slot).wait_recv()
            add(slot)
            return carry

        lax.fori_loop(1, count, take, 0)
        sums[...] = totals[...].reshape(rows, LANES).astype(BF16)
        part = out.at[pl.ds(pl.multiple_of(x * rows, 16), rows), :]
        keep = pltpu.make_async_copy(sums, part, local_sem.at[0])
        keep.start()
        keep.wait()
        across(x).start()

    def finish():
        def sent(k, carry):
            to = (me + k) % count
            share_to(to, me).wait_send()
            return carry

        lax.fori_loop(1, count, sent, 0)
        across(x).wait_send()
        across(1 - x).wait_recv()

    return start, add_up, finish


def share_kernel(adapters, *refs):
    for part in share_plan(adapters, True, *refs):
        part()


def share_scratch(count, adapters, tiles):
    dma = pltpu.SemaphoreType.DMA
    rows = adapters * SHARE_ROWS
    return [
        pltpu.VMEM((count, tiles, 16, LANES), BF16),
        pltpu.VMEM((adapters, SHARE_ROWS, LANES), F32),
        pltpu.VMEM((rows, LANES), BF16),
        dma((1,)),
        dma((count,)),
        dma((count,)),
        dma((2,)),
    ]


def share_terms(terms, names, adapters):
    rows = adapters * SHARE_ROWS
    return pl.pallas_call(
        functools.partial(share_kernel, adapters),
        in_specs=[pl.BlockSpec(memory_space=pl.ANY), pl.BlockSpec(memory_space=pltpu.VMEM)],
        out_specs=pl.BlockSpec(memory_space=pl.ANY),
        out_shape=jax.ShapeDtypeStruct((2 * rows, LANES), BF16),
        scratch_shapes=share_scratch(terms.shape[0], adapters, SHARE),
        compiler_params=pltpu.CompilerParams(
            collective_id=1, has_side_effects=True, vmem_limit_bytes=VMEM_LIMIT
        ),
        name="share_terms",
    )(terms, names)


def table_kernel(layers, *refs):
    attn, narrow, wide = refs[layers:]
    for layer in range(layers):
        source = refs[layer]
        for t in range(10 * 9 + 2 * 34):
            tile = source[t // SHARE, 0, t % SHARE].astype(F32)
            if t < 90:
                at = slice(t % 9 * LANES, (t % 9 + 1) * LANES)
                if t < 72:
                    attn[layer, t // 9, 0, :, at] = tile
                else:
                    narrow[layer, t // 9 - 8, 0, :, at] = tile
            else:
                c, p = (t - 90) // 34, (t - 90) % 34
                width = min(LANES, FF - p * LANES)
                wide[layer, c, 0, :, p * LANES : p * LANES + width] = tile[:, :width]


def gradient_tables(gathered, adapters):
    layers = len(gathered)
    count = gathered[0].shape[0] // (adapters * SHARE_ROWS)
    gathered = [g.reshape(count, adapters, SHARE, 16, LANES) for g in gathered]

    def out_block(kinds, width):
        return pl.BlockSpec((layers, kinds, 1, R, width), lambda e: (0, 0, e, 0, 0))

    return pl.pallas_call(
        functools.partial(table_kernel, layers),
        grid=(adapters,),
        in_specs=[pl.BlockSpec((count, 1, SHARE, 16, LANES), lambda e: (0, e, 0, 0, 0))] * layers,
        out_specs=[out_block(8, D), out_block(2, D), out_block(2, FF)],
        out_shape=[
            struct((layers, 8, adapters, R, D), F32),
            struct((layers, 2, adapters, R, D), F32),
            struct((layers, 2, adapters, R, FF), F32),
        ],
        compiler_params=pltpu.CompilerParams(vmem_limit_bytes=VMEM_LIMIT),
        name="gradient_tables",
    )(*gathered)


BACKWARD_STEPS = (WIDE // TILE, PAIRS, 1, H // TWIN, PAIRS)
BACKWARD_AT = (0, 9, 14, 15, 15 + H // TWIN)
SHARE_AT, PASS_AT, GATHER_AT = 7, 9, 10


def backward_kernel(adapters, spread, *refs):
    (
        gradient, w_2, gate, down_2, inner_down, inner_up, w_1, w_1_odd, up_1, narrow, normed_two_in, vec, w_o, attn,
        label, inner_o, attended, bias, stats, w_qkv, w_qkv_odd, up, inner_qkv, middle_in, qkv_in, hidden_in, normed_in,
    ) = refs[:27]
    refs = refs[27:]
    if adapters:
        terms, half, refs = refs[0], refs[1], refs[2:]
    new_gradient, new_terms = refs[:2]
    refs = refs[2:]
    if adapters:
        pair, gathered, other_half, names, refs = refs[0], refs[1], refs[2], refs[3], refs[4:]
    (
        d_branch, d_inner_down, d_inner_up, wide, residual, d_normed, heads, stat_t, delta_t, load_sem,
    ) = refs[:10]
    refs = refs[10:]
    i = pl.program_id(0)
    _, middle_at, turn_at, att_at, input_at = BACKWARD_AT
    last = input_at + PAIRS - 1

    def at_step(k):
        return pl.when(i == k)

    def place(t):
        return t if spread == SHARE else t // SHARE * spread + t % SHARE

    def put(table, value):
        for p in range(D // LANES):
            tile = value[:, p * LANES : (p + 1) * LANES]
            new_terms[place(table * (D // LANES) + p)] = tile.astype(BF16)

    def load_middle():
        return pltpu.make_async_copy(middle_in, residual, load_sem.at[0])

    def load_qkv():
        return pltpu.make_async_copy(qkv_in, wide.at[:, : 3 * D], load_sem.at[1])

    def load_hidden():
        return pltpu.make_async_copy(hidden_in, residual, load_sem.at[0])

    def load_normed_two():
        return pltpu.make_async_copy(normed_two_in, d_branch, load_sem.at[2])

    def load_normed():
        return pltpu.make_async_copy(normed_in, d_branch, load_sem.at[2])

    if adapters:
        share_start, share_sum, share_finish = share_plan(
            adapters, False, terms, names, pair, *refs[:7]
        )
        swap_sem = refs[7]
        start, events, finish = gather_plan(pair, gathered, None, *refs[8:])
        swap = pltpu.make_async_remote_copy(
            src_ref=half,
            dst_ref=other_half,
            send_sem=swap_sem.at[0],
            recv_sem=swap_sem.at[1],
            device_id=(lax.axis_index("fsdp"), 1 - lax.axis_index("seq")),
            device_id_type=MESH,
        )
        at_step(0)(share_start)
        at_step(GATHER_AT + 12)(swap.start)
        at_step(SHARE_AT)(share_sum)
        at_step(PASS_AT)(share_finish)

        @at_step(GATHER_AT)
        def _():
            start(False)

        steps = {}
        for when, event in events:
            steps.setdefault(min(GATHER_AT + 1 + int(when), last), []).append(event)
        for k, due in steps.items():

            @at_step(k)
            def _(due=due):
                for event in due:
                    event()

    @pl.when(i < middle_at)
    def _():
        @at_step(0)
        def _():
            load_middle().start()
            value = gradient[...].astype(BF16)
            d_branch[...] = value
            d_inner_down[...] = dot_t(value, narrow[0, 1]).astype(BF16)
            put(9, dot_l(inner_down[...], value))
            for t in (158, 159):
                new_terms[place(t)] = jnp.zeros((R, LANES), BF16)
            if spread > SHARE:
                for k in range(SHARE, new_terms.shape[0], spread):
                    new_terms[k] = label[...]

        left = FF - i * TILE
        d_act = dot_both_t(d_branch[...], matrix(w_2), d_inner_down[...], down_2[0, 0].T)
        x = gate[...].astype(F32)
        t = gelu_parts(x)
        half = 0.5 * (1.0 + t)
        slope = half + 0.5 * x * (1.0 - t * t) * (
            0.7978845608028654 * (1.0 + 3 * 0.044715 * x * x)
        )
        keep = lax.broadcasted_iota(jnp.int32, (1, TILE), 1) < left
        value = jnp.where(keep, slope * d_act, 0.0).astype(BF16)
        wide[:, pl.ds(pl.multiple_of(i * TILE, LANES), TILE)] = value
        made = (
            dot_l(inner_up[...], value).astype(BF16),
            dot_l(d_inner_down[...], (x * half).astype(BF16)).astype(BF16),
        )

        def put_wide(panels):
            for kind in range(2):
                for p in panels:
                    tile = made[kind][:, p * LANES : (p + 1) * LANES]
                    new_terms[place(90 + 34 * kind + 4 * i + p)] = tile

        put_wide(range(2))

        @pl.when(i < middle_at - 1)
        def _():
            put_wide(range(2, 4))


    @pl.when(jnp.logical_and(i >= middle_at, i < turn_at))
    def _():
        at_step(middle_at)(load_normed_two().start)

        @pl.when(i < turn_at - 1)
        def _():
            w = jnp.concatenate([matrix(w_1, 34), matrix(w_1_odd, 34)], axis=0)
            d_normed[i - middle_at] = dot_t(wide[:, : 34 * LANES], w)

        @at_step(turn_at - 1)
        def _():
            w = jnp.concatenate([matrix(w_1, 34), up_1[0, 0, :, : 34 * LANES]], axis=0)
            value = dot_t(wide[:, : 34 * LANES], w)
            d_normed[PAIRS - 1, :, :LANES] = value[:, :LANES]
            d_inner_up[...] = value[:, LANES : LANES + R].astype(BF16)

    def joined():
        parts = [d_normed[k] for k in range(PAIRS - 1)]
        return jnp.concatenate(parts + [d_normed[PAIRS - 1, :, :LANES]], axis=1)

    @at_step(turn_at)
    def _():
        load_qkv().start()
        load_middle().wait()
        d_two = joined() + dot(d_inner_up[...], narrow[0, 0])
        value = gradient[...] + layer_norm_back(d_two, residual[...], vec[2:3])
        load_hidden().start()
        new_gradient[...] = value
        d_out = value.astype(BF16)
        d_inner_o = dot_t(d_out, attn[0, 7]).astype(BF16)
        wide[:, 3 * D :] = (dot_t(d_out, matrix(w_o)) + dot(d_inner_o, attn[0, 3])).astype(BF16)
        put(3, dot_l(d_inner_o, attended[...]))
        put(7, dot_l(inner_o[...], d_out))
        load_normed_two().wait()
        put(8, dot_l(d_inner_up[...], d_branch[...]))
        load_normed().start()
        load_qkv().wait()
        rows = gradient.shape[0]
        lane = lax.broadcasted_iota(jnp.int32, (rows, LANES), 1)
        delta = jnp.zeros((rows, LANES), F32)
        marked = (first_lane(rows, F32(1.0)), bias[...], None)
        for h in range(H):
            for c in range(3):
                part = wide[:, c * D + h * HD : c * D + (h + 1) * HD]
                heads[c, h] = pad_lanes(part, marked[c])
            do = wide[:, 3 * D + h * HD : 3 * D + (h + 1) * HD]
            heads[3, h] = pad_lanes(do)
            o = attended[:, h * HD : (h + 1) * HD].astype(F32)
            d = jnp.sum(do.astype(F32) * o, axis=1, keepdims=True)
            delta = jnp.where(lane == h, d, delta)
        stat_t[...] = stats[...].T
        delta_t[...] = delta.T

    @pl.when(jnp.logical_and(i >= att_at, i < input_at))
    def _():
        for twin in range(TWIN):
            h = (i - att_at) * TWIN + twin
            q, k, do = heads[0, h], heads[1, h], heads[3, h]
            p = jnp.exp2(dot_t(k, q) * C2 - stat_t[pl.ds(h, 1), :])
            dv = dot(p.astype(BF16), do)
            dp = dot_t(heads[2, h], do)
            ds = (p * (dp - delta_t[pl.ds(h, 1), :])).astype(BF16)
            dk = dot(ds, q)
            dq = dot(k.T, ds)
            heads[2, h] = dv.astype(BF16)
            heads[1, h] = (dk * SCALE).astype(BF16)
            heads[0, h] = (dq * SCALE).astype(BF16).T

    @pl.when(i >= input_at)
    def _():
        @at_step(input_at)
        def _():
            load_normed().wait()
            for c in range(3):
                for h in range(H):
                    wide[:, c * D + h * HD : c * D + (h + 1) * HD] = heads[c, h][:, :HD]
            for c in range(3):
                part = wide[:, c * D : (c + 1) * D]
                put(4 + c, dot_l(inner_qkv[:, c * R : (c + 1) * R], part))

        @pl.when(i < last)
        def _():
            w = jnp.concatenate([matrix(w_qkv), matrix(w_qkv_odd)], axis=0)
            d_normed[i - input_at] = dot_t(wide[:, : 3 * D], w)

        @at_step(last)
        def _():
            w = jnp.concatenate([matrix(w_qkv), up[0]], axis=0)
            value = dot_t(wide[:, : 3 * D], w)
            d_normed[PAIRS - 1, :, :LANES] = value[:, :LANES]
            inner = value[:, LANES : LANES + 3 * R].astype(BF16)
            made = dot_l(inner, d_branch[...])
            for c in range(3):
                put(c, made[c * R : (c + 1) * R])
            load_hidden().wait()
            d_one = joined() + dot(inner, attn[0, 0:3].reshape(3 * R, D))
            new_gradient[...] += layer_norm_back(d_one, residual[...], vec[0:1])

    if adapters:

        @at_step(last)
        def _():
            finish()
            swap.wait()


def layer_backward(
    layer, gradient, saved, weights, tables, bias, label, spread, adapters=0, terms=None, half=None
):
    hidden, normed, inner_qkv, qkv, stats, attended, inner_o, middle, normed_two, inner_up, gate, inner_down = saved
    w_qkv, w_o, w_1, w_2, vectors, _ = weights
    attn, narrow, wide, up_diagonal = tables
    rows = gradient.shape[0]

    def step(i, k):
        return jnp.minimum(jnp.maximum(i - BACKWARD_AT[k], 0), BACKWARD_STEPS[k] - 1)

    def cols(count, width, k):
        return pl.BlockSpec((count, width), lambda i: (0, step(i, k)))

    hbm = pl.BlockSpec(memory_space=pl.ANY)
    operands = [
        (whole((rows, D)), gradient),
        (unit_block(TILE // 16, 9, lambda i: (TILES_AT[3] // 9 * 16 // TILE + step(i, 0), 0, 0, 0)), w_2),
        (cols(rows, TILE, 0), gate),
        (pl.BlockSpec((1, 1, R, TILE), lambda i: (layer, 1, 0, step(i, 0))), wide),
        (whole((rows, R)), inner_down),
        (whole((rows, R)), inner_up),
        (unit_block(8, PANELS[2], lambda i: (9 + 2 * step(i, 1), 0, 0, 0)), w_1),
        (unit_block(8, PANELS[2], lambda i: (10 + jnp.minimum(2 * step(i, 1), 7), 0, 0, 0)), w_1),
        (of_layer(layer, 1, R, WIDE), wide),
        (of_layer(layer, 2, R, D), narrow),
        (hbm, normed_two),
        (whole((8, D)), vectors),
        (OUT_BLOCK, w_o),
        (of_layer(layer, 8, R, D), attn),
        (whole((R, LANES)), label),
        (whole((rows, R)), inner_o),
        (whole((rows, D)), attended),
        (whole((rows, LANES - HD)), bias),
        (whole((rows, LANES)), stats),
        (unit_block(8, 27, lambda i: (2 * step(i, 4), 0, 0, 0)), w_qkv),
        (unit_block(8, 27, lambda i: (jnp.minimum(2 * step(i, 4) + 1, 8), 0, 0, 0)), w_qkv),
        (of_layer(layer, 3 * R, 3 * D), up_diagonal),
        (whole((rows, 3 * R)), inner_qkv),
        (hbm, middle),
        (hbm, qkv),
        (hbm, hidden),
        (hbm, normed),
    ]
    outs = [
        (whole((rows, D)), struct((rows, D), F32)),
        (whole((32 * spread, R, LANES)), struct((32 * spread, R, LANES), BF16)),
    ]
    scratch = [
        pltpu.VMEM((rows, D), BF16),
        pltpu.VMEM((rows, R), BF16),
        pltpu.VMEM((rows, R), BF16),
        pltpu.VMEM((rows, WIDE), BF16),
        pltpu.VMEM((rows, D), F32),
        pltpu.VMEM((PAIRS, rows, PAIR), F32),
        pltpu.VMEM((4, H, rows, LANES), BF16),
        pltpu.VMEM((LANES, rows), F32),
        pltpu.VMEM((LANES, rows), F32),
        pltpu.SemaphoreType.DMA((3,)),
    ]
    params = dict(vmem_limit_bytes=VMEM_MOST)
    if adapters:
        operands += [(hbm, terms), (hbm, half)]
        block = 2 * adapters * SHARE_ROWS
        outs += [(hbm, struct((block, LANES), BF16)), (hbm, struct((16 * block, LANES), BF16))]
        outs += [(hbm, struct(half.shape, BF16))]
        outs += [(whole((terms.shape[0], LANES)), struct((terms.shape[0], LANES), F32))]
        scratch += share_scratch(terms.shape[0], adapters, SHARE + 1) + [pltpu.SemaphoreType.DMA((2,))]
        scratch += gather_semaphores()
        params.update(collective_id=4, has_side_effects=True)
    return pl.pallas_call(
        functools.partial(backward_kernel, adapters, spread),
        grid=(sum(BACKWARD_STEPS),),
        in_specs=[spec for spec, _ in operands],
        out_specs=[spec for spec, _ in outs],
        out_shape=[shape for _, shape in outs],
        scratch_shapes=scratch,
        cost_estimate=pl.CostEstimate(
            flops=2 * rows * D * (4 * D + 2 * FF) + 20 * rows * rows * D,
            bytes_accessed=2 * D * (4 * D + 2 * FF) + 40 * rows * D,
            transcendentals=H * rows * rows,
        ),
        compiler_params=pltpu.CompilerParams(**params),
        name="layer_backward_share" if adapters else "layer_backward",
    )(*[operand for _, operand in operands])


VECTOR_ROWS = 240


def read_vectors(block, vectors, b_1, rows):
    rows[...] = block[...].astype(F32)
    for p in range(D // LANES):
        vectors[:, p * LANES : (p + 1) * LANES] = rows[pl.ds(p, 8, stride=D // LANES), :]
    b_1[...] = jnp.zeros_like(b_1)
    first = 8 * D // LANES
    for p in range(-(-FF // LANES)):
        width = min(LANES, FF - p * LANES)
        b_1[:, p * LANES : p * LANES + width] = rows[first + p : first + p + 1, :width]


def layer_vectors(flat):
    return pl.pallas_call(
        read_vectors,
        grid=(1,),
        in_specs=[pl.BlockSpec((VECTOR_ROWS, LANES), lambda i: (16 * TILES_END // VECTOR_ROWS, 0))],
        out_specs=[whole((8, D)), whole((1, WIDE))],
        out_shape=[struct((8, D), F32), struct((1, WIDE), F32)],
        scratch_shapes=[pltpu.VMEM((VECTOR_ROWS, LANES), F32)],
        name="layer_vectors",
    )(flat)


def prepare_kernel(
    scalars, attn_in, narrow_in, wide_in, mine, other, block, attn, narrow, wide, diagonal, bias, hidden, label,
    vectors, b_1, rows,
):
    slot = scalars[5]
    length, live = scalars[2 + slot], jnp.where(slot < scalars[4], 1, 0)
    read_vectors(block, vectors, b_1, rows)
    label[...] = jnp.full(label.shape, scalars[slot], jnp.int32).astype(F32).astype(BF16)
    attn[...] = attn_in[:, :, 0]
    narrow[...] = narrow_in[:, :, 0]
    wide[...] = jnp.zeros_like(wide)
    wide[:, :, :, :FF] = wide_in[:, :, 0]
    diagonal[...] = jnp.zeros_like(diagonal)
    for layer in range(attn.shape[0]):
        for c in range(3):
            diagonal[layer, c * R : (c + 1) * R, c * D : (c + 1) * D] = attn_in[layer, 4 + c, 0]
    bias[...] = key_bias(bias.shape[0], length)
    half = mine.shape[1]
    row = lax.broadcasted_iota(jnp.int32, (half, 1), 0)

    def place(at, value):
        keep = jnp.where(row + at < length, live, 0) > 0
        hidden[at : at + half] = jnp.where(keep, value.astype(F32), 0.0)

    for first in range(2):

        @pl.when(slot == first)
        def _(first=first):
            place(first * half, mine[0])
            place((1 - first) * half, other[...])


def prepare(scalars, attention_table, narrow_table, wide_table, activations, other, flat):
    layers = attention_table.shape[0]
    rows = 2 * other.shape[0]

    def picked(kinds, width):
        return pl.BlockSpec((layers, kinds, 1, R, width), lambda i, k: (0, 0, k[k[5]], 0, 0))

    def full(*shape):
        return pl.BlockSpec(shape, lambda i, k: (0,) * len(shape))

    shapes = [
        ((layers, 8, R, D), BF16),
        ((layers, 2, R, D), BF16),
        ((layers, 2, R, WIDE), BF16),
        ((layers, 3 * R, 3 * D), BF16),
        ((rows, LANES - HD), BF16),
        ((rows, D), F32),
        ((R, LANES), BF16),
        ((8, D), F32),
        ((1, WIDE), F32),
    ]
    return pl.pallas_call(
        prepare_kernel,
        grid_spec=pltpu.PrefetchScalarGridSpec(
            num_scalar_prefetch=1,
            grid=(1,),
            in_specs=[
                picked(8, D),
                picked(2, D),
                picked(2, FF),
                pl.BlockSpec((1,) + other.shape, lambda i, k: (k[5], 0, 0)),
                full(*other.shape),
                pl.BlockSpec((VECTOR_ROWS, LANES), lambda i, k: (16 * TILES_END // VECTOR_ROWS, 0)),
            ],
            out_specs=[full(*shape) for shape, _ in shapes],
            scratch_shapes=[pltpu.VMEM((VECTOR_ROWS, LANES), F32)],
        ),
        out_shape=[struct(*shape) for shape in shapes],
        compiler_params=pltpu.CompilerParams(vmem_limit_bytes=VMEM_LIMIT),
        name="prepare",
    )(scalars, attention_table, narrow_table, wide_table, activations, other, flat)


def local(
    activations,
    group_image_count,
    image_adapter_index,
    lengths,
    frozen,
    attention_adapter_weights,
    narrow_adapter_weights,
    broad_adapter_weights,
    cotangent,
):
    slots, local_len, _ = activations.shape
    seq_parts = lax.axis_size("seq")
    fsdp_parts = lax.axis_size("fsdp")
    device_count = seq_parts * fsdp_parts
    me = lax.axis_index("seq")
    seq_total = local_len * seq_parts
    layer_count = frozen.shape[0]
    adapters = attention_adapter_weights.shape[2]
    parts = seq_parts // slots
    on_block = (fsdp_parts, seq_parts, slots, layer_count) == (16, 2, 2, 2)
    slot = me // parts
    part = me % parts
    tokens = seq_total // parts
    groups = [[s * parts + p for p in range(parts)] for s in range(slots)]

    def to_image(v):
        if parts == 1 and slots == 2:
            mine = lax.dynamic_index_in_dim(v, slot, 0, keepdims=False)
            other = lax.dynamic_index_in_dim(v, 1 - slot, 0, keepdims=False)
            other = lax.ppermute(other, "seq", [(0, 1), (1, 0)])
            return jnp.where(
                slot == 0,
                jnp.concatenate([mine, other], 0),
                jnp.concatenate([other, mine], 0),
            )
        whole = lax.all_gather(v, "seq", axis=1, tiled=True)
        whole = lax.dynamic_index_in_dim(whole, slot, 0, keepdims=False)
        return lax.dynamic_slice_in_dim(whole, part * tokens, tokens, 0)

    def half_of(v, which):
        return lax.dynamic_slice_in_dim(v, which * local_len, local_len, 0)

    def to_tokens(v, other=None):
        if parts == 1 and slots == 2:
            mine = half_of(v, slot)
            if other is None:
                other = lax.ppermute(half_of(v, 1 - slot), "seq", [(0, 1), (1, 0)])
            return jnp.where(slot == 0, jnp.stack([mine, other]), jnp.stack([other, mine]))
        whole = lax.all_gather(v, "seq", axis=0, tiled=True).reshape(slots, seq_total, -1)
        return lax.dynamic_slice_in_dim(whole, me * local_len, local_len, 1)

    length = lax.dynamic_slice_in_dim(lengths, slot, 1, 0)
    adapter = lax.dynamic_index_in_dim(image_adapter_index, slot, 0, keepdims=False)
    is_live = slot < group_image_count[0]
    positions = part * tokens + jnp.arange(tokens, dtype=jnp.int32)
    row_mask = ((positions < length[0]) & is_live).astype(F32)[:, None]
    shards = lax.optimization_barrier(frozen.reshape(layer_count, -1, LANES))
    tiles = -(-(TILES_END + TILES_VECTORS) // (2 * fsdp_parts)) * 2
    if on_block:
        flat, *shards = first_gather([shards[layer] for layer in range(layer_count)], tiles)
    else:
        steps = [(d, d + 1) for d in range(fsdp_parts - 1)]
        steps = (steps, [(b, a) for a, b in steps])
        index = lax.axis_index("fsdp").astype(jnp.int32).reshape(1)
        shards = [lay_shard(index, shards[layer], tiles, steps) for layer in range(layer_count)]
    if on_block:
        other = lax.dynamic_index_in_dim(activations, 1 - slot, 0, keepdims=False)
        other = lax.ppermute(other, "seq", [(0, 1), (1, 0)])
        scalars = jnp.concatenate(
            [image_adapter_index, lengths, group_image_count, slot.astype(jnp.int32)[None]]
        )
        prepared = prepare(
            scalars,
            attention_adapter_weights,
            narrow_adapter_weights,
            broad_adapter_weights,
            activations,
            other,
            flat,
        )
        tables, (bias, hidden, label) = prepared[:4], prepared[4:7]
    else:
        def pick(table):
            return lax.dynamic_index_in_dim(table, adapter, 2, keepdims=False)

        attention_adapters = pick(attention_adapter_weights)
        narrow_adapters = pick(narrow_adapter_weights)
        wide_adapters = pick(broad_adapter_weights)
        wide_adapters = jnp.pad(wide_adapters, ((0, 0), (0, 0), (0, 0), (0, WIDE - FF)))
        lane = lax.broadcasted_iota(jnp.int32, (tokens, LANES - HD), 1)
        key = lax.broadcasted_iota(jnp.int32, (tokens, LANES - HD), 0)
        bias = jnp.where((lane == 0) & (key >= length[0]), NEG, 0.0).astype(BF16)
        hidden = to_image(activations).astype(F32) * row_mask
        up_diagonals = jnp.stack(
            [
                jnp.concatenate(
                    [
                        jnp.pad(attention_adapters[layer, 4 + c], ((0, 0), (c * D, (2 - c) * D)))
                        for c in range(3)
                    ]
                )
                for layer in range(layer_count)
            ]
        )
    stored = []
    weights = []
    for layer in range(layer_count):
        if not on_block:
            flat = lax.all_gather(shards[layer], "fsdp", axis=0, tiled=True)
            flat = jnp.pad(flat, ((0, 16 * TILES_HELD - flat.shape[0]), (0, 0)))
        if layer == layer_count - 1:
            cotangent, flat = lax.optimization_barrier((cotangent, flat))
            d_output = to_image(cotangent)
        w_qkv, w_o, w_1, w_2 = (flat.reshape(-1, panels, 16, LANES) for panels in PANELS)
        if on_block:
            vectors, b_1 = prepared[7:9] if layer == 0 else layer_vectors(flat)
            weights.append((w_qkv, w_o, w_1, w_2, vectors, b_1))
        else:
            vectors = lax.slice_in_dim(flat, 16 * TILES_END, 16 * TILES_END + 106, axis=0).reshape(-1)
            vectors, b_1 = vectors[: 8 * D].reshape(8, D).astype(F32), vectors[8 * D : 8 * D + FF]
            b_1 = jnp.pad(b_1.astype(F32), (0, WIDE - FF))[None, :]
            attn, narrow, wide = attention_adapters[layer], narrow_adapters[layer], wide_adapters[layer]
            weights.append((w_qkv, w_o, w_1, w_2, vectors, attn, narrow, wide))
        keys = None
        if on_block:
            shard = shards[layer + 1] if layer + 1 < layer_count else None
            made = layer_forward(layer, bias, hidden, weights[layer], tables, shard)
            normed, inner_qkv, qkv, attended, stats, inner_o, middle = made[:7]
            normed_two, inner_up, gate, inner_down, next_hidden = made[7:12]
            flat = made[12] if shard is not None else None
        else:
            normed, inner_qkv, qkv = qkv_forward(hidden, w_qkv, vectors, attn)
            keys = lax.all_gather(
                qkv[:, D:], "seq", axis=0, tiled=True, axis_index_groups=groups
            )
            attended, stats = attn_fwd(length, qkv, keys)
            inner_o, middle, normed_two, inner_up, gate, activated = up_forward(
                attended, hidden, w_o, vectors, attn, narrow, w_1, b_1, wide
            )
            inner_down, next_hidden = down_forward(
                activated, middle, w_2, vectors[7:8], narrow, wide
            )
        stored.append(
            (
                hidden,
                normed,
                inner_qkv,
                qkv,
                keys,
                stats,
                attended,
                inner_o,
                middle,
                normed_two,
                inner_up,
                gate,
                inner_down,
            )
        )
        hidden = next_hidden
    output = (hidden * row_mask).astype(BF16)
    other_half = None
    gradient = d_output.astype(F32) * row_mask
    collected = [None] * layer_count
    terms = None
    for layer in reversed(range(layer_count)):
        (
            layer_input,
            normed,
            inner_qkv,
            qkv,
            keys,
            stats,
            attended,
            inner_o,
            middle,
            normed_two,
            inner_up,
            gate,
            inner_down,
        ) = stored[layer]
        if not on_block:
            w_qkv, w_o, w_1, w_2, vectors, attn, narrow, wide = weights[layer]
        if on_block:
            saved = (
                layer_input, normed, inner_qkv, qkv, stats, attended, inner_o, middle, normed_two, inner_up,
                gate, inner_down,
            )
            hosting = layer + 1 < layer_count
            spread = SHARE if layer == 0 else SHARE + 1
            made = layer_backward(
                layer,
                gradient,
                saved,
                weights[layer],
                tables,
                bias,
                label,
                spread,
                adapters if hosting else 0,
                terms,
                half_of(output, 1 - slot),
            )
            gradient, terms = made[:2]
            terms = terms.reshape(device_count, spread, R, LANES)
            if hosting:
                collected[layer + 1], other_half, names = made[3:6]
            if layer == 0:
                sums = share_terms(terms, names, adapters)
                collected[layer] = gather_blocks(sums, 2, 16 * sums.shape[0])
            continue
        if not on_block:
            d_gate, g_wide, d_inner_up, g_up_2 = gate_backward(
                gradient, w_2, gate, narrow, wide, inner_down, inner_up
            )
            d_middle, d_attended, g_middle = middle_backward(
                d_gate, w_1, d_inner_up, narrow, normed_two, middle, gradient, vectors, w_o, attn,
                inner_o, attended,
            )
            d_qkv = attn_bwd(length, qkv, d_attended, attended, stats, keys)
            if parts > 1:
                d_keys = lax.psum_scatter(
                    d_qkv[1].astype(F32),
                    "seq",
                    scatter_dimension=0,
                    tiled=True,
                    axis_index_groups=groups,
                )
                d_qkv = jnp.concatenate([d_qkv[0], d_keys.astype(BF16)], axis=1)
            else:
                d_qkv = d_qkv[0]
            gradient, g_input = input_backward(
                d_qkv, w_qkv, attn, normed, inner_qkv, layer_input, d_middle, vectors
            )
        rows_narrow = jnp.concatenate(
            [
                g_input[: 3 * R],
                g_middle[:R],
                g_input[3 * R :],
                g_middle[R:],
                g_up_2,
            ]
        )
        rows_narrow = rows_narrow.astype(BF16)
        rows_wide = g_wide[:, :FF].astype(BF16)

        def shares(rows):
            share = -(-rows.shape[0] // device_count)
            rows = jnp.pad(rows, ((0, share * device_count - rows.shape[0]), (0, 0)))
            return rows.reshape(device_count, share * rows.shape[1])

        terms = [shares(rows_narrow), shares(rows_wide)]
        used = terms[0].shape[1] + terms[1].shape[1]
        label = jnp.broadcast_to(adapter.astype(BF16), (device_count, -used % LANES + LANES))
        terms = lax.all_to_all(
            jnp.concatenate(terms + [label], axis=1),
            ("fsdp", "seq"),
            split_axis=0,
            concat_axis=0,
            tiled=True,
        )
        choice = jnp.arange(adapters, dtype=F32)[:, None] == terms[:, used].astype(F32)[None, :]
        sums = jnp.dot(choice.astype(F32), terms.astype(F32), precision=lax.Precision.HIGHEST)
        sums = lax.all_gather(sums.astype(BF16), ("fsdp", "seq")).transpose(1, 0, 2)
        split = -(-10 * R // device_count) * D

        def table(part, count, width):
            part = part.reshape(adapters, -1, width)[:, : count * R]
            return part.reshape(adapters, count, R, width).transpose(1, 0, 2, 3).astype(F32)

        collected[layer] = (table(sums[:, :, :split], 10, D), table(sums[:, :, split:used], 2, FF))
    if on_block:
        grad_attn, grad_narrow, grad_wide = gradient_tables(collected, adapters)
    else:
        grad_attn = jnp.stack([entry[0][0:8] for entry in collected], axis=0)
        grad_narrow = jnp.stack([entry[0][8:10] for entry in collected], axis=0)
        grad_wide = jnp.stack([entry[1] for entry in collected], axis=0)
    output = to_tokens(output, other_half)
    input_grad = to_tokens((gradient * row_mask).astype(BF16)).astype(F32)
    return (output, input_grad, grad_attn, grad_narrow, grad_wide)


def solution(mesh):
    in_specs = (
        P("fsdp", "seq", None),
        P("fsdp"),
        P("fsdp"),
        P("fsdp"),
        P(None, "fsdp"),
        P(),
        P(),
        P(),
        P("fsdp", "seq", None),
    )
    out_specs = (P("fsdp", "seq", None), P("fsdp", "seq", None), P(), P(), P())
    return jax.shard_map(local, mesh=mesh, in_specs=in_specs, out_specs=out_specs, check_vma=False)
```

```python
import functools
import math

import jax
import jax.numpy as jnp
from jax import lax
from jax.experimental import pallas as pl
from jax.experimental.pallas import tpu as pltpu
from jax.sharding import PartitionSpec as P

D = 1152
HD = 72
H = 16
FF = 4304
R = 16
LANES = 128
BF16 = jnp.bfloat16
F32 = jnp.float32
MESH = pl.DeviceIdType.MESH
VMEM_LIMIT = 60 << 20
VMEM_MOST = 67043328
C2 = math.log2(math.e) / math.sqrt(HD)
SCALE = 1.0 / math.sqrt(HD)
NEG = -1e30
epsilon = 1e-06
CUT_OUT = 3 * D * D // LANES
CUT_UP = CUT_OUT + D * D // LANES
CUT_DOWN = CUT_UP + D * FF // LANES
CUT_VECTORS = CUT_DOWN + FF * D // LANES


def dot(a, b):
    return jnp.dot(a, b, preferred_element_type=F32)


def dot_t(a, b):
    return lax.dot_general(a, b, (((1,), (1,)), ((), ())), preferred_element_type=F32)


def dot_l(a, b):
    return lax.dot_general(a, b, (((0,), (0,)), ((), ())), preferred_element_type=F32)


PANELS = (3 * D // LANES, D // LANES, 36, D // LANES)
UNITS = (D // 16, D // 16, D // 16, FF // 16)
TILES_AT = (0, 1944, 2592, 5184)
TILES_END = 7605
TILES_VECTORS = 22
TILES_HELD = 7776
FLAT_AT = (0, CUT_OUT, CUT_UP, CUT_DOWN)
WIDE = PANELS[2] * LANES
UP_ROWS = 16 * FF // LANES
HALO = 1600


def lay_rows(d, own_rows, tiles, before, own, after, flat, held, turned):
    margin = 16 * PANELS[2]
    flat[0:HALO] = before.astype(F32)
    flat[HALO : HALO + own_rows] = own.astype(F32)
    flat[HALO + own_rows : 2 * HALO + own_rows] = after.astype(F32)
    flat_base = d * own_rows - HALO
    tile_base = d * tiles

    def span(at, units, panels):
        low = jnp.maximum(tile_base - at, 0) // panels
        high = jnp.maximum(tile_base + tiles - at + panels - 1, 0) // panels
        high = jnp.minimum(high, units)
        return low, jnp.maximum(high, low)

    for at, start, units, panels in zip(
        TILES_AT + (TILES_END,),
        FLAT_AT + (CUT_VECTORS,),
        UNITS + (TILES_VECTORS,),
        PANELS + (1,),
    ):
        low, high = span(at, units, panels)
        if start == CUT_UP:
            lane = lax.broadcasted_iota(jnp.int32, (8, LANES), 1)

            def up_units(b, carry):
                u = low + 8 * b
                source = pl.multiple_of(start + UP_ROWS * u - flat_base, 2)
                for j in range(16):
                    first, shift = (FF * j) // LANES, (FF * j) % LANES
                    turn = LANES - shift
                    now = flat[pl.ds(source + first, 8, stride=UP_ROWS), :]
                    now = pltpu.roll(now, turn, 1) if shift else now
                    for c in range(34):
                        value = now
                        if c < 33 or shift > LANES - FF % LANES:
                            now = flat[pl.ds(source + first + c + 1, 8, stride=UP_ROWS), :]
                            now = pltpu.roll(now, turn, 1) if shift else now
                            if shift:
                                value = jnp.where(lane < turn, value, now)
                        if c == 33:
                            value = jnp.where(lane < FF - 33 * LANES, value, 0.0)
                        turned[pl.ds(16 * c + j, 8, stride=16 * PANELS[2]), :] = value
                target = pl.multiple_of(16 * (at + PANELS[2] * u - tile_base) + margin, 16)
                held[pl.ds(target, 8 * 16 * PANELS[2]), :] = turned[...].astype(BF16)
                return carry

            turned[...] = jnp.zeros_like(turned)
            lax.fori_loop(0, (high - low + 7) // 8, up_units, 0)
        else:

            def unit(u, carry):
                source = pl.multiple_of(start + 16 * panels * u - flat_base, 16)
                target = pl.multiple_of(16 * (at + panels * u - tile_base) + margin, 16)
                for c in range(panels):
                    value = flat[pl.ds(source + c, 16, stride=panels), :]
                    held[pl.ds(target + 16 * c, 16), :] = value.astype(BF16)
                return carry

            lax.fori_loop(low, high, unit, 0)


def lay_kernel(own_rows, tiles, index_ref, before, own, after, out, flat, held, turned):
    margin = 16 * PANELS[2]
    lay_rows(index_ref[0], own_rows, tiles, before[...], own[...], after[...], flat, held, turned)
    out[...] = held[margin : margin + 16 * tiles]


def lay_scratch(own_rows, tiles):
    margin = 16 * PANELS[2]
    return [
        pltpu.VMEM((own_rows + 2 * HALO + 8 * UP_ROWS, LANES), F32),
        pltpu.VMEM((16 * tiles + 10 * margin, LANES), BF16),
        pltpu.VMEM((8 * margin, LANES), F32),
    ]


def lay_shard(index, shard, tiles, perms):
    own_rows = shard.shape[0]
    before = lax.ppermute(shard[own_rows - HALO :], "fsdp", perms[0])
    after = lax.ppermute(shard[:HALO], "fsdp", perms[1])
    vm = pl.BlockSpec(memory_space=pltpu.VMEM)
    return pl.pallas_call(
        functools.partial(lay_kernel, own_rows, tiles),
        in_specs=[pl.BlockSpec(memory_space=pltpu.SMEM), vm, vm, vm],
        out_specs=vm,
        out_shape=jax.ShapeDtypeStruct((16 * tiles, LANES), BF16),
        scratch_shapes=lay_scratch(own_rows, tiles),
        compiler_params=pltpu.CompilerParams(vmem_limit_bytes=VMEM_LIMIT),
        name="lay_shard",
    )(index, before, shard, after)


def pad_lanes(x, extra=None):
    if extra is None:
        extra = jnp.zeros((x.shape[0], LANES - HD), x.dtype)
    return jnp.concatenate([x, extra], axis=1)


def first_lane(rows, value):
    lane = lax.broadcasted_iota(jnp.int32, (rows, LANES - HD), 1)
    return jnp.where(lane == 0, value, 0.0).astype(BF16)


def key_bias(rows, length):
    key = lax.broadcasted_iota(jnp.int32, (rows, LANES - HD), 0)
    return first_lane(rows, jnp.where(key < length, 0.0, NEG))


def attn_fwd_kernel(offset, len_ref, qkv_ref, kv_ref, o_ref, st_ref, q_s, k_s, v_s):
    if kv_ref is None:
        kv_ref = qkv_ref
    rows, keys = qkv_ref.shape[0], kv_ref.shape[0]
    one = first_lane(rows, F32(1.0))
    bias = key_bias(keys, len_ref[0])
    for h in range(H):
        q_s[h] = pad_lanes(qkv_ref[:, h * HD : (h + 1) * HD], one)
        k_s[h] = pad_lanes(kv_ref[:, offset + h * HD : offset + (h + 1) * HD], bias)
        v_s[h] = pad_lanes(kv_ref[:, offset + D + h * HD : offset + D + (h + 1) * HD])
    st_ref[...] = jnp.zeros_like(st_ref)
    lane = lax.broadcasted_iota(jnp.int32, (rows, LANES), 1)

    def body(h, carry):
        s = dot_t(q_s[h], k_s[h])
        m = jnp.max(s, axis=1, keepdims=True)
        p = jnp.exp2((s - m) * C2)
        total = jnp.sum(p, axis=1, keepdims=True)
        o = dot(p.astype(BF16), v_s[h])
        q_s[h] = (o * (1.0 / total)).astype(BF16)
        st_ref[...] = jnp.where(lane == h, m * C2 + jnp.log2(total), st_ref[...])
        return carry

    lax.fori_loop(0, H, body, 0)
    for h in range(H):
        o_ref[:, h * HD : (h + 1) * HD] = q_s[h][:, :HD]


def attn_fwd(length, qkv, kv=None):
    rows = qkv.shape[0]
    keys = rows if kv is None else kv.shape[0]
    vm = pl.BlockSpec(memory_space=pltpu.VMEM)
    if kv is None:
        kernel = lambda a, b, *rest: attn_fwd_kernel(D, a, b, None, *rest)
        operands = (length, qkv)
    else:
        kernel = functools.partial(attn_fwd_kernel, 0)
        operands = (length, qkv, kv)
    return pl.pallas_call(
        kernel,
        in_specs=[pl.BlockSpec(memory_space=pltpu.SMEM)] + [vm] * (len(operands) - 1),
        out_specs=[vm, vm],
        out_shape=[
            jax.ShapeDtypeStruct((rows, D), BF16),
            jax.ShapeDtypeStruct((rows, LANES), F32),
        ],
        scratch_shapes=[
            pltpu.VMEM((H, rows, LANES), BF16),
            pltpu.VMEM((H, keys, LANES), BF16),
            pltpu.VMEM((H, keys, LANES), BF16),
        ],
        cost_estimate=pl.CostEstimate(
            flops=H * rows * keys * 256 * 4, bytes_accessed=rows * D * 8, transcendentals=H * rows * keys
        ),
        compiler_params=pltpu.CompilerParams(vmem_limit_bytes=VMEM_LIMIT),
        name="attention_forward",
    )(*operands)


def attn_bwd_kernel(
    offset, len_ref, qkv_ref, kv_ref, do_ref, o_ref, st_ref, dq_ref, dkv_ref, q_s, k_s, v_s, do_s, st_t, dl_t
):
    if kv_ref is None:
        kv_ref, dkv_ref = qkv_ref, dq_ref
    rows, keys = qkv_ref.shape[0], kv_ref.shape[0]
    one = first_lane(rows, F32(1.0))
    bias = key_bias(keys, len_ref[0])
    lane = lax.broadcasted_iota(jnp.int32, (rows, LANES), 1)
    delta = jnp.zeros((rows, LANES), F32)
    for h in range(H):
        q_s[h] = pad_lanes(qkv_ref[:, h * HD : (h + 1) * HD], one)
        k_s[h] = pad_lanes(kv_ref[:, offset + h * HD : offset + (h + 1) * HD], bias)
        v_s[h] = pad_lanes(kv_ref[:, offset + D + h * HD : offset + D + (h + 1) * HD])
        do = do_ref[:, h * HD : (h + 1) * HD]
        do_s[h] = pad_lanes(do)
        o = o_ref[:, h * HD : (h + 1) * HD].astype(F32)
        d = jnp.sum(do.astype(F32) * o, axis=1, keepdims=True)
        delta = jnp.where(lane == h, d, delta)
    st_t[...] = st_ref[...].T
    dl_t[...] = delta.T

    def body(h, carry):
        q, k, do = q_s[h], k_s[h], do_s[h]
        p = jnp.exp2(dot_t(k, q) * C2 - st_t[pl.ds(h, 1), :])
        dv = dot(p.astype(BF16), do)
        dp = dot_t(v_s[h], do)
        ds = (p * (dp - dl_t[pl.ds(h, 1), :])).astype(BF16)
        dk = dot(ds, q)
        dq = dot(k.T, ds)
        v_s[h] = dv.astype(BF16)
        k_s[h] = (dk * SCALE).astype(BF16)
        q_s[h] = (dq * SCALE).astype(BF16).T
        return carry

    lax.fori_loop(0, H, body, 0)
    for h in range(H):
        dq_ref[:, h * HD : (h + 1) * HD] = q_s[h][:, :HD]
        dkv_ref[:, offset + h * HD : offset + (h + 1) * HD] = k_s[h][:, :HD]
        dkv_ref[:, offset + D + h * HD : offset + D + (h + 1) * HD] = v_s[h][:, :HD]


def attn_bwd(length, qkv, do, o, st, kv=None):
    rows = qkv.shape[0]
    keys = rows if kv is None else kv.shape[0]
    vm = pl.BlockSpec(memory_space=pltpu.VMEM)
    if kv is None:
        kernel = lambda a, b, c, d, e, f, *rest: attn_bwd_kernel(
            D, a, b, None, c, d, e, f, None, *rest
        )
        operands = (length, qkv, do, o, st)
        outs = [jax.ShapeDtypeStruct((rows, 3 * D), BF16)]
    else:
        kernel = functools.partial(attn_bwd_kernel, 0)
        operands = (length, qkv, kv, do, o, st)
        outs = [jax.ShapeDtypeStruct((rows, D), BF16), jax.ShapeDtypeStruct((keys, 2 * D), BF16)]
    return pl.pallas_call(
        kernel,
        in_specs=[pl.BlockSpec(memory_space=pltpu.SMEM)] + [vm] * (len(operands) - 1),
        out_specs=[vm] * len(outs),
        out_shape=outs,
        scratch_shapes=[
            pltpu.VMEM((H, rows, LANES), BF16),
            pltpu.VMEM((H, keys, LANES), BF16),
            pltpu.VMEM((H, keys, LANES), BF16),
            pltpu.VMEM((H, rows, LANES), BF16),
            pltpu.VMEM((LANES, rows), F32),
            pltpu.VMEM((LANES, rows), F32),
        ],
        cost_estimate=pl.CostEstimate(
            flops=H * rows * keys * 256 * 10, bytes_accessed=rows * D * 16, transcendentals=H * rows * keys
        ),
        compiler_params=pltpu.CompilerParams(vmem_limit_bytes=VMEM_LIMIT),
        name="attention_backward",
    )(*operands)


LARGE_BLOCK = 4096


def gather_plan(
    src, out, stage, local_sem, z_recv, y_recv, b_recv, h_recv, c_recv_own, c_recv_z, c_recv_y, c_recv_b, c_recv_h,
    up_send, down_send, y_send, b_send, h_send, c_send_own, c_send_z, c_send_y, c_send_b, c_send_h, pieces=2,
):
    rows = src.shape[0]
    if rows >= LARGE_BLOCK:
        unit = rows // 6 // 16 * 16 + 16
        sizes = [unit, unit, rows // 2 - 2 * unit, rows // 2 - 2 * unit, unit]
        begins = [0, unit, 2 * unit, rows // 2, rows - 2 * unit]
    else:
        sizes = [rows // pieces] * pieces
        begins = [k * (rows // pieces) for k in range(pieces)]
    chunks, across_y = len(sizes), (len(sizes) + 1) // 2
    lend = chunks == 5
    x = lax.axis_index("seq")
    f = lax.axis_index("fsdp")
    z, y, c = f // 4, (f // 2) % 2, f % 2

    def place(zb, yb, j, side, cb=None):
        owner = (zb * 2 + yb) * 2 + (c if cb is None else cb)
        begin = jnp.where(side == 0, begins[j], rows - begins[j] - sizes[j])
        return pl.multiple_of(owner * rows + begin, 16), sizes[j]

    def view(spot):
        return out.at[pl.ds(spot[0], spot[1]), :]

    def device(zb, yb, cb, xb):
        return ((zb * 2 + yb) * 2 + cb, xb)

    up, down = device(z + 1, y, c, x), device(z - 1, y, c, x)
    beside, across, mate = device(z, 1 - y, c, x), device(z, y, c, 1 - x), device(z, y, 1 - c, x)

    def copy(spot, send, recv, to, source=None):
        return pltpu.make_async_remote_copy(
            src_ref=view(spot) if source is None else source,
            dst_ref=view(spot),
            send_sem=send,
            recv_sem=recv,
            device_id=to,
            device_id_type=MESH,
        )

    def arrived(spot, recv):
        copy(spot, local_sem.at[1], recv, mate).wait_recv()

    def own(j):
        begin = jnp.where(x == 0, begins[j], rows - begins[j] - sizes[j])
        return src.at[pl.ds(pl.multiple_of(begin, 16), sizes[j]), :]

    whole = (pl.multiple_of(f * rows, 16), rows)
    keep = pltpu.make_async_copy(src if stage is None else stage, view(whole), local_sem.at[0])

    def greet():
        barrier = pltpu.get_barrier_semaphore()
        for to in (beside, across, mate):
            pl.semaphore_signal(barrier, inc=1, device_id=to, device_id_type=MESH)

        @pl.when(z < 3)
        def _():
            pl.semaphore_signal(barrier, inc=1, device_id=up, device_id_type=MESH)

        @pl.when(z > 0)
        def _():
            pl.semaphore_signal(barrier, inc=1, device_id=down, device_id_type=MESH)

        pl.semaphore_wait(barrier, 3 + jnp.where(z < 3, 1, 0) + jnp.where(z > 0, 1, 0))

    def start(first=True):
        if first:
            greet()
        for j in range(chunks):
            spot = place(z, y, j, x)

            @pl.when(z < 3)
            def _():
                copy(spot, up_send.at[z, j], z_recv.at[z, j], up, own(j)).start()

            @pl.when(z > 0)
            def _():
                copy(spot, down_send.at[z, j], z_recv.at[z, j], down, own(j)).start()

            if j < across_y:
                copy(spot, y_send.at[z, j], y_recv.at[z, j], beside, own(j)).start()
        copy(whole, c_send_own.at[0], c_recv_own.at[0], mate, src).start()
        if stage is None:
            keep.start()
        else:
            fetch = pltpu.make_async_copy(src, stage, local_sem.at[0])
            fetch.start()
            fetch.wait()
            keep.start()

    def z_event(d, j):
        def flow(zb, onward, to, sends):
            spot = place(zb, y, j, x)
            arrived(spot, z_recv.at[zb, j])

            @pl.when(onward)
            def _():
                copy(spot, sends.at[zb, j], z_recv.at[zb, j], to).start()

            if j == 0 and lend:
                copy(spot, b_send.at[zb], b_recv.at[zb], across).start()
            if j < across_y:
                copy(spot, y_send.at[zb, j], y_recv.at[zb, j], beside).start()
            copy(spot, c_send_z.at[zb, j], c_recv_z.at[zb, j], mate).start()

        @pl.when(z - d >= 0)
        def _():
            flow(z - d, z < 3, up, up_send)

        @pl.when(z + d <= 3)
        def _():
            flow(z + d, z > 0, down, down_send)

    def each(d, act):
        if d == 0:
            act(z)
            return

        @pl.when(z - d >= 0)
        def _():
            act(z - d)

        @pl.when(z + d <= 3)
        def _():
            act(z + d)

    def y_event(d, j):
        def act(zb):
            spot = place(zb, 1 - y, j, x)
            arrived(spot, y_recv.at[zb, j])
            copy(spot, h_send.at[zb, j], h_recv.at[zb, j], across).start()
            copy(spot, c_send_y.at[zb, j], c_recv_y.at[zb, j], mate).start()

        each(d, act)

    def b_event(d):
        def act(zb):
            spot = place(zb, y, 0, 1 - x)
            arrived(spot, b_recv.at[zb])
            copy(spot, c_send_b.at[zb], c_recv_b.at[zb], mate).start()

        each(d, act)

    def h_event(d, j):
        def act(zb):
            spot = place(zb, 1 - y, j, 1 - x)
            arrived(spot, h_recv.at[zb, j])
            copy(spot, c_send_h.at[zb, j], c_recv_h.at[zb, j], mate).start()

        each(d, act)

    events = []
    for d in range(4):
        for j in range(chunks):
            at = (d - 1) * chunks + j + 1 if d else 0
            if d:
                events.append((at, functools.partial(z_event, d, j)))
                if j == 0 and lend:
                    events.append((at + 2, functools.partial(b_event, d)))
            if j < across_y:
                ready = at + 1.5 if d else j + 1
                events.append((ready, functools.partial(y_event, d, j)))
                events.append((ready + 2, functools.partial(h_event, d, j)))
    def finish():
        keep.wait()
        other = 1 - c

        def core_spot(zb, yb, j, side):
            return place(zb, yb, j, side, other)

        arrived((pl.multiple_of(((z * 2 + y) * 2 + other) * rows, 16), rows), c_recv_own.at[0])
        copy(whole, c_send_own.at[0], c_recv_own.at[0], mate).wait_send()
        for d in range(4):
            def drain(zb, d=d):
                for j in range(chunks):
                    if d:
                        arrived(core_spot(zb, y, j, x), c_recv_z.at[zb, j])
                        copy(place(zb, y, j, x), c_send_z.at[zb, j], c_recv_z.at[zb, j], mate).wait_send()
                    if j < across_y:
                        arrived(core_spot(zb, 1 - y, j, x), c_recv_y.at[zb, j])
                        arrived(core_spot(zb, 1 - y, j, 1 - x), c_recv_h.at[zb, j])
                        spot = place(zb, 1 - y, j, x)
                        copy(spot, c_send_y.at[zb, j], c_recv_y.at[zb, j], mate).wait_send()
                        copy(spot, h_send.at[zb, j], h_recv.at[zb, j], across).wait_send()
                        spot = place(zb, 1 - y, j, 1 - x)
                        copy(spot, c_send_h.at[zb, j], c_recv_h.at[zb, j], mate).wait_send()
                        spot = place(zb, y, j, x)
                        copy(spot, y_send.at[zb, j], y_recv.at[zb, j], beside).wait_send()
                if d and lend:
                    arrived(core_spot(zb, y, 0, 1 - x), c_recv_b.at[zb])
                    spot = place(zb, y, 0, 1 - x)
                    copy(spot, c_send_b.at[zb], c_recv_b.at[zb], mate).wait_send()
                    spot = place(zb, y, 0, x)
                    copy(spot, b_send.at[zb], b_recv.at[zb], across).wait_send()

            each(d, drain)
            for j in range(chunks):
                @pl.when(jnp.logical_and(z - d >= 0, z < 3))
                def _():
                    zb = z - d
                    copy(place(zb, y, j, x), up_send.at[zb, j], z_recv.at[zb, j], up).wait_send()

                @pl.when(jnp.logical_and(z + d <= 3, z > 0))
                def _():
                    zb = z + d
                    copy(place(zb, y, j, x), down_send.at[zb, j], z_recv.at[zb, j], down).wait_send()

    return start, sorted(events, key=lambda e: e[0]), finish


def gather_kernel(*refs):
    start, events, finish = gather_plan(*refs, pieces=4)
    start()
    for _, event in events:
        event()
    finish()


def gather_semaphores():
    dma = pltpu.SemaphoreType.DMA
    core = [dma((1,)), dma((4, 5)), dma((4, 3)), dma((4,)), dma((4, 3))]
    links = [dma((4, 5)), dma((4, 3)), dma((4,)), dma((4, 3))]
    return [dma((2,))] + links + core + [dma((4, 5))] + links + core


def gather_blocks(shard, collective_id, held_rows):
    rows = shard.shape[0]
    return pl.pallas_call(
        gather_kernel,
        in_specs=[pl.BlockSpec(memory_space=pl.ANY)],
        out_specs=pl.BlockSpec(memory_space=pl.ANY),
        out_shape=jax.ShapeDtypeStruct((held_rows, LANES), BF16),
        scratch_shapes=[pltpu.VMEM((rows, LANES), BF16)] + gather_semaphores(),
        compiler_params=pltpu.CompilerParams(collective_id=collective_id, has_side_effects=True, vmem_limit_bytes=VMEM_LIMIT),
        name="gather_blocks",
    )(shard)


def gelu_parts(x):
    inner = 0.7978845608028654 * (x + 0.044715 * x * x * x)
    return jnp.tanh(inner)


def layer_norm(tensor, gain, offset):
    average = jnp.mean(tensor, axis=-1, keepdims=True)
    centred = tensor - average
    variance = jnp.mean(centred * centred, axis=-1, keepdims=True)
    return centred * lax.rsqrt(variance + epsilon) * gain + offset


def layer_norm_back(d_out, tensor, gain):
    average = jnp.mean(tensor, axis=-1, keepdims=True)
    centred = tensor - average
    variance = jnp.mean(centred * centred, axis=-1, keepdims=True)
    scale = lax.rsqrt(variance + epsilon)
    normal = centred * scale
    d_normal = d_out * gain
    mean_d = jnp.mean(d_normal, axis=-1, keepdims=True)
    mean_dn = jnp.mean(d_normal * normal, axis=-1, keepdims=True)
    return (d_normal - mean_d - normal * mean_dn) * scale


def dot_both(x, w, inner, up):
    cut = w.shape[0] // 256 * 256
    tail = dot(
        jnp.concatenate([x[:, cut:], inner], axis=1), jnp.concatenate([w[cut:], up], axis=0)
    )
    return dot(x[:, :cut], w[:cut]) + tail


def dot_both_t(x, w, inner, up_t):
    cut = w.shape[1] // 256 * 256
    tail = dot_t(
        jnp.concatenate([x[:, cut:], inner], axis=1), jnp.concatenate([w[:, cut:], up_t], axis=1)
    )
    return dot_t(x[:, :cut], w[:, :cut]) + tail


def matrix(ref, count=None):
    units, panels = ref.shape[:2]
    return jnp.concatenate(
        [ref[:, p].reshape(units * 16, LANES) for p in range(count or panels)], axis=1
    )


def unit_block(units, panels, place):
    return pl.BlockSpec((units, panels, 16, LANES), place)


def whole(shape):
    return pl.BlockSpec(shape, lambda i: (0,) * len(shape), pipeline_mode=pl.Buffered(1))


def columns(rows, width):
    return pl.BlockSpec((rows, width), lambda i: (0, i))


def struct(shape, dtype):
    return jax.ShapeDtypeStruct(shape, dtype)


def dense_params(flops, bytes_accessed):
    return dict(
        cost_estimate=pl.CostEstimate(
            flops=flops, bytes_accessed=bytes_accessed, transcendentals=0
        ),
        compiler_params=pltpu.CompilerParams(vmem_limit_bytes=VMEM_LIMIT),
    )


def qkv_kernel(hidden, w, vec, down, up, normed, inner, qkv, parts):
    c = pl.program_id(0)

    @pl.when(c == 0)
    def _():
        value = layer_norm(hidden[...], vec[0:1], vec[1:2]).astype(BF16)
        normed[...] = value
        narrow = dot_t(value, down[...]).astype(BF16)
        inner[...] = narrow
        for part in range(3):
            parts[part] = narrow[:, part * R : (part + 1) * R]

    bias = vec[pl.ds(jnp.where(c == 2, 5, 4), 1), :] * jnp.where(c == 1, 0.0, 1.0)
    qkv[...] = (dot_both(normed[...], matrix(w), parts[c], up[0]) + bias).astype(BF16)


def qkv_forward(hidden, w_qkv, vectors, attn):
    rows = hidden.shape[0]
    return pl.pallas_call(
        qkv_kernel,
        grid=(3,),
        in_specs=[
            whole((rows, D)),
            unit_block(72, 9, lambda i: (0, i, 0, 0)),
            whole((8, D)),
            whole((3 * R, D)),
            pl.BlockSpec((1, R, D), lambda i: (i, 0, 0)),
        ],
        out_specs=[whole((rows, D)), whole((rows, 3 * R)), columns(rows, D)],
        out_shape=[
            struct((rows, D), BF16),
            struct((rows, 3 * R), BF16),
            struct((rows, 3 * D), BF16),
        ],
        scratch_shapes=[pltpu.VMEM((3, rows, R), BF16)],
        name="qkv_forward",
        **dense_params(6 * rows * D * D, 14 * rows * D + 6 * D * D),
    )(hidden, w_qkv, vectors, attn[0:3].reshape(3 * R, D), attn[4:7])


TILE = 512
OUT_BLOCK = pl.BlockSpec(
    (72, 9, 16, LANES), lambda i: (3, 0, 0, 0), pipeline_mode=pl.Buffered(1)
)


def up_kernel(
    attended, hidden, w_o, vec, down_o, up_o, down_1, w_1, b_1, up_1,
    inner_o, middle, normed, inner_up, gate, activated,
):
    @pl.when(pl.program_id(0) == 0)
    def _():
        narrow = dot_t(attended[...], down_o[...]).astype(BF16)
        inner_o[...] = narrow
        middle[...] = hidden[...] + (dot_both(attended[...], matrix(w_o), narrow, up_o[...]) + vec[6:7])
        value = layer_norm(middle[...], vec[2:3], vec[3:4]).astype(BF16)
        normed[...] = value
        inner_up[...] = dot_t(value, down_1[...]).astype(BF16)

    x = dot_both(normed[...], matrix(w_1), inner_up[...], up_1[...]) + b_1[...]
    gate[...] = x.astype(BF16)
    activated[...] = (0.5 * x * (1.0 + gelu_parts(x))).astype(BF16)


def up_forward(attended, hidden, w_o, vectors, attn, narrow, w_1, b_1, wide):
    rows = hidden.shape[0]
    return pl.pallas_call(
        up_kernel,
        grid=(WIDE // TILE,),
        in_specs=[
            whole((rows, D)),
            whole((rows, D)),
            OUT_BLOCK,
            whole((8, D)),
            whole((R, D)),
            whole((R, D)),
            whole((R, D)),
            unit_block(72, 4, lambda i: (1, i, 0, 0)),
            columns(1, TILE),
            columns(R, TILE),
        ],
        out_specs=[
            whole((rows, R)),
            whole((rows, D)),
            whole((rows, D)),
            whole((rows, R)),
            columns(rows, TILE),
            columns(rows, TILE),
        ],
        out_shape=[
            struct((rows, R), BF16),
            struct((rows, D), F32),
            struct((rows, D), BF16),
            struct((rows, R), BF16),
            struct((rows, WIDE), BF16),
            struct((rows, WIDE), BF16),
        ],
        name="up_forward",
        **dense_params(2 * rows * D * (D + FF), 12 * rows * D + 4 * rows * FF + 2 * D * (D + FF)),
    )(attended, hidden, w_o, vectors, attn[3], attn[7], narrow[0], w_1, b_1, wide[0])


THIRD = D // 3


def down_kernel(activated, middle, w_2, b_2, down_2, up_2, inner, hidden):
    @pl.when(pl.program_id(0) == 0)
    def _():
        inner[...] = dot_t(activated[...], down_2[...]).astype(BF16)

    value = activated[:, :FF]

    hidden[...] = middle[...] + (
        dot(value, matrix(w_2)) + b_2[...] + dot(inner[...], up_2[...])
    )


def down_forward(activated, middle, w_2, b_2, narrow, wide):
    rows = middle.shape[0]
    return pl.pallas_call(
        down_kernel,
        grid=(3,),
        in_specs=[
            whole((rows, WIDE)),
            columns(rows, THIRD),
            pl.BlockSpec(
                (pl.Element(UNITS[3]), pl.Element(3), pl.Element(16), pl.Element(LANES)),
                lambda i: (TILES_AT[3] // 9, 3 * i, 0, 0),
            ),
            columns(1, THIRD),
            whole((R, WIDE)),
            columns(R, THIRD),
        ],
        out_specs=[whole((rows, R)), columns(rows, THIRD)],
        out_shape=[struct((rows, R), BF16), struct((rows, D), F32)],
        name="down_forward",
        **dense_params(2 * rows * D * FF, 8 * rows * D + 2 * rows * FF + 2 * D * FF),
    )(activated, middle, w_2, b_2, wide[1], narrow[1])


def gate_kernel(
    gradient, w_2, gate, down_2, up_1, up_2, inner_down, inner_up, d_gate, g_wide, d_inner_up, g_up_2,
    d_branch, d_inner_down, total,
):
    i = pl.program_id(0)

    @pl.when(i == 0)
    def _():
        value = gradient[...].astype(BF16)
        d_branch[...] = value
        d_inner_down[...] = dot_t(value, up_2[...]).astype(BF16)
        g_up_2[...] = dot_l(inner_down[...], value)
        total[...] = jnp.zeros_like(total)

    left = FF - i * TILE
    down = down_2[...]
    d_act = dot_t(d_branch[...], matrix(w_2)) + dot(d_inner_down[...], down)
    x = gate[...].astype(F32)
    t = gelu_parts(x)
    half = 0.5 * (1.0 + t)
    slope = half + 0.5 * x * (1.0 - t * t) * (
        0.7978845608028654 * (1.0 + 3 * 0.044715 * x * x)
    )
    keep = lax.broadcasted_iota(jnp.int32, (1, TILE), 1) < left
    value = jnp.where(keep, slope * d_act, 0.0).astype(BF16)
    d_gate[...] = value
    total[...] += dot_t(value, up_1[...])
    g_wide[0:R] = dot_l(inner_up[...], value)
    g_wide[R : 2 * R] = dot_l(d_inner_down[...], (x * half).astype(BF16))

    @pl.when(i == pl.num_programs(0) - 1)
    def _():
        d_inner_up[...] = total[...].astype(BF16)


def gate_backward(gradient, w_2, gate, narrow, wide, inner_down, inner_up):
    rows = gradient.shape[0]
    return pl.pallas_call(
        gate_kernel,
        grid=(WIDE // TILE,),
        in_specs=[
            whole((rows, D)),
            unit_block(TILE // 16, 9, lambda i: (TILES_AT[3] // 9 * 16 // TILE + i, 0, 0, 0)),
            columns(rows, TILE),
            columns(R, TILE),
            columns(R, TILE),
            whole((R, D)),
            whole((rows, R)),
            whole((rows, R)),
        ],
        out_specs=[columns(rows, TILE), columns(2 * R, TILE), whole((rows, R)), whole((R, D))],
        out_shape=[
            struct((rows, WIDE), BF16),
            struct((2 * R, WIDE), F32),
            struct((rows, R), BF16),
            struct((R, D), F32),
        ],
        scratch_shapes=[
            pltpu.VMEM((rows, D), BF16),
            pltpu.VMEM((rows, R), BF16),
            pltpu.VMEM((rows, R), F32),
        ],
        name="gate_backward",
        **dense_params(2 * rows * D * FF, 4 * rows * D + 4 * rows * FF + 2 * D * FF),
    )(gradient, w_2, gate, wide[1], wide[0], narrow[1], inner_down, inner_up)


def middle_kernel(
    d_gate, w_1, d_inner_up, down_1, normed, middle, gradient, vec, w_o, down_o, up_o, inner_o, attended,
    d_middle, d_attended, g_rows, d_normed,
):
    i = pl.program_id(0)
    at = pl.ds(pl.multiple_of(i * THIRD, LANES), THIRD)
    d_normed[:, at] = dot_t(d_gate[:, : 34 * LANES], matrix(w_1, 34)) + dot(
        d_inner_up[...], down_1[:, at]
    )

    @pl.when(i == pl.num_programs(0) - 1)
    def _():
        value = gradient[...] + layer_norm_back(d_normed[...], middle[...], vec[2:3])
        d_middle[...] = value
        d_out = value.astype(BF16)
        d_inner_o = dot_t(d_out, up_o[...]).astype(BF16)
        d_attended[...] = (dot_t(d_out, matrix(w_o)) + dot(d_inner_o, down_o[...])).astype(BF16)
        g_rows[0:R] = dot_l(d_inner_o, attended[...])
        g_rows[R : 2 * R] = dot_l(inner_o[...], d_out)
        g_rows[2 * R : 3 * R] = dot_l(d_inner_up[...], normed[...])


def middle_backward(
    d_gate, w_1, d_inner_up, narrow, normed, middle, gradient, vectors, w_o, attn, inner_o, attended
):
    rows = gradient.shape[0]
    return pl.pallas_call(
        middle_kernel,
        grid=(3,),
        in_specs=[
            whole((rows, WIDE)),
            unit_block(THIRD // 16, PANELS[2], lambda i: (3 + i, 0, 0, 0)),
            whole((rows, R)),
            whole((R, D)),
            whole((rows, D)),
            whole((rows, D)),
            whole((rows, D)),
            whole((8, D)),
            OUT_BLOCK,
            whole((R, D)),
            whole((R, D)),
            whole((rows, R)),
            whole((rows, D)),
        ],
        out_specs=[whole((rows, D)), whole((rows, D)), whole((3 * R, D))],
        out_shape=[
            struct((rows, D), F32),
            struct((rows, D), BF16),
            struct((3 * R, D), F32),
        ],
        scratch_shapes=[pltpu.VMEM((rows, D), F32)],
        name="middle_backward",
        **dense_params(2 * rows * D * (D + FF), 18 * rows * D + 2 * rows * FF + 2 * D * (D + FF)),
    )(
        d_gate, w_1, d_inner_up, narrow[0], normed, middle, gradient, vectors, w_o, attn[3], attn[7],
        inner_o, attended,
    )


def input_kernel(
    d_qkv, w_qkv, down, up, normed, inner, hidden, d_middle, vec, gradient, g_rows, d_normed, d_inner
):
    i = pl.program_id(0)

    @pl.when(i == 0)
    def _():
        for c in range(3):
            part = d_qkv[:, c * D : (c + 1) * D]
            d_inner[:, c * R : (c + 1) * R] = dot_t(part, up[c]).astype(BF16)
            g_rows[(3 + c) * R : (4 + c) * R] = dot_l(inner[:, c * R : (c + 1) * R], part)
        g_rows[0 : 3 * R] = dot_l(d_inner[...], normed[...])

    at = pl.ds(pl.multiple_of(i * THIRD, LANES), THIRD)
    d_normed[:, at] = dot_t(d_qkv[...], matrix(w_qkv)) + dot(d_inner[...], down[:, at])

    @pl.when(i == pl.num_programs(0) - 1)
    def _():
        gradient[...] = d_middle[...] + layer_norm_back(d_normed[...], hidden[...], vec[0:1])


def input_backward(d_qkv, w_qkv, attn, normed, inner, hidden, d_middle, vectors):
    rows = hidden.shape[0]
    return pl.pallas_call(
        input_kernel,
        grid=(3,),
        in_specs=[
            whole((rows, 3 * D)),
            unit_block(THIRD // 16, 27, lambda i: (i, 0, 0, 0)),
            whole((3 * R, D)),
            whole((3, R, D)),
            whole((rows, D)),
            whole((rows, 3 * R)),
            whole((rows, D)),
            whole((rows, D)),
            whole((8, D)),
        ],
        out_specs=[whole((rows, D)), whole((6 * R, D))],
        out_shape=[struct((rows, D), F32), struct((6 * R, D), F32)],
        scratch_shapes=[pltpu.VMEM((rows, D), F32), pltpu.VMEM((rows, 3 * R), BF16)],
        name="input_backward",
        **dense_params(6 * rows * D * D, 20 * rows * D + 6 * D * D),
    )(d_qkv, w_qkv, attn[0:3].reshape(3 * R, D), attn[4:7], normed, inner, hidden, d_middle, vectors)


PAIR = 2 * LANES
PAIRS = -(-D // PAIR)
TWIN = 2
FOUR = 4
FORWARD_STEPS = (3, H // FOUR, WIDE // TILE, PAIRS)
FORWARD_AT = (0, 3, 3 + H // FOUR, 3 + H // FOUR + WIDE // TILE)
FORWARD_BEGINS = (
    [4.5 * i for i in range(3)]
    + [14 + 6 * i for i in range(H // FOUR)]
    + [38 + (5 if i else 0) + 2.6 * i for i in range(WIDE // TILE)]
    + [65 + 3 * i for i in range(PAIRS)]
)
CHUNK_TIME = 7.4


def of_layer(layer, *shape):
    return pl.BlockSpec(
        (1,) + shape, lambda i: (layer,) + (0,) * len(shape), pipeline_mode=pl.Buffered(1)
    )


def forward_kernel(with_gather, *refs):
    (
        bias_lane, hidden, w_qkv, vec, attn, w_o, narrow_in, w_1, b_1, up_1, w_2, w_2_odd, b_2, down_2, up_2,
    ) = refs[:15]
    refs = refs[15:]
    if with_gather:
        shard, refs = refs[0], refs[1:]
    (
        normed, inner_qkv, qkv, attended, stats, inner_o, middle, normed_two, inner_up, gate, inner_down,
        next_hidden,
    ) = refs[:12]
    refs = refs[12:]
    if with_gather:
        flat, refs = refs[0], refs[1:]
    heads, activated, parts = refs[:3]
    i = pl.program_id(0)
    rows = hidden.shape[0]
    _, att_at, up_at, down_at = FORWARD_AT
    last = down_at + PAIRS - 1

    def at_step(k):
        return pl.when(i == k)

    if with_gather:
        start, events, finish = gather_plan(shard, flat, None, *refs[3:])
        at_step(0)(start)
        steps = [[] for _ in FORWARD_BEGINS]
        late = []
        for when, event in events:
            ready = [k for k, begin in enumerate(FORWARD_BEGINS) if begin >= CHUNK_TIME * when + 4]
            (steps[ready[0]] if ready else late).append(event)
        for k, due in enumerate(steps):
            if due:

                @at_step(k)
                def _(due=due):
                    for event in due:
                        event()

    @pl.when(i < att_at)
    def _():
        @at_step(0)
        def _():
            value = layer_norm(hidden[...], vec[0:1], vec[1:2]).astype(BF16)
            normed[...] = value
            narrow = dot_t(value, attn[0, 0:3].reshape(3 * R, D)).astype(BF16)
            inner_qkv[...] = narrow
            for part in range(3):
                parts[part] = narrow[:, part * R : (part + 1) * R]
            stats[...] = jnp.zeros_like(stats)

        bias = vec[pl.ds(jnp.where(i == 2, 5, 4), 1), :] * jnp.where(i == 1, 0.0, 1.0)
        value = (dot_both(normed[...], matrix(w_qkv), parts[i], attn[0, 4 + i]) + bias).astype(BF16)
        qkv[...] = value
        mark = jnp.where(i == 0, first_lane(rows, F32(1.0)), jnp.where(i == 1, bias_lane[...], jnp.zeros_like(bias_lane[...])))
        for h in range(H):
            heads[i, h] = pad_lanes(value[:, h * HD : (h + 1) * HD], mark)

    @pl.when(jnp.logical_and(i >= att_at, i < up_at))
    def _():
        lane = lax.broadcasted_iota(jnp.int32, (rows, LANES), 1)
        pair_at = (i - att_at) * FOUR
        scores = [dot_t(heads[0, pair_at + k], heads[1, pair_at + k]) for k in range(FOUR)]
        kept = stats[...]
        for k in range(FOUR):
            h, s = pair_at + k, scores[k]
            m = jnp.max(s, axis=1, keepdims=True)
            p = jnp.exp2((s - m) * C2)
            total = jnp.sum(p, axis=1, keepdims=True)
            o = dot(p.astype(BF16), heads[2, h])
            heads[0, h] = (o * (1.0 / total)).astype(BF16)
            kept = jnp.where(lane == h, m * C2 + jnp.log2(total), kept)
        stats[...] = kept

    @pl.when(jnp.logical_and(i >= up_at, i < down_at))
    def _():
        t = i - up_at

        @at_step(up_at)
        def _():
            for h in range(H):
                attended[:, h * HD : (h + 1) * HD] = heads[0, h][:, :HD]
            value = attended[...]
            narrow = dot_t(value, attn[0, 3]).astype(BF16)
            inner_o[...] = narrow
            middle[...] = hidden[...] + (dot_both(value, matrix(w_o), narrow, attn[0, 7]) + vec[6:7])
            value = layer_norm(middle[...], vec[2:3], vec[3:4]).astype(BF16)
            normed_two[...] = value
            inner_up[...] = dot_t(value, narrow_in[0, 0]).astype(BF16)

        x = dot_both(normed_two[...], matrix(w_1), inner_up[...], up_1[0, 0]) + b_1[...]
        gate[...] = x.astype(BF16)
        value = (0.5 * x * (1.0 + gelu_parts(x))).astype(BF16)
        activated[:, pl.ds(pl.multiple_of(t * TILE, LANES), TILE)] = value

    @pl.when(i >= down_at)
    def _():
        @at_step(down_at)
        def _():
            w = jnp.concatenate([matrix(w_2.at[: UNITS[3]]), down_2[0, 0].T[:FF]], axis=1)
            value = dot(activated[:, :FF], w)
            narrow = value[:, LANES : LANES + R].astype(BF16)
            inner_down[...] = narrow
            value = value[:, :LANES] + b_2[:, :LANES] + dot(narrow, up_2[0, 0, :, :LANES])
            next_hidden[:, :LANES] = middle[:, D - LANES :] + value

        @pl.when(i > down_at)
        def _():
            at = pl.ds(pl.multiple_of((i - down_at - 1) * PAIR, LANES), PAIR)
            w = jnp.concatenate([matrix(w.at[: UNITS[3]]) for w in (w_2, w_2_odd)], axis=1)
            value = dot(activated[:, :FF], w) + b_2[...] + dot(inner_down[...], up_2[0, 0])
            next_hidden[...] = middle[:, at] + value

    if with_gather:

        @at_step(last)
        def _():
            for event in late:
                event()
            finish()


def layer_forward(layer, bias, hidden, weights, tables, shard=None):
    w_qkv, w_o, w_1, w_2, vectors, b_1 = weights
    attn, narrow, wide, _ = tables
    rows = hidden.shape[0]
    _, att_at, up_at, down_at = FORWARD_AT

    def step(i, k):
        return jnp.minimum(jnp.maximum(i - FORWARD_AT[k], 0), FORWARD_STEPS[k] - 1)

    def cols(count, width, k):
        return pl.BlockSpec((count, width), lambda i: (0, step(i, k)))

    def pair(i):
        return jnp.where(step(i, 3) == 0, PAIRS - 1, step(i, 3) - 1)

    def pairs(count):
        return pl.BlockSpec((count, PAIR), lambda i: (0, pair(i)))

    operands = [
        bias, hidden, w_qkv, vectors, attn, w_o, narrow, w_1, b_1, wide, w_2, w_2, vectors[7:8], wide, narrow,
    ]
    in_specs = [
        whole((rows, LANES - HD)),
        whole((rows, D)),
        unit_block(72, 9, lambda i: (0, step(i, 0), 0, 0)),
        whole((8, D)),
        of_layer(layer, 8, R, D),
        OUT_BLOCK,
        of_layer(layer, 2, R, D),
        unit_block(72, 4, lambda i: (1, step(i, 2), 0, 0)),
        cols(1, TILE, 2),
        pl.BlockSpec((1, 1, R, TILE), lambda i: (layer, 0, 0, step(i, 2))),
        unit_block(288, 1, lambda i: (2, 2 * pair(i), 0, 0)),
        unit_block(288, 1, lambda i: (2, jnp.minimum(2 * pair(i) + 1, 8), 0, 0)),
        pairs(1),
        pl.BlockSpec((1, 1, R, WIDE), lambda i: (layer, 1, 0, 0), pipeline_mode=pl.Buffered(1)),
        pl.BlockSpec((1, 1, R, PAIR), lambda i: (layer, 1, 0, pair(i))),
    ]
    outs = [
        (whole((rows, D)), struct((rows, D), BF16)),
        (whole((rows, 3 * R)), struct((rows, 3 * R), BF16)),
        (cols(rows, D, 0), struct((rows, 3 * D), BF16)),
        (whole((rows, D)), struct((rows, D), BF16)),
        (whole((rows, LANES)), struct((rows, LANES), F32)),
        (whole((rows, R)), struct((rows, R), BF16)),
        (whole((rows, D)), struct((rows, D), F32)),
        (whole((rows, D)), struct((rows, D), BF16)),
        (whole((rows, R)), struct((rows, R), BF16)),
        (cols(rows, TILE, 2), struct((rows, WIDE), BF16)),
        (whole((rows, R)), struct((rows, R), BF16)),
        (pairs(rows), struct((rows, D), F32)),
    ]
    scratch = [
        pltpu.VMEM((3, H, rows, LANES), BF16),
        pltpu.VMEM((rows, WIDE), BF16),
        pltpu.VMEM((3, rows, R), BF16),
    ]
    params = dict(vmem_limit_bytes=VMEM_MOST)
    if shard is not None:
        operands.append(shard)
        in_specs.append(pl.BlockSpec(memory_space=pl.ANY))
        outs.append(
            (pl.BlockSpec(memory_space=pl.ANY), struct((16 * TILES_HELD, LANES), BF16))
        )
        scratch += gather_semaphores()
        params.update(collective_id=3, has_side_effects=True)
    return pl.pallas_call(
        functools.partial(forward_kernel, shard is not None),
        grid=(sum(FORWARD_STEPS),),
        in_specs=in_specs,
        out_specs=[spec for spec, _ in outs],
        out_shape=[shape for _, shape in outs],
        scratch_shapes=scratch,
        cost_estimate=pl.CostEstimate(
            flops=2 * rows * D * (4 * D + 2 * FF) + 8 * rows * rows * D,
            bytes_accessed=2 * D * (4 * D + 2 * FF) + 30 * rows * D,
            transcendentals=H * rows * rows,
        ),
        compiler_params=pltpu.CompilerParams(**params),
        name="layer_forward_gather" if shard is not None else "layer_forward",
    )(*operands)


def first_gather_kernel(tiles, shard_a, shard_b, gathered, laid_a, laid_b, own, halo, flat, held, turned, *sems):
    own_sem, halo_send, halo_recv = sems[:3]
    f = lax.axis_index("fsdp")
    x = lax.axis_index("seq")
    z = f // 4
    rows = shard_a.shape[0]
    last = lax.axis_size("fsdp") - 1
    margin = 16 * PANELS[2]
    barrier = pltpu.get_barrier_semaphore()
    start, events, finish = gather_plan(laid_a, gathered, None, *sems[3:])

    def greet(to):
        pl.semaphore_signal(barrier, inc=1, device_id=to, device_id_type=MESH)

    y, c = (f // 2) % 2, f % 2
    for to in ((f + 2 - 4 * y, x), (f, 1 - x), (f + 1 - 2 * c, x)):
        greet(to)
    for there, step in ((z < 3, 4), (z > 0, -4), (f < last, 1), (f > 0, -1)):

        @pl.when(there)
        def _(step=step):
            greet((f + step, x))

    expected = 3
    for there in (z < 3, z > 0, f < last, f > 0):
        expected = expected + jnp.where(there, 1, 0)
    pl.semaphore_wait(barrier, expected)

    def halo_copy(layer, side):
        source = (shard_a, shard_b)[layer].at[pl.ds((rows - HALO) * (1 - side), HALO), :]
        return pltpu.make_async_remote_copy(
            src_ref=source,
            dst_ref=halo.at[layer, side],
            send_sem=halo_send.at[layer, side],
            recv_sem=halo_recv.at[layer, side],
            device_id=(f + 1 - 2 * side, x),
            device_id_type=MESH,
        )

    def sends(side):
        return f < last if side == 0 else f > 0

    def takes(side):
        return sends(1 - side)

    for layer in range(2):
        for side in range(2):

            @pl.when(sends(side))
            def _(layer=layer, side=side):
                halo_copy(layer, side).start()

    def lay(layer, source, laid):
        fetch = pltpu.make_async_copy(source, own, own_sem.at[0])
        fetch.start()
        fetch.wait()
        for side in range(2):

            @pl.when(takes(side))
            def _(side=side):
                halo_copy(layer, side).wait_recv()

            @pl.when(jnp.logical_not(takes(side)))
            def _(side=side):
                halo[layer, side] = jnp.zeros((HALO, LANES), BF16)

        lay_rows(f, rows, tiles, halo[layer, 0], own[...], halo[layer, 1], flat, held, turned)
        keep = pltpu.make_async_copy(held.at[pl.ds(margin, 16 * tiles), :], laid, own_sem.at[0])
        keep.start()
        keep.wait()

    lay(0, shard_a, laid_a)
    start(False)
    lay(1, shard_b, laid_b)
    for _, event in events:
        event()
    finish()
    for layer in range(2):
        for side in range(2):

            @pl.when(sends(side))
            def _(layer=layer, side=side):
                halo_copy(layer, side).wait_send()


def first_gather(shards, tiles):
    rows = shards[0].shape[0]
    dma = pltpu.SemaphoreType.DMA
    hbm = pl.BlockSpec(memory_space=pl.ANY)
    laid = jax.ShapeDtypeStruct((16 * tiles, LANES), BF16)
    return pl.pallas_call(
        functools.partial(first_gather_kernel, tiles),
        in_specs=[hbm, hbm],
        out_specs=[hbm, hbm, hbm],
        out_shape=[jax.ShapeDtypeStruct((16 * TILES_HELD, LANES), BF16), laid, laid],
        scratch_shapes=[pltpu.VMEM((rows, LANES), BF16), pltpu.VMEM((2, 2, HALO, LANES), BF16)]
        + lay_scratch(rows, tiles)
        + [dma((1,)), dma((2, 2)), dma((2, 2))]
        + gather_semaphores(),
        compiler_params=pltpu.CompilerParams(
            collective_id=0, has_side_effects=True, vmem_limit_bytes=VMEM_MOST
        ),
        name="first_gather",
    )(*shards)


SHARE = 5
SHARE_ROWS = SHARE * 16


def share_plan(
    adapters, named, terms, names, out, held, totals, sums, local_sem, send, recv, pair_sem
):
    x = lax.axis_index("seq")
    f = lax.axis_index("fsdp")
    count = terms.shape[0]
    me = f * 2 + x
    rows = adapters * SHARE_ROWS

    def device(k):
        return (k // 2, k % 2)

    def share_to(to, slot):
        return pltpu.make_async_remote_copy(
            src_ref=terms.at[to],
            dst_ref=held.at[slot],
            send_sem=send.at[to],
            recv_sem=recv.at[slot],
            device_id=device(to),
            device_id_type=MESH,
        )

    def own():
        return pltpu.make_async_copy(terms.at[me], held.at[me], local_sem.at[0])

    def across(side):
        part = out.at[pl.ds(pl.multiple_of(side * rows, 16), rows), :]
        return pltpu.make_async_remote_copy(
            src_ref=part,
            dst_ref=part,
            send_sem=pair_sem.at[0],
            recv_sem=pair_sem.at[1],
            device_id=(f, 1 - x),
            device_id_type=MESH,
        )

    def start():
        barrier = pltpu.get_barrier_semaphore()

        def greet(k, carry):
            to = (me + k) % count
            pl.semaphore_signal(barrier, inc=1, device_id=device(to), device_id_type=MESH)
            return carry

        lax.fori_loop(1, count, greet, 0)
        pl.semaphore_wait(barrier, count - 1)

        def post(k, carry):
            to = (me + k) % count
            share_to(to, me).start()
            return carry

        lax.fori_loop(1, count, post, 0)
        own().start()

    def add_up():
        totals[...] = jnp.zeros_like(totals)

        def add(slot):
            value = held[slot, :SHARE].reshape(SHARE_ROWS, LANES).astype(F32)
            if named:
                name = names[pl.ds(slot, 1), :]
            else:
                name = held[slot, SHARE].astype(F32)[0:1]
                names[pl.ds(slot, 1), :] = name
            for e in range(adapters):
                totals[e] += jnp.where(name == float(e), value, 0.0)

        own().wait()
        add(me)

        def take(k, carry):
            slot = (me + count - k) % count
            share_to(slot, slot).wait_recv()
            add(slot)
            return carry

        lax.fori_loop(1, count, take, 0)
        sums[...] = totals[...].reshape(rows, LANES).astype(BF16)
        part = out.at[pl.ds(pl.multiple_of(x * rows, 16), rows), :]
        keep = pltpu.make_async_copy(sums, part, local_sem.at[0])
        keep.start()
        keep.wait()
        across(x).start()

    def finish():
        def sent(k, carry):
            to = (me + k) % count
            share_to(to, me).wait_send()
            return carry

        lax.fori_loop(1, count, sent, 0)
        across(x).wait_send()
        across(1 - x).wait_recv()

    return start, add_up, finish


def share_kernel(adapters, *refs):
    for part in share_plan(adapters, True, *refs):
        part()


def share_scratch(count, adapters, tiles):
    dma = pltpu.SemaphoreType.DMA
    rows = adapters * SHARE_ROWS
    return [
        pltpu.VMEM((count, tiles, 16, LANES), BF16),
        pltpu.VMEM((adapters, SHARE_ROWS, LANES), F32),
        pltpu.VMEM((rows, LANES), BF16),
        dma((1,)),
        dma((count,)),
        dma((count,)),
        dma((2,)),
    ]


def share_terms(terms, names, adapters):
    rows = adapters * SHARE_ROWS
    return pl.pallas_call(
        functools.partial(share_kernel, adapters),
        in_specs=[pl.BlockSpec(memory_space=pl.ANY), pl.BlockSpec(memory_space=pltpu.VMEM)],
        out_specs=pl.BlockSpec(memory_space=pl.ANY),
        out_shape=jax.ShapeDtypeStruct((2 * rows, LANES), BF16),
        scratch_shapes=share_scratch(terms.shape[0], adapters, SHARE),
        compiler_params=pltpu.CompilerParams(
            collective_id=1, has_side_effects=True, vmem_limit_bytes=VMEM_LIMIT
        ),
        name="share_terms",
    )(terms, names)


def table_kernel(layers, *refs):
    attn, narrow, wide = refs[layers:]
    for layer in range(layers):
        source = refs[layer]
        for t in range(10 * 9 + 2 * 34):
            tile = source[t // SHARE, 0, t % SHARE].astype(F32)
            if t < 90:
                at = slice(t % 9 * LANES, (t % 9 + 1) * LANES)
                if t < 72:
                    attn[layer, t // 9, 0, :, at] = tile
                else:
                    narrow[layer, t // 9 - 8, 0, :, at] = tile
            else:
                c, p = (t - 90) // 34, (t - 90) % 34
                width = min(LANES, FF - p * LANES)
                wide[layer, c, 0, :, p * LANES : p * LANES + width] = tile[:, :width]


def gradient_tables(gathered, adapters):
    layers = len(gathered)
    count = gathered[0].shape[0] // (adapters * SHARE_ROWS)
    gathered = [g.reshape(count, adapters, SHARE, 16, LANES) for g in gathered]

    def out_block(kinds, width):
        return pl.BlockSpec((layers, kinds, 1, R, width), lambda e: (0, 0, e, 0, 0))

    return pl.pallas_call(
        functools.partial(table_kernel, layers),
        grid=(adapters,),
        in_specs=[pl.BlockSpec((count, 1, SHARE, 16, LANES), lambda e: (0, e, 0, 0, 0))] * layers,
        out_specs=[out_block(8, D), out_block(2, D), out_block(2, FF)],
        out_shape=[
            struct((layers, 8, adapters, R, D), F32),
            struct((layers, 2, adapters, R, D), F32),
            struct((layers, 2, adapters, R, FF), F32),
        ],
        compiler_params=pltpu.CompilerParams(vmem_limit_bytes=VMEM_LIMIT),
        name="gradient_tables",
    )(*gathered)


BACKWARD_STEPS = (WIDE // TILE, PAIRS, 1, H // TWIN, PAIRS)
BACKWARD_AT = (0, 9, 14, 15, 15 + H // TWIN)
SHARE_AT, PASS_AT, GATHER_AT = 7, 9, 10


def backward_kernel(adapters, spread, *refs):
    (
        gradient, w_2, gate, down_2, inner_down, inner_up, w_1, w_1_odd, up_1, narrow, normed_two_in, vec, w_o, attn,
        label, inner_o, attended, bias, stats, w_qkv, w_qkv_odd, up, inner_qkv, middle_in, qkv_in, hidden_in, normed_in,
    ) = refs[:27]
    refs = refs[27:]
    if adapters:
        terms, half, refs = refs[0], refs[1], refs[2:]
    new_gradient, new_terms = refs[:2]
    refs = refs[2:]
    if adapters:
        pair, gathered, other_half, names, refs = refs[0], refs[1], refs[2], refs[3], refs[4:]
    (
        d_branch, d_inner_down, d_inner_up, wide, residual, d_normed, heads, stat_t, delta_t, load_sem,
    ) = refs[:10]
    refs = refs[10:]
    i = pl.program_id(0)
    _, middle_at, turn_at, att_at, input_at = BACKWARD_AT
    last = input_at + PAIRS - 1

    def at_step(k):
        return pl.when(i == k)

    def place(t):
        return t if spread == SHARE else t // SHARE * spread + t % SHARE

    def put(table, value):
        for p in range(D // LANES):
            tile = value[:, p * LANES : (p + 1) * LANES]
            new_terms[place(table * (D // LANES) + p)] = tile.astype(BF16)

    def load_middle():
        return pltpu.make_async_copy(middle_in, residual, load_sem.at[0])

    def load_qkv():
        return pltpu.make_async_copy(qkv_in, wide.at[:, : 3 * D], load_sem.at[1])

    def load_hidden():
        return pltpu.make_async_copy(hidden_in, residual, load_sem.at[0])

    def load_normed_two():
        return pltpu.make_async_copy(normed_two_in, d_branch, load_sem.at[2])

    def load_normed():
        return pltpu.make_async_copy(normed_in, d_branch, load_sem.at[2])

    if adapters:
        share_start, share_sum, share_finish = share_plan(
            adapters, False, terms, names, pair, *refs[:7]
        )
        swap_sem = refs[7]
        start, events, finish = gather_plan(pair, gathered, None, *refs[8:])
        swap = pltpu.make_async_remote_copy(
            src_ref=half,
            dst_ref=other_half,
            send_sem=swap_sem.at[0],
            recv_sem=swap_sem.at[1],
            device_id=(lax.axis_index("fsdp"), 1 - lax.axis_index("seq")),
            device_id_type=MESH,
        )
        at_step(0)(share_start)
        at_step(GATHER_AT + 12)(swap.start)
        at_step(SHARE_AT)(share_sum)
        at_step(PASS_AT)(share_finish)

        @at_step(GATHER_AT)
        def _():
            start(False)

        steps = {}
        for when, event in events:
            steps.setdefault(min(GATHER_AT + 1 + int(when), last), []).append(event)
        for k, due in steps.items():

            @at_step(k)
            def _(due=due):
                for event in due:
                    event()

    @pl.when(i < middle_at)
    def _():
        @at_step(0)
        def _():
            load_middle().start()
            value = gradient[...].astype(BF16)
            d_branch[...] = value
            d_inner_down[...] = dot_t(value, narrow[0, 1]).astype(BF16)
            put(9, dot_l(inner_down[...], value))
            for t in (158, 159):
                new_terms[place(t)] = jnp.zeros((R, LANES), BF16)
            if spread > SHARE:
                for k in range(SHARE, new_terms.shape[0], spread):
                    new_terms[k] = label[...]

        left = FF - i * TILE
        d_act = dot_both_t(d_branch[...], matrix(w_2), d_inner_down[...], down_2[0, 0].T)
        x = gate[...].astype(F32)
        t = gelu_parts(x)
        half = 0.5 * (1.0 + t)
        slope = half + 0.5 * x * (1.0 - t * t) * (
            0.7978845608028654 * (1.0 + 3 * 0.044715 * x * x)
        )
        keep = lax.broadcasted_iota(jnp.int32, (1, TILE), 1) < left
        value = jnp.where(keep, slope * d_act, 0.0).astype(BF16)
        wide[:, pl.ds(pl.multiple_of(i * TILE, LANES), TILE)] = value
        made = (
            dot_l(inner_up[...], value).astype(BF16),
            dot_l(d_inner_down[...], (x * half).astype(BF16)).astype(BF16),
        )

        def put_wide(panels):
            for kind in range(2):
                for p in panels:
                    tile = made[kind][:, p * LANES : (p + 1) * LANES]
                    new_terms[place(90 + 34 * kind + 4 * i + p)] = tile

        put_wide(range(2))

        @pl.when(i < middle_at - 1)
        def _():
            put_wide(range(2, 4))


    @pl.when(jnp.logical_and(i >= middle_at, i < turn_at))
    def _():
        at_step(middle_at)(load_normed_two().start)

        @pl.when(i < turn_at - 1)
        def _():
            w = jnp.concatenate([matrix(w_1, 34), matrix(w_1_odd, 34)], axis=0)
            d_normed[i - middle_at] = dot_t(wide[:, : 34 * LANES], w)

        @at_step(turn_at - 1)
        def _():
            w = jnp.concatenate([matrix(w_1, 34), up_1[0, 0, :, : 34 * LANES]], axis=0)
            value = dot_t(wide[:, : 34 * LANES], w)
            d_normed[PAIRS - 1, :, :LANES] = value[:, :LANES]
            d_inner_up[...] = value[:, LANES : LANES + R].astype(BF16)

    def joined():
        parts = [d_normed[k] for k in range(PAIRS - 1)]
        return jnp.concatenate(parts + [d_normed[PAIRS - 1, :, :LANES]], axis=1)

    @at_step(turn_at)
    def _():
        load_qkv().start()
        load_middle().wait()
        d_two = joined() + dot(d_inner_up[...], narrow[0, 0])
        value = gradient[...] + layer_norm_back(d_two, residual[...], vec[2:3])
        load_hidden().start()
        new_gradient[...] = value
        d_out = value.astype(BF16)
        d_inner_o = dot_t(d_out, attn[0, 7]).astype(BF16)
        wide[:, 3 * D :] = (dot_t(d_out, matrix(w_o)) + dot(d_inner_o, attn[0, 3])).astype(BF16)
        put(3, dot_l(d_inner_o, attended[...]))
        put(7, dot_l(inner_o[...], d_out))
        load_normed_two().wait()
        put(8, dot_l(d_inner_up[...], d_branch[...]))
        load_normed().start()
        load_qkv().wait()
        rows = gradient.shape[0]
        lane = lax.broadcasted_iota(jnp.int32, (rows, LANES), 1)
        delta = jnp.zeros((rows, LANES), F32)
        marked = (first_lane(rows, F32(1.0)), bias[...], None)
        for h in range(H):
            for c in range(3):
                part = wide[:, c * D + h * HD : c * D + (h + 1) * HD]
                heads[c, h] = pad_lanes(part, marked[c])
            do = wide[:, 3 * D + h * HD : 3 * D + (h + 1) * HD]
            heads[3, h] = pad_lanes(do)
            o = attended[:, h * HD : (h + 1) * HD].astype(F32)
            d = jnp.sum(do.astype(F32) * o, axis=1, keepdims=True)
            delta = jnp.where(lane == h, d, delta)
        stat_t[...] = stats[...].T
        delta_t[...] = delta.T

    @pl.when(jnp.logical_and(i >= att_at, i < input_at))
    def _():
        for twin in range(TWIN):
            h = (i - att_at) * TWIN + twin
            q, k, do = heads[0, h], heads[1, h], heads[3, h]
            p = jnp.exp2(dot_t(k, q) * C2 - stat_t[pl.ds(h, 1), :])
            dv = dot(p.astype(BF16), do)
            dp = dot_t(heads[2, h], do)
            ds = (p * (dp - delta_t[pl.ds(h, 1), :])).astype(BF16)
            dk = dot(ds, q)
            dq = dot(k.T, ds)
            heads[2, h] = dv.astype(BF16)
            heads[1, h] = (dk * SCALE).astype(BF16)
            heads[0, h] = (dq * SCALE).astype(BF16).T

    @pl.when(i >= input_at)
    def _():
        @at_step(input_at)
        def _():
            load_normed().wait()
            for c in range(3):
                for h in range(H):
                    wide[:, c * D + h * HD : c * D + (h + 1) * HD] = heads[c, h][:, :HD]
            for c in range(3):
                part = wide[:, c * D : (c + 1) * D]
                put(4 + c, dot_l(inner_qkv[:, c * R : (c + 1) * R], part))

        @pl.when(i < last)
        def _():
            w = jnp.concatenate([matrix(w_qkv), matrix(w_qkv_odd)], axis=0)
            d_normed[i - input_at] = dot_t(wide[:, : 3 * D], w)

        @at_step(last)
        def _():
            w = jnp.concatenate([matrix(w_qkv), up[0]], axis=0)
            value = dot_t(wide[:, : 3 * D], w)
            d_normed[PAIRS - 1, :, :LANES] = value[:, :LANES]
            inner = value[:, LANES : LANES + 3 * R].astype(BF16)
            made = dot_l(inner, d_branch[...])
            for c in range(3):
                put(c, made[c * R : (c + 1) * R])
            load_hidden().wait()
            d_one = joined() + dot(inner, attn[0, 0:3].reshape(3 * R, D))
            new_gradient[...] += layer_norm_back(d_one, residual[...], vec[0:1])

    if adapters:

        @at_step(last)
        def _():
            finish()
            swap.wait()


def layer_backward(
    layer, gradient, saved, weights, tables, bias, label, spread, adapters=0, terms=None, half=None
):
    hidden, normed, inner_qkv, qkv, stats, attended, inner_o, middle, normed_two, inner_up, gate, inner_down = saved
    w_qkv, w_o, w_1, w_2, vectors, _ = weights
    attn, narrow, wide, up_diagonal = tables
    rows = gradient.shape[0]

    def step(i, k):
        return jnp.minimum(jnp.maximum(i - BACKWARD_AT[k], 0), BACKWARD_STEPS[k] - 1)

    def cols(count, width, k):
        return pl.BlockSpec((count, width), lambda i: (0, step(i, k)))

    hbm = pl.BlockSpec(memory_space=pl.ANY)
    operands = [
        (whole((rows, D)), gradient),
        (unit_block(TILE // 16, 9, lambda i: (TILES_AT[3] // 9 * 16 // TILE + step(i, 0), 0, 0, 0)), w_2),
        (cols(rows, TILE, 0), gate),
        (pl.BlockSpec((1, 1, R, TILE), lambda i: (layer, 1, 0, step(i, 0))), wide),
        (whole((rows, R)), inner_down),
        (whole((rows, R)), inner_up),
        (unit_block(8, PANELS[2], lambda i: (9 + 2 * step(i, 1), 0, 0, 0)), w_1),
        (unit_block(8, PANELS[2], lambda i: (10 + jnp.minimum(2 * step(i, 1), 7), 0, 0, 0)), w_1),
        (of_layer(layer, 1, R, WIDE), wide),
        (of_layer(layer, 2, R, D), narrow),
        (hbm, normed_two),
        (whole((8, D)), vectors),
        (OUT_BLOCK, w_o),
        (of_layer(layer, 8, R, D), attn),
        (whole((R, LANES)), label),
        (whole((rows, R)), inner_o),
        (whole((rows, D)), attended),
        (whole((rows, LANES - HD)), bias),
        (whole((rows, LANES)), stats),
        (unit_block(8, 27, lambda i: (2 * step(i, 4), 0, 0, 0)), w_qkv),
        (unit_block(8, 27, lambda i: (jnp.minimum(2 * step(i, 4) + 1, 8), 0, 0, 0)), w_qkv),
        (of_layer(layer, 3 * R, 3 * D), up_diagonal),
        (whole((rows, 3 * R)), inner_qkv),
        (hbm, middle),
        (hbm, qkv),
        (hbm, hidden),
        (hbm, normed),
    ]
    outs = [
        (whole((rows, D)), struct((rows, D), F32)),
        (whole((32 * spread, R, LANES)), struct((32 * spread, R, LANES), BF16)),
    ]
    scratch = [
        pltpu.VMEM((rows, D), BF16),
        pltpu.VMEM((rows, R), BF16),
        pltpu.VMEM((rows, R), BF16),
        pltpu.VMEM((rows, WIDE), BF16),
        pltpu.VMEM((rows, D), F32),
        pltpu.VMEM((PAIRS, rows, PAIR), F32),
        pltpu.VMEM((4, H, rows, LANES), BF16),
        pltpu.VMEM((LANES, rows), F32),
        pltpu.VMEM((LANES, rows), F32),
        pltpu.SemaphoreType.DMA((3,)),
    ]
    params = dict(vmem_limit_bytes=VMEM_MOST)
    if adapters:
        operands += [(hbm, terms), (hbm, half)]
        block = 2 * adapters * SHARE_ROWS
        outs += [(hbm, struct((block, LANES), BF16)), (hbm, struct((16 * block, LANES), BF16))]
        outs += [(hbm, struct(half.shape, BF16))]
        outs += [(whole((terms.shape[0], LANES)), struct((terms.shape[0], LANES), F32))]
        scratch += share_scratch(terms.shape[0], adapters, SHARE + 1) + [pltpu.SemaphoreType.DMA((2,))]
        scratch += gather_semaphores()
        params.update(collective_id=4, has_side_effects=True)
    return pl.pallas_call(
        functools.partial(backward_kernel, adapters, spread),
        grid=(sum(BACKWARD_STEPS),),
        in_specs=[spec for spec, _ in operands],
        out_specs=[spec for spec, _ in outs],
        out_shape=[shape for _, shape in outs],
        scratch_shapes=scratch,
        cost_estimate=pl.CostEstimate(
            flops=2 * rows * D * (4 * D + 2 * FF) + 20 * rows * rows * D,
            bytes_accessed=2 * D * (4 * D + 2 * FF) + 40 * rows * D,
            transcendentals=H * rows * rows,
        ),
        compiler_params=pltpu.CompilerParams(**params),
        name="layer_backward_share" if adapters else "layer_backward",
    )(*[operand for _, operand in operands])


VECTOR_ROWS = 240


def read_vectors(block, vectors, b_1, rows):
    rows[...] = block[...].astype(F32)
    for p in range(D // LANES):
        vectors[:, p * LANES : (p + 1) * LANES] = rows[pl.ds(p, 8, stride=D // LANES), :]
    b_1[...] = jnp.zeros_like(b_1)
    first = 8 * D // LANES
    for p in range(-(-FF // LANES)):
        width = min(LANES, FF - p * LANES)
        b_1[:, p * LANES : p * LANES + width] = rows[first + p : first + p + 1, :width]


def layer_vectors(flat):
    return pl.pallas_call(
        read_vectors,
        grid=(1,),
        in_specs=[pl.BlockSpec((VECTOR_ROWS, LANES), lambda i: (16 * TILES_END // VECTOR_ROWS, 0))],
        out_specs=[whole((8, D)), whole((1, WIDE))],
        out_shape=[struct((8, D), F32), struct((1, WIDE), F32)],
        scratch_shapes=[pltpu.VMEM((VECTOR_ROWS, LANES), F32)],
        name="layer_vectors",
    )(flat)


def prepare_kernel(
    scalars, attn_in, narrow_in, wide_in, mine, other, block, attn, narrow, wide, diagonal, bias, hidden, label,
    vectors, b_1, rows,
):
    slot = scalars[5]
    length, live = scalars[2 + slot], jnp.where(slot < scalars[4], 1, 0)
    read_vectors(block, vectors, b_1, rows)
    label[...] = jnp.full(label.shape, scalars[slot], jnp.int32).astype(F32).astype(BF16)
    attn[...] = attn_in[:, :, 0]
    narrow[...] = narrow_in[:, :, 0]
    wide[...] = jnp.zeros_like(wide)
    wide[:, :, :, :FF] = wide_in[:, :, 0]
    diagonal[...] = jnp.zeros_like(diagonal)
    for layer in range(attn.shape[0]):
        for c in range(3):
            diagonal[layer, c * R : (c + 1) * R, c * D : (c + 1) * D] = attn_in[layer, 4 + c, 0]
    bias[...] = key_bias(bias.shape[0], length)
    half = mine.shape[1]
    row = lax.broadcasted_iota(jnp.int32, (half, 1), 0)

    def place(at, value):
        keep = jnp.where(row + at < length, live, 0) > 0
        hidden[at : at + half] = jnp.where(keep, value.astype(F32), 0.0)

    for first in range(2):

        @pl.when(slot == first)
        def _(first=first):
            place(first * half, mine[0])
            place((1 - first) * half, other[...])


def prepare(scalars, attention_table, narrow_table, wide_table, activations, other, flat):
    layers = attention_table.shape[0]
    rows = 2 * other.shape[0]

    def picked(kinds, width):
        return pl.BlockSpec((layers, kinds, 1, R, width), lambda i, k: (0, 0, k[k[5]], 0, 0))

    def full(*shape):
        return pl.BlockSpec(shape, lambda i, k: (0,) * len(shape))

    shapes = [
        ((layers, 8, R, D), BF16),
        ((layers, 2, R, D), BF16),
        ((layers, 2, R, WIDE), BF16),
        ((layers, 3 * R, 3 * D), BF16),
        ((rows, LANES - HD), BF16),
        ((rows, D), F32),
        ((R, LANES), BF16),
        ((8, D), F32),
        ((1, WIDE), F32),
    ]
    return pl.pallas_call(
        prepare_kernel,
        grid_spec=pltpu.PrefetchScalarGridSpec(
            num_scalar_prefetch=1,
            grid=(1,),
            in_specs=[
                picked(8, D),
                picked(2, D),
                picked(2, FF),
                pl.BlockSpec((1,) + other.shape, lambda i, k: (k[5], 0, 0)),
                full(*other.shape),
                pl.BlockSpec((VECTOR_ROWS, LANES), lambda i, k: (16 * TILES_END // VECTOR_ROWS, 0)),
            ],
            out_specs=[full(*shape) for shape, _ in shapes],
            scratch_shapes=[pltpu.VMEM((VECTOR_ROWS, LANES), F32)],
        ),
        out_shape=[struct(*shape) for shape in shapes],
        compiler_params=pltpu.CompilerParams(vmem_limit_bytes=VMEM_LIMIT),
        name="prepare",
    )(scalars, attention_table, narrow_table, wide_table, activations, other, flat)


def local(
    activations,
    group_image_count,
    image_adapter_index,
    lengths,
    frozen,
    attention_adapter_weights,
    narrow_adapter_weights,
    broad_adapter_weights,
    cotangent,
):
    slots, local_len, _ = activations.shape
    seq_parts = lax.axis_size("seq")
    fsdp_parts = lax.axis_size("fsdp")
    device_count = seq_parts * fsdp_parts
    me = lax.axis_index("seq")
    seq_total = local_len * seq_parts
    layer_count = frozen.shape[0]
    adapters = attention_adapter_weights.shape[2]
    parts = seq_parts // slots
    on_block = (fsdp_parts, seq_parts, slots, layer_count) == (16, 2, 2, 2)
    slot = me // parts
    part = me % parts
    tokens = seq_total // parts
    groups = [[s * parts + p for p in range(parts)] for s in range(slots)]

    def to_image(v):
        if parts == 1 and slots == 2:
            mine = lax.dynamic_index_in_dim(v, slot, 0, keepdims=False)
            other = lax.dynamic_index_in_dim(v, 1 - slot, 0, keepdims=False)
            other = lax.ppermute(other, "seq", [(0, 1), (1, 0)])
            return jnp.where(
                slot == 0,
                jnp.concatenate([mine, other], 0),
                jnp.concatenate([other, mine], 0),
            )
        whole = lax.all_gather(v, "seq", axis=1, tiled=True)
        whole = lax.dynamic_index_in_dim(whole, slot, 0, keepdims=False)
        return lax.dynamic_slice_in_dim(whole, part * tokens, tokens, 0)

    def half_of(v, which):
        return lax.dynamic_slice_in_dim(v, which * local_len, local_len, 0)

    def to_tokens(v, other=None):
        if parts == 1 and slots == 2:
            mine = half_of(v, slot)
            if other is None:
                other = lax.ppermute(half_of(v, 1 - slot), "seq", [(0, 1), (1, 0)])
            return jnp.where(slot == 0, jnp.stack([mine, other]), jnp.stack([other, mine]))
        whole = lax.all_gather(v, "seq", axis=0, tiled=True).reshape(slots, seq_total, -1)
        return lax.dynamic_slice_in_dim(whole, me * local_len, local_len, 1)

    length = lax.dynamic_slice_in_dim(lengths, slot, 1, 0)
    adapter = lax.dynamic_index_in_dim(image_adapter_index, slot, 0, keepdims=False)
    is_live = slot < group_image_count[0]
    positions = part * tokens + jnp.arange(tokens, dtype=jnp.int32)
    row_mask = ((positions < length[0]) & is_live).astype(F32)[:, None]
    shards = lax.optimization_barrier(frozen.reshape(layer_count, -1, LANES))
    tiles = -(-(TILES_END + TILES_VECTORS) // (2 * fsdp_parts)) * 2
    if on_block:
        flat, *shards = first_gather([shards[layer] for layer in range(layer_count)], tiles)
    else:
        steps = [(d, d + 1) for d in range(fsdp_parts - 1)]
        steps = (steps, [(b, a) for a, b in steps])
        index = lax.axis_index("fsdp").astype(jnp.int32).reshape(1)
        shards = [lay_shard(index, shards[layer], tiles, steps) for layer in range(layer_count)]
    if on_block:
        other = lax.dynamic_index_in_dim(activations, 1 - slot, 0, keepdims=False)
        other = lax.ppermute(other, "seq", [(0, 1), (1, 0)])
        scalars = jnp.concatenate(
            [image_adapter_index, lengths, group_image_count, slot.astype(jnp.int32)[None]]
        )
        prepared = prepare(
            scalars,
            attention_adapter_weights,
            narrow_adapter_weights,
            broad_adapter_weights,
            activations,
            other,
            flat,
        )
        tables, (bias, hidden, label) = prepared[:4], prepared[4:7]
    else:
        def pick(table):
            return lax.dynamic_index_in_dim(table, adapter, 2, keepdims=False)

        attention_adapters = pick(attention_adapter_weights)
        narrow_adapters = pick(narrow_adapter_weights)
        wide_adapters = pick(broad_adapter_weights)
        wide_adapters = jnp.pad(wide_adapters, ((0, 0), (0, 0), (0, 0), (0, WIDE - FF)))
        lane = lax.broadcasted_iota(jnp.int32, (tokens, LANES - HD), 1)
        key = lax.broadcasted_iota(jnp.int32, (tokens, LANES - HD), 0)
        bias = jnp.where((lane == 0) & (key >= length[0]), NEG, 0.0).astype(BF16)
        hidden = to_image(activations).astype(F32) * row_mask
        up_diagonals = jnp.stack(
            [
                jnp.concatenate(
                    [
                        jnp.pad(attention_adapters[layer, 4 + c], ((0, 0), (c * D, (2 - c) * D)))
                        for c in range(3)
                    ]
                )
                for layer in range(layer_count)
            ]
        )
    stored = []
    weights = []
    for layer in range(layer_count):
        if not on_block:
            flat = lax.all_gather(shards[layer], "fsdp", axis=0, tiled=True)
            flat = jnp.pad(flat, ((0, 16 * TILES_HELD - flat.shape[0]), (0, 0)))
        if layer == layer_count - 1:
            cotangent, flat = lax.optimization_barrier((cotangent, flat))
            d_output = to_image(cotangent)
        w_qkv, w_o, w_1, w_2 = (flat.reshape(-1, panels, 16, LANES) for panels in PANELS)
        if on_block:
            vectors, b_1 = prepared[7:9] if layer == 0 else layer_vectors(flat)
            weights.append((w_qkv, w_o, w_1, w_2, vectors, b_1))
        else:
            vectors = lax.slice_in_dim(flat, 16 * TILES_END, 16 * TILES_END + 106, axis=0).reshape(-1)
            vectors, b_1 = vectors[: 8 * D].reshape(8, D).astype(F32), vectors[8 * D : 8 * D + FF]
            b_1 = jnp.pad(b_1.astype(F32), (0, WIDE - FF))[None, :]
            attn, narrow, wide = attention_adapters[layer], narrow_adapters[layer], wide_adapters[layer]
            weights.append((w_qkv, w_o, w_1, w_2, vectors, attn, narrow, wide))
        keys = None
        if on_block:
            shard = shards[layer + 1] if layer + 1 < layer_count else None
            made = layer_forward(layer, bias, hidden, weights[layer], tables, shard)
            normed, inner_qkv, qkv, attended, stats, inner_o, middle = made[:7]
            normed_two, inner_up, gate, inner_down, next_hidden = made[7:12]
            flat = made[12] if shard is not None else None
        else:
            normed, inner_qkv, qkv = qkv_forward(hidden, w_qkv, vectors, attn)
            keys = lax.all_gather(
                qkv[:, D:], "seq", axis=0, tiled=True, axis_index_groups=groups
            )
            attended, stats = attn_fwd(length, qkv, keys)
            inner_o, middle, normed_two, inner_up, gate, activated = up_forward(
                attended, hidden, w_o, vectors, attn, narrow, w_1, b_1, wide
            )
            inner_down, next_hidden = down_forward(
                activated, middle, w_2, vectors[7:8], narrow, wide
            )
        stored.append(
            (
                hidden,
                normed,
                inner_qkv,
                qkv,
                keys,
                stats,
                attended,
                inner_o,
                middle,
                normed_two,
                inner_up,
                gate,
                inner_down,
            )
        )
        hidden = next_hidden
    output = (hidden * row_mask).astype(BF16)
    other_half = None
    gradient = d_output.astype(F32) * row_mask
    collected = [None] * layer_count
    terms = None
    for layer in reversed(range(layer_count)):
        (
            layer_input,
            normed,
            inner_qkv,
            qkv,
            keys,
            stats,
            attended,
            inner_o,
            middle,
            normed_two,
            inner_up,
            gate,
            inner_down,
        ) = stored[layer]
        if not on_block:
            w_qkv, w_o, w_1, w_2, vectors, attn, narrow, wide = weights[layer]
        if on_block:
            saved = (
                layer_input, normed, inner_qkv, qkv, stats, attended, inner_o, middle, normed_two, inner_up,
                gate, inner_down,
            )
            hosting = layer + 1 < layer_count
            spread = SHARE if layer == 0 else SHARE + 1
            made = layer_backward(
                layer,
                gradient,
                saved,
                weights[layer],
                tables,
                bias,
                label,
                spread,
                adapters if hosting else 0,
                terms,
                half_of(output, 1 - slot),
            )
            gradient, terms = made[:2]
            terms = terms.reshape(device_count, spread, R, LANES)
            if hosting:
                collected[layer + 1], other_half, names = made[3:6]
            if layer == 0:
                sums = share_terms(terms, names, adapters)
                collected[layer] = gather_blocks(sums, 2, 16 * sums.shape[0])
            continue
        if not on_block:
            d_gate, g_wide, d_inner_up, g_up_2 = gate_backward(
                gradient, w_2, gate, narrow, wide, inner_down, inner_up
            )
            d_middle, d_attended, g_middle = middle_backward(
                d_gate, w_1, d_inner_up, narrow, normed_two, middle, gradient, vectors, w_o, attn,
                inner_o, attended,
            )
            d_qkv = attn_bwd(length, qkv, d_attended, attended, stats, keys)
            if parts > 1:
                d_keys = lax.psum_scatter(
                    d_qkv[1].astype(F32),
                    "seq",
                    scatter_dimension=0,
                    tiled=True,
                    axis_index_groups=groups,
                )
                d_qkv = jnp.concatenate([d_qkv[0], d_keys.astype(BF16)], axis=1)
            else:
                d_qkv = d_qkv[0]
            gradient, g_input = input_backward(
                d_qkv, w_qkv, attn, normed, inner_qkv, layer_input, d_middle, vectors
            )
        rows_narrow = jnp.concatenate(
            [
                g_input[: 3 * R],
                g_middle[:R],
                g_input[3 * R :],
                g_middle[R:],
                g_up_2,
            ]
        )
        rows_narrow = rows_narrow.astype(BF16)
        rows_wide = g_wide[:, :FF].astype(BF16)

        def shares(rows):
            share = -(-rows.shape[0] // device_count)
            rows = jnp.pad(rows, ((0, share * device_count - rows.shape[0]), (0, 0)))
            return rows.reshape(device_count, share * rows.shape[1])

        terms = [shares(rows_narrow), shares(rows_wide)]
        used = terms[0].shape[1] + terms[1].shape[1]
        label = jnp.broadcast_to(adapter.astype(BF16), (device_count, -used % LANES + LANES))
        terms = lax.all_to_all(
            jnp.concatenate(terms + [label], axis=1),
            ("fsdp", "seq"),
            split_axis=0,
            concat_axis=0,
            tiled=True,
        )
        choice = jnp.arange(adapters, dtype=F32)[:, None] == terms[:, used].astype(F32)[None, :]
        sums = jnp.dot(choice.astype(F32), terms.astype(F32), precision=lax.Precision.HIGHEST)
        sums = lax.all_gather(sums.astype(BF16), ("fsdp", "seq")).transpose(1, 0, 2)
        split = -(-10 * R // device_count) * D

        def table(part, count, width):
            part = part.reshape(adapters, -1, width)[:, : count * R]
            return part.reshape(adapters, count, R, width).transpose(1, 0, 2, 3).astype(F32)

        collected[layer] = (table(sums[:, :, :split], 10, D), table(sums[:, :, split:used], 2, FF))
    if on_block:
        grad_attn, grad_narrow, grad_wide = gradient_tables(collected, adapters)
    else:
        grad_attn = jnp.stack([entry[0][0:8] for entry in collected], axis=0)
        grad_narrow = jnp.stack([entry[0][8:10] for entry in collected], axis=0)
        grad_wide = jnp.stack([entry[1] for entry in collected], axis=0)
    output = to_tokens(output, other_half)
    input_grad = to_tokens((gradient * row_mask).astype(BF16)).astype(F32)
    return (output, input_grad, grad_attn, grad_narrow, grad_wide)


def solution(mesh):
    in_specs = (
        P("fsdp", "seq", None),
        P("fsdp"),
        P("fsdp"),
        P("fsdp"),
        P(None, "fsdp"),
        P(),
        P(),
        P(),
        P("fsdp", "seq", None),
    )
    out_specs = (P("fsdp", "seq", None), P("fsdp", "seq", None), P(), P(), P())
    return jax.shard_map(local, mesh=mesh, in_specs=in_specs, out_specs=out_specs, check_vma=False)
```

```python
import functools
import math

import jax
import jax.numpy as jnp
from jax import lax
from jax.experimental import pallas as pl
from jax.experimental.pallas import tpu as pltpu
from jax.sharding import PartitionSpec as P

D = 1152
HD = 72
H = 16
FF = 4304
R = 16
LANES = 128
BF16 = jnp.bfloat16
F32 = jnp.float32
MESH = pl.DeviceIdType.MESH
VMEM_LIMIT = 60 << 20
VMEM_MOST = 67043328
C2 = math.log2(math.e) / math.sqrt(HD)
SCALE = 1.0 / math.sqrt(HD)
NEG = -1e30
epsilon = 1e-06
CUT_OUT = 3 * D * D // LANES
CUT_UP = CUT_OUT + D * D // LANES
CUT_DOWN = CUT_UP + D * FF // LANES
CUT_VECTORS = CUT_DOWN + FF * D // LANES


def dot(a, b):
    return jnp.dot(a, b, preferred_element_type=F32)


def dot_t(a, b):
    return lax.dot_general(a, b, (((1,), (1,)), ((), ())), preferred_element_type=F32)


def dot_l(a, b):
    return lax.dot_general(a, b, (((0,), (0,)), ((), ())), preferred_element_type=F32)


PANELS = (3 * D // LANES, D // LANES, 36, D // LANES)
UNITS = (D // 16, D // 16, D // 16, FF // 16)
TILES_AT = (0, 1944, 2592, 5184)
TILES_END = 7605
TILES_VECTORS = 22
TILES_HELD = 7776
FLAT_AT = (0, CUT_OUT, CUT_UP, CUT_DOWN)
WIDE = PANELS[2] * LANES
UP_ROWS = 16 * FF // LANES
HALO = 1600


def lay_rows(d, own_rows, tiles, before, own, after, flat, held, turned):
    margin = 16 * PANELS[2]
    flat[0:HALO] = before.astype(F32)
    flat[HALO : HALO + own_rows] = own.astype(F32)
    flat[HALO + own_rows : 2 * HALO + own_rows] = after.astype(F32)
    flat_base = d * own_rows - HALO
    tile_base = d * tiles

    def span(at, units, panels):
        low = jnp.maximum(tile_base - at, 0) // panels
        high = jnp.maximum(tile_base + tiles - at + panels - 1, 0) // panels
        high = jnp.minimum(high, units)
        return low, jnp.maximum(high, low)

    for at, start, units, panels in zip(
        TILES_AT + (TILES_END,),
        FLAT_AT + (CUT_VECTORS,),
        UNITS + (TILES_VECTORS,),
        PANELS + (1,),
    ):
        low, high = span(at, units, panels)
        if start == CUT_UP:
            lane = lax.broadcasted_iota(jnp.int32, (8, LANES), 1)

            def up_units(b, carry):
                u = low + 8 * b
                source = pl.multiple_of(start + UP_ROWS * u - flat_base, 2)
                for j in range(16):
                    first, shift = (FF * j) // LANES, (FF * j) % LANES
                    turn = LANES - shift
                    now = flat[pl.ds(source + first, 8, stride=UP_ROWS), :]
                    now = pltpu.roll(now, turn, 1) if shift else now
                    for c in range(34):
                        value = now
                        if c < 33 or shift > LANES - FF % LANES:
                            now = flat[pl.ds(source + first + c + 1, 8, stride=UP_ROWS), :]
                            now = pltpu.roll(now, turn, 1) if shift else now
                            if shift:
                                value = jnp.where(lane < turn, value, now)
                        if c == 33:
                            value = jnp.where(lane < FF - 33 * LANES, value, 0.0)
                        turned[pl.ds(16 * c + j, 8, stride=16 * PANELS[2]), :] = value
                target = pl.multiple_of(16 * (at + PANELS[2] * u - tile_base) + margin, 16)
                held[pl.ds(target, 8 * 16 * PANELS[2]), :] = turned[...].astype(BF16)
                return carry

            turned[...] = jnp.zeros_like(turned)
            lax.fori_loop(0, (high - low + 7) // 8, up_units, 0)
        else:

            def unit(u, carry):
                source = pl.multiple_of(start + 16 * panels * u - flat_base, 16)
                target = pl.multiple_of(16 * (at + panels * u - tile_base) + margin, 16)
                for c in range(panels):
                    value = flat[pl.ds(source + c, 16, stride=panels), :]
                    held[pl.ds(target + 16 * c, 16), :] = value.astype(BF16)
                return carry

            lax.fori_loop(low, high, unit, 0)


def lay_kernel(own_rows, tiles, index_ref, before, own, after, out, flat, held, turned):
    margin = 16 * PANELS[2]
    lay_rows(index_ref[0], own_rows, tiles, before[...], own[...], after[...], flat, held, turned)
    out[...] = held[margin : margin + 16 * tiles]


def lay_scratch(own_rows, tiles):
    margin = 16 * PANELS[2]
    return [
        pltpu.VMEM((own_rows + 2 * HALO + 8 * UP_ROWS, LANES), F32),
        pltpu.VMEM((16 * tiles + 10 * margin, LANES), BF16),
        pltpu.VMEM((8 * margin, LANES), F32),
    ]


def lay_shard(index, shard, tiles, perms):
    own_rows = shard.shape[0]
    before = lax.ppermute(shard[own_rows - HALO :], "fsdp", perms[0])
    after = lax.ppermute(shard[:HALO], "fsdp", perms[1])
    vm = pl.BlockSpec(memory_space=pltpu.VMEM)
    return pl.pallas_call(
        functools.partial(lay_kernel, own_rows, tiles),
        in_specs=[pl.BlockSpec(memory_space=pltpu.SMEM), vm, vm, vm],
        out_specs=vm,
        out_shape=jax.ShapeDtypeStruct((16 * tiles, LANES), BF16),
        scratch_shapes=lay_scratch(own_rows, tiles),
        compiler_params=pltpu.CompilerParams(vmem_limit_bytes=VMEM_LIMIT),
        name="lay_shard",
    )(index, before, shard, after)


def pad_lanes(x, extra=None):
    if extra is None:
        extra = jnp.zeros((x.shape[0], LANES - HD), x.dtype)
    return jnp.concatenate([x, extra], axis=1)


def first_lane(rows, value):
    lane = lax.broadcasted_iota(jnp.int32, (rows, LANES - HD), 1)
    return jnp.where(lane == 0, value, 0.0).astype(BF16)


def key_bias(rows, length):
    key = lax.broadcasted_iota(jnp.int32, (rows, LANES - HD), 0)
    return first_lane(rows, jnp.where(key < length, 0.0, NEG))


def attn_fwd_kernel(offset, len_ref, qkv_ref, kv_ref, o_ref, st_ref, q_s, k_s, v_s):
    if kv_ref is None:
        kv_ref = qkv_ref
    rows, keys = qkv_ref.shape[0], kv_ref.shape[0]
    one = first_lane(rows, F32(1.0))
    bias = key_bias(keys, len_ref[0])
    for h in range(H):
        q_s[h] = pad_lanes(qkv_ref[:, h * HD : (h + 1) * HD], one)
        k_s[h] = pad_lanes(kv_ref[:, offset + h * HD : offset + (h + 1) * HD], bias)
        v_s[h] = pad_lanes(kv_ref[:, offset + D + h * HD : offset + D + (h + 1) * HD])
    st_ref[...] = jnp.zeros_like(st_ref)
    lane = lax.broadcasted_iota(jnp.int32, (rows, LANES), 1)

    def body(h, carry):
        s = dot_t(q_s[h], k_s[h])
        m = jnp.max(s, axis=1, keepdims=True)
        p = jnp.exp2((s - m) * C2)
        total = jnp.sum(p, axis=1, keepdims=True)
        o = dot(p.astype(BF16), v_s[h])
        q_s[h] = (o * (1.0 / total)).astype(BF16)
        st_ref[...] = jnp.where(lane == h, m * C2 + jnp.log2(total), st_ref[...])
        return carry

    lax.fori_loop(0, H, body, 0)
    for h in range(H):
        o_ref[:, h * HD : (h + 1) * HD] = q_s[h][:, :HD]


def attn_fwd(length, qkv, kv=None):
    rows = qkv.shape[0]
    keys = rows if kv is None else kv.shape[0]
    vm = pl.BlockSpec(memory_space=pltpu.VMEM)
    if kv is None:
        kernel = lambda a, b, *rest: attn_fwd_kernel(D, a, b, None, *rest)
        operands = (length, qkv)
    else:
        kernel = functools.partial(attn_fwd_kernel, 0)
        operands = (length, qkv, kv)
    return pl.pallas_call(
        kernel,
        in_specs=[pl.BlockSpec(memory_space=pltpu.SMEM)] + [vm] * (len(operands) - 1),
        out_specs=[vm, vm],
        out_shape=[
            jax.ShapeDtypeStruct((rows, D), BF16),
            jax.ShapeDtypeStruct((rows, LANES), F32),
        ],
        scratch_shapes=[
            pltpu.VMEM((H, rows, LANES), BF16),
            pltpu.VMEM((H, keys, LANES), BF16),
            pltpu.VMEM((H, keys, LANES), BF16),
        ],
        cost_estimate=pl.CostEstimate(
            flops=H * rows * keys * 256 * 4, bytes_accessed=rows * D * 8, transcendentals=H * rows * keys
        ),
        compiler_params=pltpu.CompilerParams(vmem_limit_bytes=VMEM_LIMIT),
        name="attention_forward",
    )(*operands)


def attn_bwd_kernel(
    offset, len_ref, qkv_ref, kv_ref, do_ref, o_ref, st_ref, dq_ref, dkv_ref, q_s, k_s, v_s, do_s, st_t, dl_t
):
    if kv_ref is None:
        kv_ref, dkv_ref = qkv_ref, dq_ref
    rows, keys = qkv_ref.shape[0], kv_ref.shape[0]
    one = first_lane(rows, F32(1.0))
    bias = key_bias(keys, len_ref[0])
    lane = lax.broadcasted_iota(jnp.int32, (rows, LANES), 1)
    delta = jnp.zeros((rows, LANES), F32)
    for h in range(H):
        q_s[h] = pad_lanes(qkv_ref[:, h * HD : (h + 1) * HD], one)
        k_s[h] = pad_lanes(kv_ref[:, offset + h * HD : offset + (h + 1) * HD], bias)
        v_s[h] = pad_lanes(kv_ref[:, offset + D + h * HD : offset + D + (h + 1) * HD])
        do = do_ref[:, h * HD : (h + 1) * HD]
        do_s[h] = pad_lanes(do)
        o = o_ref[:, h * HD : (h + 1) * HD].astype(F32)
        d = jnp.sum(do.astype(F32) * o, axis=1, keepdims=True)
        delta = jnp.where(lane == h, d, delta)
    st_t[...] = st_ref[...].T
    dl_t[...] = delta.T

    def body(h, carry):
        q, k, do = q_s[h], k_s[h], do_s[h]
        p = jnp.exp2(dot_t(k, q) * C2 - st_t[pl.ds(h, 1), :])
        dv = dot(p.astype(BF16), do)
        dp = dot_t(v_s[h], do)
        ds = (p * (dp - dl_t[pl.ds(h, 1), :])).astype(BF16)
        dk = dot(ds, q)
        dq = dot(k.T, ds)
        v_s[h] = dv.astype(BF16)
        k_s[h] = (dk * SCALE).astype(BF16)
        q_s[h] = (dq * SCALE).astype(BF16).T
        return carry

    lax.fori_loop(0, H, body, 0)
    for h in range(H):
        dq_ref[:, h * HD : (h + 1) * HD] = q_s[h][:, :HD]
        dkv_ref[:, offset + h * HD : offset + (h + 1) * HD] = k_s[h][:, :HD]
        dkv_ref[:, offset + D + h * HD : offset + D + (h + 1) * HD] = v_s[h][:, :HD]


def attn_bwd(length, qkv, do, o, st, kv=None):
    rows = qkv.shape[0]
    keys = rows if kv is None else kv.shape[0]
    vm = pl.BlockSpec(memory_space=pltpu.VMEM)
    if kv is None:
        kernel = lambda a, b, c, d, e, f, *rest: attn_bwd_kernel(
            D, a, b, None, c, d, e, f, None, *rest
        )
        operands = (length, qkv, do, o, st)
        outs = [jax.ShapeDtypeStruct((rows, 3 * D), BF16)]
    else:
        kernel = functools.partial(attn_bwd_kernel, 0)
        operands = (length, qkv, kv, do, o, st)
        outs = [jax.ShapeDtypeStruct((rows, D), BF16), jax.ShapeDtypeStruct((keys, 2 * D), BF16)]
    return pl.pallas_call(
        kernel,
        in_specs=[pl.BlockSpec(memory_space=pltpu.SMEM)] + [vm] * (len(operands) - 1),
        out_specs=[vm] * len(outs),
        out_shape=outs,
        scratch_shapes=[
            pltpu.VMEM((H, rows, LANES), BF16),
            pltpu.VMEM((H, keys, LANES), BF16),
            pltpu.VMEM((H, keys, LANES), BF16),
            pltpu.VMEM((H, rows, LANES), BF16),
            pltpu.VMEM((LANES, rows), F32),
            pltpu.VMEM((LANES, rows), F32),
        ],
        cost_estimate=pl.CostEstimate(
            flops=H * rows * keys * 256 * 10, bytes_accessed=rows * D * 16, transcendentals=H * rows * keys
        ),
        compiler_params=pltpu.CompilerParams(vmem_limit_bytes=VMEM_LIMIT),
        name="attention_backward",
    )(*operands)


LARGE_BLOCK = 4096


def gather_plan(
    src, out, stage, local_sem, z_recv, y_recv, b_recv, h_recv, c_recv_own, c_recv_z, c_recv_y, c_recv_b, c_recv_h,
    up_send, down_send, y_send, b_send, h_send, c_send_own, c_send_z, c_send_y, c_send_b, c_send_h, pieces=2,
):
    rows = src.shape[0]
    if rows >= LARGE_BLOCK:
        unit = rows // 6 // 16 * 16 + 16
        sizes = [unit, unit, rows // 2 - 2 * unit, rows // 2 - 2 * unit, unit]
        begins = [0, unit, 2 * unit, rows // 2, rows - 2 * unit]
    else:
        sizes = [rows // pieces] * pieces
        begins = [k * (rows // pieces) for k in range(pieces)]
    chunks, across_y = len(sizes), (len(sizes) + 1) // 2
    lend = chunks == 5
    x = lax.axis_index("seq")
    f = lax.axis_index("fsdp")
    z, y, c = f // 4, (f // 2) % 2, f % 2

    def place(zb, yb, j, side, cb=None):
        owner = (zb * 2 + yb) * 2 + (c if cb is None else cb)
        begin = jnp.where(side == 0, begins[j], rows - begins[j] - sizes[j])
        return pl.multiple_of(owner * rows + begin, 16), sizes[j]

    def view(spot):
        return out.at[pl.ds(spot[0], spot[1]), :]

    def device(zb, yb, cb, xb):
        return ((zb * 2 + yb) * 2 + cb, xb)

    up, down = device(z + 1, y, c, x), device(z - 1, y, c, x)
    beside, across, mate = device(z, 1 - y, c, x), device(z, y, c, 1 - x), device(z, y, 1 - c, x)

    def copy(spot, send, recv, to, source=None):
        return pltpu.make_async_remote_copy(
            src_ref=view(spot) if source is None else source,
            dst_ref=view(spot),
            send_sem=send,
            recv_sem=recv,
            device_id=to,
            device_id_type=MESH,
        )

    def arrived(spot, recv):
        copy(spot, local_sem.at[1], recv, mate).wait_recv()

    def own(j):
        begin = jnp.where(x == 0, begins[j], rows - begins[j] - sizes[j])
        return src.at[pl.ds(pl.multiple_of(begin, 16), sizes[j]), :]

    whole = (pl.multiple_of(f * rows, 16), rows)
    keep = pltpu.make_async_copy(src if stage is None else stage, view(whole), local_sem.at[0])

    def greet():
        barrier = pltpu.get_barrier_semaphore()
        for to in (beside, across, mate):
            pl.semaphore_signal(barrier, inc=1, device_id=to, device_id_type=MESH)

        @pl.when(z < 3)
        def _():
            pl.semaphore_signal(barrier, inc=1, device_id=up, device_id_type=MESH)

        @pl.when(z > 0)
        def _():
            pl.semaphore_signal(barrier, inc=1, device_id=down, device_id_type=MESH)

        pl.semaphore_wait(barrier, 3 + jnp.where(z < 3, 1, 0) + jnp.where(z > 0, 1, 0))

    def start(first=True):
        if first:
            greet()
        for j in range(chunks):
            spot = place(z, y, j, x)

            @pl.when(z < 3)
            def _():
                copy(spot, up_send.at[z, j], z_recv.at[z, j], up, own(j)).start()

            @pl.when(z > 0)
            def _():
                copy(spot, down_send.at[z, j], z_recv.at[z, j], down, own(j)).start()

            if j < across_y:
                copy(spot, y_send.at[z, j], y_recv.at[z, j], beside, own(j)).start()
        copy(whole, c_send_own.at[0], c_recv_own.at[0], mate, src).start()
        if stage is None:
            keep.start()
        else:
            fetch = pltpu.make_async_copy(src, stage, local_sem.at[0])
            fetch.start()
            fetch.wait()
            keep.start()

    def z_event(d, j):
        def flow(zb, onward, to, sends):
            spot = place(zb, y, j, x)
            arrived(spot, z_recv.at[zb, j])

            @pl.when(onward)
            def _():
                copy(spot, sends.at[zb, j], z_recv.at[zb, j], to).start()

            if j == 0 and lend:
                copy(spot, b_send.at[zb], b_recv.at[zb], across).start()
            if j < across_y:
                copy(spot, y_send.at[zb, j], y_recv.at[zb, j], beside).start()
            copy(spot, c_send_z.at[zb, j], c_recv_z.at[zb, j], mate).start()

        @pl.when(z - d >= 0)
        def _():
            flow(z - d, z < 3, up, up_send)

        @pl.when(z + d <= 3)
        def _():
            flow(z + d, z > 0, down, down_send)

    def each(d, act):
        if d == 0:
            act(z)
            return

        @pl.when(z - d >= 0)
        def _():
            act(z - d)

        @pl.when(z + d <= 3)
        def _():
            act(z + d)

    def y_event(d, j):
        def act(zb):
            spot = place(zb, 1 - y, j, x)
            arrived(spot, y_recv.at[zb, j])
            copy(spot, h_send.at[zb, j], h_recv.at[zb, j], across).start()
            copy(spot, c_send_y.at[zb, j], c_recv_y.at[zb, j], mate).start()

        each(d, act)

    def b_event(d):
        def act(zb):
            spot = place(zb, y, 0, 1 - x)
            arrived(spot, b_recv.at[zb])
            copy(spot, c_send_b.at[zb], c_recv_b.at[zb], mate).start()

        each(d, act)

    def h_event(d, j):
        def act(zb):
            spot = place(zb, 1 - y, j, 1 - x)
            arrived(spot, h_recv.at[zb, j])
            copy(spot, c_send_h.at[zb, j], c_recv_h.at[zb, j], mate).start()

        each(d, act)

    events = []
    for d in range(4):
        for j in range(chunks):
            at = (d - 1) * chunks + j + 1 if d else 0
            if d:
                events.append((at, functools.partial(z_event, d, j)))
                if j == 0 and lend:
                    events.append((at + 2, functools.partial(b_event, d)))
            if j < across_y:
                ready = at + 1.5 if d else j + 1
                events.append((ready, functools.partial(y_event, d, j)))
                events.append((ready + 2, functools.partial(h_event, d, j)))
    def finish():
        keep.wait()
        other = 1 - c

        def core_spot(zb, yb, j, side):
            return place(zb, yb, j, side, other)

        arrived((pl.multiple_of(((z * 2 + y) * 2 + other) * rows, 16), rows), c_recv_own.at[0])
        copy(whole, c_send_own.at[0], c_recv_own.at[0], mate).wait_send()
        for d in range(4):
            def drain(zb, d=d):
                for j in range(chunks):
                    if d:
                        arrived(core_spot(zb, y, j, x), c_recv_z.at[zb, j])
                        copy(place(zb, y, j, x), c_send_z.at[zb, j], c_recv_z.at[zb, j], mate).wait_send()
                    if j < across_y:
                        arrived(core_spot(zb, 1 - y, j, x), c_recv_y.at[zb, j])
                        arrived(core_spot(zb, 1 - y, j, 1 - x), c_recv_h.at[zb, j])
                        spot = place(zb, 1 - y, j, x)
                        copy(spot, c_send_y.at[zb, j], c_recv_y.at[zb, j], mate).wait_send()
                        copy(spot, h_send.at[zb, j], h_recv.at[zb, j], across).wait_send()
                        spot = place(zb, 1 - y, j, 1 - x)
                        copy(spot, c_send_h.at[zb, j], c_recv_h.at[zb, j], mate).wait_send()
                        spot = place(zb, y, j, x)
                        copy(spot, y_send.at[zb, j], y_recv.at[zb, j], beside).wait_send()
                if d and lend:
                    arrived(core_spot(zb, y, 0, 1 - x), c_recv_b.at[zb])
                    spot = place(zb, y, 0, 1 - x)
                    copy(spot, c_send_b.at[zb], c_recv_b.at[zb], mate).wait_send()
                    spot = place(zb, y, 0, x)
                    copy(spot, b_send.at[zb], b_recv.at[zb], across).wait_send()

            each(d, drain)
            for j in range(chunks):
                @pl.when(jnp.logical_and(z - d >= 0, z < 3))
                def _():
                    zb = z - d
                    copy(place(zb, y, j, x), up_send.at[zb, j], z_recv.at[zb, j], up).wait_send()

                @pl.when(jnp.logical_and(z + d <= 3, z > 0))
                def _():
                    zb = z + d
                    copy(place(zb, y, j, x), down_send.at[zb, j], z_recv.at[zb, j], down).wait_send()

    return start, sorted(events, key=lambda e: e[0]), finish


def gather_kernel(*refs):
    start, events, finish = gather_plan(*refs, pieces=4)
    start()
    for _, event in events:
        event()
    finish()


def gather_semaphores():
    dma = pltpu.SemaphoreType.DMA
    core = [dma((1,)), dma((4, 5)), dma((4, 3)), dma((4,)), dma((4, 3))]
    links = [dma((4, 5)), dma((4, 3)), dma((4,)), dma((4, 3))]
    return [dma((2,))] + links + core + [dma((4, 5))] + links + core


def gather_blocks(shard, collective_id, held_rows):
    rows = shard.shape[0]
    return pl.pallas_call(
        gather_kernel,
        in_specs=[pl.BlockSpec(memory_space=pl.ANY)],
        out_specs=pl.BlockSpec(memory_space=pl.ANY),
        out_shape=jax.ShapeDtypeStruct((held_rows, LANES), BF16),
        scratch_shapes=[pltpu.VMEM((rows, LANES), BF16)] + gather_semaphores(),
        compiler_params=pltpu.CompilerParams(collective_id=collective_id, has_side_effects=True, vmem_limit_bytes=VMEM_LIMIT),
        name="gather_blocks",
    )(shard)


def gelu_parts(x):
    inner = 0.7978845608028654 * (x + 0.044715 * x * x * x)
    return jnp.tanh(inner)


def layer_norm(tensor, gain, offset):
    average = jnp.mean(tensor, axis=-1, keepdims=True)
    centred = tensor - average
    variance = jnp.mean(centred * centred, axis=-1, keepdims=True)
    return centred * lax.rsqrt(variance + epsilon) * gain + offset


def layer_norm_back(d_out, tensor, gain):
    average = jnp.mean(tensor, axis=-1, keepdims=True)
    centred = tensor - average
    variance = jnp.mean(centred * centred, axis=-1, keepdims=True)
    scale = lax.rsqrt(variance + epsilon)
    normal = centred * scale
    d_normal = d_out * gain
    mean_d = jnp.mean(d_normal, axis=-1, keepdims=True)
    mean_dn = jnp.mean(d_normal * normal, axis=-1, keepdims=True)
    return (d_normal - mean_d - normal * mean_dn) * scale


def dot_both(x, w, inner, up):
    cut = w.shape[0] // 256 * 256
    tail = dot(
        jnp.concatenate([x[:, cut:], inner], axis=1), jnp.concatenate([w[cut:], up], axis=0)
    )
    return dot(x[:, :cut], w[:cut]) + tail


def dot_both_t(x, w, inner, up_t):
    cut = w.shape[1] // 256 * 256
    tail = dot_t(
        jnp.concatenate([x[:, cut:], inner], axis=1), jnp.concatenate([w[:, cut:], up_t], axis=1)
    )
    return dot_t(x[:, :cut], w[:, :cut]) + tail


def matrix(ref, count=None):
    units, panels = ref.shape[:2]
    return jnp.concatenate(
        [ref[:, p].reshape(units * 16, LANES) for p in range(count or panels)], axis=1
    )


def unit_block(units, panels, place):
    return pl.BlockSpec((units, panels, 16, LANES), place)


def whole(shape):
    return pl.BlockSpec(shape, lambda i: (0,) * len(shape), pipeline_mode=pl.Buffered(1))


def columns(rows, width):
    return pl.BlockSpec((rows, width), lambda i: (0, i))


def struct(shape, dtype):
    return jax.ShapeDtypeStruct(shape, dtype)


def dense_params(flops, bytes_accessed):
    return dict(
        cost_estimate=pl.CostEstimate(
            flops=flops, bytes_accessed=bytes_accessed, transcendentals=0
        ),
        compiler_params=pltpu.CompilerParams(vmem_limit_bytes=VMEM_LIMIT),
    )


def qkv_kernel(hidden, w, vec, down, up, normed, inner, qkv, parts):
    c = pl.program_id(0)

    @pl.when(c == 0)
    def _():
        value = layer_norm(hidden[...], vec[0:1], vec[1:2]).astype(BF16)
        normed[...] = value
        narrow = dot_t(value, down[...]).astype(BF16)
        inner[...] = narrow
        for part in range(3):
            parts[part] = narrow[:, part * R : (part + 1) * R]

    bias = vec[pl.ds(jnp.where(c == 2, 5, 4), 1), :] * jnp.where(c == 1, 0.0, 1.0)
    qkv[...] = (dot_both(normed[...], matrix(w), parts[c], up[0]) + bias).astype(BF16)


def qkv_forward(hidden, w_qkv, vectors, attn):
    rows = hidden.shape[0]
    return pl.pallas_call(
        qkv_kernel,
        grid=(3,),
        in_specs=[
            whole((rows, D)),
            unit_block(72, 9, lambda i: (0, i, 0, 0)),
            whole((8, D)),
            whole((3 * R, D)),
            pl.BlockSpec((1, R, D), lambda i: (i, 0, 0)),
        ],
        out_specs=[whole((rows, D)), whole((rows, 3 * R)), columns(rows, D)],
        out_shape=[
            struct((rows, D), BF16),
            struct((rows, 3 * R), BF16),
            struct((rows, 3 * D), BF16),
        ],
        scratch_shapes=[pltpu.VMEM((3, rows, R), BF16)],
        name="qkv_forward",
        **dense_params(6 * rows * D * D, 14 * rows * D + 6 * D * D),
    )(hidden, w_qkv, vectors, attn[0:3].reshape(3 * R, D), attn[4:7])


TILE = 512
OUT_BLOCK = pl.BlockSpec(
    (72, 9, 16, LANES), lambda i: (3, 0, 0, 0), pipeline_mode=pl.Buffered(1)
)


def up_kernel(
    attended, hidden, w_o, vec, down_o, up_o, down_1, w_1, b_1, up_1,
    inner_o, middle, normed, inner_up, gate, activated,
):
    @pl.when(pl.program_id(0) == 0)
    def _():
        narrow = dot_t(attended[...], down_o[...]).astype(BF16)
        inner_o[...] = narrow
        middle[...] = hidden[...] + (dot_both(attended[...], matrix(w_o), narrow, up_o[...]) + vec[6:7])
        value = layer_norm(middle[...], vec[2:3], vec[3:4]).astype(BF16)
        normed[...] = value
        inner_up[...] = dot_t(value, down_1[...]).astype(BF16)

    x = dot_both(normed[...], matrix(w_1), inner_up[...], up_1[...]) + b_1[...]
    gate[...] = x.astype(BF16)
    activated[...] = (0.5 * x * (1.0 + gelu_parts(x))).astype(BF16)


def up_forward(attended, hidden, w_o, vectors, attn, narrow, w_1, b_1, wide):
    rows = hidden.shape[0]
    return pl.pallas_call(
        up_kernel,
        grid=(WIDE // TILE,),
        in_specs=[
            whole((rows, D)),
            whole((rows, D)),
            OUT_BLOCK,
            whole((8, D)),
            whole((R, D)),
            whole((R, D)),
            whole((R, D)),
            unit_block(72, 4, lambda i: (1, i, 0, 0)),
            columns(1, TILE),
            columns(R, TILE),
        ],
        out_specs=[
            whole((rows, R)),
            whole((rows, D)),
            whole((rows, D)),
            whole((rows, R)),
            columns(rows, TILE),
            columns(rows, TILE),
        ],
        out_shape=[
            struct((rows, R), BF16),
            struct((rows, D), F32),
            struct((rows, D), BF16),
            struct((rows, R), BF16),
            struct((rows, WIDE), BF16),
            struct((rows, WIDE), BF16),
        ],
        name="up_forward",
        **dense_params(2 * rows * D * (D + FF), 12 * rows * D + 4 * rows * FF + 2 * D * (D + FF)),
    )(attended, hidden, w_o, vectors, attn[3], attn[7], narrow[0], w_1, b_1, wide[0])


THIRD = D // 3


def down_kernel(activated, middle, w_2, b_2, down_2, up_2, inner, hidden):
    @pl.when(pl.program_id(0) == 0)
    def _():
        inner[...] = dot_t(activated[...], down_2[...]).astype(BF16)

    value = activated[:, :FF]

    hidden[...] = middle[...] + (
        dot(value, matrix(w_2)) + b_2[...] + dot(inner[...], up_2[...])
    )


def down_forward(activated, middle, w_2, b_2, narrow, wide):
    rows = middle.shape[0]
    return pl.pallas_call(
        down_kernel,
        grid=(3,),
        in_specs=[
            whole((rows, WIDE)),
            columns(rows, THIRD),
            pl.BlockSpec(
                (pl.Element(UNITS[3]), pl.Element(3), pl.Element(16), pl.Element(LANES)),
                lambda i: (TILES_AT[3] // 9, 3 * i, 0, 0),
            ),
            columns(1, THIRD),
            whole((R, WIDE)),
            columns(R, THIRD),
        ],
        out_specs=[whole((rows, R)), columns(rows, THIRD)],
        out_shape=[struct((rows, R), BF16), struct((rows, D), F32)],
        name="down_forward",
        **dense_params(2 * rows * D * FF, 8 * rows * D + 2 * rows * FF + 2 * D * FF),
    )(activated, middle, w_2, b_2, wide[1], narrow[1])


def gate_kernel(
    gradient, w_2, gate, down_2, up_1, up_2, inner_down, inner_up, d_gate, g_wide, d_inner_up, g_up_2,
    d_branch, d_inner_down, total,
):
    i = pl.program_id(0)

    @pl.when(i == 0)
    def _():
        value = gradient[...].astype(BF16)
        d_branch[...] = value
        d_inner_down[...] = dot_t(value, up_2[...]).astype(BF16)
        g_up_2[...] = dot_l(inner_down[...], value)
        total[...] = jnp.zeros_like(total)

    left = FF - i * TILE
    down = down_2[...]
    d_act = dot_t(d_branch[...], matrix(w_2)) + dot(d_inner_down[...], down)
    x = gate[...].astype(F32)
    t = gelu_parts(x)
    half = 0.5 * (1.0 + t)
    slope = half + 0.5 * x * (1.0 - t * t) * (
        0.7978845608028654 * (1.0 + 3 * 0.044715 * x * x)
    )
    keep = lax.broadcasted_iota(jnp.int32, (1, TILE), 1) < left
    value = jnp.where(keep, slope * d_act, 0.0).astype(BF16)
    d_gate[...] = value
    total[...] += dot_t(value, up_1[...])
    g_wide[0:R] = dot_l(inner_up[...], value)
    g_wide[R : 2 * R] = dot_l(d_inner_down[...], (x * half).astype(BF16))

    @pl.when(i == pl.num_programs(0) - 1)
    def _():
        d_inner_up[...] = total[...].astype(BF16)


def gate_backward(gradient, w_2, gate, narrow, wide, inner_down, inner_up):
    rows = gradient.shape[0]
    return pl.pallas_call(
        gate_kernel,
        grid=(WIDE // TILE,),
        in_specs=[
            whole((rows, D)),
            unit_block(TILE // 16, 9, lambda i: (TILES_AT[3] // 9 * 16 // TILE + i, 0, 0, 0)),
            columns(rows, TILE),
            columns(R, TILE),
            columns(R, TILE),
            whole((R, D)),
            whole((rows, R)),
            whole((rows, R)),
        ],
        out_specs=[columns(rows, TILE), columns(2 * R, TILE), whole((rows, R)), whole((R, D))],
        out_shape=[
            struct((rows, WIDE), BF16),
            struct((2 * R, WIDE), F32),
            struct((rows, R), BF16),
            struct((R, D), F32),
        ],
        scratch_shapes=[
            pltpu.VMEM((rows, D), BF16),
            pltpu.VMEM((rows, R), BF16),
            pltpu.VMEM((rows, R), F32),
        ],
        name="gate_backward",
        **dense_params(2 * rows * D * FF, 4 * rows * D + 4 * rows * FF + 2 * D * FF),
    )(gradient, w_2, gate, wide[1], wide[0], narrow[1], inner_down, inner_up)


def middle_kernel(
    d_gate, w_1, d_inner_up, down_1, normed, middle, gradient, vec, w_o, down_o, up_o, inner_o, attended,
    d_middle, d_attended, g_rows, d_normed,
):
    i = pl.program_id(0)
    at = pl.ds(pl.multiple_of(i * THIRD, LANES), THIRD)
    d_normed[:, at] = dot_t(d_gate[:, : 34 * LANES], matrix(w_1, 34)) + dot(
        d_inner_up[...], down_1[:, at]
    )

    @pl.when(i == pl.num_programs(0) - 1)
    def _():
        value = gradient[...] + layer_norm_back(d_normed[...], middle[...], vec[2:3])
        d_middle[...] = value
        d_out = value.astype(BF16)
        d_inner_o = dot_t(d_out, up_o[...]).astype(BF16)
        d_attended[...] = (dot_t(d_out, matrix(w_o)) + dot(d_inner_o, down_o[...])).astype(BF16)
        g_rows[0:R] = dot_l(d_inner_o, attended[...])
        g_rows[R : 2 * R] = dot_l(inner_o[...], d_out)
        g_rows[2 * R : 3 * R] = dot_l(d_inner_up[...], normed[...])


def middle_backward(
    d_gate, w_1, d_inner_up, narrow, normed, middle, gradient, vectors, w_o, attn, inner_o, attended
):
    rows = gradient.shape[0]
    return pl.pallas_call(
        middle_kernel,
        grid=(3,),
        in_specs=[
            whole((rows, WIDE)),
            unit_block(THIRD // 16, PANELS[2], lambda i: (3 + i, 0, 0, 0)),
            whole((rows, R)),
            whole((R, D)),
            whole((rows, D)),
            whole((rows, D)),
            whole((rows, D)),
            whole((8, D)),
            OUT_BLOCK,
            whole((R, D)),
            whole((R, D)),
            whole((rows, R)),
            whole((rows, D)),
        ],
        out_specs=[whole((rows, D)), whole((rows, D)), whole((3 * R, D))],
        out_shape=[
            struct((rows, D), F32),
            struct((rows, D), BF16),
            struct((3 * R, D), F32),
        ],
        scratch_shapes=[pltpu.VMEM((rows, D), F32)],
        name="middle_backward",
        **dense_params(2 * rows * D * (D + FF), 18 * rows * D + 2 * rows * FF + 2 * D * (D + FF)),
    )(
        d_gate, w_1, d_inner_up, narrow[0], normed, middle, gradient, vectors, w_o, attn[3], attn[7],
        inner_o, attended,
    )


def input_kernel(
    d_qkv, w_qkv, down, up, normed, inner, hidden, d_middle, vec, gradient, g_rows, d_normed, d_inner
):
    i = pl.program_id(0)

    @pl.when(i == 0)
    def _():
        for c in range(3):
            part = d_qkv[:, c * D : (c + 1) * D]
            d_inner[:, c * R : (c + 1) * R] = dot_t(part, up[c]).astype(BF16)
            g_rows[(3 + c) * R : (4 + c) * R] = dot_l(inner[:, c * R : (c + 1) * R], part)
        g_rows[0 : 3 * R] = dot_l(d_inner[...], normed[...])

    at = pl.ds(pl.multiple_of(i * THIRD, LANES), THIRD)
    d_normed[:, at] = dot_t(d_qkv[...], matrix(w_qkv)) + dot(d_inner[...], down[:, at])

    @pl.when(i == pl.num_programs(0) - 1)
    def _():
        gradient[...] = d_middle[...] + layer_norm_back(d_normed[...], hidden[...], vec[0:1])


def input_backward(d_qkv, w_qkv, attn, normed, inner, hidden, d_middle, vectors):
    rows = hidden.shape[0]
    return pl.pallas_call(
        input_kernel,
        grid=(3,),
        in_specs=[
            whole((rows, 3 * D)),
            unit_block(THIRD // 16, 27, lambda i: (i, 0, 0, 0)),
            whole((3 * R, D)),
            whole((3, R, D)),
            whole((rows, D)),
            whole((rows, 3 * R)),
            whole((rows, D)),
            whole((rows, D)),
            whole((8, D)),
        ],
        out_specs=[whole((rows, D)), whole((6 * R, D))],
        out_shape=[struct((rows, D), F32), struct((6 * R, D), F32)],
        scratch_shapes=[pltpu.VMEM((rows, D), F32), pltpu.VMEM((rows, 3 * R), BF16)],
        name="input_backward",
        **dense_params(6 * rows * D * D, 20 * rows * D + 6 * D * D),
    )(d_qkv, w_qkv, attn[0:3].reshape(3 * R, D), attn[4:7], normed, inner, hidden, d_middle, vectors)


PAIR = 2 * LANES
PAIRS = -(-D // PAIR)
FOUR = 4
FORWARD_STEPS = (3, H // FOUR, WIDE // TILE, PAIRS)
FORWARD_AT = (0, 3, 3 + H // FOUR, 3 + H // FOUR + WIDE // TILE)
FORWARD_BEGINS = (
    [4.5 * i for i in range(3)]
    + [14 + 6 * i for i in range(H // FOUR)]
    + [38 + (5 if i else 0) + 2.6 * i for i in range(WIDE // TILE)]
    + [65 + 3 * i for i in range(PAIRS)]
)
CHUNK_TIME = 7.4


def of_layer(layer, *shape):
    return pl.BlockSpec(
        (1,) + shape, lambda i: (layer,) + (0,) * len(shape), pipeline_mode=pl.Buffered(1)
    )


def forward_kernel(with_gather, *refs):
    (
        bias_lane, hidden, w_qkv, vec, attn, w_o, narrow_in, w_1, b_1, up_1, w_2, w_2_odd, b_2, down_2, up_2,
    ) = refs[:15]
    refs = refs[15:]
    if with_gather:
        shard, refs = refs[0], refs[1:]
    (
        normed, inner_qkv, qkv, attended, stats, inner_o, middle, normed_two, inner_up, gate, inner_down,
        next_hidden,
    ) = refs[:12]
    refs = refs[12:]
    if with_gather:
        flat, refs = refs[0], refs[1:]
    heads, activated, parts = refs[:3]
    i = pl.program_id(0)
    rows = hidden.shape[0]
    _, att_at, up_at, down_at = FORWARD_AT
    last = down_at + PAIRS - 1

    def at_step(k):
        return pl.when(i == k)

    if with_gather:
        start, events, finish = gather_plan(shard, flat, None, *refs[3:])
        at_step(0)(start)
        steps = [[] for _ in FORWARD_BEGINS]
        late = []
        for when, event in events:
            ready = [k for k, begin in enumerate(FORWARD_BEGINS) if begin >= CHUNK_TIME * when + 4]
            (steps[ready[0]] if ready else late).append(event)
        for k, due in enumerate(steps):
            if due:

                @at_step(k)
                def _(due=due):
                    for event in due:
                        event()

    @pl.when(i < att_at)
    def _():
        @at_step(0)
        def _():
            value = layer_norm(hidden[...], vec[0:1], vec[1:2]).astype(BF16)
            normed[...] = value
            narrow = dot_t(value, attn[0, 0:3].reshape(3 * R, D)).astype(BF16)
            inner_qkv[...] = narrow
            for part in range(3):
                parts[part] = narrow[:, part * R : (part + 1) * R]
            stats[...] = jnp.zeros_like(stats)

        bias = vec[pl.ds(jnp.where(i == 2, 5, 4), 1), :] * jnp.where(i == 1, 0.0, 1.0)
        value = (dot_both(normed[...], matrix(w_qkv), parts[i], attn[0, 4 + i]) + bias).astype(BF16)
        qkv[...] = value
        mark = jnp.where(i == 0, first_lane(rows, F32(1.0)), jnp.where(i == 1, bias_lane[...], jnp.zeros_like(bias_lane[...])))
        for h in range(H):
            heads[i, h] = pad_lanes(value[:, h * HD : (h + 1) * HD], mark)

    @pl.when(jnp.logical_and(i >= att_at, i < up_at))
    def _():
        lane = lax.broadcasted_iota(jnp.int32, (rows, LANES), 1)
        pair_at = (i - att_at) * FOUR
        scores = [dot_t(heads[0, pair_at + k], heads[1, pair_at + k]) for k in range(FOUR)]
        kept = stats[...]
        for k in range(FOUR):
            h, s = pair_at + k, scores[k]
            m = jnp.max(s, axis=1, keepdims=True)
            p = jnp.exp2((s - m) * C2)
            total = jnp.sum(p, axis=1, keepdims=True)
            o = dot(p.astype(BF16), heads[2, h])
            heads[0, h] = (o * (1.0 / total)).astype(BF16)
            kept = jnp.where(lane == h, m * C2 + jnp.log2(total), kept)
        stats[...] = kept

    @pl.when(jnp.logical_and(i >= up_at, i < down_at))
    def _():
        t = i - up_at

        @at_step(up_at)
        def _():
            for h in range(H):
                attended[:, h * HD : (h + 1) * HD] = heads[0, h][:, :HD]
            value = attended[...]
            narrow = dot_t(value, attn[0, 3]).astype(BF16)
            inner_o[...] = narrow
            middle[...] = hidden[...] + (dot_both(value, matrix(w_o), narrow, attn[0, 7]) + vec[6:7])
            value = layer_norm(middle[...], vec[2:3], vec[3:4]).astype(BF16)
            normed_two[...] = value
            inner_up[...] = dot_t(value, narrow_in[0, 0]).astype(BF16)

        x = dot_both(normed_two[...], matrix(w_1), inner_up[...], up_1[0, 0]) + b_1[...]
        gate[...] = x.astype(BF16)
        value = (0.5 * x * (1.0 + gelu_parts(x))).astype(BF16)
        activated[:, pl.ds(pl.multiple_of(t * TILE, LANES), TILE)] = value

    @pl.when(i >= down_at)
    def _():
        @at_step(down_at)
        def _():
            w = jnp.concatenate([matrix(w_2.at[: UNITS[3]]), down_2[0, 0].T[:FF]], axis=1)
            value = dot(activated[:, :FF], w)
            narrow = value[:, LANES : LANES + R].astype(BF16)
            inner_down[...] = narrow
            value = value[:, :LANES] + b_2[:, :LANES] + dot(narrow, up_2[0, 0, :, :LANES])
            next_hidden[:, :LANES] = middle[:, D - LANES :] + value

        @pl.when(i > down_at)
        def _():
            at = pl.ds(pl.multiple_of((i - down_at - 1) * PAIR, LANES), PAIR)
            w = jnp.concatenate([matrix(w.at[: UNITS[3]]) for w in (w_2, w_2_odd)], axis=1)
            value = dot(activated[:, :FF], w) + b_2[...] + dot(inner_down[...], up_2[0, 0])
            next_hidden[...] = middle[:, at] + value

    if with_gather:

        @at_step(last)
        def _():
            for event in late:
                event()
            finish()


def layer_forward(layer, bias, hidden, weights, tables, shard=None):
    w_qkv, w_o, w_1, w_2, vectors, b_1 = weights
    attn, narrow, wide, _ = tables
    rows = hidden.shape[0]
    _, att_at, up_at, down_at = FORWARD_AT

    def step(i, k):
        return jnp.minimum(jnp.maximum(i - FORWARD_AT[k], 0), FORWARD_STEPS[k] - 1)

    def cols(count, width, k):
        return pl.BlockSpec((count, width), lambda i: (0, step(i, k)))

    def pair(i):
        return jnp.where(step(i, 3) == 0, PAIRS - 1, step(i, 3) - 1)

    def pairs(count):
        return pl.BlockSpec((count, PAIR), lambda i: (0, pair(i)))

    operands = [
        bias, hidden, w_qkv, vectors, attn, w_o, narrow, w_1, b_1, wide, w_2, w_2, vectors[7:8], wide, narrow,
    ]
    in_specs = [
        whole((rows, LANES - HD)),
        whole((rows, D)),
        unit_block(72, 9, lambda i: (0, step(i, 0), 0, 0)),
        whole((8, D)),
        of_layer(layer, 8, R, D),
        OUT_BLOCK,
        of_layer(layer, 2, R, D),
        unit_block(72, 4, lambda i: (1, step(i, 2), 0, 0)),
        cols(1, TILE, 2),
        pl.BlockSpec((1, 1, R, TILE), lambda i: (layer, 0, 0, step(i, 2))),
        unit_block(288, 1, lambda i: (2, 2 * pair(i), 0, 0)),
        unit_block(288, 1, lambda i: (2, jnp.minimum(2 * pair(i) + 1, 8), 0, 0)),
        pairs(1),
        pl.BlockSpec((1, 1, R, WIDE), lambda i: (layer, 1, 0, 0), pipeline_mode=pl.Buffered(1)),
        pl.BlockSpec((1, 1, R, PAIR), lambda i: (layer, 1, 0, pair(i))),
    ]
    outs = [
        (whole((rows, D)), struct((rows, D), BF16)),
        (whole((rows, 3 * R)), struct((rows, 3 * R), BF16)),
        (cols(rows, D, 0), struct((rows, 3 * D), BF16)),
        (whole((rows, D)), struct((rows, D), BF16)),
        (whole((rows, LANES)), struct((rows, LANES), F32)),
        (whole((rows, R)), struct((rows, R), BF16)),
        (whole((rows, D)), struct((rows, D), F32)),
        (whole((rows, D)), struct((rows, D), BF16)),
        (whole((rows, R)), struct((rows, R), BF16)),
        (cols(rows, TILE, 2), struct((rows, WIDE), BF16)),
        (whole((rows, R)), struct((rows, R), BF16)),
        (pairs(rows), struct((rows, D), F32)),
    ]
    scratch = [
        pltpu.VMEM((3, H, rows, LANES), BF16),
        pltpu.VMEM((rows, WIDE), BF16),
        pltpu.VMEM((3, rows, R), BF16),
    ]
    params = dict(vmem_limit_bytes=VMEM_MOST)
    if shard is not None:
        operands.append(shard)
        in_specs.append(pl.BlockSpec(memory_space=pl.ANY))
        outs.append(
            (pl.BlockSpec(memory_space=pl.ANY), struct((16 * TILES_HELD, LANES), BF16))
        )
        scratch += gather_semaphores()
        params.update(collective_id=3, has_side_effects=True)
    return pl.pallas_call(
        functools.partial(forward_kernel, shard is not None),
        grid=(sum(FORWARD_STEPS),),
        in_specs=in_specs,
        out_specs=[spec for spec, _ in outs],
        out_shape=[shape for _, shape in outs],
        scratch_shapes=scratch,
        cost_estimate=pl.CostEstimate(
            flops=2 * rows * D * (4 * D + 2 * FF) + 8 * rows * rows * D,
            bytes_accessed=2 * D * (4 * D + 2 * FF) + 30 * rows * D,
            transcendentals=H * rows * rows,
        ),
        compiler_params=pltpu.CompilerParams(**params),
        name="layer_forward_gather" if shard is not None else "layer_forward",
    )(*operands)


def first_gather_kernel(tiles, shard_a, shard_b, gathered, laid_a, laid_b, own, halo, flat, held, turned, *sems):
    own_sem, halo_send, halo_recv = sems[:3]
    f = lax.axis_index("fsdp")
    x = lax.axis_index("seq")
    z = f // 4
    rows = shard_a.shape[0]
    last = lax.axis_size("fsdp") - 1
    margin = 16 * PANELS[2]
    barrier = pltpu.get_barrier_semaphore()
    start, events, finish = gather_plan(laid_a, gathered, None, *sems[3:])

    def greet(to):
        pl.semaphore_signal(barrier, inc=1, device_id=to, device_id_type=MESH)

    y, c = (f // 2) % 2, f % 2
    for to in ((f + 2 - 4 * y, x), (f, 1 - x), (f + 1 - 2 * c, x)):
        greet(to)
    for there, step in ((z < 3, 4), (z > 0, -4), (f < last, 1), (f > 0, -1)):

        @pl.when(there)
        def _(step=step):
            greet((f + step, x))

    expected = 3
    for there in (z < 3, z > 0, f < last, f > 0):
        expected = expected + jnp.where(there, 1, 0)
    pl.semaphore_wait(barrier, expected)

    def halo_copy(layer, side):
        source = (shard_a, shard_b)[layer].at[pl.ds((rows - HALO) * (1 - side), HALO), :]
        return pltpu.make_async_remote_copy(
            src_ref=source,
            dst_ref=halo.at[layer, side],
            send_sem=halo_send.at[layer, side],
            recv_sem=halo_recv.at[layer, side],
            device_id=(f + 1 - 2 * side, x),
            device_id_type=MESH,
        )

    def sends(side):
        return f < last if side == 0 else f > 0

    def takes(side):
        return sends(1 - side)

    for layer in range(2):
        for side in range(2):

            @pl.when(sends(side))
            def _(layer=layer, side=side):
                halo_copy(layer, side).start()

    def lay(layer, source, laid):
        fetch = pltpu.make_async_copy(source, own, own_sem.at[0])
        fetch.start()
        fetch.wait()
        for side in range(2):

            @pl.when(takes(side))
            def _(side=side):
                halo_copy(layer, side).wait_recv()

            @pl.when(jnp.logical_not(takes(side)))
            def _(side=side):
                halo[layer, side] = jnp.zeros((HALO, LANES), BF16)

        lay_rows(f, rows, tiles, halo[layer, 0], own[...], halo[layer, 1], flat, held, turned)
        keep = pltpu.make_async_copy(held.at[pl.ds(margin, 16 * tiles), :], laid, own_sem.at[0])
        keep.start()
        keep.wait()

    lay(0, shard_a, laid_a)
    start(False)
    lay(1, shard_b, laid_b)
    for _, event in events:
        event()
    finish()
    for layer in range(2):
        for side in range(2):

            @pl.when(sends(side))
            def _(layer=layer, side=side):
                halo_copy(layer, side).wait_send()


def first_gather(shards, tiles):
    rows = shards[0].shape[0]
    dma = pltpu.SemaphoreType.DMA
    hbm = pl.BlockSpec(memory_space=pl.ANY)
    laid = jax.ShapeDtypeStruct((16 * tiles, LANES), BF16)
    return pl.pallas_call(
        functools.partial(first_gather_kernel, tiles),
        in_specs=[hbm, hbm],
        out_specs=[hbm, hbm, hbm],
        out_shape=[jax.ShapeDtypeStruct((16 * TILES_HELD, LANES), BF16), laid, laid],
        scratch_shapes=[pltpu.VMEM((rows, LANES), BF16), pltpu.VMEM((2, 2, HALO, LANES), BF16)]
        + lay_scratch(rows, tiles)
        + [dma((1,)), dma((2, 2)), dma((2, 2))]
        + gather_semaphores(),
        compiler_params=pltpu.CompilerParams(
            collective_id=0, has_side_effects=True, vmem_limit_bytes=VMEM_MOST
        ),
        name="first_gather",
    )(*shards)


SHARE = 5
SHARE_ROWS = SHARE * 16


def share_plan(
    adapters, named, terms, names, out, held, totals, sums, local_sem, send, recv, pair_sem
):
    x = lax.axis_index("seq")
    f = lax.axis_index("fsdp")
    count = terms.shape[0]
    me = f * 2 + x
    rows = adapters * SHARE_ROWS

    def device(k):
        return (k // 2, k % 2)

    def share_to(to, slot):
        return pltpu.make_async_remote_copy(
            src_ref=terms.at[to],
            dst_ref=held.at[slot],
            send_sem=send.at[to],
            recv_sem=recv.at[slot],
            device_id=device(to),
            device_id_type=MESH,
        )

    def own():
        return pltpu.make_async_copy(terms.at[me], held.at[me], local_sem.at[0])

    def across(side):
        part = out.at[pl.ds(pl.multiple_of(side * rows, 16), rows), :]
        return pltpu.make_async_remote_copy(
            src_ref=part,
            dst_ref=part,
            send_sem=pair_sem.at[0],
            recv_sem=pair_sem.at[1],
            device_id=(f, 1 - x),
            device_id_type=MESH,
        )

    def start():
        barrier = pltpu.get_barrier_semaphore()

        def greet(k, carry):
            to = (me + k) % count
            pl.semaphore_signal(barrier, inc=1, device_id=device(to), device_id_type=MESH)
            return carry

        lax.fori_loop(1, count, greet, 0)
        pl.semaphore_wait(barrier, count - 1)

        def post(k, carry):
            to = (me + k) % count
            share_to(to, me).start()
            return carry

        lax.fori_loop(1, count, post, 0)
        own().start()

    def add_up():
        totals[...] = jnp.zeros_like(totals)

        def add(slot):
            value = held[slot, :SHARE].reshape(SHARE_ROWS, LANES).astype(F32)
            if named:
                name = names[pl.ds(slot, 1), :]
            else:
                name = held[slot, SHARE].astype(F32)[0:1]
                names[pl.ds(slot, 1), :] = name
            for e in range(adapters):
                totals[e] += jnp.where(name == float(e), value, 0.0)

        own().wait()
        add(me)

        def take(k, carry):
            slot = (me + count - k) % count
            share_to(slot, slot).wait_recv()
            add(slot)
            return carry

        lax.fori_loop(1, count, take, 0)
        sums[...] = totals[...].reshape(rows, LANES).astype(BF16)
        part = out.at[pl.ds(pl.multiple_of(x * rows, 16), rows), :]
        keep = pltpu.make_async_copy(sums, part, local_sem.at[0])
        keep.start()
        keep.wait()
        across(x).start()

    def finish():
        def sent(k, carry):
            to = (me + k) % count
            share_to(to, me).wait_send()
            return carry

        lax.fori_loop(1, count, sent, 0)
        across(x).wait_send()
        across(1 - x).wait_recv()

    return start, add_up, finish


def share_kernel(adapters, *refs):
    for part in share_plan(adapters, True, *refs):
        part()


def share_scratch(count, adapters, tiles):
    dma = pltpu.SemaphoreType.DMA
    rows = adapters * SHARE_ROWS
    return [
        pltpu.VMEM((count, tiles, 16, LANES), BF16),
        pltpu.VMEM((adapters, SHARE_ROWS, LANES), F32),
        pltpu.VMEM((rows, LANES), BF16),
        dma((1,)),
        dma((count,)),
        dma((count,)),
        dma((2,)),
    ]


def share_terms(terms, names, adapters):
    rows = adapters * SHARE_ROWS
    return pl.pallas_call(
        functools.partial(share_kernel, adapters),
        in_specs=[pl.BlockSpec(memory_space=pl.ANY), pl.BlockSpec(memory_space=pltpu.VMEM)],
        out_specs=pl.BlockSpec(memory_space=pl.ANY),
        out_shape=jax.ShapeDtypeStruct((2 * rows, LANES), BF16),
        scratch_shapes=share_scratch(terms.shape[0], adapters, SHARE),
        compiler_params=pltpu.CompilerParams(
            collective_id=1, has_side_effects=True, vmem_limit_bytes=VMEM_LIMIT
        ),
        name="share_terms",
    )(terms, names)


def table_kernel(layers, *refs):
    attn, narrow, wide = refs[layers:]
    for layer in range(layers):
        source = refs[layer]
        for t in range(10 * 9 + 2 * 34):
            tile = source[t // SHARE, 0, t % SHARE].astype(F32)
            if t < 90:
                at = slice(t % 9 * LANES, (t % 9 + 1) * LANES)
                if t < 72:
                    attn[layer, t // 9, 0, :, at] = tile
                else:
                    narrow[layer, t // 9 - 8, 0, :, at] = tile
            else:
                c, p = (t - 90) // 34, (t - 90) % 34
                width = min(LANES, FF - p * LANES)
                wide[layer, c, 0, :, p * LANES : p * LANES + width] = tile[:, :width]


def gradient_tables(gathered, adapters):
    layers = len(gathered)
    count = gathered[0].shape[0] // (adapters * SHARE_ROWS)
    gathered = [g.reshape(count, adapters, SHARE, 16, LANES) for g in gathered]

    def out_block(kinds, width):
        return pl.BlockSpec((layers, kinds, 1, R, width), lambda e: (0, 0, e, 0, 0))

    return pl.pallas_call(
        functools.partial(table_kernel, layers),
        grid=(adapters,),
        in_specs=[pl.BlockSpec((count, 1, SHARE, 16, LANES), lambda e: (0, e, 0, 0, 0))] * layers,
        out_specs=[out_block(8, D), out_block(2, D), out_block(2, FF)],
        out_shape=[
            struct((layers, 8, adapters, R, D), F32),
            struct((layers, 2, adapters, R, D), F32),
            struct((layers, 2, adapters, R, FF), F32),
        ],
        compiler_params=pltpu.CompilerParams(vmem_limit_bytes=VMEM_LIMIT),
        name="gradient_tables",
    )(*gathered)


BACKWARD_STEPS = (WIDE // TILE, PAIRS, 1, H // FOUR, PAIRS)
BACKWARD_AT = (0, 9, 14, 15, 15 + H // FOUR)
SHARE_AT, PASS_AT, GATHER_AT = 7, 9, 10


def backward_kernel(adapters, spread, *refs):
    (
        gradient, w_2, gate, down_2, inner_down, inner_up, w_1, w_1_odd, up_1, narrow, normed_two_in, vec, w_o, attn,
        label, inner_o, attended, bias, stats, w_qkv, w_qkv_odd, up, inner_qkv, middle_in, qkv_in, hidden_in, normed_in,
    ) = refs[:27]
    refs = refs[27:]
    if adapters:
        terms, half, refs = refs[0], refs[1], refs[2:]
    new_gradient, new_terms = refs[:2]
    refs = refs[2:]
    if adapters:
        pair, gathered, other_half, names, refs = refs[0], refs[1], refs[2], refs[3], refs[4:]
    (
        d_branch, d_inner_down, d_inner_up, wide, residual, d_normed, heads, stat_t, delta_t, load_sem,
    ) = refs[:10]
    refs = refs[10:]
    i = pl.program_id(0)
    _, middle_at, turn_at, att_at, input_at = BACKWARD_AT
    last = input_at + PAIRS - 1

    def at_step(k):
        return pl.when(i == k)

    def place(t):
        return t if spread == SHARE else t // SHARE * spread + t % SHARE

    def put(table, value):
        for p in range(D // LANES):
            tile = value[:, p * LANES : (p + 1) * LANES]
            new_terms[place(table * (D // LANES) + p)] = tile.astype(BF16)

    def load_middle():
        return pltpu.make_async_copy(middle_in, residual, load_sem.at[0])

    def load_qkv():
        return pltpu.make_async_copy(qkv_in, wide.at[:, : 3 * D], load_sem.at[1])

    def load_hidden():
        return pltpu.make_async_copy(hidden_in, residual, load_sem.at[0])

    def load_normed_two():
        return pltpu.make_async_copy(normed_two_in, d_branch, load_sem.at[2])

    def load_normed():
        return pltpu.make_async_copy(normed_in, d_branch, load_sem.at[2])

    if adapters:
        share_start, share_sum, share_finish = share_plan(
            adapters, False, terms, names, pair, *refs[:7]
        )
        swap_sem = refs[7]
        start, events, finish = gather_plan(pair, gathered, None, *refs[8:])
        swap = pltpu.make_async_remote_copy(
            src_ref=half,
            dst_ref=other_half,
            send_sem=swap_sem.at[0],
            recv_sem=swap_sem.at[1],
            device_id=(lax.axis_index("fsdp"), 1 - lax.axis_index("seq")),
            device_id_type=MESH,
        )
        at_step(0)(share_start)
        at_step(GATHER_AT + 9)(swap.start)
        at_step(SHARE_AT)(share_sum)
        at_step(PASS_AT)(share_finish)

        @at_step(GATHER_AT)
        def _():
            start(False)

        steps = {}
        for when, event in events:
            steps.setdefault(min(GATHER_AT + 1 + int(when), last), []).append(event)
        for k, due in steps.items():

            @at_step(k)
            def _(due=due):
                for event in due:
                    event()

    @pl.when(i < middle_at)
    def _():
        @at_step(0)
        def _():
            load_middle().start()
            value = gradient[...].astype(BF16)
            d_branch[...] = value
            d_inner_down[...] = dot_t(value, narrow[0, 1]).astype(BF16)
            put(9, dot_l(inner_down[...], value))
            for t in (158, 159):
                new_terms[place(t)] = jnp.zeros((R, LANES), BF16)
            if spread > SHARE:
                for k in range(SHARE, new_terms.shape[0], spread):
                    new_terms[k] = label[...]

        left = FF - i * TILE
        d_act = dot_both_t(d_branch[...], matrix(w_2), d_inner_down[...], down_2[0, 0].T)
        x = gate[...].astype(F32)
        t = gelu_parts(x)
        half = 0.5 * (1.0 + t)
        slope = half + 0.5 * x * (1.0 - t * t) * (
            0.7978845608028654 * (1.0 + 3 * 0.044715 * x * x)
        )
        keep = lax.broadcasted_iota(jnp.int32, (1, TILE), 1) < left
        value = jnp.where(keep, slope * d_act, 0.0).astype(BF16)
        wide[:, pl.ds(pl.multiple_of(i * TILE, LANES), TILE)] = value
        made = (
            dot_l(inner_up[...], value).astype(BF16),
            dot_l(d_inner_down[...], (x * half).astype(BF16)).astype(BF16),
        )

        def put_wide(panels):
            for kind in range(2):
                for p in panels:
                    tile = made[kind][:, p * LANES : (p + 1) * LANES]
                    new_terms[place(90 + 34 * kind + 4 * i + p)] = tile

        put_wide(range(2))

        @pl.when(i < middle_at - 1)
        def _():
            put_wide(range(2, 4))


    @pl.when(jnp.logical_and(i >= middle_at, i < turn_at))
    def _():
        at_step(middle_at)(load_normed_two().start)

        @pl.when(i < turn_at - 1)
        def _():
            w = jnp.concatenate([matrix(w_1, 34), matrix(w_1_odd, 34)], axis=0)
            d_normed[i - middle_at] = dot_t(wide[:, : 34 * LANES], w)

        @at_step(turn_at - 1)
        def _():
            w = jnp.concatenate([matrix(w_1, 34), up_1[0, 0, :, : 34 * LANES]], axis=0)
            value = dot_t(wide[:, : 34 * LANES], w)
            d_normed[PAIRS - 1, :, :LANES] = value[:, :LANES]
            d_inner_up[...] = value[:, LANES : LANES + R].astype(BF16)

    def joined():
        parts = [d_normed[k] for k in range(PAIRS - 1)]
        return jnp.concatenate(parts + [d_normed[PAIRS - 1, :, :LANES]], axis=1)

    @at_step(turn_at)
    def _():
        load_qkv().start()
        load_middle().wait()
        d_two = joined() + dot(d_inner_up[...], narrow[0, 0])
        value = gradient[...] + layer_norm_back(d_two, residual[...], vec[2:3])
        load_hidden().start()
        new_gradient[...] = value
        d_out = value.astype(BF16)
        d_inner_o = dot_t(d_out, attn[0, 7]).astype(BF16)
        wide[:, 3 * D :] = (dot_t(d_out, matrix(w_o)) + dot(d_inner_o, attn[0, 3])).astype(BF16)
        put(3, dot_l(d_inner_o, attended[...]))
        put(7, dot_l(inner_o[...], d_out))
        load_normed_two().wait()
        put(8, dot_l(d_inner_up[...], d_branch[...]))
        load_normed().start()
        load_qkv().wait()
        rows = gradient.shape[0]
        lane = lax.broadcasted_iota(jnp.int32, (rows, LANES), 1)
        delta = jnp.zeros((rows, LANES), F32)
        marked = (first_lane(rows, F32(1.0)), bias[...], None)
        for h in range(H):
            for c in range(3):
                part = wide[:, c * D + h * HD : c * D + (h + 1) * HD]
                heads[c, h] = pad_lanes(part, marked[c])
            do = wide[:, 3 * D + h * HD : 3 * D + (h + 1) * HD]
            heads[3, h] = pad_lanes(do)
            o = attended[:, h * HD : (h + 1) * HD].astype(F32)
            d = jnp.sum(do.astype(F32) * o, axis=1, keepdims=True)
            delta = jnp.where(lane == h, d, delta)
        stat_t[...] = stats[...].T
        delta_t[...] = delta.T

    @pl.when(jnp.logical_and(i >= att_at, i < input_at))
    def _():
        for twin in range(FOUR):
            h = (i - att_at) * FOUR + twin
            q, k, do = heads[0, h], heads[1, h], heads[3, h]
            p = jnp.exp2(dot_t(k, q) * C2 - stat_t[pl.ds(h, 1), :])
            dv = dot(p.astype(BF16), do)
            dp = dot_t(heads[2, h], do)
            ds = (p * (dp - delta_t[pl.ds(h, 1), :])).astype(BF16)
            dk = dot(ds, q)
            dq = dot(k.T, ds)
            heads[2, h] = dv.astype(BF16)
            heads[1, h] = (dk * SCALE).astype(BF16)
            heads[0, h] = (dq * SCALE).astype(BF16).T

    @pl.when(i >= input_at)
    def _():
        @at_step(input_at)
        def _():
            load_normed().wait()
            for c in range(3):
                for h in range(H):
                    wide[:, c * D + h * HD : c * D + (h + 1) * HD] = heads[c, h][:, :HD]
            for c in range(3):
                part = wide[:, c * D : (c + 1) * D]
                put(4 + c, dot_l(inner_qkv[:, c * R : (c + 1) * R], part))

        @pl.when(i < last)
        def _():
            w = jnp.concatenate([matrix(w_qkv), matrix(w_qkv_odd)], axis=0)
            d_normed[i - input_at] = dot_t(wide[:, : 3 * D], w)

        @at_step(last)
        def _():
            w = jnp.concatenate([matrix(w_qkv), up[0]], axis=0)
            value = dot_t(wide[:, : 3 * D], w)
            d_normed[PAIRS - 1, :, :LANES] = value[:, :LANES]
            inner = value[:, LANES : LANES + 3 * R].astype(BF16)
            made = dot_l(inner, d_branch[...])
            for c in range(3):
                put(c, made[c * R : (c + 1) * R])
            load_hidden().wait()
            d_one = joined() + dot(inner, attn[0, 0:3].reshape(3 * R, D))
            new_gradient[...] += layer_norm_back(d_one, residual[...], vec[0:1])

    if adapters:

        @at_step(last)
        def _():
            finish()
            swap.wait()


def layer_backward(
    layer, gradient, saved, weights, tables, bias, label, spread, adapters=0, terms=None, half=None
):
    hidden, normed, inner_qkv, qkv, stats, attended, inner_o, middle, normed_two, inner_up, gate, inner_down = saved
    w_qkv, w_o, w_1, w_2, vectors, _ = weights
    attn, narrow, wide, up_diagonal = tables
    rows = gradient.shape[0]

    def step(i, k):
        return jnp.minimum(jnp.maximum(i - BACKWARD_AT[k], 0), BACKWARD_STEPS[k] - 1)

    def cols(count, width, k):
        return pl.BlockSpec((count, width), lambda i: (0, step(i, k)))

    hbm = pl.BlockSpec(memory_space=pl.ANY)
    operands = [
        (whole((rows, D)), gradient),
        (unit_block(TILE // 16, 9, lambda i: (TILES_AT[3] // 9 * 16 // TILE + step(i, 0), 0, 0, 0)), w_2),
        (cols(rows, TILE, 0), gate),
        (pl.BlockSpec((1, 1, R, TILE), lambda i: (layer, 1, 0, step(i, 0))), wide),
        (whole((rows, R)), inner_down),
        (whole((rows, R)), inner_up),
        (unit_block(8, PANELS[2], lambda i: (9 + 2 * step(i, 1), 0, 0, 0)), w_1),
        (unit_block(8, PANELS[2], lambda i: (10 + jnp.minimum(2 * step(i, 1), 7), 0, 0, 0)), w_1),
        (of_layer(layer, 1, R, WIDE), wide),
        (of_layer(layer, 2, R, D), narrow),
        (hbm, normed_two),
        (whole((8, D)), vectors),
        (OUT_BLOCK, w_o),
        (of_layer(layer, 8, R, D), attn),
        (whole((R, LANES)), label),
        (whole((rows, R)), inner_o),
        (whole((rows, D)), attended),
        (whole((rows, LANES - HD)), bias),
        (whole((rows, LANES)), stats),
        (unit_block(8, 27, lambda i: (2 * step(i, 4), 0, 0, 0)), w_qkv),
        (unit_block(8, 27, lambda i: (jnp.minimum(2 * step(i, 4) + 1, 8), 0, 0, 0)), w_qkv),
        (of_layer(layer, 3 * R, 3 * D), up_diagonal),
        (whole((rows, 3 * R)), inner_qkv),
        (hbm, middle),
        (hbm, qkv),
        (hbm, hidden),
        (hbm, normed),
    ]
    outs = [
        (whole((rows, D)), struct((rows, D), F32)),
        (whole((32 * spread, R, LANES)), struct((32 * spread, R, LANES), BF16)),
    ]
    scratch = [
        pltpu.VMEM((rows, D), BF16),
        pltpu.VMEM((rows, R), BF16),
        pltpu.VMEM((rows, R), BF16),
        pltpu.VMEM((rows, WIDE), BF16),
        pltpu.VMEM((rows, D), F32),
        pltpu.VMEM((PAIRS, rows, PAIR), F32),
        pltpu.VMEM((4, H, rows, LANES), BF16),
        pltpu.VMEM((LANES, rows), F32),
        pltpu.VMEM((LANES, rows), F32),
        pltpu.SemaphoreType.DMA((3,)),
    ]
    params = dict(vmem_limit_bytes=VMEM_MOST)
    if adapters:
        operands += [(hbm, terms), (hbm, half)]
        block = 2 * adapters * SHARE_ROWS
        outs += [(hbm, struct((block, LANES), BF16)), (hbm, struct((16 * block, LANES), BF16))]
        outs += [(hbm, struct(half.shape, BF16))]
        outs += [(whole((terms.shape[0], LANES)), struct((terms.shape[0], LANES), F32))]
        scratch += share_scratch(terms.shape[0], adapters, SHARE + 1) + [pltpu.SemaphoreType.DMA((2,))]
        scratch += gather_semaphores()
        params.update(collective_id=4, has_side_effects=True)
    return pl.pallas_call(
        functools.partial(backward_kernel, adapters, spread),
        grid=(sum(BACKWARD_STEPS),),
        in_specs=[spec for spec, _ in operands],
        out_specs=[spec for spec, _ in outs],
        out_shape=[shape for _, shape in outs],
        scratch_shapes=scratch,
        cost_estimate=pl.CostEstimate(
            flops=2 * rows * D * (4 * D + 2 * FF) + 20 * rows * rows * D,
            bytes_accessed=2 * D * (4 * D + 2 * FF) + 40 * rows * D,
            transcendentals=H * rows * rows,
        ),
        compiler_params=pltpu.CompilerParams(**params),
        name="layer_backward_share" if adapters else "layer_backward",
    )(*[operand for _, operand in operands])


VECTOR_ROWS = 240


def read_vectors(block, vectors, b_1, rows):
    rows[...] = block[...].astype(F32)
    for p in range(D // LANES):
        vectors[:, p * LANES : (p + 1) * LANES] = rows[pl.ds(p, 8, stride=D // LANES), :]
    b_1[...] = jnp.zeros_like(b_1)
    first = 8 * D // LANES
    for p in range(-(-FF // LANES)):
        width = min(LANES, FF - p * LANES)
        b_1[:, p * LANES : p * LANES + width] = rows[first + p : first + p + 1, :width]


def layer_vectors(flat):
    return pl.pallas_call(
        read_vectors,
        grid=(1,),
        in_specs=[pl.BlockSpec((VECTOR_ROWS, LANES), lambda i: (16 * TILES_END // VECTOR_ROWS, 0))],
        out_specs=[whole((8, D)), whole((1, WIDE))],
        out_shape=[struct((8, D), F32), struct((1, WIDE), F32)],
        scratch_shapes=[pltpu.VMEM((VECTOR_ROWS, LANES), F32)],
        name="layer_vectors",
    )(flat)


def prepare_kernel(
    scalars, attn_in, narrow_in, wide_in, mine, other, block, attn, narrow, wide, diagonal, bias, hidden, label,
    vectors, b_1, rows,
):
    slot = scalars[5]
    length, live = scalars[2 + slot], jnp.where(slot < scalars[4], 1, 0)
    read_vectors(block, vectors, b_1, rows)
    label[...] = jnp.full(label.shape, scalars[slot], jnp.int32).astype(F32).astype(BF16)
    attn[...] = attn_in[:, :, 0]
    narrow[...] = narrow_in[:, :, 0]
    wide[...] = jnp.zeros_like(wide)
    wide[:, :, :, :FF] = wide_in[:, :, 0]
    diagonal[...] = jnp.zeros_like(diagonal)
    for layer in range(attn.shape[0]):
        for c in range(3):
            diagonal[layer, c * R : (c + 1) * R, c * D : (c + 1) * D] = attn_in[layer, 4 + c, 0]
    bias[...] = key_bias(bias.shape[0], length)
    half = mine.shape[1]
    row = lax.broadcasted_iota(jnp.int32, (half, 1), 0)

    def place(at, value):
        keep = jnp.where(row + at < length, live, 0) > 0
        hidden[at : at + half] = jnp.where(keep, value.astype(F32), 0.0)

    for first in range(2):

        @pl.when(slot == first)
        def _(first=first):
            place(first * half, mine[0])
            place((1 - first) * half, other[...])


def prepare(scalars, attention_table, narrow_table, wide_table, activations, other, flat):
    layers = attention_table.shape[0]
    rows = 2 * other.shape[0]

    def picked(kinds, width):
        return pl.BlockSpec((layers, kinds, 1, R, width), lambda i, k: (0, 0, k[k[5]], 0, 0))

    def full(*shape):
        return pl.BlockSpec(shape, lambda i, k: (0,) * len(shape))

    shapes = [
        ((layers, 8, R, D), BF16),
        ((layers, 2, R, D), BF16),
        ((layers, 2, R, WIDE), BF16),
        ((layers, 3 * R, 3 * D), BF16),
        ((rows, LANES - HD), BF16),
        ((rows, D), F32),
        ((R, LANES), BF16),
        ((8, D), F32),
        ((1, WIDE), F32),
    ]
    return pl.pallas_call(
        prepare_kernel,
        grid_spec=pltpu.PrefetchScalarGridSpec(
            num_scalar_prefetch=1,
            grid=(1,),
            in_specs=[
                picked(8, D),
                picked(2, D),
                picked(2, FF),
                pl.BlockSpec((1,) + other.shape, lambda i, k: (k[5], 0, 0)),
                full(*other.shape),
                pl.BlockSpec((VECTOR_ROWS, LANES), lambda i, k: (16 * TILES_END // VECTOR_ROWS, 0)),
            ],
            out_specs=[full(*shape) for shape, _ in shapes],
            scratch_shapes=[pltpu.VMEM((VECTOR_ROWS, LANES), F32)],
        ),
        out_shape=[struct(*shape) for shape in shapes],
        compiler_params=pltpu.CompilerParams(vmem_limit_bytes=VMEM_LIMIT),
        name="prepare",
    )(scalars, attention_table, narrow_table, wide_table, activations, other, flat)


def local(
    activations,
    group_image_count,
    image_adapter_index,
    lengths,
    frozen,
    attention_adapter_weights,
    narrow_adapter_weights,
    broad_adapter_weights,
    cotangent,
):
    slots, local_len, _ = activations.shape
    seq_parts = lax.axis_size("seq")
    fsdp_parts = lax.axis_size("fsdp")
    device_count = seq_parts * fsdp_parts
    me = lax.axis_index("seq")
    seq_total = local_len * seq_parts
    layer_count = frozen.shape[0]
    adapters = attention_adapter_weights.shape[2]
    parts = seq_parts // slots
    on_block = (fsdp_parts, seq_parts, slots, layer_count) == (16, 2, 2, 2)
    slot = me // parts
    part = me % parts
    tokens = seq_total // parts
    groups = [[s * parts + p for p in range(parts)] for s in range(slots)]

    def to_image(v):
        if parts == 1 and slots == 2:
            mine = lax.dynamic_index_in_dim(v, slot, 0, keepdims=False)
            other = lax.dynamic_index_in_dim(v, 1 - slot, 0, keepdims=False)
            other = lax.ppermute(other, "seq", [(0, 1), (1, 0)])
            return jnp.where(
                slot == 0,
                jnp.concatenate([mine, other], 0),
                jnp.concatenate([other, mine], 0),
            )
        whole = lax.all_gather(v, "seq", axis=1, tiled=True)
        whole = lax.dynamic_index_in_dim(whole, slot, 0, keepdims=False)
        return lax.dynamic_slice_in_dim(whole, part * tokens, tokens, 0)

    def half_of(v, which):
        return lax.dynamic_slice_in_dim(v, which * local_len, local_len, 0)

    def to_tokens(v, other=None):
        if parts == 1 and slots == 2:
            mine = half_of(v, slot)
            if other is None:
                other = lax.ppermute(half_of(v, 1 - slot), "seq", [(0, 1), (1, 0)])
            return jnp.where(slot == 0, jnp.stack([mine, other]), jnp.stack([other, mine]))
        whole = lax.all_gather(v, "seq", axis=0, tiled=True).reshape(slots, seq_total, -1)
        return lax.dynamic_slice_in_dim(whole, me * local_len, local_len, 1)

    length = lax.dynamic_slice_in_dim(lengths, slot, 1, 0)
    adapter = lax.dynamic_index_in_dim(image_adapter_index, slot, 0, keepdims=False)
    is_live = slot < group_image_count[0]
    positions = part * tokens + jnp.arange(tokens, dtype=jnp.int32)
    row_mask = ((positions < length[0]) & is_live).astype(F32)[:, None]
    shards = lax.optimization_barrier(frozen.reshape(layer_count, -1, LANES))
    tiles = -(-(TILES_END + TILES_VECTORS) // (2 * fsdp_parts)) * 2
    if on_block:
        flat, *shards = first_gather([shards[layer] for layer in range(layer_count)], tiles)
    else:
        steps = [(d, d + 1) for d in range(fsdp_parts - 1)]
        steps = (steps, [(b, a) for a, b in steps])
        index = lax.axis_index("fsdp").astype(jnp.int32).reshape(1)
        shards = [lay_shard(index, shards[layer], tiles, steps) for layer in range(layer_count)]
    if on_block:
        other = lax.dynamic_index_in_dim(activations, 1 - slot, 0, keepdims=False)
        other = lax.ppermute(other, "seq", [(0, 1), (1, 0)])
        scalars = jnp.concatenate(
            [image_adapter_index, lengths, group_image_count, slot.astype(jnp.int32)[None]]
        )
        prepared = prepare(
            scalars,
            attention_adapter_weights,
            narrow_adapter_weights,
            broad_adapter_weights,
            activations,
            other,
            flat,
        )
        tables, (bias, hidden, label) = prepared[:4], prepared[4:7]
    else:
        def pick(table):
            return lax.dynamic_index_in_dim(table, adapter, 2, keepdims=False)

        attention_adapters = pick(attention_adapter_weights)
        narrow_adapters = pick(narrow_adapter_weights)
        wide_adapters = pick(broad_adapter_weights)
        wide_adapters = jnp.pad(wide_adapters, ((0, 0), (0, 0), (0, 0), (0, WIDE - FF)))
        lane = lax.broadcasted_iota(jnp.int32, (tokens, LANES - HD), 1)
        key = lax.broadcasted_iota(jnp.int32, (tokens, LANES - HD), 0)
        bias = jnp.where((lane == 0) & (key >= length[0]), NEG, 0.0).astype(BF16)
        hidden = to_image(activations).astype(F32) * row_mask
        up_diagonals = jnp.stack(
            [
                jnp.concatenate(
                    [
                        jnp.pad(attention_adapters[layer, 4 + c], ((0, 0), (c * D, (2 - c) * D)))
                        for c in range(3)
                    ]
                )
                for layer in range(layer_count)
            ]
        )
    stored = []
    weights = []
    for layer in range(layer_count):
        if not on_block:
            flat = lax.all_gather(shards[layer], "fsdp", axis=0, tiled=True)
            flat = jnp.pad(flat, ((0, 16 * TILES_HELD - flat.shape[0]), (0, 0)))
        if layer == layer_count - 1:
            cotangent, flat = lax.optimization_barrier((cotangent, flat))
            d_output = to_image(cotangent)
        w_qkv, w_o, w_1, w_2 = (flat.reshape(-1, panels, 16, LANES) for panels in PANELS)
        if on_block:
            vectors, b_1 = prepared[7:9] if layer == 0 else layer_vectors(flat)
            weights.append((w_qkv, w_o, w_1, w_2, vectors, b_1))
        else:
            vectors = lax.slice_in_dim(flat, 16 * TILES_END, 16 * TILES_END + 106, axis=0).reshape(-1)
            vectors, b_1 = vectors[: 8 * D].reshape(8, D).astype(F32), vectors[8 * D : 8 * D + FF]
            b_1 = jnp.pad(b_1.astype(F32), (0, WIDE - FF))[None, :]
            attn, narrow, wide = attention_adapters[layer], narrow_adapters[layer], wide_adapters[layer]
            weights.append((w_qkv, w_o, w_1, w_2, vectors, attn, narrow, wide))
        keys = None
        if on_block:
            shard = shards[layer + 1] if layer + 1 < layer_count else None
            made = layer_forward(layer, bias, hidden, weights[layer], tables, shard)
            normed, inner_qkv, qkv, attended, stats, inner_o, middle = made[:7]
            normed_two, inner_up, gate, inner_down, next_hidden = made[7:12]
            flat = made[12] if shard is not None else None
        else:
            normed, inner_qkv, qkv = qkv_forward(hidden, w_qkv, vectors, attn)
            keys = lax.all_gather(
                qkv[:, D:], "seq", axis=0, tiled=True, axis_index_groups=groups
            )
            attended, stats = attn_fwd(length, qkv, keys)
            inner_o, middle, normed_two, inner_up, gate, activated = up_forward(
                attended, hidden, w_o, vectors, attn, narrow, w_1, b_1, wide
            )
            inner_down, next_hidden = down_forward(
                activated, middle, w_2, vectors[7:8], narrow, wide
            )
        stored.append(
            (
                hidden,
                normed,
                inner_qkv,
                qkv,
                keys,
                stats,
                attended,
                inner_o,
                middle,
                normed_two,
                inner_up,
                gate,
                inner_down,
            )
        )
        hidden = next_hidden
    output = (hidden * row_mask).astype(BF16)
    other_half = None
    gradient = d_output.astype(F32) * row_mask
    collected = [None] * layer_count
    terms = None
    for layer in reversed(range(layer_count)):
        (
            layer_input,
            normed,
            inner_qkv,
            qkv,
            keys,
            stats,
            attended,
            inner_o,
            middle,
            normed_two,
            inner_up,
            gate,
            inner_down,
        ) = stored[layer]
        if not on_block:
            w_qkv, w_o, w_1, w_2, vectors, attn, narrow, wide = weights[layer]
        if on_block:
            saved = (
                layer_input, normed, inner_qkv, qkv, stats, attended, inner_o, middle, normed_two, inner_up,
                gate, inner_down,
            )
            hosting = layer + 1 < layer_count
            spread = SHARE if layer == 0 else SHARE + 1
            made = layer_backward(
                layer,
                gradient,
                saved,
                weights[layer],
                tables,
                bias,
                label,
                spread,
                adapters if hosting else 0,
                terms,
                half_of(output, 1 - slot),
            )
            gradient, terms = made[:2]
            terms = terms.reshape(device_count, spread, R, LANES)
            if hosting:
                collected[layer + 1], other_half, names = made[3:6]
            if layer == 0:
                sums = share_terms(terms, names, adapters)
                collected[layer] = gather_blocks(sums, 2, 16 * sums.shape[0])
            continue
        if not on_block:
            d_gate, g_wide, d_inner_up, g_up_2 = gate_backward(
                gradient, w_2, gate, narrow, wide, inner_down, inner_up
            )
            d_middle, d_attended, g_middle = middle_backward(
                d_gate, w_1, d_inner_up, narrow, normed_two, middle, gradient, vectors, w_o, attn,
                inner_o, attended,
            )
            d_qkv = attn_bwd(length, qkv, d_attended, attended, stats, keys)
            if parts > 1:
                d_keys = lax.psum_scatter(
                    d_qkv[1].astype(F32),
                    "seq",
                    scatter_dimension=0,
                    tiled=True,
                    axis_index_groups=groups,
                )
                d_qkv = jnp.concatenate([d_qkv[0], d_keys.astype(BF16)], axis=1)
            else:
                d_qkv = d_qkv[0]
            gradient, g_input = input_backward(
                d_qkv, w_qkv, attn, normed, inner_qkv, layer_input, d_middle, vectors
            )
        rows_narrow = jnp.concatenate(
            [
                g_input[: 3 * R],
                g_middle[:R],
                g_input[3 * R :],
                g_middle[R:],
                g_up_2,
            ]
        )
        rows_narrow = rows_narrow.astype(BF16)
        rows_wide = g_wide[:, :FF].astype(BF16)

        def shares(rows):
            share = -(-rows.shape[0] // device_count)
            rows = jnp.pad(rows, ((0, share * device_count - rows.shape[0]), (0, 0)))
            return rows.reshape(device_count, share * rows.shape[1])

        terms = [shares(rows_narrow), shares(rows_wide)]
        used = terms[0].shape[1] + terms[1].shape[1]
        label = jnp.broadcast_to(adapter.astype(BF16), (device_count, -used % LANES + LANES))
        terms = lax.all_to_all(
            jnp.concatenate(terms + [label], axis=1),
            ("fsdp", "seq"),
            split_axis=0,
            concat_axis=0,
            tiled=True,
        )
        choice = jnp.arange(adapters, dtype=F32)[:, None] == terms[:, used].astype(F32)[None, :]
        sums = jnp.dot(choice.astype(F32), terms.astype(F32), precision=lax.Precision.HIGHEST)
        sums = lax.all_gather(sums.astype(BF16), ("fsdp", "seq")).transpose(1, 0, 2)
        split = -(-10 * R // device_count) * D

        def table(part, count, width):
            part = part.reshape(adapters, -1, width)[:, : count * R]
            return part.reshape(adapters, count, R, width).transpose(1, 0, 2, 3).astype(F32)

        collected[layer] = (table(sums[:, :, :split], 10, D), table(sums[:, :, split:used], 2, FF))
    if on_block:
        grad_attn, grad_narrow, grad_wide = gradient_tables(collected, adapters)
    else:
        grad_attn = jnp.stack([entry[0][0:8] for entry in collected], axis=0)
        grad_narrow = jnp.stack([entry[0][8:10] for entry in collected], axis=0)
        grad_wide = jnp.stack([entry[1] for entry in collected], axis=0)
    output = to_tokens(output, other_half)
    input_grad = to_tokens((gradient * row_mask).astype(BF16)).astype(F32)
    return (output, input_grad, grad_attn, grad_narrow, grad_wide)


def solution(mesh):
    in_specs = (
        P("fsdp", "seq", None),
        P("fsdp"),
        P("fsdp"),
        P("fsdp"),
        P(None, "fsdp"),
        P(),
        P(),
        P(),
        P("fsdp", "seq", None),
    )
    out_specs = (P("fsdp", "seq", None), P("fsdp", "seq", None), P(), P(), P())
    return jax.shard_map(local, mesh=mesh, in_specs=in_specs, out_specs=out_specs, check_vma=False)
```
